32 devices in a mesh: px: 4 (over z), py: 8 (over y, x, core).
Axes of the slice: x: 2, y: 2, z: 4, core: 2. Of those that a mesh axis runs over, the one named last changes fastest.
Arguments:
- charge: float32 [32, 768, 768], P(('px', 'py')), may hold values from -5 to 5
Outputs:
- potential_field: float32 [32, 768, 768], P(('px', 'py'))
The draws below stay inside these ranges and needn't reach their ends.
All inputs are finite; a program needn't handle non-finite values.
Results may differ from the reference program's by a relative error of at most 0.0003.
Values sent between devices are 32-bit elements; how exact they have to be, the bound alone decides.
No kernel may reach another device: no remote copies, remote signals or barrier semaphores. Data moves between devices by JAX's collectives and lax.ppermute only.
A program may use at most 192 MiB of HBM per device.

```python
import math
import jax
import jax.numpy as jnp
from jax import lax

GRID = 768
PANELS = 128
ZD = 1
NZ = 32


def draw_charge(key, part):
    depth_index = jnp.arange(NZ, dtype=jnp.float32)[:, None, None]
    row_index = jnp.arange(GRID, dtype=jnp.float32)[None, :, None]
    col_index = jnp.arange(GRID, dtype=jnp.float32)[None, None, :]
    centre = (GRID - 1) / 2.0
    middle = (NZ - 1) / 2.0
    radial_width = GRID / 5.0
    depth_width = NZ / 6.0
    envelope = jnp.exp(-((row_index - centre) * (row_index - centre) + (col_index - centre) * (col_index - centre)) / (2.0 * radial_width * radial_width) - (depth_index - middle) * (depth_index - middle) / (2.0 * depth_width * depth_width))
    jitter = jax.random.truncated_normal(key, -4.0, 4.0, (NZ, GRID, GRID), jnp.float32)
    strength = 0.4
    return (jitter + strength / (radial_width * depth_width) * envelope).astype(jnp.float32)


def setup_inputs(seed: int = 0) -> dict:
    seeds = jax.random.split(jax.random.key(seed), 2)
    charge = draw_charge(jax.random.fold_in(seeds[1], 71), 0)
    return {"charge": charge}


HIGHEST = lax.Precision.HIGHEST
FOUR_PI = 4.0 * math.pi

def sine_table(length):
    orders = jnp.arange(1, length + 1, dtype=jnp.int32)
    phases = orders[:, None] * orders[None, :] % (2 * (length + 1))
    factor = (2.0 / (length + 1.0)) ** 0.5
    return factor * jnp.sin(jnp.pi * phases.astype(jnp.float32) / (length + 1.0))

def eigen_values(length):
    orders = jnp.arange(1, length + 1, dtype=jnp.float32)
    return 2.0 - 2.0 * jnp.cos(jnp.pi * orders / (length + 1.0))

def plane_sine(planes, sine_grid):
    along_x = jnp.einsum('zyx,xk->zyk', planes, sine_grid, precision=HIGHEST)
    return jnp.einsum('ky,zyx->zkx', sine_grid, along_x, precision=HIGHEST)

def poisson_solve(source, sine_grid, sine_depth, divisor):
    spectrum = plane_sine(source, sine_grid)
    spectrum = jnp.einsum('wz,zyx->wyx', sine_depth, spectrum, precision=HIGHEST) / divisor
    spectrum = jnp.einsum('wz,zyx->wyx', sine_depth, spectrum, precision=HIGHEST)
    return plane_sine(spectrum, sine_grid)

def panel_centres(panels, grid_cells, depth_planes, side_rows):
    panel_edge = grid_cells // panels
    lane_centre = jnp.arange(panels, dtype=jnp.float32) * panel_edge + (panel_edge - 1) / 2.0
    face_count = panels * panels
    face_rows = jnp.repeat(lane_centre, panels)
    face_cols = jnp.tile(lane_centre, panels)
    level_centre = jnp.arange(side_rows, dtype=jnp.float32) * depth_planes + (depth_planes - 1) / 2.0
    low_edge = jnp.full((panels,), -1.0, jnp.float32)
    high_edge = jnp.full((panels,), float(grid_cells), jnp.float32)
    side_rows_c = jnp.tile(jnp.concatenate([low_edge, high_edge, lane_centre, lane_centre]), side_rows)
    side_cols = jnp.tile(jnp.concatenate([lane_centre, lane_centre, low_edge, high_edge]), side_rows)
    side_depth = jnp.repeat(level_centre, 4 * panels)
    centre_depth = jnp.concatenate([jnp.full((face_count,), -1.0, jnp.float32), jnp.full((face_count,), float(depth_planes * side_rows), jnp.float32), side_depth])
    centre_row = jnp.concatenate([face_rows, face_rows, side_rows_c])
    centre_col = jnp.concatenate([face_cols, face_cols, side_cols])
    return (centre_depth, centre_row, centre_col)

def reference(charge):
    panel_edge = GRID // PANELS
    side_rows = NZ // ZD
    face_count = PANELS * PANELS
    sine_grid = sine_table(GRID)
    sine_depth = sine_table(NZ)
    eigen_grid = eigen_values(GRID)
    divisor = eigen_values(NZ)[:, None, None] + eigen_grid[None, :, None] + eigen_grid[None, None, :]
    screened = poisson_solve(charge, sine_grid, sine_depth, divisor)

    def block_sum(one_plane):
        return one_plane.reshape(PANELS, panel_edge, PANELS, panel_edge).sum(axis=(1, 3)).reshape(-1)

    def line_sums(boundary_line):
        return boundary_line.reshape(side_rows, ZD, PANELS, panel_edge).sum(axis=(1, 3))
    sides = jnp.stack([line_sums(screened[:, 0, :]), line_sums(screened[:, -1, :]), line_sums(screened[:, :, 0]), line_sums(screened[:, :, -1])], axis=1)
    panel_charge = jnp.concatenate([block_sum(screened[0]), block_sum(screened[-1]), sides.reshape(-1)])
    centres = panel_centres(PANELS, GRID, ZD, side_rows)
    softening = panel_edge * panel_edge / 4.0

    def field_block(targets):
        distance = (targets[0][:, None] - centres[0][None, :]) * (targets[0][:, None] - centres[0][None, :])
        distance = distance + (targets[1][:, None] - centres[1][None, :]) * (targets[1][:, None] - centres[1][None, :])
        distance = distance + (targets[2][:, None] - centres[2][None, :]) * (targets[2][:, None] - centres[2][None, :])
        return lax.optimization_barrier(jnp.sum(panel_charge[None, :] * lax.rsqrt(distance + softening), axis=1)) / FOUR_PI
    blocked = tuple((column.reshape(-1, 4 * PANELS) for column in centres))
    potential = lax.map(field_block, blocked).reshape(-1)
    face_low = jnp.repeat(jnp.repeat(potential[:face_count].reshape(PANELS, PANELS), panel_edge, axis=0), panel_edge, axis=1)
    face_high = jnp.repeat(jnp.repeat(potential[face_count:2 * face_count].reshape(PANELS, PANELS), panel_edge, axis=0), panel_edge, axis=1)
    side_field = potential[2 * face_count:].reshape(side_rows, 4, PANELS)
    side_lines = jnp.repeat(jnp.repeat(side_field, panel_edge, axis=2), ZD, axis=0)
    source = charge.at[0].add(face_low)
    source = source.at[-1].add(face_high)
    source = source.at[:, 0, :].add(side_lines[:, 0, :])
    source = source.at[:, -1, :].add(side_lines[:, 1, :])
    source = source.at[:, :, 0].add(side_lines[:, 2, :])
    source = source.at[:, :, -1].add(side_lines[:, 3, :])
    return poisson_solve(source, sine_grid, sine_depth, divisor)
```

```python
import functools
import math

import jax
import jax.numpy as jnp
import numpy as np
from jax import lax
from jax.experimental import pallas as pl
from jax.experimental.pallas import tpu as pltpu
from jax.sharding import PartitionSpec as P

PANELS = 128
HIGHEST = lax.Precision.HIGHEST
FOUR_PI = 4.0 * math.pi
AXES = ("px", "py")


def dot(a, b, dims=((1,), (0,)), precision=HIGHEST):
    return lax.dot_general(
        a, b, (dims, ((), ())), precision=precision, preferred_element_type=jnp.float32
    )


def sine_table(n):
    order = np.arange(1, n + 1, dtype=np.int64)
    phase = (order[:, None] * order[None, :]) % (2 * (n + 1))
    return np.sqrt(2.0 / (n + 1)) * np.sin(np.pi * phase / (n + 1.0))


def eigen_values(n):
    return 2.0 - 2.0 * np.cos(np.pi * np.arange(1, n + 1) / (n + 1.0))


def fold_panels(grid, edge):
    sums = sine_table(grid).reshape(grid, PANELS, edge).sum(2)[:, : PANELS // 2]
    even = (np.arange(grid) % 2 == 0)[:, None]
    return np.concatenate([np.where(even, sums, 0.0), np.where(even, 0.0, sums)], axis=1)


def wave_basis(n):
    place = np.arange(n // 2) - (n - 1) / 2.0
    even = np.cos(np.pi * np.arange(n)[:, None] * place[None, :] / n)
    even *= np.sqrt(np.where(np.arange(n) == 0, 1.0, 2.0) / n)[:, None]
    odd = np.sin(np.pi * np.arange(1, n + 1)[:, None] * place[None, :] / n)
    odd *= np.sqrt(np.where(np.arange(1, n + 1) == n, 1.0, 2.0) / n)[:, None]
    return even, odd


def wave_values(n):
    distance = np.arange(n)[:, None]
    order = np.concatenate([np.arange(n), np.arange(1, n + 1)])[None, :]
    return np.where(distance == 0, 1.0, 2.0) * np.cos(np.pi * distance * order / n)


def panel_tables(depth, grid, edge):
    half = depth // 2
    soft = edge * edge / 4.0
    hb = PANELS // 2

    def kernel(dz, dy, dx):
        return 1.0 / np.sqrt(dz * dz + dy * dy + dx * dx + soft) / FOUR_PI

    step = edge * np.arange(PANELS, dtype=np.float64)
    near = step + (edge - 1) / 2.0 + 1.0
    vx = wave_values(PANELS)
    vz = wave_values(depth)
    even, odd = wave_basis(PANELS)
    zero = np.zeros_like(even)
    basis_x = np.concatenate(
        [np.concatenate([even, zero], 1), np.concatenate([zero, odd], 1)], 0
    )
    basis_z = np.stack(wave_basis(depth))
    face = []
    for sign in (1.0, -1.0):
        k = kernel(0.0, step[:, None], step[None, :])
        k = k + sign * kernel(depth + 1.0, step[:, None], step[None, :])
        face.append(vx.T @ k @ vx)
    z = np.arange(depth, dtype=np.float64)
    side = []
    for sign in (1.0, -1.0):
        k = kernel(z[:, None], 0.0, step[None, :])
        k = k + sign * kernel(z[:, None], grid + 1.0, step[None, :])
        side.append(np.stack([vz[:, :depth].T @ k @ vx, vz[:, depth:].T @ k @ vx]))
    j = np.arange(1, depth + 1, dtype=np.float64)
    k = kernel(j[:, None, None], near[None, :, None], step[None, None, :]) @ vx
    k_own, k_far = k[:half], k[::-1][:half]
    mixed = []
    for sign in (1.0, -1.0):
        m = k_own + sign * k_far
        front, back = m[:, :hb], m[:, ::-1][:, :hb]
        mixed.append(np.concatenate([front + back, front - back], 1))
    k = kernel(z[:, None, None], near[None, :, None], near[None, None, :])
    front, back = k[:, :hb], k[:, ::-1][:, :hb]
    k = np.concatenate([front + back, front - back], 1)
    front, back = k[:, :, :hb], k[:, :, ::-1][:, :, :hb]
    k = np.concatenate([front + back, front - back], 2).reshape(depth, -1)
    corner = [
        (vz[:, s * depth : (s + 1) * depth].T @ k).reshape(depth, PANELS, PANELS)
        for s in (0, 1)
    ]
    return dict(
        basis_x=basis_x,
        basis_z=basis_z,
        face=np.stack(face),
        side=np.stack(side, 1),
        mixed=np.stack(mixed),
        corner=np.stack(corner),
    )


def panel_potential(face, sides, tb):
    hb = PANELS // 2
    bx, bz = tb["basis_x"], tb["basis_z"]
    ein = functools.partial(jnp.einsum, precision=HIGHEST)
    out_face = 0.0
    out_side = []
    hat = ein("sapjb,mb->sapjm", sides, bx)
    zhat = ein("snj,sapjm->sapnm", bz, hat)
    side_zm = tb["side"][:, None] * zhat
    side_m = ein("snj,sapnm->sapjm", bz, side_zm)
    face_out_hat = []
    for axis in (0, 1):
        f = face if axis == 0 else face.swapaxes(1, 2)
        fx = ein("syb,mb->sym", f, bx)
        if axis == 0:
            full = ein("ny,sym->snm", bx, fx) * tb["face"]
            face_m = ein("ny,snm->sym", bx, full)
        else:
            face_m = 0.0
        mix = tb["mixed"].reshape(2, -1, 2, hb, 2 * PANELS)
        fq = fx.reshape(2, 1, 2, hb, 2 * PANELS)
        to_face = (mix * hat[:, axis].swapaxes(1, 2)[:, :, :, None, :]).sum(1)
        face_m = face_m + to_face.reshape(2, PANELS, 2 * PANELS)
        to_side = (mix * fq).sum(3).swapaxes(1, 2)
        face_out_hat.append(ein("sym,mb->syb", face_m, bx))
        out_side.append(ein("sapjm,mb->sapjb", (side_m[:, axis] + to_side)[:, None], bx)[:, 0])
    out_face = face_out_hat[0] + face_out_hat[1].swapaxes(1, 2)
    zs = ein("snj,sapjb->sapnb", bz, sides)
    n = zs.shape[3]
    corner = tb["corner"].reshape(2, n, 2, hb, 2, hb)
    ys = zs[:, 0].reshape(2, 2, n, 2, hb)
    xs = zs[:, 1].reshape(2, 2, n, 2, hb)
    to_y = jnp.einsum("sntbuc,suntb->stnuc", corner, xs, precision=HIGHEST)
    to_x = jnp.einsum("sntbuc,stnuc->suntb", corner, ys, precision=HIGHEST)
    both = jnp.stack([to_y, to_x], 1).reshape(2, 2, 2, n, PANELS)
    both = ein("snj,sapnb->sapjb", bz, both)
    return out_face, jnp.stack(out_side, 1) + both


def sweep_body(half_ref, f_ref, mu_ref, g_ref, last_ref):
    planes = f_ref.shape[0]
    upper = half_ref[0]
    diag = mu_ref[...] + 2.0
    coef = 1.0 / diag
    for j in range(planes):
        place = jnp.where(upper == 1, planes - 1 - j, j)
        if j == 0:
            value = f_ref[place] * coef
        else:
            coef = 1.0 / (diag - coef)
            value = (f_ref[place] + value) * coef
        g_ref[j] = value
    last_ref[...] = value


def sweep(upper, spectrum, mu):
    planes, rows, cols = spectrum.shape
    width = 128
    block = pl.BlockSpec((planes, rows, width), lambda i, u: (0, 0, i))
    flat = pl.BlockSpec((rows, width), lambda i, u: (0, i))
    return pl.pallas_call(
        sweep_body,
        grid_spec=pltpu.PrefetchScalarGridSpec(
            num_scalar_prefetch=1,
            grid=(cols // width,),
            in_specs=[block, flat],
            out_specs=[block, flat],
        ),
        out_shape=[
            jax.ShapeDtypeStruct(spectrum.shape, jnp.float32),
            jax.ShapeDtypeStruct((rows, cols), jnp.float32),
        ],
    )(upper, spectrum, mu)


def finish_body(half_ref, g_ref, mu_ref, far_ref, u_ref, edge_ref, coef_ref):
    planes = g_ref.shape[0]
    upper = half_ref[0]
    diag = mu_ref[...] + 2.0
    coef = 1.0 / diag
    coef_ref[0] = coef
    for j in range(1, planes):
        coef = 1.0 / (diag - coef)
        coef_ref[j] = coef
    value = (far_ref[...] + coef * g_ref[planes - 1]) / (1.0 - coef * coef)
    for j in range(planes - 1, -1, -1):
        value = g_ref[j] + coef_ref[j] * value
        u_ref[jnp.where(upper == 1, planes - 1 - j, j)] = value
    edge_ref[...] = value


def finish(upper, g, mu, far):
    planes, rows, cols = g.shape
    width = 128
    block = pl.BlockSpec((planes, rows, width), lambda i, u: (0, 0, i))
    flat = pl.BlockSpec((rows, width), lambda i, u: (0, i))
    return pl.pallas_call(
        finish_body,
        grid_spec=pltpu.PrefetchScalarGridSpec(
            num_scalar_prefetch=1,
            grid=(cols // width,),
            in_specs=[block, flat, flat],
            out_specs=[block, flat],
            scratch_shapes=[pltpu.VMEM((planes, rows, width), jnp.float32)],
        ),
        out_shape=[
            jax.ShapeDtypeStruct(g.shape, jnp.float32),
            jax.ShapeDtypeStruct((rows, cols), jnp.float32),
        ],
    )(upper, g, mu, far)


def ghost_body(
    half_ref, u_ref, mu_ref, row_ref, col_ref, along_ref, across_ref, near_ref, far_ref,
    out_ref, coef_ref, g_ref,
):
    planes, rows, width = u_ref.shape
    upper = half_ref[0]
    diag = mu_ref[...] + 2.0
    row_odd = lax.broadcasted_iota(jnp.int32, (rows, width), 0) % 2 == 1
    col_odd = lax.broadcasted_iota(jnp.int32, (rows, width), 1) % 2 == 1
    row_value, col_value = row_ref[...], col_ref[...]

    def layer(index):
        even = along_ref[index : index + 1, :]
        odd = along_ref[2 * planes + index : 2 * planes + index + 1, :]
        side_y = row_value * jnp.where(row_odd, odd, even)
        even = across_ref[:, index : index + 1]
        odd = across_ref[:, 2 * planes + index : 2 * planes + index + 1]
        return side_y + col_value * jnp.where(col_odd, odd, even)

    coef = 1.0 / diag
    own = (layer(0) + near_ref[...]) * coef
    far = (layer(planes) + far_ref[...]) * coef
    coef_ref[0] = coef
    g_ref[0] = own
    for j in range(1, planes):
        coef = 1.0 / (diag - coef)
        own = (layer(j) + own) * coef
        far = (layer(planes + j) + far) * coef
        coef_ref[j] = coef
        g_ref[j] = own
    value = (far + coef * own) / (1.0 - coef * coef)
    for j in range(planes - 1, -1, -1):
        value = g_ref[j] + coef_ref[j] * value
        place = jnp.where(upper == 1, planes - 1 - j, j)
        out_ref[place] = u_ref[place] + value


def add_ghost(upper, u, mu, row_value, col_value, along, across, near, far):
    planes, rows, cols = u.shape
    width = 128
    block = pl.BlockSpec((planes, rows, width), lambda i, u: (0, 0, i))
    flat = pl.BlockSpec((rows, width), lambda i, u: (0, i))
    return pl.pallas_call(
        ghost_body,
        grid_spec=pltpu.PrefetchScalarGridSpec(
            num_scalar_prefetch=1,
            grid=(cols // width,),
            in_specs=[
                block,
                flat,
                pl.BlockSpec((rows, 1), lambda i, u: (0, 0)),
                pl.BlockSpec((1, width), lambda i, u: (0, i)),
                pl.BlockSpec((4 * planes, width), lambda i, u: (0, i)),
                pl.BlockSpec((rows, 4 * planes), lambda i, u: (0, 0)),
                flat,
                flat,
            ],
            out_specs=block,
            scratch_shapes=[
                pltpu.VMEM((planes, rows, width), jnp.float32),
                pltpu.VMEM((planes, rows, width), jnp.float32),
            ],
        ),
        out_shape=jax.ShapeDtypeStruct(u.shape, jnp.float32),
    )(upper, u, mu, row_value, col_value, along, across, near, far)


def build(mesh, grid, depth):
    slow, fast = mesh.shape["px"], mesh.shape["py"]
    devices = slow * fast
    half = devices // 2
    rows = grid // half
    edge = grid // PANELS
    groups = [list(range(half)), list(range(half, devices))]
    tables = {
        name: value.astype(np.float32) for name, value in panel_tables(depth, grid, edge).items()
    }
    sine_np = sine_table(grid).astype(np.float32)
    eigen_np = eigen_values(grid)
    fold_np = fold_panels(grid, edge).astype(np.float32)

    def exchange(x):
        return lax.all_to_all(
            x, AXES, split_axis=0, concat_axis=0, tiled=True, axis_index_groups=groups
        )

    def hop(x, bit):
        return lax.ppermute(x, "px", [(i, i ^ bit) for i in range(slow)])

    def on_device(charge):
        rank = lax.axis_index(AXES)
        upper = (rank // half).astype(jnp.int32).reshape(1)
        is_upper = rank // half == 1
        start = (rank % half) * rows
        sine = jnp.asarray(sine_np)
        fold = jnp.asarray(fold_np)
        tb = {name: jnp.asarray(value) for name, value in tables.items()}
        eigen = jnp.asarray(eigen_np.astype(np.float32))
        edge_value = jnp.asarray(sine_np[:, 0])
        my_eigen = lax.dynamic_slice_in_dim(eigen, start, rows, 0)
        my_edge = lax.dynamic_slice_in_dim(edge_value, start, rows, 0)
        my_fold = lax.dynamic_slice_in_dim(fold, start, rows, 0)
        mu = my_eigen[:, None] + eigen[None, :]
        parity = jnp.arange(grid) % 2
        edge_pair = jnp.stack([edge_value * (parity == 0), edge_value * (parity == 1)])
        my_pair = jnp.stack([my_edge * (parity[:rows] == 0), my_edge * (parity[:rows] == 1)])

        plane = charge.reshape(grid, grid)
        spectrum = dot(sine, dot(plane, sine))
        spectrum = exchange(spectrum.reshape(half, rows, grid))
        g, last = sweep(upper, spectrum, mu)
        far = lax.ppermute(last, AXES, [(i, i ^ half) for i in range(devices)])
        u, outer = finish(upper, g, mu, far)

        face = dot(my_fold, dot(outer, fold), ((0,), (0,)))
        lines_y = jnp.einsum("tk,jkx->tjx", my_pair, u, precision=HIGHEST)
        lines_y = jnp.einsum("tjx,xb->tjb", lines_y, fold, precision=HIGHEST)
        lines_x = jnp.einsum("jkx,tx->tjk", u, edge_pair, precision=HIGHEST)
        lines_x = jnp.einsum("tjk,kb->tjb", lines_x, my_fold, precision=HIGHEST)
        lines = jnp.stack([lines_y, lines_x])
        lines = jnp.where(is_upper, lines[:, :, ::-1], lines)
        part = jnp.concatenate([face, lines.reshape(-1, PANELS)])
        part = lax.all_gather(part, "py", axis=0, tiled=False).sum(0)
        bit = 1
        while bit < slow // 2:
            part = part + hop(part, bit)
            bit *= 2
        other = hop(part, bit)
        both = jnp.stack([part + other, part - other]) * 0.5
        face_q = both[:, :PANELS]
        side_q = both[:, PANELS:].reshape(2, 2, 2, half, PANELS)
        face_v, side_v = panel_potential(face_q, side_q, tb)
        face_v = jnp.stack([face_v[0] + face_v[1], face_v[0] - face_v[1]])
        side_v = jnp.stack([side_v[0] + side_v[1], side_v[0] - side_v[1]])
        near, distant = (
            4.0 * dot(dot(my_fold, face_v[i]), fold, ((1,), (1,))) for i in (0, 1)
        )
        along = side_v[:, 0].swapaxes(0, 1).reshape(4 * half, PANELS)
        across = side_v[:, 1].swapaxes(0, 1).reshape(4 * half, PANELS)
        along = 4.0 * dot(along, fold, ((1,), (1,)))
        across = 4.0 * dot(my_fold, across, ((1,), (1,)))
        u = add_ghost(
            upper, u, mu, my_edge[:, None], edge_value[None, :], along, across, near, distant
        )
        u = exchange(u).reshape(grid, grid)
        return dot(dot(sine, u), sine)[None]

    return on_device


def solution(mesh):
    spec = P(AXES, None, None)

    def run(charge):
        depth, grid, _ = charge.shape
        body = build(mesh, grid, depth)
        return jax.shard_map(body, mesh=mesh, in_specs=(spec,), out_specs=spec, check_vma=False)(
            charge
        )

    return run
```

```python
import functools
import math

import jax
import jax.numpy as jnp
import numpy as np
from jax import lax
from jax.experimental import pallas as pl
from jax.experimental.pallas import tpu as pltpu
from jax.sharding import PartitionSpec as P

PANELS = 128
HIGHEST = lax.Precision.HIGHEST
HIGH = lax.Precision.HIGH
FOUR_PI = 4.0 * math.pi
AXES = ("px", "py")


def dot(a, b, dims=((1,), (0,)), precision=HIGHEST):
    return lax.dot_general(
        a, b, (dims, ((), ())), precision=precision, preferred_element_type=jnp.float32
    )


def sine_table(n):
    order = np.arange(1, n + 1, dtype=np.int64)
    phase = (order[:, None] * order[None, :]) % (2 * (n + 1))
    return np.sqrt(2.0 / (n + 1)) * np.sin(np.pi * phase / (n + 1.0))


def eigen_values(n):
    return 2.0 - 2.0 * np.cos(np.pi * np.arange(1, n + 1) / (n + 1.0))


def fold_panels(grid, edge):
    sums = sine_table(grid).reshape(grid, PANELS, edge).sum(2)[:, : PANELS // 2]
    even = (np.arange(grid) % 2 == 0)[:, None]
    return np.concatenate([np.where(even, sums, 0.0), np.where(even, 0.0, sums)], axis=1)


def wave_basis(n):
    place = np.arange(n // 2) - (n - 1) / 2.0
    even = np.cos(np.pi * np.arange(n)[:, None] * place[None, :] / n)
    even *= np.sqrt(np.where(np.arange(n) == 0, 1.0, 2.0) / n)[:, None]
    odd = np.sin(np.pi * np.arange(1, n + 1)[:, None] * place[None, :] / n)
    odd *= np.sqrt(np.where(np.arange(1, n + 1) == n, 1.0, 2.0) / n)[:, None]
    return even, odd


def wave_values(n):
    distance = np.arange(n)[:, None]
    order = np.concatenate([np.arange(n), np.arange(1, n + 1)])[None, :]
    return np.where(distance == 0, 1.0, 2.0) * np.cos(np.pi * distance * order / n)


def panel_tables(depth, grid, edge):
    half = depth // 2
    soft = edge * edge / 4.0
    hb = PANELS // 2

    def kernel(dz, dy, dx):
        return 1.0 / np.sqrt(dz * dz + dy * dy + dx * dx + soft) / FOUR_PI

    step = edge * np.arange(PANELS, dtype=np.float64)
    near = step + (edge - 1) / 2.0 + 1.0
    vx = wave_values(PANELS)
    vz = wave_values(depth)
    even, odd = wave_basis(PANELS)
    zero = np.zeros_like(even)
    basis_x = np.concatenate(
        [np.concatenate([even, zero], 1), np.concatenate([zero, odd], 1)], 0
    )
    basis_z = np.stack(wave_basis(depth))
    face = []
    for sign in (1.0, -1.0):
        k = kernel(0.0, step[:, None], step[None, :])
        k = k + sign * kernel(depth + 1.0, step[:, None], step[None, :])
        face.append(vx.T @ k @ vx)
    z = np.arange(depth, dtype=np.float64)
    side = []
    for sign in (1.0, -1.0):
        k = kernel(z[:, None], 0.0, step[None, :])
        k = k + sign * kernel(z[:, None], grid + 1.0, step[None, :])
        side.append(np.stack([vz[:, :depth].T @ k @ vx, vz[:, depth:].T @ k @ vx]))
    j = np.arange(1, depth + 1, dtype=np.float64)
    k = kernel(j[:, None, None], near[None, :, None], step[None, None, :]) @ vx
    k_own, k_far = k[:half], k[::-1][:half]
    mixed = []
    for sign in (1.0, -1.0):
        m = k_own + sign * k_far
        front, back = m[:, :hb], m[:, ::-1][:, :hb]
        mixed.append(np.concatenate([front + back, front - back], 1))
    k = kernel(z[:, None, None], near[None, :, None], near[None, None, :])
    front, back = k[:, :hb], k[:, ::-1][:, :hb]
    k = np.concatenate([front + back, front - back], 1)
    front, back = k[:, :, :hb], k[:, :, ::-1][:, :, :hb]
    k = np.concatenate([front + back, front - back], 2).reshape(depth, -1)
    corner = [
        (vz[:, s * depth : (s + 1) * depth].T @ k).reshape(depth, PANELS, PANELS)
        for s in (0, 1)
    ]
    return dict(
        basis_x=basis_x,
        basis_z=basis_z,
        face=np.stack(face),
        side=np.stack(side, 1),
        mixed=np.stack(mixed),
        corner=np.stack(corner),
    )


def panel_potential(face, sides, tb):
    hb = PANELS // 2
    bx, bz = tb["basis_x"], tb["basis_z"]
    ein = functools.partial(jnp.einsum, precision=HIGHEST)
    out_face = 0.0
    out_side = []
    hat = ein("sapjb,mb->sapjm", sides, bx)
    zhat = ein("snj,sapjm->sapnm", bz, hat)
    side_zm = tb["side"][:, None] * zhat
    side_m = ein("snj,sapnm->sapjm", bz, side_zm)
    face_out_hat = []
    for axis in (0, 1):
        f = face if axis == 0 else face.swapaxes(1, 2)
        fx = ein("syb,mb->sym", f, bx)
        if axis == 0:
            full = ein("ny,sym->snm", bx, fx) * tb["face"]
            face_m = ein("ny,snm->sym", bx, full)
        else:
            face_m = 0.0
        mix = tb["mixed"].reshape(2, -1, 2, hb, 2 * PANELS)
        fq = fx.reshape(2, 1, 2, hb, 2 * PANELS)
        to_face = (mix * hat[:, axis].swapaxes(1, 2)[:, :, :, None, :]).sum(1)
        face_m = face_m + to_face.reshape(2, PANELS, 2 * PANELS)
        to_side = (mix * fq).sum(3).swapaxes(1, 2)
        face_out_hat.append(ein("sym,mb->syb", face_m, bx))
        out_side.append(ein("sapjm,mb->sapjb", (side_m[:, axis] + to_side)[:, None], bx)[:, 0])
    out_face = face_out_hat[0] + face_out_hat[1].swapaxes(1, 2)
    zs = ein("snj,sapjb->sapnb", bz, sides)
    n = zs.shape[3]
    corner = tb["corner"].reshape(2, n, 2, hb, 2, hb)
    ys = zs[:, 0].reshape(2, 2, n, 2, hb)
    xs = zs[:, 1].reshape(2, 2, n, 2, hb)
    to_y = jnp.einsum("sntbuc,suntb->stnuc", corner, xs, precision=HIGHEST)
    to_x = jnp.einsum("sntbuc,stnuc->suntb", corner, ys, precision=HIGHEST)
    both = jnp.stack([to_y, to_x], 1).reshape(2, 2, 2, n, PANELS)
    both = ein("snj,sapnb->sapjb", bz, both)
    return out_face, jnp.stack(out_side, 1) + both


WIDTH = 256


def block_specs(planes, rows):
    block = pl.BlockSpec((planes, rows, WIDTH), lambda i, *_: (0, 0, i))
    flat = pl.BlockSpec((rows, WIDTH), lambda i, *_: (0, i))
    return block, flat


def factor_body(mu_ref, coef_ref, join_ref):
    planes = coef_ref.shape[0]
    for col in range(0, WIDTH, 128):
        part = slice(col, col + 128)
        diag = mu_ref[:, part] + 2.0
        coef = 1.0 / diag
        coef_ref[0, :, part] = coef
        for j in range(1, planes):
            coef = 1.0 / (diag - coef)
            coef_ref[j, :, part] = coef
        join_ref[:, part] = 1.0 / (1.0 - coef * coef)


def factors(mu, planes):
    rows, cols = mu.shape
    block, flat = block_specs(planes, rows)
    return pl.pallas_call(
        factor_body,
        grid=(cols // WIDTH,),
        in_specs=[flat],
        out_specs=[block, flat],
        out_shape=[
            jax.ShapeDtypeStruct((planes, rows, cols), jnp.float32),
            jax.ShapeDtypeStruct((rows, cols), jnp.float32),
        ],
        cost_estimate=pl.CostEstimate(
            flops=20 * planes * rows * cols, bytes_accessed=4 * planes * rows * cols, transcendentals=0
        ),
    )(mu)


def sweep_body(half_ref, f_ref, coef_ref, g_ref, last_ref):
    planes = f_ref.shape[0]
    upper = half_ref[0]
    value = jnp.zeros_like(last_ref)
    for j in range(planes):
        place = jnp.where(upper == 1, planes - 1 - j, j)
        value = (f_ref[place] + value) * coef_ref[j]
        g_ref[j] = value
    last_ref[...] = value


def sweep(upper, spectrum, coef):
    planes, rows, cols = spectrum.shape
    block, flat = block_specs(planes, rows)
    return pl.pallas_call(
        sweep_body,
        grid_spec=pltpu.PrefetchScalarGridSpec(
            num_scalar_prefetch=1,
            grid=(cols // WIDTH,),
            in_specs=[block, block],
            out_specs=[block, flat],
        ),
        out_shape=[
            jax.ShapeDtypeStruct(spectrum.shape, jnp.float32),
            jax.ShapeDtypeStruct((rows, cols), jnp.float32),
        ],
    )(upper, spectrum, coef)


def finish_body(half_ref, g_ref, coef_ref, join_ref, far_ref, u_ref, edge_ref):
    planes = g_ref.shape[0]
    upper = half_ref[0]
    value = (far_ref[...] + coef_ref[planes - 1] * g_ref[planes - 1]) * join_ref[...]
    for j in range(planes - 1, -1, -1):
        value = g_ref[j] + coef_ref[j] * value
        u_ref[jnp.where(upper == 1, planes - 1 - j, j)] = value
    edge_ref[...] = value


def finish(upper, g, coef, join, far):
    planes, rows, cols = g.shape
    block, flat = block_specs(planes, rows)
    return pl.pallas_call(
        finish_body,
        grid_spec=pltpu.PrefetchScalarGridSpec(
            num_scalar_prefetch=1,
            grid=(cols // WIDTH,),
            in_specs=[block, block, flat, flat],
            out_specs=[block, flat],
        ),
        out_shape=[
            jax.ShapeDtypeStruct(g.shape, jnp.float32),
            jax.ShapeDtypeStruct((rows, cols), jnp.float32),
        ],
    )(upper, g, coef, join, far)


def ghost_body(
    half_ref, u_ref, coef_ref, join_ref, row_ref, col_ref, along_ref, across_ref, near_ref,
    far_ref, out_ref, g_ref,
):
    planes, rows, width = u_ref.shape
    upper = half_ref[0]
    row_odd = lax.broadcasted_iota(jnp.int32, (rows, width), 0) % 2 == 1
    col_odd = lax.broadcasted_iota(jnp.int32, (rows, width), 1) % 2 == 1
    row_value, col_value = row_ref[...], col_ref[...]

    def layer(index):
        even = along_ref[index : index + 1, :]
        odd = along_ref[2 * planes + index : 2 * planes + index + 1, :]
        side_y = row_value * jnp.where(row_odd, odd, even)
        even = across_ref[:, index : index + 1]
        odd = across_ref[:, 2 * planes + index : 2 * planes + index + 1]
        return side_y + col_value * jnp.where(col_odd, odd, even)

    own, far = near_ref[...], far_ref[...]
    for j in range(planes):
        coef = coef_ref[j]
        own = (layer(j) + own) * coef
        far = (layer(planes + j) + far) * coef
        g_ref[j] = own
    value = (far + coef * own) * join_ref[...]
    for j in range(planes - 1, -1, -1):
        value = g_ref[j] + coef_ref[j] * value
        place = jnp.where(upper == 1, planes - 1 - j, j)
        out_ref[place] = u_ref[place] + value


def add_ghost(upper, u, coef, join, row_value, col_value, along, across, near, far):
    planes, rows, cols = u.shape
    block, flat = block_specs(planes, rows)
    return pl.pallas_call(
        ghost_body,
        grid_spec=pltpu.PrefetchScalarGridSpec(
            num_scalar_prefetch=1,
            grid=(cols // WIDTH,),
            in_specs=[
                block,
                block,
                flat,
                pl.BlockSpec((rows, 1), lambda i, u: (0, 0)),
                pl.BlockSpec((1, WIDTH), lambda i, u: (0, i)),
                pl.BlockSpec((4 * planes, WIDTH), lambda i, u: (0, i)),
                pl.BlockSpec((rows, 4 * planes), lambda i, u: (0, 0)),
                flat,
                flat,
            ],
            out_specs=block,
            scratch_shapes=[pltpu.VMEM((planes, rows, WIDTH), jnp.float32)],
        ),
        out_shape=jax.ShapeDtypeStruct(u.shape, jnp.float32),
    )(upper, u, coef, join, row_value, col_value, along, across, near, far)


def build(mesh, grid, depth):
    slow, fast = mesh.shape["px"], mesh.shape["py"]
    devices = slow * fast
    half = devices // 2
    rows = grid // half
    edge = grid // PANELS
    groups = [list(range(half)), list(range(half, devices))]
    tables = {
        name: value.astype(np.float32) for name, value in panel_tables(depth, grid, edge).items()
    }
    sine_np = sine_table(grid).astype(np.float32)
    eigen_np = eigen_values(grid)
    fold_np = fold_panels(grid, edge).astype(np.float32)

    def exchange(x):
        return lax.all_to_all(
            x, AXES, split_axis=0, concat_axis=0, tiled=True, axis_index_groups=groups
        )

    def hop(x, bit):
        return lax.ppermute(x, "px", [(i, i ^ bit) for i in range(slow)])

    def on_device(charge):
        rank = lax.axis_index(AXES)
        upper = (rank // half).astype(jnp.int32).reshape(1)
        is_upper = rank // half == 1
        start = (rank % half) * rows
        sine = jnp.asarray(sine_np)
        fold = jnp.asarray(fold_np)
        tb = {name: jnp.asarray(value) for name, value in tables.items()}
        eigen = jnp.asarray(eigen_np.astype(np.float32))
        edge_value = jnp.asarray(sine_np[:, 0])
        my_eigen = lax.dynamic_slice_in_dim(eigen, start, rows, 0)
        my_edge = lax.dynamic_slice_in_dim(edge_value, start, rows, 0)
        my_fold = lax.dynamic_slice_in_dim(fold, start, rows, 0)
        mu = my_eigen[:, None] + eigen[None, :]
        parity = jnp.arange(grid) % 2
        edge_pair = jnp.stack([edge_value * (parity == 0), edge_value * (parity == 1)])
        my_pair = jnp.stack([my_edge * (parity[:rows] == 0), my_edge * (parity[:rows] == 1)])

        plane = charge.reshape(grid, grid)
        spectrum = dot(sine, dot(plane, sine, precision=HIGH), precision=HIGH)
        spectrum = exchange(spectrum.reshape(half, rows, grid))
        coef, join = factors(mu, half)
        g, last = sweep(upper, spectrum, coef)
        far = lax.ppermute(last, AXES, [(i, i ^ half) for i in range(devices)])
        u, outer = finish(upper, g, coef, join, far)

        face = dot(my_fold, dot(outer, fold), ((0,), (0,)))
        lines_y = jnp.einsum("tk,jkx->tjx", my_pair, u, precision=HIGHEST)
        lines_y = jnp.einsum("tjx,xb->tjb", lines_y, fold, precision=HIGHEST)
        lines_x = jnp.einsum("jkx,tx->tjk", u, edge_pair, precision=HIGHEST)
        lines_x = jnp.einsum("tjk,kb->tjb", lines_x, my_fold, precision=HIGHEST)
        lines = jnp.stack([lines_y, lines_x])
        lines = jnp.where(is_upper, lines[:, :, ::-1], lines)
        part = jnp.concatenate([face, lines.reshape(-1, PANELS)])
        part = lax.all_gather(part, "py", axis=0, tiled=False).sum(0)
        bit = 1
        while bit < slow // 2:
            part = part + hop(part, bit)
            bit *= 2
        other = hop(part, bit)
        both = jnp.stack([part + other, part - other]) * 0.5
        face_q = both[:, :PANELS]
        side_q = both[:, PANELS:].reshape(2, 2, 2, half, PANELS)
        face_v, side_v = panel_potential(face_q, side_q, tb)
        face_v = jnp.stack([face_v[0] + face_v[1], face_v[0] - face_v[1]])
        side_v = jnp.stack([side_v[0] + side_v[1], side_v[0] - side_v[1]])
        near, distant = (
            4.0 * dot(dot(my_fold, face_v[i]), fold, ((1,), (1,))) for i in (0, 1)
        )
        along = side_v[:, 0].swapaxes(0, 1).reshape(4 * half, PANELS)
        across = side_v[:, 1].swapaxes(0, 1).reshape(4 * half, PANELS)
        along = 4.0 * dot(along, fold, ((1,), (1,)))
        across = 4.0 * dot(my_fold, across, ((1,), (1,)))
        u = add_ghost(
            upper, u, coef, join, my_edge[:, None], edge_value[None, :], along, across, near, distant
        )
        u = exchange(u).reshape(grid, grid)
        return dot(dot(sine, u, precision=HIGH), sine, precision=HIGH)[None]

    return on_device


def solution(mesh):
    spec = P(AXES, None, None)

    def run(charge):
        depth, grid, _ = charge.shape
        body = build(mesh, grid, depth)
        return jax.shard_map(body, mesh=mesh, in_specs=(spec,), out_specs=spec, check_vma=False)(
            charge
        )

    return run
```

```python
import functools
import math

import jax
import jax.numpy as jnp
import numpy as np
from jax import lax
from jax.experimental import pallas as pl
from jax.experimental.pallas import tpu as pltpu
from jax.sharding import PartitionSpec as P

PANELS = 128
HIGHEST = lax.Precision.HIGHEST
HIGH = lax.Precision.HIGH
FOUR_PI = 4.0 * math.pi
AXES = ("px", "py")


def dot(a, b, dims=((1,), (0,)), precision=HIGHEST):
    return lax.dot_general(
        a, b, (dims, ((), ())), precision=precision, preferred_element_type=jnp.float32
    )


def sine_table(n):
    order = np.arange(1, n + 1, dtype=np.int64)
    phase = (order[:, None] * order[None, :]) % (2 * (n + 1))
    return np.sqrt(2.0 / (n + 1)) * np.sin(np.pi * phase / (n + 1.0))


def eigen_values(n):
    return 2.0 - 2.0 * np.cos(np.pi * np.arange(1, n + 1) / (n + 1.0))


def fold_panels(grid, edge):
    sums = sine_table(grid).reshape(grid, PANELS, edge).sum(2)[:, : PANELS // 2]
    even = (np.arange(grid) % 2 == 0)[:, None]
    return np.concatenate([np.where(even, sums, 0.0), np.where(even, 0.0, sums)], axis=1)


def wave_basis(n):
    place = np.arange(n // 2) - (n - 1) / 2.0
    even = np.cos(np.pi * np.arange(n)[:, None] * place[None, :] / n)
    even *= np.sqrt(np.where(np.arange(n) == 0, 1.0, 2.0) / n)[:, None]
    odd = np.sin(np.pi * np.arange(1, n + 1)[:, None] * place[None, :] / n)
    odd *= np.sqrt(np.where(np.arange(1, n + 1) == n, 1.0, 2.0) / n)[:, None]
    return even, odd


def wave_values(n):
    distance = np.arange(n)[:, None]
    order = np.concatenate([np.arange(n), np.arange(1, n + 1)])[None, :]
    return np.where(distance == 0, 1.0, 2.0) * np.cos(np.pi * distance * order / n)


def distance_power(*squares):
    return lax.rsqrt(functools.reduce(lambda a, b: a + b, squares))


def iota(shape, axis):
    return lax.broadcasted_iota(jnp.int32, shape, axis).astype(jnp.float32)


def mixed_body(edge, depth, wave_ref, out_ref):
    hb = PANELS // 2
    soft = edge * edge / 4.0
    level = (pl.program_id(0) + 1).astype(jnp.float32)
    shape = (hb, PANELS)
    first = (edge - 1) / 2.0 + 1.0
    front = iota(shape, 0) * edge + first
    back = (PANELS - 1 - iota(shape, 0)) * edge + first
    along = iota(shape, 1) * edge
    along = along * along + soft
    front = front * front + along
    back = back * back + along
    own = level * level
    far = (depth + 1.0 - level) * (depth + 1.0 - level)
    own_front, own_back = distance_power(front, own), distance_power(back, own)
    far_front, far_back = distance_power(front, far), distance_power(back, far)
    rows = []
    for sign in (1.0, -1.0):
        one, two = own_front + sign * far_front, own_back + sign * far_back
        rows += [one + two, one - two]
    value = dot(jnp.concatenate(rows, 0), wave_ref[...])
    out_ref[0, 0] = value[:PANELS]
    out_ref[1, 0] = value[PANELS:]


def mixed_table(edge, depth, wave):
    half = depth // 2
    return pl.pallas_call(
        functools.partial(mixed_body, edge, depth),
        grid=(half,),
        in_specs=[pl.BlockSpec((PANELS, 2 * PANELS), lambda i: (0, 0))],
        out_specs=pl.BlockSpec((2, 1, PANELS, 2 * PANELS), lambda i: (0, i, 0, 0)),
        out_shape=jax.ShapeDtypeStruct((2, half, PANELS, 2 * PANELS), jnp.float32),
        cost_estimate=pl.CostEstimate(
            flops=2 * depth * PANELS**3, bytes_accessed=4 * depth * PANELS * PANELS,
            transcendentals=0,
        ),
    )(wave)


STRIP = 8


def corner_body(edge, depth, wave_ref, front_ref, back_ref):
    hb = PANELS // 2
    soft = edge * edge / 4.0
    shape = (hb, 2 * depth)
    first = (edge - 1) / 2.0 + 1.0
    lane = lax.broadcasted_iota(jnp.int32, shape, 1)
    odd = lane >= depth
    level = jnp.where(odd, lane - depth, lane).astype(jnp.float32)
    sign = jnp.where(odd, -1.0, 1.0)
    level = level * level + soft
    near = iota(shape, 0) * edge + first
    distant = (PANELS - 1 - iota(shape, 0)) * edge + first
    near = near * near + level
    distant = distant * distant + level
    sums, gaps = [], []
    for k in range(STRIP):
        b = (pl.program_id(0) * STRIP + k).astype(jnp.float32)
        front = b * edge + first
        back = (PANELS - 1 - b) * edge + first
        front, back = front * front, back * back
        one = distance_power(near, front) + sign * distance_power(distant, front)
        two = distance_power(near, back) + sign * distance_power(distant, back)
        sums.append(one + two)
        gaps.append(one - two)
    wave = wave_ref[...]
    front_ref[...] = dot(jnp.concatenate(sums, 0), wave).reshape(front_ref.shape)
    back_ref[...] = dot(jnp.concatenate(gaps, 0), wave).reshape(back_ref.shape)


def corner_table(edge, depth, wave):
    hb = PANELS // 2
    width = 4 * depth
    block = pl.BlockSpec((STRIP, hb, width), lambda i: (i, 0, 0))
    shape = jax.ShapeDtypeStruct((hb, hb, width), jnp.float32)
    return pl.pallas_call(
        functools.partial(corner_body, edge, depth),
        grid=(hb // STRIP,),
        in_specs=[pl.BlockSpec((2 * depth, width), lambda i: (0, 0))],
        out_specs=[block, block],
        out_shape=[shape, shape],
        cost_estimate=pl.CostEstimate(
            flops=2 * depth * PANELS**3, bytes_accessed=4 * depth * PANELS * PANELS,
            transcendentals=0,
        ),
    )(wave)


def small_tables(depth, grid, edge):
    half = depth // 2
    soft = edge * edge / 4.0

    def kernel(dz, dy, dx):
        return 1.0 / np.sqrt(dz * dz + dy * dy + dx * dx + soft) / FOUR_PI

    step = edge * np.arange(PANELS, dtype=np.float64)
    vx = wave_values(PANELS)
    vz = wave_values(depth)
    even, odd = wave_basis(PANELS)
    zero = np.zeros_like(even)
    basis_x = np.concatenate(
        [np.concatenate([even, zero], 1), np.concatenate([zero, odd], 1)], 0
    )
    bz = np.stack(wave_basis(depth))
    face, side = [], []
    z = np.arange(depth, dtype=np.float64)
    for s, sign in enumerate((1.0, -1.0)):
        k = kernel(0.0, step[:, None], step[None, :])
        k = k + sign * kernel(depth + 1.0, step[:, None], step[None, :])
        face.append(vx.T @ k @ vx)
        for other in (1.0, -1.0):
            k = kernel(z[:, None], 0.0, step[None, :])
            k = k + other * kernel(z[:, None], grid + 1.0, step[None, :])
            side.append(vz[:, s * depth : (s + 1) * depth].T @ k @ vx)
    level = np.zeros((2, 2, half, 2, 2, depth))
    cross = np.zeros((2, 2, half, 2, 2, depth))
    turn = np.zeros((2, 2, 2, half, 2, 2, 2, depth))
    for s in (0, 1):
        for t in (0, 1):
            level[s, t, :, s, t] = bz[s].T
            cross[s, t, :, t, s] = bz[s].T
            for x in (0, 1):
                turn[x, s, t, :, t, x, s] = bz[s].T
    lift = np.zeros((2, depth, 2, 2, depth))
    for x in (0, 1):
        for s in (0, 1):
            lift[x, :, x, s] = vz[:, s * depth : (s + 1) * depth]
    return dict(
        basis=basis_x,
        face=np.stack(face),
        side=np.concatenate(side),
        level=level.reshape(4 * half, 4 * depth),
        cross=cross.reshape(4 * half, 4 * depth),
        turn=turn.reshape(2, 4 * half, 8 * depth),
        wave_x=vx / FOUR_PI,
        lift=lift.reshape(2 * depth, 4 * depth) / FOUR_PI,
    )


NT = ((1,), (1,))
TN = ((0,), (0,))


def panels_body(
    own_ref, other_ref, basis_ref, face_ref, side_ref, level_ref, cross_ref, turn_ref,
    mixed_ref, front_ref, back_ref, face_out_ref, side_out_ref,
    fx_ref, hat_ref, acc_ref, toside_ref, xs_ref, tox_ref,
):
    half = mixed_ref.shape[1]
    hb = PANELS // 2
    total = (own_ref[...] + other_ref[...]) * 0.5
    gap = (own_ref[...] - other_ref[...]) * 0.5
    basis = basis_ref[...]
    level = level_ref[...]
    faces = [total[:PANELS], gap[:PANELS]]
    sides = []
    for axis in (0, 1):
        rows = slice(PANELS + axis * 2 * half, PANELS + (axis + 1) * 2 * half)
        sides.append(jnp.concatenate([total[rows], gap[rows]], 0))
        hat_ref[axis] = dot(sides[axis], basis, NT)
    for s in (0, 1):
        fx_ref[0, s] = dot(faces[s], basis, NT)
        fx_ref[1, s] = dot(faces[s], basis, ((0,), (1,)))

    for s in (0, 1):

        def face_rows(block, _, s=s):
            at = pl.multiple_of(block * 8, 8)
            odd = (block >= 8).astype(jnp.int32)
            base = (2 * s + odd) * half

            def add(chunk, acc):
                one, two = acc
                for k in range(8):
                    j = chunk * 8 + k
                    t = mixed_ref[s, j, pl.ds(at, 8), :]
                    one = one + t * hat_ref[0, pl.ds(base + j, 1), :]
                    two = two + t * hat_ref[1, pl.ds(base + j, 1), :]
                return one, two

            zero = jnp.zeros((8, 2 * PANELS), jnp.float32)
            one, two = lax.fori_loop(0, half // 8, add, (zero, zero))
            acc_ref[0, s, pl.ds(at, 8), :] = one
            acc_ref[1, s, pl.ds(at, 8), :] = two
            return 0

        lax.fori_loop(0, PANELS // 8, face_rows, 0)

        def side_rows(j, _, s=s):
            for t in (0, 1):
                sums = [None, None]
                for block in range(hb // 8):
                    rows = slice(t * hb + block * 8, t * hb + block * 8 + 8)
                    table = mixed_ref[s, j, rows, :]
                    for axis in (0, 1):
                        term = table * fx_ref[axis, s, rows, :]
                        sums[axis] = term if block == 0 else sums[axis] + term
                for axis in (0, 1):
                    toside_ref[axis, pl.ds((2 * s + t) * half + j, 1), :] = jnp.sum(
                        sums[axis], axis=0, keepdims=True
                    )
            return 0

        lax.fori_loop(0, half, side_rows, 0)

    xs_ref[...] = dot(sides[1], cross_ref[...], TN)
    ys = dot(sides[0][:, :hb], turn_ref[0], TN) + dot(sides[0][:, hb:], turn_ref[1], TN)
    width = xs_ref.shape[1]
    to_y = []
    for t, table_ref in ((0, front_ref), (1, back_ref)):
        mine = ys[:, t * width : (t + 1) * width]

        def corner_rows(b, acc, t=t, table_ref=table_ref, mine=mine):
            table = table_ref[b]
            row = pl.ds(t * hb + b, 1)
            tox_ref[row, :] = jnp.sum(table * mine, axis=0, keepdims=True)
            return acc + table * xs_ref[row, :]

        to_y.append(lax.fori_loop(0, hb, corner_rows, jnp.zeros((hb, width), jnp.float32)))
    to_y = jnp.concatenate(to_y, 1)
    corner = [
        jnp.concatenate([dot(turn_ref[x], to_y, NT) for x in (0, 1)], 1),
        dot(cross_ref[...], tox_ref[...], NT),
    ]
    for axis in (0, 1):
        waves = dot(level, hat_ref[axis], TN) * side_ref[...]
        waves = dot(level, waves) + toside_ref[axis]
        value = dot(waves, basis) + corner[axis]
        even, odd = value[: 2 * half], value[2 * half :]
        for part, v in ((0, even + odd), (1, even - odd)):
            for t in (0, 1):
                at = (2 * t + part) * half
                side_out_ref[axis, at : at + half, :] = v[t * half : (t + 1) * half]
    value = []
    for s in (0, 1):
        full = dot(basis, fx_ref[0, s]) * face_ref[s]
        rows = dot(basis, full, TN) + acc_ref[0, s]
        value.append(dot(rows, basis) + dot(basis, acc_ref[1, s], ((0,), (1,))))
    face_out_ref[0] = value[0] + value[1]
    face_out_ref[1] = value[0] - value[1]


def panel_potential(own, other, tb, mixed, corner):
    half = mixed.shape[1]
    width = corner[0].shape[2]
    f32 = jnp.float32
    return pl.pallas_call(
        panels_body,
        out_shape=[
            jax.ShapeDtypeStruct((2, PANELS, PANELS), f32),
            jax.ShapeDtypeStruct((2, 4 * half, PANELS), f32),
        ],
        scratch_shapes=[
            pltpu.VMEM((2, 2, PANELS, 2 * PANELS), f32),
            pltpu.VMEM((2, 4 * half, 2 * PANELS), f32),
            pltpu.VMEM((2, 2, PANELS, 2 * PANELS), f32),
            pltpu.VMEM((2, 4 * half, 2 * PANELS), f32),
            pltpu.VMEM((PANELS, width), f32),
            pltpu.VMEM((PANELS, width), f32),
        ],
    )(
        own, other, tb["basis"], tb["face"], tb["side"], tb["level"], tb["cross"], tb["turn"],
        mixed, *corner,
    )


WIDTH = 256


def block_specs(planes, rows):
    block = pl.BlockSpec((planes, rows, WIDTH), lambda i, *_: (0, 0, i))
    flat = pl.BlockSpec((rows, WIDTH), lambda i, *_: (0, i))
    return block, flat


def factor_body(mu_ref, coef_ref, join_ref):
    planes = coef_ref.shape[0]
    for col in range(0, WIDTH, 128):
        part = slice(col, col + 128)
        diag = mu_ref[:, part] + 2.0
        coef = 1.0 / diag
        coef_ref[0, :, part] = coef
        for j in range(1, planes):
            coef = 1.0 / (diag - coef)
            coef_ref[j, :, part] = coef
        join_ref[:, part] = 1.0 / (1.0 - coef * coef)


def factors(mu, planes):
    rows, cols = mu.shape
    block, flat = block_specs(planes, rows)
    return pl.pallas_call(
        factor_body,
        grid=(cols // WIDTH,),
        in_specs=[flat],
        out_specs=[block, flat],
        out_shape=[
            jax.ShapeDtypeStruct((planes, rows, cols), jnp.float32),
            jax.ShapeDtypeStruct((rows, cols), jnp.float32),
        ],
        cost_estimate=pl.CostEstimate(
            flops=20 * planes * rows * cols, bytes_accessed=4 * planes * rows * cols, transcendentals=0
        ),
    )(mu)


def sweep_body(half_ref, f_ref, coef_ref, g_ref, last_ref):
    planes = f_ref.shape[0]
    upper = half_ref[0]
    value = jnp.zeros_like(last_ref)
    for j in range(planes):
        place = jnp.where(upper == 1, planes - 1 - j, j)
        value = (f_ref[place] + value) * coef_ref[j]
        g_ref[j] = value
    last_ref[...] = value


def sweep(upper, spectrum, coef):
    planes, rows, cols = spectrum.shape
    block, flat = block_specs(planes, rows)
    return pl.pallas_call(
        sweep_body,
        grid_spec=pltpu.PrefetchScalarGridSpec(
            num_scalar_prefetch=1,
            grid=(cols // WIDTH,),
            in_specs=[block, block],
            out_specs=[block, flat],
        ),
        out_shape=[
            jax.ShapeDtypeStruct(spectrum.shape, jnp.float32),
            jax.ShapeDtypeStruct((rows, cols), jnp.float32),
        ],
    )(upper, spectrum, coef)


def finish_body(half_ref, g_ref, coef_ref, join_ref, far_ref, u_ref, edge_ref):
    planes = g_ref.shape[0]
    upper = half_ref[0]
    value = (far_ref[...] + coef_ref[planes - 1] * g_ref[planes - 1]) * join_ref[...]
    for j in range(planes - 1, -1, -1):
        value = g_ref[j] + coef_ref[j] * value
        u_ref[jnp.where(upper == 1, planes - 1 - j, j)] = value
    edge_ref[...] = value


def finish(upper, g, coef, join, far):
    planes, rows, cols = g.shape
    block, flat = block_specs(planes, rows)
    return pl.pallas_call(
        finish_body,
        grid_spec=pltpu.PrefetchScalarGridSpec(
            num_scalar_prefetch=1,
            grid=(cols // WIDTH,),
            in_specs=[block, block, flat, flat],
            out_specs=[block, flat],
        ),
        out_shape=[
            jax.ShapeDtypeStruct(g.shape, jnp.float32),
            jax.ShapeDtypeStruct((rows, cols), jnp.float32),
        ],
    )(upper, g, coef, join, far)


def ghost_body(
    half_ref, u_ref, coef_ref, join_ref, row_ref, col_ref, along_ref, across_ref, near_ref,
    far_ref, out_ref, g_ref,
):
    planes, rows, width = u_ref.shape
    upper = half_ref[0]
    row_odd = lax.broadcasted_iota(jnp.int32, (rows, width), 0) % 2 == 1
    col_odd = lax.broadcasted_iota(jnp.int32, (rows, width), 1) % 2 == 1
    row_value, col_value = row_ref[...], col_ref[...]

    def layer(index):
        even = along_ref[index : index + 1, :]
        odd = along_ref[2 * planes + index : 2 * planes + index + 1, :]
        side_y = row_value * jnp.where(row_odd, odd, even)
        even = across_ref[:, index : index + 1]
        odd = across_ref[:, 2 * planes + index : 2 * planes + index + 1]
        return side_y + col_value * jnp.where(col_odd, odd, even)

    own, far = near_ref[...], far_ref[...]
    for j in range(planes):
        coef = coef_ref[j]
        own = (layer(j) + own) * coef
        far = (layer(planes + j) + far) * coef
        g_ref[j] = own
    value = (far + coef * own) * join_ref[...]
    for j in range(planes - 1, -1, -1):
        value = g_ref[j] + coef_ref[j] * value
        place = jnp.where(upper == 1, planes - 1 - j, j)
        out_ref[place] = u_ref[place] + value


def add_ghost(upper, u, coef, join, row_value, col_value, along, across, near, far):
    planes, rows, cols = u.shape
    block, flat = block_specs(planes, rows)
    return pl.pallas_call(
        ghost_body,
        grid_spec=pltpu.PrefetchScalarGridSpec(
            num_scalar_prefetch=1,
            grid=(cols // WIDTH,),
            in_specs=[
                block,
                block,
                flat,
                pl.BlockSpec((rows, 1), lambda i, u: (0, 0)),
                pl.BlockSpec((1, WIDTH), lambda i, u: (0, i)),
                pl.BlockSpec((4 * planes, WIDTH), lambda i, u: (0, i)),
                pl.BlockSpec((rows, 4 * planes), lambda i, u: (0, 0)),
                flat,
                flat,
            ],
            out_specs=block,
            scratch_shapes=[pltpu.VMEM((planes, rows, WIDTH), jnp.float32)],
        ),
        out_shape=jax.ShapeDtypeStruct(u.shape, jnp.float32),
    )(upper, u, coef, join, row_value, col_value, along, across, near, far)


def build(mesh, grid, depth):
    slow, fast = mesh.shape["px"], mesh.shape["py"]
    devices = slow * fast
    half = devices // 2
    rows = grid // half
    edge = grid // PANELS
    groups = [list(range(half)), list(range(half, devices))]
    tables = {
        name: value.astype(np.float32) for name, value in small_tables(depth, grid, edge).items()
    }
    sine_np = sine_table(grid).astype(np.float32)
    eigen_np = eigen_values(grid)
    fold_np = fold_panels(grid, edge).astype(np.float32)

    def exchange(x):
        return lax.all_to_all(
            x, AXES, split_axis=0, concat_axis=0, tiled=True, axis_index_groups=groups
        )

    def hop(x, bit):
        return lax.ppermute(x, "px", [(i, i ^ bit) for i in range(slow)])

    def on_device(charge):
        rank = lax.axis_index(AXES)
        upper = (rank // half).astype(jnp.int32).reshape(1)
        is_upper = rank // half == 1
        start = (rank % half) * rows
        sine = jnp.asarray(sine_np)
        fold = jnp.asarray(fold_np)
        tb = {name: jnp.asarray(value) for name, value in tables.items()}
        eigen = jnp.asarray(eigen_np.astype(np.float32))
        edge_value = jnp.asarray(sine_np[:, 0])
        my_eigen = lax.dynamic_slice_in_dim(eigen, start, rows, 0)
        my_edge = lax.dynamic_slice_in_dim(edge_value, start, rows, 0)
        my_fold = lax.dynamic_slice_in_dim(fold, start, rows, 0)
        mu = my_eigen[:, None] + eigen[None, :]
        parity = jnp.arange(grid) % 2
        edge_pair = jnp.stack([edge_value * (parity == 0), edge_value * (parity == 1)])
        my_pair = jnp.stack([my_edge * (parity[:rows] == 0), my_edge * (parity[:rows] == 1)])

        plane = charge.reshape(grid, grid)
        spectrum = dot(sine, dot(plane, sine, precision=HIGH), precision=HIGH)
        spectrum = exchange(spectrum.reshape(half, rows, grid))
        coef, join = factors(mu, half)
        mixed = mixed_table(edge, depth, tb["wave_x"])
        corner = corner_table(edge, depth, tb["lift"])
        spectrum, mixed, corner = lax.optimization_barrier((spectrum, mixed, corner))
        g, last = sweep(upper, spectrum, coef)
        far = lax.ppermute(last, AXES, [(i, i ^ half) for i in range(devices)])
        u, outer = finish(upper, g, coef, join, far)

        face = dot(my_fold, dot(outer, fold), ((0,), (0,)))
        lines_y = jnp.einsum("tk,jkx->tjx", my_pair, u, precision=HIGHEST)
        lines_y = jnp.einsum("tjx,xb->tjb", lines_y, fold, precision=HIGHEST)
        lines_x = jnp.einsum("jkx,tx->tjk", u, edge_pair, precision=HIGHEST)
        lines_x = jnp.einsum("tjk,kb->tjb", lines_x, my_fold, precision=HIGHEST)
        lines = jnp.stack([lines_y, lines_x])
        lines = jnp.where(is_upper, lines[:, :, ::-1], lines)
        part = jnp.concatenate([face, lines.reshape(-1, PANELS)])
        part = lax.all_gather(part, "py", axis=0, tiled=False).sum(0)
        bit = 1
        while bit < slow // 2:
            part = part + hop(part, bit)
            bit *= 2
        other = hop(part, bit)
        face_v, side_v = panel_potential(part, other, tb, mixed, corner)
        near, distant = (
            4.0 * dot(dot(my_fold, face_v[i]), fold, ((1,), (1,))) for i in (0, 1)
        )
        along = 4.0 * dot(side_v[0], fold, ((1,), (1,)))
        across = 4.0 * dot(my_fold, side_v[1], ((1,), (1,)))
        u = add_ghost(
            upper, u, coef, join, my_edge[:, None], edge_value[None, :], along, across, near, distant
        )
        u = exchange(u).reshape(grid, grid)
        return dot(dot(sine, u, precision=HIGH), sine, precision=HIGH)[None]

    return on_device


def solution(mesh):
    spec = P(AXES, None, None)

    def run(charge):
        depth, grid, _ = charge.shape
        body = build(mesh, grid, depth)
        return jax.shard_map(body, mesh=mesh, in_specs=(spec,), out_specs=spec, check_vma=False)(
            charge
        )

    return run
```

```python
import functools
import math

import jax
import jax.numpy as jnp
import numpy as np
from jax import lax
from jax.experimental import pallas as pl
from jax.experimental.pallas import tpu as pltpu
from jax.sharding import PartitionSpec as P

PANELS = 128
HIGHEST = lax.Precision.HIGHEST
HIGH = lax.Precision.HIGH
FOUR_PI = 4.0 * math.pi
AXES = ("px", "py")


def dot(a, b, dims=((1,), (0,)), precision=HIGHEST):
    return lax.dot_general(
        a, b, (dims, ((), ())), precision=precision, preferred_element_type=jnp.float32
    )


def sine_table(n):
    order = np.arange(1, n + 1, dtype=np.int64)
    phase = (order[:, None] * order[None, :]) % (2 * (n + 1))
    return np.sqrt(2.0 / (n + 1)) * np.sin(np.pi * phase / (n + 1.0))


def eigen_values(n):
    return 2.0 - 2.0 * np.cos(np.pi * np.arange(1, n + 1) / (n + 1.0))


def fold_panels(grid, edge):
    sums = sine_table(grid).reshape(grid, PANELS, edge).sum(2)[:, : PANELS // 2]
    even = (np.arange(grid) % 2 == 0)[:, None]
    return np.concatenate([np.where(even, sums, 0.0), np.where(even, 0.0, sums)], axis=1)


def wave_basis(n):
    place = np.arange(n // 2) - (n - 1) / 2.0
    even = np.cos(np.pi * np.arange(n)[:, None] * place[None, :] / n)
    even *= np.sqrt(np.where(np.arange(n) == 0, 1.0, 2.0) / n)[:, None]
    odd = np.sin(np.pi * np.arange(1, n + 1)[:, None] * place[None, :] / n)
    odd *= np.sqrt(np.where(np.arange(1, n + 1) == n, 1.0, 2.0) / n)[:, None]
    return even, odd


def wave_values(n):
    distance = np.arange(n)[:, None]
    order = np.concatenate([np.arange(n), np.arange(1, n + 1)])[None, :]
    return np.where(distance == 0, 1.0, 2.0) * np.cos(np.pi * distance * order / n)


def distance_power(*squares):
    return lax.rsqrt(functools.reduce(lambda a, b: a + b, squares))


def iota(shape, axis):
    return lax.broadcasted_iota(jnp.int32, shape, axis).astype(jnp.float32)


def mixed_body(edge, depth, wave_ref, out_ref):
    hb = PANELS // 2
    soft = edge * edge / 4.0
    level = (pl.program_id(0) + 1).astype(jnp.float32)
    shape = (hb, PANELS)
    first = (edge - 1) / 2.0 + 1.0
    front = iota(shape, 0) * edge + first
    back = (PANELS - 1 - iota(shape, 0)) * edge + first
    along = iota(shape, 1) * edge
    along = along * along + soft
    front = front * front + along
    back = back * back + along
    own = level * level
    far = (depth + 1.0 - level) * (depth + 1.0 - level)
    own_front, own_back = distance_power(front, own), distance_power(back, own)
    far_front, far_back = distance_power(front, far), distance_power(back, far)
    rows = []
    for sign in (1.0, -1.0):
        one, two = own_front + sign * far_front, own_back + sign * far_back
        rows += [one + two, one - two]
    value = dot(jnp.concatenate(rows, 0), wave_ref[...])
    out_ref[0, 0] = value[:PANELS]
    out_ref[1, 0] = value[PANELS:]


def mixed_table(edge, depth, wave):
    half = depth // 2
    return pl.pallas_call(
        functools.partial(mixed_body, edge, depth),
        grid=(half,),
        in_specs=[pl.BlockSpec((PANELS, 2 * PANELS), lambda i: (0, 0))],
        out_specs=pl.BlockSpec((2, 1, PANELS, 2 * PANELS), lambda i: (0, i, 0, 0)),
        out_shape=jax.ShapeDtypeStruct((2, half, PANELS, 2 * PANELS), jnp.float32),
        cost_estimate=pl.CostEstimate(
            flops=2 * depth * PANELS**3, bytes_accessed=4 * depth * PANELS * PANELS,
            transcendentals=0,
        ),
    )(wave)


STRIP = 8


def corner_body(edge, depth, wave_ref, front_ref, back_ref):
    hb = PANELS // 2
    soft = edge * edge / 4.0
    shape = (hb, 2 * depth)
    first = (edge - 1) / 2.0 + 1.0
    lane = lax.broadcasted_iota(jnp.int32, shape, 1)
    odd = lane >= depth
    level = jnp.where(odd, lane - depth, lane).astype(jnp.float32)
    sign = jnp.where(odd, -1.0, 1.0)
    level = level * level + soft
    near = iota(shape, 0) * edge + first
    distant = (PANELS - 1 - iota(shape, 0)) * edge + first
    near = near * near + level
    distant = distant * distant + level
    sums, gaps = [], []
    for k in range(STRIP):
        b = (pl.program_id(0) * STRIP + k).astype(jnp.float32)
        front = b * edge + first
        back = (PANELS - 1 - b) * edge + first
        front, back = front * front, back * back
        one = distance_power(near, front) + sign * distance_power(distant, front)
        two = distance_power(near, back) + sign * distance_power(distant, back)
        sums.append(one + two)
        gaps.append(one - two)
    wave = wave_ref[...]
    front_ref[...] = dot(jnp.concatenate(sums, 0), wave).reshape(front_ref.shape)
    back_ref[...] = dot(jnp.concatenate(gaps, 0), wave).reshape(back_ref.shape)


def corner_table(edge, depth, wave):
    hb = PANELS // 2
    width = 4 * depth
    block = pl.BlockSpec((STRIP, hb, width), lambda i: (i, 0, 0))
    shape = jax.ShapeDtypeStruct((hb, hb, width), jnp.float32)
    return pl.pallas_call(
        functools.partial(corner_body, edge, depth),
        grid=(hb // STRIP,),
        in_specs=[pl.BlockSpec((2 * depth, width), lambda i: (0, 0))],
        out_specs=[block, block],
        out_shape=[shape, shape],
        cost_estimate=pl.CostEstimate(
            flops=2 * depth * PANELS**3, bytes_accessed=4 * depth * PANELS * PANELS,
            transcendentals=0,
        ),
    )(wave)


def small_tables(depth, grid, edge):
    half = depth // 2
    soft = edge * edge / 4.0

    def kernel(dz, dy, dx):
        return 1.0 / np.sqrt(dz * dz + dy * dy + dx * dx + soft) / FOUR_PI

    step = edge * np.arange(PANELS, dtype=np.float64)
    vx = wave_values(PANELS)
    vz = wave_values(depth)
    even, odd = wave_basis(PANELS)
    zero = np.zeros_like(even)
    basis_x = np.concatenate(
        [np.concatenate([even, zero], 1), np.concatenate([zero, odd], 1)], 0
    )
    bz = np.stack(wave_basis(depth))
    face, side = [], []
    z = np.arange(depth, dtype=np.float64)
    for s, sign in enumerate((1.0, -1.0)):
        k = kernel(0.0, step[:, None], step[None, :])
        k = k + sign * kernel(depth + 1.0, step[:, None], step[None, :])
        face.append(vx.T @ k @ vx)
        for other in (1.0, -1.0):
            k = kernel(z[:, None], 0.0, step[None, :])
            k = k + other * kernel(z[:, None], grid + 1.0, step[None, :])
            side.append(vz[:, s * depth : (s + 1) * depth].T @ k @ vx)
    level = np.zeros((2, 2, half, 2, 2, depth))
    cross = np.zeros((2, 2, half, 2, 2, depth))
    turn = np.zeros((2, 2, 2, half, 2, 2, 2, depth))
    for s in (0, 1):
        for t in (0, 1):
            level[s, t, :, s, t] = bz[s].T
            cross[s, t, :, t, s] = bz[s].T
            for x in (0, 1):
                turn[x, s, t, :, t, x, s] = bz[s].T
    lift = np.zeros((2, depth, 2, 2, depth))
    for x in (0, 1):
        for s in (0, 1):
            lift[x, :, x, s] = vz[:, s * depth : (s + 1) * depth]
    return dict(
        basis=basis_x,
        face=np.stack(face),
        side=np.concatenate(side),
        level=level.reshape(4 * half, 4 * depth),
        cross=cross.reshape(4 * half, 4 * depth),
        turn=turn.reshape(2, 4 * half, 8 * depth),
        wave_x=vx / FOUR_PI,
        lift=lift.reshape(2 * depth, 4 * depth) / FOUR_PI,
    )


NT = ((1,), (1,))
TN = ((0,), (0,))


def panels_body(
    own_ref, other_ref, basis_ref, face_ref, side_ref, level_ref, cross_ref, turn_ref,
    mixed_ref, front_ref, back_ref, face_out_ref, side_out_ref,
    fx_ref, hat_ref, acc_ref, toside_ref, xs_ref, tox_ref,
):
    half = mixed_ref.shape[1]
    hb = PANELS // 2
    total = (own_ref[...] + other_ref[...]) * 0.5
    gap = (own_ref[...] - other_ref[...]) * 0.5
    basis = basis_ref[...]
    level = level_ref[...]
    faces = [total[:PANELS], gap[:PANELS]]
    sides = []
    for axis in (0, 1):
        rows = slice(PANELS + axis * 2 * half, PANELS + (axis + 1) * 2 * half)
        sides.append(jnp.concatenate([total[rows], gap[rows]], 0))
        hat_ref[axis] = dot(sides[axis], basis, NT)
    for s in (0, 1):
        fx_ref[0, s] = dot(faces[s], basis, NT)
        fx_ref[1, s] = dot(faces[s], basis, ((0,), (1,)))

    for s in (0, 1):

        def face_rows(block, _, s=s):
            at = pl.multiple_of(block * 8, 8)
            odd = (block >= 8).astype(jnp.int32)
            base = (2 * s + odd) * half

            def add(chunk, acc):
                one, two = acc
                for k in range(8):
                    j = chunk * 8 + k
                    t = mixed_ref[s, j, pl.ds(at, 8), :]
                    one = one + t * hat_ref[0, pl.ds(base + j, 1), :]
                    two = two + t * hat_ref[1, pl.ds(base + j, 1), :]
                return one, two

            zero = jnp.zeros((8, 2 * PANELS), jnp.float32)
            one, two = lax.fori_loop(0, half // 8, add, (zero, zero))
            acc_ref[0, s, pl.ds(at, 8), :] = one
            acc_ref[1, s, pl.ds(at, 8), :] = two
            return 0

        lax.fori_loop(0, PANELS // 8, face_rows, 0)

        def side_rows(j, _, s=s):
            for t in (0, 1):
                sums = [None, None]
                for block in range(hb // 8):
                    rows = slice(t * hb + block * 8, t * hb + block * 8 + 8)
                    table = mixed_ref[s, j, rows, :]
                    for axis in (0, 1):
                        term = table * fx_ref[axis, s, rows, :]
                        sums[axis] = term if block == 0 else sums[axis] + term
                for axis in (0, 1):
                    toside_ref[axis, pl.ds((2 * s + t) * half + j, 1), :] = jnp.sum(
                        sums[axis], axis=0, keepdims=True
                    )
            return 0

        lax.fori_loop(0, half, side_rows, 0)

    xs_ref[...] = dot(sides[1], cross_ref[...], TN)
    ys = dot(sides[0][:, :hb], turn_ref[0], TN) + dot(sides[0][:, hb:], turn_ref[1], TN)
    width = xs_ref.shape[1]
    to_y = []
    for t, table_ref in ((0, front_ref), (1, back_ref)):
        mine = ys[:, t * width : (t + 1) * width]

        def corner_rows(b, acc, t=t, table_ref=table_ref, mine=mine):
            table = table_ref[b]
            row = pl.ds(t * hb + b, 1)
            tox_ref[row, :] = jnp.sum(table * mine, axis=0, keepdims=True)
            return acc + table * xs_ref[row, :]

        to_y.append(lax.fori_loop(0, hb, corner_rows, jnp.zeros((hb, width), jnp.float32)))
    to_y = jnp.concatenate(to_y, 1)
    corner = [
        jnp.concatenate([dot(turn_ref[x], to_y, NT) for x in (0, 1)], 1),
        dot(cross_ref[...], tox_ref[...], NT),
    ]
    for axis in (0, 1):
        waves = dot(level, hat_ref[axis], TN) * side_ref[...]
        waves = dot(level, waves) + toside_ref[axis]
        value = dot(waves, basis) + corner[axis]
        even, odd = value[: 2 * half], value[2 * half :]
        for part, v in ((0, even + odd), (1, even - odd)):
            for t in (0, 1):
                at = (2 * t + part) * half
                side_out_ref[axis, at : at + half, :] = v[t * half : (t + 1) * half]
    value = []
    for s in (0, 1):
        full = dot(basis, fx_ref[0, s]) * face_ref[s]
        rows = dot(basis, full, TN) + acc_ref[0, s]
        value.append(dot(rows, basis) + dot(basis, acc_ref[1, s], ((0,), (1,))))
    face_out_ref[0] = value[0] + value[1]
    face_out_ref[1] = value[0] - value[1]


def panel_potential(own, other, tb, mixed, corner):
    half = mixed.shape[1]
    width = corner[0].shape[2]
    f32 = jnp.float32
    return pl.pallas_call(
        panels_body,
        out_shape=[
            jax.ShapeDtypeStruct((2, PANELS, PANELS), f32),
            jax.ShapeDtypeStruct((2, 4 * half, PANELS), f32),
        ],
        scratch_shapes=[
            pltpu.VMEM((2, 2, PANELS, 2 * PANELS), f32),
            pltpu.VMEM((2, 4 * half, 2 * PANELS), f32),
            pltpu.VMEM((2, 2, PANELS, 2 * PANELS), f32),
            pltpu.VMEM((2, 4 * half, 2 * PANELS), f32),
            pltpu.VMEM((PANELS, width), f32),
            pltpu.VMEM((PANELS, width), f32),
        ],
    )(
        own, other, tb["basis"], tb["face"], tb["side"], tb["level"], tb["cross"], tb["turn"],
        mixed, *corner,
    )


WIDTH = 256


def block_specs(planes, rows):
    block = pl.BlockSpec((planes, rows, WIDTH), lambda i, *_: (0, 0, i))
    flat = pl.BlockSpec((rows, WIDTH), lambda i, *_: (0, i))
    return block, flat


def factor_body(mu_ref, coef_ref, join_ref):
    planes = coef_ref.shape[0]
    for col in range(0, WIDTH, 128):
        part = slice(col, col + 128)
        diag = mu_ref[:, part] + 2.0
        coef = 1.0 / diag
        coef_ref[0, :, part] = coef
        for j in range(1, planes):
            coef = 1.0 / (diag - coef)
            coef_ref[j, :, part] = coef
        join_ref[:, part] = 1.0 / (1.0 - coef * coef)


def factors(mu, planes):
    rows, cols = mu.shape
    block, flat = block_specs(planes, rows)
    return pl.pallas_call(
        factor_body,
        grid=(cols // WIDTH,),
        in_specs=[flat],
        out_specs=[block, flat],
        out_shape=[
            jax.ShapeDtypeStruct((planes, rows, cols), jnp.float32),
            jax.ShapeDtypeStruct((rows, cols), jnp.float32),
        ],
        cost_estimate=pl.CostEstimate(
            flops=20 * planes * rows * cols, bytes_accessed=4 * planes * rows * cols, transcendentals=0
        ),
    )(mu)


def sweep_body(half_ref, f_ref, coef_ref, g_ref, last_ref):
    planes = f_ref.shape[0]
    upper = half_ref[0]
    value = jnp.zeros_like(last_ref)
    for j in range(planes):
        place = jnp.where(upper == 1, planes - 1 - j, j)
        value = (f_ref[place] + value) * coef_ref[j]
        g_ref[j] = value
    last_ref[...] = value


def sweep(upper, spectrum, coef):
    planes, rows, cols = spectrum.shape
    block, flat = block_specs(planes, rows)
    return pl.pallas_call(
        sweep_body,
        grid_spec=pltpu.PrefetchScalarGridSpec(
            num_scalar_prefetch=1,
            grid=(cols // WIDTH,),
            in_specs=[block, block],
            out_specs=[block, flat],
        ),
        out_shape=[
            jax.ShapeDtypeStruct(spectrum.shape, jnp.float32),
            jax.ShapeDtypeStruct((rows, cols), jnp.float32),
        ],
    )(upper, spectrum, coef)


def finish_body(half_ref, g_ref, coef_ref, join_ref, far_ref, u_ref, edge_ref):
    planes = g_ref.shape[0]
    upper = half_ref[0]
    value = (far_ref[...] + coef_ref[planes - 1] * g_ref[planes - 1]) * join_ref[...]
    for j in range(planes - 1, -1, -1):
        value = g_ref[j] + coef_ref[j] * value
        u_ref[jnp.where(upper == 1, planes - 1 - j, j)] = value
    edge_ref[...] = value


def finish(upper, g, coef, join, far):
    planes, rows, cols = g.shape
    block, flat = block_specs(planes, rows)
    return pl.pallas_call(
        finish_body,
        grid_spec=pltpu.PrefetchScalarGridSpec(
            num_scalar_prefetch=1,
            grid=(cols // WIDTH,),
            in_specs=[block, block, flat, flat],
            out_specs=[block, flat],
        ),
        out_shape=[
            jax.ShapeDtypeStruct(g.shape, jnp.float32),
            jax.ShapeDtypeStruct((rows, cols), jnp.float32),
        ],
    )(upper, g, coef, join, far)


def ghost_body(
    half_ref, u_ref, coef_ref, join_ref, row_ref, col_ref, along_ref, across_ref, near_ref,
    far_ref, out_ref, g_ref,
):
    planes, rows, width = u_ref.shape
    upper = half_ref[0]
    row_odd = lax.broadcasted_iota(jnp.int32, (rows, width), 0) % 2 == 1
    col_odd = lax.broadcasted_iota(jnp.int32, (rows, width), 1) % 2 == 1
    row_value, col_value = row_ref[...], col_ref[...]

    def layer(index):
        even = along_ref[index : index + 1, :]
        odd = along_ref[2 * planes + index : 2 * planes + index + 1, :]
        side_y = row_value * jnp.where(row_odd, odd, even)
        even = across_ref[:, index : index + 1]
        odd = across_ref[:, 2 * planes + index : 2 * planes + index + 1]
        return side_y + col_value * jnp.where(col_odd, odd, even)

    own, far = near_ref[...], far_ref[...]
    for j in range(planes):
        coef = coef_ref[j]
        own = (layer(j) + own) * coef
        far = (layer(planes + j) + far) * coef
        g_ref[j] = own
    value = (far + coef * own) * join_ref[...]
    for j in range(planes - 1, -1, -1):
        value = g_ref[j] + coef_ref[j] * value
        place = jnp.where(upper == 1, planes - 1 - j, j)
        out_ref[place] = u_ref[place] + value


def add_ghost(upper, u, coef, join, row_value, col_value, along, across, near, far):
    planes, rows, cols = u.shape
    block, flat = block_specs(planes, rows)
    return pl.pallas_call(
        ghost_body,
        grid_spec=pltpu.PrefetchScalarGridSpec(
            num_scalar_prefetch=1,
            grid=(cols // WIDTH,),
            in_specs=[
                block,
                block,
                flat,
                pl.BlockSpec((rows, 1), lambda i, u: (0, 0)),
                pl.BlockSpec((1, WIDTH), lambda i, u: (0, i)),
                pl.BlockSpec((4 * planes, WIDTH), lambda i, u: (0, i)),
                pl.BlockSpec((rows, 4 * planes), lambda i, u: (0, 0)),
                flat,
                flat,
            ],
            out_specs=block,
            scratch_shapes=[pltpu.VMEM((planes, rows, WIDTH), jnp.float32)],
        ),
        out_shape=jax.ShapeDtypeStruct(u.shape, jnp.float32),
    )(upper, u, coef, join, row_value, col_value, along, across, near, far)


def boundary_body(
    half_ref, g_ref, coef_ref, join_ref, far_ref, row_ref, col_ref, fold_ref, mine_ref,
    pick_row_ref, pick_col_ref, u_ref, part_ref, face_ref, rows_ref, cols_ref, stage_ref,
):
    planes, rows, width = g_ref.shape
    upper = half_ref[0]
    step = pl.program_id(0)

    @pl.when(step == 0)
    def _():
        face_ref[...] = jnp.zeros_like(face_ref)
        rows_ref[...] = jnp.zeros_like(rows_ref)
        cols_ref[...] = jnp.zeros_like(cols_ref)

    row_value, col_value = row_ref[...], col_ref[...]
    value = (far_ref[...] + coef_ref[planes - 1] * g_ref[planes - 1]) * join_ref[...]
    for j in range(planes - 1, -1, -1):
        value = g_ref[j] + coef_ref[j] * value
        u_ref[jnp.where(upper == 1, planes - 1 - j, j)] = value
        by_row = value * row_value
        total = by_row[:8]
        for k in range(8, rows, 8):
            total = total + by_row[k : k + 8]
        stage_ref[8 * j : 8 * j + 8, :] = total
        by_col = value * col_value
        total = by_col[:, :PANELS]
        for k in range(PANELS, width, PANELS):
            total = total + by_col[:, k : k + PANELS]
        cols_ref[:, j * PANELS : (j + 1) * PANELS] += total
    fold = fold_ref[...]
    face_ref[...] += dot(value, fold)
    rows_ref[...] += dot(stage_ref[...], fold)

    @pl.when(step == pl.num_programs(0) - 1)
    def _():
        mine = mine_ref[...]
        part_ref[:PANELS, :] = dot(mine, face_ref[...], TN)
        part_ref[PANELS : PANELS + 2 * planes, :] = dot(pick_row_ref[...], rows_ref[...])
        part_ref[PANELS + 2 * planes :, :] = dot(
            dot(cols_ref[...], pick_col_ref[...]), mine, TN
        )


def finish_boundary(upper, g, coef, join, far, row_value, col_value, fold, mine):
    planes, rows, cols = g.shape
    block, flat = block_specs(planes, rows)
    pick_row = np.zeros((2, planes, planes, 8), np.float32)
    pick_col = np.zeros((planes, PANELS, 2, planes), np.float32)
    for j in range(planes):
        for t in (0, 1):
            pick_row[t, j, j, t::2] = 1.0
            pick_col[j, t::2, t, j] = 1.0
    whole = lambda shape: pl.BlockSpec(shape, lambda i, u: (0, 0))
    f32 = jnp.float32
    return pl.pallas_call(
        boundary_body,
        grid_spec=pltpu.PrefetchScalarGridSpec(
            num_scalar_prefetch=1,
            grid=(cols // WIDTH,),
            in_specs=[
                block,
                block,
                flat,
                flat,
                whole((rows, 1)),
                pl.BlockSpec((1, WIDTH), lambda i, u: (0, i)),
                pl.BlockSpec((WIDTH, PANELS), lambda i, u: (i, 0)),
                whole((rows, PANELS)),
                whole((2 * planes, 8 * planes)),
                whole((planes * PANELS, 2 * planes)),
            ],
            out_specs=[block, whole((PANELS + 4 * planes, PANELS))],
            scratch_shapes=[
                pltpu.VMEM((rows, PANELS), f32),
                pltpu.VMEM((8 * planes, PANELS), f32),
                pltpu.VMEM((rows, planes * PANELS), f32),
                pltpu.VMEM((8 * planes, WIDTH), f32),
            ],
        ),
        out_shape=[
            jax.ShapeDtypeStruct(g.shape, f32),
            jax.ShapeDtypeStruct((PANELS + 4 * planes, PANELS), f32),
        ],
    )(
        upper, g, coef, join, far, row_value, col_value, fold, mine,
        pick_row.reshape(2 * planes, -1), pick_col.reshape(-1, 2 * planes),
    )


TINY = 2.0**-60
GROUP = 16


def weight_body(depth, place_ref, row_ref, col_ref, low_ref, high_ref):
    place = place_ref[0]

    def rows(index, _):
        at = pl.ds(pl.multiple_of(index * GROUP, GROUP), GROUP)
        diag = row_ref[at, :] + col_ref[...] + 2.0

        def step(_, pair):
            return pair[1], diag * pair[1] - pair[0]

        zero = diag - diag
        pair = (zero, zero + 1.0)
        pair = lax.fori_loop(0, place - 1, step, pair)
        near = pair[1]
        pair = lax.fori_loop(0, depth + 1 - 2 * place, step, pair)
        distant = pair[1]
        pair = lax.fori_loop(0, place, step, pair)
        scale = 1.0 / pair[1]
        low_ref[at, :] = distant * scale
        high_ref[at, :] = near * scale
        return 0

    lax.fori_loop(0, low_ref.shape[0] // GROUP, rows, 0)


def weights(depth, place, row_eigen, col_eigen, block):
    grid = row_eigen.shape[0]
    out = jax.ShapeDtypeStruct((grid, grid), jnp.float32)
    spec = pl.BlockSpec((block, grid), lambda i, u: (i, 0))
    return pl.pallas_call(
        functools.partial(weight_body, depth),
        grid_spec=pltpu.PrefetchScalarGridSpec(
            num_scalar_prefetch=1,
            grid=(grid // block,),
            in_specs=[
                pl.BlockSpec((block, 1), lambda i, u: (i, 0)),
                pl.BlockSpec((1, grid), lambda i, u: (0, 0)),
            ],
            out_specs=[spec, spec],
        ),
        out_shape=[out, out],
        cost_estimate=pl.CostEstimate(
            flops=4 * depth * grid * grid, bytes_accessed=8 * grid * grid, transcendentals=0
        ),
    )(place, row_eigen, col_eigen)


def plane_body(
    depth, place_ref, u_ref, low_ref, high_ref, row_eigen_ref, col_eigen_ref, row_ref, col_ref,
    face_ref, side_ref, rows_fold_ref, fold_ref, out_ref, along_ref, across_ref, near_ref,
    distant_ref,
):
    half = depth // 2
    block, grid = u_ref.shape
    place = place_ref[0]
    levels = [k if k < half else half + depth - 1 - k for k in range(depth)]

    @pl.when(pl.program_id(0) == 0)
    def _():
        along = dot(side_ref[0], fold_ref[...], NT) * (4.0 * TINY / col_ref[...])
        odd = lax.broadcasted_iota(jnp.int32, (GROUP, grid), 0) % 2 == 1
        for k, at in enumerate(levels):
            even_row = along[at : at + 1, :]
            odd_row = along[depth + at : depth + at + 1, :]
            along_ref[k] = jnp.where(odd, odd_row, even_row)

    rows_fold = rows_fold_ref[...]
    across = dot(rows_fold, side_ref[1], NT) * (4.0 * TINY / row_ref[...])
    near_ref[...] = 4.0 * dot(dot(rows_fold, face_ref[0]), fold_ref[...], NT)
    distant_ref[...] = 4.0 * dot(dot(rows_fold, face_ref[1]), fold_ref[...], NT)
    odd = lax.broadcasted_iota(jnp.int32, (block, PANELS), 1) % 2 == 1
    for k, at in enumerate(levels):
        across_ref[k] = jnp.where(
            odd, across[:, depth + at : depth + at + 1], across[:, at : at + 1]
        )
    copies = grid // PANELS

    def rows(index, _):
        at = pl.ds(pl.multiple_of(index * GROUP, GROUP), GROUP)
        diag = row_eigen_ref[at, :] + col_eigen_ref[...] + 2.0
        zero = diag - diag

        def layer(k):
            return along_ref[k] + jnp.concatenate([across_ref[k, at, :]] * copies, 1)

        def down(k, pair):
            return layer(place - 1 - k) + (diag * pair[0] - pair[1]), pair[0]

        def up(k, pair):
            return layer(place + k) + (diag * pair[0] - pair[1]), pair[0]

        lower = lax.fori_loop(0, place, down, (zero, zero))[0]
        upper = lax.fori_loop(0, depth - place, up, (zero, zero))[0]
        both = row_ref[at, :] * col_ref[...] * (1.0 / TINY)
        out_ref[at, :] = (
            u_ref[at, :]
            + low_ref[at, :] * (both * lower + near_ref[at, :])
            + high_ref[at, :] * (both * upper + distant_ref[at, :])
        )
        return 0

    lax.fori_loop(0, block // GROUP, rows, 0)


def plane_layers(depth, place, u, low, high, eigen, edge_value, face_v, side_v, fold, block):
    grid = u.shape[0]
    f32 = jnp.float32
    wide = pl.BlockSpec((block, grid), lambda i, u: (i, 0))
    tall = pl.BlockSpec((block, 1), lambda i, u: (i, 0))
    flat = pl.BlockSpec((1, grid), lambda i, u: (0, 0))
    return pl.pallas_call(
        functools.partial(plane_body, depth),
        grid_spec=pltpu.PrefetchScalarGridSpec(
            num_scalar_prefetch=1,
            grid=(grid // block,),
            in_specs=[
                wide,
                wide,
                wide,
                tall,
                flat,
                tall,
                flat,
                pl.BlockSpec(face_v.shape, lambda i, u: (0, 0, 0)),
                pl.BlockSpec(side_v.shape, lambda i, u: (0, 0, 0)),
                pl.BlockSpec((block, PANELS), lambda i, u: (i, 0)),
                pl.BlockSpec((grid, PANELS), lambda i, u: (0, 0)),
            ],
            out_specs=wide,
            scratch_shapes=[
                pltpu.VMEM((depth, GROUP, grid), f32),
                pltpu.VMEM((depth, block, PANELS), f32),
                pltpu.VMEM((block, grid), f32),
                pltpu.VMEM((block, grid), f32),
            ],
        ),
        out_shape=jax.ShapeDtypeStruct((grid, grid), f32),
    )(
        place, u, low, high, eigen[:, None], eigen[None, :], edge_value[:, None],
        edge_value[None, :], face_v, side_v, fold, fold,
    )


def build(mesh, grid, depth):
    slow, fast = mesh.shape["px"], mesh.shape["py"]
    devices = slow * fast
    half = devices // 2
    rows = grid // half
    edge = grid // PANELS
    groups = [list(range(half)), list(range(half, devices))]
    local = depth <= 32 and rows % 8 == 0
    block = grid // 8
    tables = {
        name: value.astype(np.float32) for name, value in small_tables(depth, grid, edge).items()
    }
    sine_np = sine_table(grid).astype(np.float32)
    eigen_np = eigen_values(grid)
    fold_np = fold_panels(grid, edge).astype(np.float32)

    def exchange(x):
        return lax.all_to_all(
            x, AXES, split_axis=0, concat_axis=0, tiled=True, axis_index_groups=groups
        )

    def hop(x, bit):
        return lax.ppermute(x, "px", [(i, i ^ bit) for i in range(slow)])

    def on_device(charge):
        rank = lax.axis_index(AXES)
        upper = (rank // half).astype(jnp.int32).reshape(1)
        is_upper = rank // half == 1
        start = (rank % half) * rows
        sine = jnp.asarray(sine_np)
        fold = jnp.asarray(fold_np)
        tb = {name: jnp.asarray(value) for name, value in tables.items()}
        eigen = jnp.asarray(eigen_np.astype(np.float32))
        edge_value = jnp.asarray(sine_np[:, 0])
        my_eigen = lax.dynamic_slice_in_dim(eigen, start, rows, 0)
        my_edge = lax.dynamic_slice_in_dim(edge_value, start, rows, 0)
        my_fold = lax.dynamic_slice_in_dim(fold, start, rows, 0)
        mu = my_eigen[:, None] + eigen[None, :]
        parity = jnp.arange(grid) % 2
        edge_pair = jnp.stack([edge_value * (parity == 0), edge_value * (parity == 1)])
        my_pair = jnp.stack([my_edge * (parity[:rows] == 0), my_edge * (parity[:rows] == 1)])

        plane = charge.reshape(grid, grid)
        spectrum = dot(sine, dot(plane, sine, precision=HIGH), precision=HIGH)
        spectrum = exchange(spectrum.reshape(half, rows, grid))
        coef, join = factors(mu, half)
        mixed = mixed_table(edge, depth, tb["wave_x"])
        corner = corner_table(edge, depth, tb["lift"])
        if local:
            index = (rank % half).astype(jnp.int32)
            place = jnp.where(is_upper, half - index, index + 1).reshape(1)
            weight = weights(depth, place, eigen[:, None], eigen[None, :], block)
            spectrum, mixed, corner, weight = lax.optimization_barrier(
                (spectrum, mixed, corner, weight)
            )
        else:
            spectrum, mixed, corner = lax.optimization_barrier((spectrum, mixed, corner))
        g, last = sweep(upper, spectrum, coef)
        far = lax.ppermute(last, AXES, [(i, i ^ half) for i in range(devices)])
        if local:
            u, part = finish_boundary(
                upper, g, coef, join, far, my_edge[:, None], edge_value[None, :], fold, my_fold
            )
            u = exchange(u).reshape(grid, grid)
        else:
            u, outer = finish(upper, g, coef, join, far)

            face = dot(my_fold, dot(outer, fold), ((0,), (0,)))
            lines_y = jnp.einsum("tk,jkx->tjx", my_pair, u, precision=HIGHEST)
            lines_y = jnp.einsum("tjx,xb->tjb", lines_y, fold, precision=HIGHEST)
            lines_x = jnp.einsum("jkx,tx->tjk", u, edge_pair, precision=HIGHEST)
            lines_x = jnp.einsum("tjk,kb->tjb", lines_x, my_fold, precision=HIGHEST)
            lines = jnp.stack([lines_y, lines_x])
            lines = jnp.where(is_upper, lines[:, :, ::-1], lines)
            part = jnp.concatenate([face, lines.reshape(-1, PANELS)])
        part = lax.all_gather(part, "py", axis=0, tiled=False).sum(0)
        bit = 1
        while bit < slow // 2:
            part = part + hop(part, bit)
            bit *= 2
        other = hop(part, bit)
        face_v, side_v = panel_potential(part, other, tb, mixed, corner)
        if local:
            u = plane_layers(
                depth, place, u, *weight, eigen, edge_value, face_v, side_v, fold, block
            )
        else:
            near, distant = (
                4.0 * dot(dot(my_fold, face_v[i]), fold, ((1,), (1,))) for i in (0, 1)
            )
            along = 4.0 * dot(side_v[0], fold, ((1,), (1,)))
            across = 4.0 * dot(my_fold, side_v[1], ((1,), (1,)))
            u = add_ghost(
                upper, u, coef, join, my_edge[:, None], edge_value[None, :], along, across, near, distant
            )
            u = exchange(u).reshape(grid, grid)
        return dot(dot(sine, u, precision=HIGH), sine, precision=HIGH)[None]

    return on_device


def solution(mesh):
    spec = P(AXES, None, None)

    def run(charge):
        depth, grid, _ = charge.shape
        body = build(mesh, grid, depth)
        return jax.shard_map(body, mesh=mesh, in_specs=(spec,), out_specs=spec, check_vma=False)(
            charge
        )

    return run
```

```python
import functools
import math

import jax
import jax.numpy as jnp
import numpy as np
from jax import lax
from jax.experimental import pallas as pl
from jax.experimental.pallas import tpu as pltpu
from jax.sharding import PartitionSpec as P

PANELS = 128
HIGHEST = lax.Precision.HIGHEST
HIGH = lax.Precision.HIGH
FOUR_PI = 4.0 * math.pi
AXES = ("px", "py")


def dot(a, b, dims=((1,), (0,)), precision=HIGHEST):
    return lax.dot_general(
        a, b, (dims, ((), ())), precision=precision, preferred_element_type=jnp.float32
    )


def sine_table(n):
    order = np.arange(1, n + 1, dtype=np.int64)
    phase = (order[:, None] * order[None, :]) % (2 * (n + 1))
    return np.sqrt(2.0 / (n + 1)) * np.sin(np.pi * phase / (n + 1.0))


def eigen_values(n):
    return 2.0 - 2.0 * np.cos(np.pi * np.arange(1, n + 1) / (n + 1.0))


def fold_panels(grid, edge):
    sums = sine_table(grid).reshape(grid, PANELS, edge).sum(2)[:, : PANELS // 2]
    even = (np.arange(grid) % 2 == 0)[:, None]
    return np.concatenate([np.where(even, sums, 0.0), np.where(even, 0.0, sums)], axis=1)


def wave_basis(n):
    place = np.arange(n // 2) - (n - 1) / 2.0
    even = np.cos(np.pi * np.arange(n)[:, None] * place[None, :] / n)
    even *= np.sqrt(np.where(np.arange(n) == 0, 1.0, 2.0) / n)[:, None]
    odd = np.sin(np.pi * np.arange(1, n + 1)[:, None] * place[None, :] / n)
    odd *= np.sqrt(np.where(np.arange(1, n + 1) == n, 1.0, 2.0) / n)[:, None]
    return even, odd


def wave_values(n):
    distance = np.arange(n)[:, None]
    order = np.concatenate([np.arange(n), np.arange(1, n + 1)])[None, :]
    return np.where(distance == 0, 1.0, 2.0) * np.cos(np.pi * distance * order / n)


def halves(value):
    high = value.astype(jnp.bfloat16)
    return high, (value - high.astype(jnp.float32)).astype(jnp.bfloat16)


def bf16_dot(a, b):
    return lax.dot_general(a, b, (((1,), (0,)), ((), ())), preferred_element_type=jnp.float32)


STRIPE = 256


def product_body(count, high_ref, low_ref, *refs):
    in_refs, out_ref, mid_high_ref, mid_low_ref = refs[:count], *refs[count:]
    grid = out_ref.shape[0]

    def first(index, _):
        at = pl.ds(pl.multiple_of(index * STRIPE, STRIPE), STRIPE)
        value = in_refs[0][at, :]
        if count == 3:
            value = jnp.concatenate([value + in_refs[1][at, :], in_refs[2][at, :]], 1)
        high, low = halves(value)
        value = bf16_dot(high, high_ref[...])
        value = value + bf16_dot(high, low_ref[...])
        value = value + bf16_dot(low, high_ref[...])
        high, low = halves(value)
        mid_high_ref[at, :] = high
        mid_low_ref[at, :] = low
        return 0

    lax.fori_loop(0, grid // STRIPE, first, 0)

    def second(index, _):
        at = pl.ds(pl.multiple_of(index * STRIPE, STRIPE), STRIPE)
        value = bf16_dot(high_ref[at, :], mid_high_ref[...])
        value = value + bf16_dot(high_ref[at, :], mid_low_ref[...])
        value = value + bf16_dot(low_ref[at, :], mid_high_ref[...])
        out_ref[at, :] = value
        return 0

    lax.fori_loop(0, grid // STRIPE, second, 0)


def double_product(values, high, low):
    grid = high.shape[0]
    return pl.pallas_call(
        functools.partial(product_body, len(values)),
        out_shape=jax.ShapeDtypeStruct((grid, grid), jnp.float32),
        scratch_shapes=[
            pltpu.VMEM((grid, grid), jnp.bfloat16),
            pltpu.VMEM((grid, grid), jnp.bfloat16),
        ],
    )(high, low, *values)


def distance_power(*squares):
    return lax.rsqrt(functools.reduce(lambda a, b: a + b, squares))


def iota(shape, axis):
    return lax.broadcasted_iota(jnp.int32, shape, axis).astype(jnp.float32)


LEVELS = 4


def mixed_body(edge, depth, wave_ref, out_ref):
    hb = PANELS // 2
    soft = edge * edge / 4.0
    shape = (hb, PANELS)
    first = (edge - 1) / 2.0 + 1.0
    front = iota(shape, 0) * edge + first
    back = (PANELS - 1 - iota(shape, 0)) * edge + first
    along = iota(shape, 1) * edge
    along = along * along + soft
    front = front * front + along
    back = back * back + along
    rows = []
    for k in range(LEVELS):
        level = (pl.program_id(0) * LEVELS + k + 1).astype(jnp.float32)
        own = level * level
        far = (depth + 1.0 - level) * (depth + 1.0 - level)
        own_front, own_back = distance_power(front, own), distance_power(back, own)
        far_front, far_back = distance_power(front, far), distance_power(back, far)
        for sign in (1.0, -1.0):
            one, two = own_front + sign * far_front, own_back + sign * far_back
            rows += [one + two, one - two]
    value = dot(jnp.concatenate(rows, 0), wave_ref[...])
    for k in range(LEVELS):
        for s in (0, 1):
            at = (2 * k + s) * PANELS
            out_ref[s, k] = value[at : at + PANELS]


def mixed_table(edge, depth, wave):
    half = depth // 2
    return pl.pallas_call(
        functools.partial(mixed_body, edge, depth),
        grid=(half // LEVELS,),
        in_specs=[pl.BlockSpec((PANELS, 2 * PANELS), lambda i: (0, 0))],
        out_specs=pl.BlockSpec((2, LEVELS, PANELS, 2 * PANELS), lambda i: (0, i, 0, 0)),
        out_shape=jax.ShapeDtypeStruct((2, half, PANELS, 2 * PANELS), jnp.float32),
        cost_estimate=pl.CostEstimate(
            flops=2 * depth * PANELS**3, bytes_accessed=4 * depth * PANELS * PANELS,
            transcendentals=0,
        ),
    )(wave)


STRIP = 8


def corner_body(edge, depth, wave_ref, front_ref, back_ref):
    hb = PANELS // 2
    soft = edge * edge / 4.0
    shape = (hb, 2 * depth)
    first = (edge - 1) / 2.0 + 1.0
    lane = lax.broadcasted_iota(jnp.int32, shape, 1)
    odd = lane >= depth
    level = jnp.where(odd, lane - depth, lane).astype(jnp.float32)
    sign = jnp.where(odd, -1.0, 1.0)
    level = level * level + soft
    near = iota(shape, 0) * edge + first
    distant = (PANELS - 1 - iota(shape, 0)) * edge + first
    near = near * near + level
    distant = distant * distant + level
    sums, gaps = [], []
    for k in range(STRIP):
        b = (pl.program_id(0) * STRIP + k).astype(jnp.float32)
        front = b * edge + first
        back = (PANELS - 1 - b) * edge + first
        front, back = front * front, back * back
        one = distance_power(near, front) + sign * distance_power(distant, front)
        two = distance_power(near, back) + sign * distance_power(distant, back)
        sums.append(one + two)
        gaps.append(one - two)
    wave = wave_ref[...]
    front_ref[...] = dot(jnp.concatenate(sums, 0), wave).reshape(front_ref.shape)
    back_ref[...] = dot(jnp.concatenate(gaps, 0), wave).reshape(back_ref.shape)


def corner_table(edge, depth, wave):
    hb = PANELS // 2
    width = 4 * depth
    block = pl.BlockSpec((STRIP, hb, width), lambda i: (i, 0, 0))
    shape = jax.ShapeDtypeStruct((hb, hb, width), jnp.float32)
    return pl.pallas_call(
        functools.partial(corner_body, edge, depth),
        grid=(hb // STRIP,),
        in_specs=[pl.BlockSpec((2 * depth, width), lambda i: (0, 0))],
        out_specs=[block, block],
        out_shape=[shape, shape],
        cost_estimate=pl.CostEstimate(
            flops=2 * depth * PANELS**3, bytes_accessed=4 * depth * PANELS * PANELS,
            transcendentals=0,
        ),
    )(wave)


def small_tables(depth, grid, edge):
    half = depth // 2
    soft = edge * edge / 4.0

    def kernel(dz, dy, dx):
        return 1.0 / np.sqrt(dz * dz + dy * dy + dx * dx + soft) / FOUR_PI

    step = edge * np.arange(PANELS, dtype=np.float64)
    vx = wave_values(PANELS)
    vz = wave_values(depth)
    even, odd = wave_basis(PANELS)
    zero = np.zeros_like(even)
    basis_x = np.concatenate(
        [np.concatenate([even, zero], 1), np.concatenate([zero, odd], 1)], 0
    )
    bz = np.stack(wave_basis(depth))
    face, side = [], []
    z = np.arange(depth, dtype=np.float64)
    for s, sign in enumerate((1.0, -1.0)):
        k = kernel(0.0, step[:, None], step[None, :])
        k = k + sign * kernel(depth + 1.0, step[:, None], step[None, :])
        face.append(vx.T @ k @ vx)
        for other in (1.0, -1.0):
            k = kernel(z[:, None], 0.0, step[None, :])
            k = k + other * kernel(z[:, None], grid + 1.0, step[None, :])
            side.append(vz[:, s * depth : (s + 1) * depth].T @ k @ vx)
    level = np.zeros((2, 2, half, 2, 2, depth))
    cross = np.zeros((2, 2, half, 2, 2, depth))
    turn = np.zeros((2, 2, 2, half, 2, 2, 2, depth))
    for s in (0, 1):
        for t in (0, 1):
            level[s, t, :, s, t] = bz[s].T
            cross[s, t, :, t, s] = bz[s].T
            for x in (0, 1):
                turn[x, s, t, :, t, x, s] = bz[s].T
    lift = np.zeros((2, depth, 2, 2, depth))
    for x in (0, 1):
        for s in (0, 1):
            lift[x, :, x, s] = vz[:, s * depth : (s + 1) * depth]
    return dict(
        basis=basis_x,
        face=np.stack(face),
        side=np.concatenate(side),
        level=level.reshape(4 * half, 4 * depth),
        cross=cross.reshape(4 * half, 4 * depth),
        turn=turn.reshape(2, 4 * half, 8 * depth),
        wave_x=vx / FOUR_PI,
        lift=lift.reshape(2 * depth, 4 * depth) / FOUR_PI,
    )


NT = ((1,), (1,))
TN = ((0,), (0,))


def panels_body(
    own_ref, other_ref, basis_ref, face_ref, side_ref, level_ref, cross_ref, turn_ref,
    mixed_ref, front_ref, back_ref, face_out_ref, side_out_ref,
    fx_ref, hat_ref, acc_ref, toside_ref, xs_ref, tox_ref,
):
    half = mixed_ref.shape[1]
    hb = PANELS // 2
    total = (own_ref[...] + other_ref[...]) * 0.5
    gap = (own_ref[...] - other_ref[...]) * 0.5
    basis = basis_ref[...]
    level = level_ref[...]
    faces = [total[:PANELS], gap[:PANELS]]
    sides = []
    for axis in (0, 1):
        rows = slice(PANELS + axis * 2 * half, PANELS + (axis + 1) * 2 * half)
        sides.append(jnp.concatenate([total[rows], gap[rows]], 0))
        hat_ref[axis] = dot(sides[axis], basis, NT)
    for s in (0, 1):
        fx_ref[0, s] = dot(faces[s], basis, NT)
        fx_ref[1, s] = dot(faces[s], basis, ((0,), (1,)))

    for s in (0, 1):

        def face_rows(block, _, s=s):
            at = pl.multiple_of(block * 8, 8)
            odd = (block >= 8).astype(jnp.int32)
            base = (2 * s + odd) * half

            def add(chunk, acc):
                one, two = acc
                for k in range(8):
                    j = chunk * 8 + k
                    t = mixed_ref[s, j, pl.ds(at, 8), :]
                    one = one + t * hat_ref[0, pl.ds(base + j, 1), :]
                    two = two + t * hat_ref[1, pl.ds(base + j, 1), :]
                return one, two

            zero = jnp.zeros((8, 2 * PANELS), jnp.float32)
            one, two = lax.fori_loop(0, half // 8, add, (zero, zero))
            acc_ref[0, s, pl.ds(at, 8), :] = one
            acc_ref[1, s, pl.ds(at, 8), :] = two
            return 0

        lax.fori_loop(0, PANELS // 8, face_rows, 0)

        def side_rows(j, _, s=s):
            for t in (0, 1):
                sums = [None, None]
                for block in range(hb // 8):
                    rows = slice(t * hb + block * 8, t * hb + block * 8 + 8)
                    table = mixed_ref[s, j, rows, :]
                    for axis in (0, 1):
                        term = table * fx_ref[axis, s, rows, :]
                        sums[axis] = term if block == 0 else sums[axis] + term
                for axis in (0, 1):
                    toside_ref[axis, pl.ds((2 * s + t) * half + j, 1), :] = jnp.sum(
                        sums[axis], axis=0, keepdims=True
                    )
            return 0

        lax.fori_loop(0, half, side_rows, 0)

    xs_ref[...] = dot(sides[1], cross_ref[...], TN)
    ys = dot(sides[0][:, :hb], turn_ref[0], TN) + dot(sides[0][:, hb:], turn_ref[1], TN)
    width = xs_ref.shape[1]
    to_y = []
    for t, table_ref in ((0, front_ref), (1, back_ref)):
        mine = ys[:, t * width : (t + 1) * width]

        def corner_rows(b, acc, t=t, table_ref=table_ref, mine=mine):
            table = table_ref[b]
            row = pl.ds(t * hb + b, 1)
            tox_ref[row, :] = jnp.sum(table * mine, axis=0, keepdims=True)
            return acc + table * xs_ref[row, :]

        to_y.append(lax.fori_loop(0, hb, corner_rows, jnp.zeros((hb, width), jnp.float32)))
    to_y = jnp.concatenate(to_y, 1)
    corner = [
        jnp.concatenate([dot(turn_ref[x], to_y, NT) for x in (0, 1)], 1),
        dot(cross_ref[...], tox_ref[...], NT),
    ]
    for axis in (0, 1):
        waves = dot(level, hat_ref[axis], TN) * side_ref[...]
        waves = dot(level, waves) + toside_ref[axis]
        value = dot(waves, basis) + corner[axis]
        even, odd = value[: 2 * half], value[2 * half :]
        for part, v in ((0, even + odd), (1, even - odd)):
            for t in (0, 1):
                at = (2 * t + part) * half
                side_out_ref[axis, at : at + half, :] = v[t * half : (t + 1) * half]
    value = []
    for s in (0, 1):
        full = dot(basis, fx_ref[0, s]) * face_ref[s]
        rows = dot(basis, full, TN) + acc_ref[0, s]
        value.append(dot(rows, basis) + dot(basis, acc_ref[1, s], ((0,), (1,))))
    face_out_ref[0] = value[0] + value[1]
    face_out_ref[1] = value[0] - value[1]


def panel_potential(own, other, tb, mixed, corner):
    half = mixed.shape[1]
    width = corner[0].shape[2]
    f32 = jnp.float32
    return pl.pallas_call(
        panels_body,
        out_shape=[
            jax.ShapeDtypeStruct((2, PANELS, PANELS), f32),
            jax.ShapeDtypeStruct((2, 4 * half, PANELS), f32),
        ],
        scratch_shapes=[
            pltpu.VMEM((2, 2, PANELS, 2 * PANELS), f32),
            pltpu.VMEM((2, 4 * half, 2 * PANELS), f32),
            pltpu.VMEM((2, 2, PANELS, 2 * PANELS), f32),
            pltpu.VMEM((2, 4 * half, 2 * PANELS), f32),
            pltpu.VMEM((PANELS, width), f32),
            pltpu.VMEM((PANELS, width), f32),
        ],
    )(
        own, other, tb["basis"], tb["face"], tb["side"], tb["level"], tb["cross"], tb["turn"],
        mixed, *corner,
    )


WIDTH = 256


def block_specs(planes, rows, width=WIDTH, first=0):
    block = pl.BlockSpec((planes, rows, width), lambda i, *_: (0, 0, i + first))
    flat = pl.BlockSpec((rows, width), lambda i, *_: (0, i + first))
    return block, flat


def factor_body(mu_ref, coef_ref, join_ref):
    planes = coef_ref.shape[0]
    for col in range(0, WIDTH, 128):
        part = slice(col, col + 128)
        diag = mu_ref[:, part] + 2.0
        coef = 1.0 / diag
        coef_ref[0, :, part] = coef
        for j in range(1, planes):
            coef = 1.0 / (diag - coef)
            coef_ref[j, :, part] = coef
        join_ref[:, part] = 1.0 / (1.0 - coef * coef)


def factors(mu, planes):
    rows, cols = mu.shape
    block, flat = block_specs(planes, rows)
    return pl.pallas_call(
        factor_body,
        grid=(cols // WIDTH,),
        in_specs=[flat],
        out_specs=[block, flat],
        out_shape=[
            jax.ShapeDtypeStruct((planes, rows, cols), jnp.float32),
            jax.ShapeDtypeStruct((rows, cols), jnp.float32),
        ],
        cost_estimate=pl.CostEstimate(
            flops=20 * planes * rows * cols, bytes_accessed=4 * planes * rows * cols, transcendentals=0
        ),
    )(mu)


def sweep_body(half_ref, f_ref, coef_ref, g_ref, last_ref):
    planes = f_ref.shape[0]
    upper = half_ref[0]
    value = jnp.zeros_like(last_ref)
    for j in range(planes):
        place = jnp.where(upper == 1, planes - 1 - j, j)
        value = (f_ref[place] + value) * coef_ref[j]
        g_ref[j] = value
    last_ref[...] = value


def sweep(upper, spectrum, coef):
    planes, rows, cols = spectrum.shape
    block, flat = block_specs(planes, rows)
    return pl.pallas_call(
        sweep_body,
        grid_spec=pltpu.PrefetchScalarGridSpec(
            num_scalar_prefetch=1,
            grid=(cols // WIDTH,),
            in_specs=[block, block],
            out_specs=[block, flat],
        ),
        out_shape=[
            jax.ShapeDtypeStruct(spectrum.shape, jnp.float32),
            jax.ShapeDtypeStruct((rows, cols), jnp.float32),
        ],
    )(upper, spectrum, coef)


def finish_body(half_ref, g_ref, coef_ref, join_ref, far_ref, u_ref, edge_ref):
    planes = g_ref.shape[0]
    upper = half_ref[0]
    value = (far_ref[...] + coef_ref[planes - 1] * g_ref[planes - 1]) * join_ref[...]
    for j in range(planes - 1, -1, -1):
        value = g_ref[j] + coef_ref[j] * value
        u_ref[jnp.where(upper == 1, planes - 1 - j, j)] = value
    edge_ref[...] = value


def finish(upper, g, coef, join, far):
    planes, rows, cols = g.shape
    block, flat = block_specs(planes, rows)
    return pl.pallas_call(
        finish_body,
        grid_spec=pltpu.PrefetchScalarGridSpec(
            num_scalar_prefetch=1,
            grid=(cols // WIDTH,),
            in_specs=[block, block, flat, flat],
            out_specs=[block, flat],
        ),
        out_shape=[
            jax.ShapeDtypeStruct(g.shape, jnp.float32),
            jax.ShapeDtypeStruct((rows, cols), jnp.float32),
        ],
    )(upper, g, coef, join, far)


def ghost_body(
    half_ref, u_ref, coef_ref, join_ref, row_ref, col_ref, along_ref, across_ref, near_ref,
    far_ref, out_ref, g_ref,
):
    planes, rows, width = u_ref.shape
    upper = half_ref[0]
    row_odd = lax.broadcasted_iota(jnp.int32, (rows, width), 0) % 2 == 1
    col_odd = lax.broadcasted_iota(jnp.int32, (rows, width), 1) % 2 == 1
    row_value, col_value = row_ref[...], col_ref[...]

    def layer(index):
        even = along_ref[index : index + 1, :]
        odd = along_ref[2 * planes + index : 2 * planes + index + 1, :]
        side_y = row_value * jnp.where(row_odd, odd, even)
        even = across_ref[:, index : index + 1]
        odd = across_ref[:, 2 * planes + index : 2 * planes + index + 1]
        return side_y + col_value * jnp.where(col_odd, odd, even)

    own, far = near_ref[...], far_ref[...]
    for j in range(planes):
        coef = coef_ref[j]
        own = (layer(j) + own) * coef
        far = (layer(planes + j) + far) * coef
        g_ref[j] = own
    value = (far + coef * own) * join_ref[...]
    for j in range(planes - 1, -1, -1):
        value = g_ref[j] + coef_ref[j] * value
        place = jnp.where(upper == 1, planes - 1 - j, j)
        out_ref[place] = u_ref[place] + value


def add_ghost(upper, u, coef, join, row_value, col_value, along, across, near, far, width=WIDTH, first=0):
    planes, rows, cols = u.shape
    block, flat = block_specs(planes, rows, width)
    far_block, far_flat = block_specs(planes, rows, width, first)
    return pl.pallas_call(
        ghost_body,
        grid_spec=pltpu.PrefetchScalarGridSpec(
            num_scalar_prefetch=1,
            grid=(cols // width,),
            in_specs=[
                block,
                far_block,
                far_flat,
                pl.BlockSpec((rows, 1), lambda i, u: (0, 0)),
                pl.BlockSpec((1, width), lambda i, u: (0, i + first)),
                pl.BlockSpec((4 * planes, width), lambda i, u: (0, i)),
                pl.BlockSpec((rows, 4 * planes), lambda i, u: (0, 0)),
                flat,
                flat,
            ],
            out_specs=block,
            scratch_shapes=[pltpu.VMEM((planes, rows, width), jnp.float32)],
        ),
        out_shape=jax.ShapeDtypeStruct(u.shape, jnp.float32),
    )(upper, u, coef, join, row_value, col_value, along, across, near, far)


def boundary_body(
    half_ref, g_ref, coef_ref, join_ref, far_ref, row_ref, col_ref, fold_ref, mine_ref,
    pick_row_ref, pick_col_ref, front_ref, back_ref, part_ref, face_ref, rows_ref, cols_ref,
    stage_ref, u_ref,
):
    planes, rows, width = g_ref.shape
    upper = half_ref[0]
    step = pl.program_id(0)

    @pl.when(step == 0)
    def _():
        face_ref[...] = jnp.zeros_like(face_ref)
        rows_ref[...] = jnp.zeros_like(rows_ref)
        cols_ref[...] = jnp.zeros_like(cols_ref)

    row_value, col_value = row_ref[...], col_ref[...]
    value = (far_ref[...] + coef_ref[planes - 1] * g_ref[planes - 1]) * join_ref[...]
    for j in range(planes - 1, -1, -1):
        value = g_ref[j] + coef_ref[j] * value
        u_ref[jnp.where(upper == 1, planes - 1 - j, j)] = value
        by_row = value * row_value
        total = by_row[:8]
        for k in range(8, rows, 8):
            total = total + by_row[k : k + 8]
        stage_ref[8 * j : 8 * j + 8, :] = total
        by_col = value * col_value
        total = by_col[:, :PANELS]
        for k in range(PANELS, width, PANELS):
            total = total + by_col[:, k : k + PANELS]
        cols_ref[:, j * PANELS : (j + 1) * PANELS] += total
    for target, turn in ((front_ref, 0), (back_ref, 1)):

        @pl.when(step == turn)
        def _(target=target):
            target[...] = u_ref[...]

    fold = fold_ref[...]
    face_ref[...] += dot(value, fold)
    rows_ref[...] += dot(stage_ref[...], fold)

    @pl.when(step == pl.num_programs(0) - 1)
    def _():
        mine = mine_ref[...]
        part_ref[:PANELS, :] = dot(mine, face_ref[...], TN)
        part_ref[PANELS : PANELS + 2 * planes, :] = dot(pick_row_ref[...], rows_ref[...])
        part_ref[PANELS + 2 * planes :, :] = dot(
            dot(cols_ref[...], pick_col_ref[...]), mine, TN
        )


def finish_boundary(upper, g, coef, join, far, row_value, col_value, fold, mine):
    planes, rows, cols = g.shape
    width = cols // 2
    block, flat = block_specs(planes, rows, width)
    still = pl.BlockSpec((planes, rows, width), lambda i, u: (0, 0, 0))
    pick_row = np.zeros((2, planes, planes, 8), np.float32)
    pick_col = np.zeros((planes, PANELS, 2, planes), np.float32)
    for j in range(planes):
        for t in (0, 1):
            pick_row[t, j, j, t::2] = 1.0
            pick_col[j, t::2, t, j] = 1.0
    whole = lambda shape: pl.BlockSpec(shape, lambda i, u: (0, 0))
    f32 = jnp.float32
    return pl.pallas_call(
        boundary_body,
        grid_spec=pltpu.PrefetchScalarGridSpec(
            num_scalar_prefetch=1,
            grid=(2,),
            in_specs=[
                block,
                block,
                flat,
                flat,
                whole((rows, 1)),
                pl.BlockSpec((1, width), lambda i, u: (0, i)),
                pl.BlockSpec((width, PANELS), lambda i, u: (i, 0)),
                whole((rows, PANELS)),
                whole((2 * planes, 8 * planes)),
                whole((planes * PANELS, 2 * planes)),
            ],
            out_specs=[still, still, whole((PANELS + 4 * planes, PANELS))],
            scratch_shapes=[
                pltpu.VMEM((rows, PANELS), f32),
                pltpu.VMEM((8 * planes, PANELS), f32),
                pltpu.VMEM((rows, planes * PANELS), f32),
                pltpu.VMEM((8 * planes, width), f32),
                pltpu.VMEM((planes, rows, width), f32),
            ],
        ),
        out_shape=[
            jax.ShapeDtypeStruct((planes, rows, width), f32),
            jax.ShapeDtypeStruct((planes, rows, width), f32),
            jax.ShapeDtypeStruct((PANELS + 4 * planes, PANELS), f32),
        ],
    )(
        upper, g, coef, join, far, row_value, col_value, fold, mine,
        pick_row.reshape(2 * planes, -1), pick_col.reshape(-1, 2 * planes),
    )


TINY = 2.0**-60
GROUP = 32
UNROLL = 4
TALL = 24
LANES = 384


def whole_steps(count):
    return (count + UNROLL - 1) // UNROLL * UNROLL


def weight_body(depth, place_ref, row_ref, col_ref, low_ref, high_ref):
    place = place_ref[0]
    first_steps = whole_steps(place - 1)
    behind = (first_steps - (place - 1)).astype(jnp.float32)
    pairs = depth // 2 - place

    def rows(index, _):
        at = pl.ds(pl.multiple_of(index * GROUP, GROUP), GROUP)
        diag = row_ref[at, :] + col_ref[...] + 2.0

        def advance(count, pair):
            for _ in range(count):
                pair = (pair[1], diag * pair[1] - pair[0])
            return pair

        zero = diag - diag
        back, here = zero, zero + 1.0
        for k in range(1, UNROLL):
            step = diag * back - here
            take = behind >= k
            back, here = jnp.where(take, step, back), jnp.where(take, back, here)
        pair = lax.fori_loop(
            0, first_steps // UNROLL, lambda _, pair: advance(UNROLL, pair), (back, here)
        )
        before, near = pair
        pair = advance(1, pair)
        pair = lax.fori_loop(0, pairs // 2, lambda _, pair: advance(4, pair), pair)
        pair = lax.fori_loop(0, pairs % 2, lambda _, pair: advance(2, pair), pair)
        distant = pair[1]
        after = diag * distant - pair[0]
        scale = 1.0 / (near * after - before * distant)
        low_ref[at, :] = distant * scale
        high_ref[at, :] = near * scale
        return 0

    lax.fori_loop(0, low_ref.shape[0] // GROUP, rows, 0)


def weights(depth, place, row_eigen, col_eigen, block):
    grid, cols = row_eigen.shape[0], col_eigen.shape[1]
    out = jax.ShapeDtypeStruct((grid, cols), jnp.float32)
    spec = pl.BlockSpec((block, cols), lambda i, u: (i, 0))
    return pl.pallas_call(
        functools.partial(weight_body, depth),
        grid_spec=pltpu.PrefetchScalarGridSpec(
            num_scalar_prefetch=1,
            grid=(grid // block,),
            in_specs=[
                pl.BlockSpec((block, 1), lambda i, u: (i, 0)),
                pl.BlockSpec((1, cols), lambda i, u: (0, 0)),
            ],
            out_specs=[spec, spec],
        ),
        out_shape=[out, out],
        cost_estimate=pl.CostEstimate(
            flops=4 * depth * grid * cols, bytes_accessed=8 * grid * cols, transcendentals=0
        ),
    )(place, row_eigen, col_eigen)


def plane_body(
    depth, place_ref, low_ref, high_ref, row_eigen_ref, col_eigen_ref, row_ref, col_ref,
    near_ref, distant_ref, side_ref, rows_fold_ref, fold_ref, out_ref, along_ref, across_ref,
    pick_ref,
):
    half = depth // 2
    block, grid = out_ref.shape
    place = place_ref[0]
    levels = [k if k < half else half + depth - 1 - k for k in range(depth)]
    base = whole_steps(half)
    lower_steps = whole_steps(place)
    upper_steps = whole_steps(depth - place)

    def slot(k):
        return jnp.where(
            k < place, lower_steps - 1 - k, base + upper_steps - depth + k
        )

    @pl.when(pl.program_id(0) == 0)
    def _():
        along = dot(side_ref[0], fold_ref[...], NT) * (4.0 * TINY / col_ref[...])
        odd = lax.broadcasted_iota(jnp.int32, (8, grid), 0) % 2 == 1
        for k in range(UNROLL - 1):
            along_ref[k] = jnp.zeros((8, grid), jnp.float32)
            along_ref[base + k] = jnp.zeros((8, grid), jnp.float32)
            across_ref[k] = jnp.zeros((block, PANELS), jnp.float32)
            across_ref[base + k] = jnp.zeros((block, PANELS), jnp.float32)
        for k, at in enumerate(levels):
            even_row = along[at : at + 1, :]
            odd_row = along[depth + at : depth + at + 1, :]
            along_ref[slot(k)] = jnp.where(odd, odd_row, even_row)
        shape = (2 * depth, depth * PANELS)
        column = lax.broadcasted_iota(jnp.int32, shape, 1)
        row = lax.broadcasted_iota(jnp.int32, shape, 0)
        layer = column // PANELS
        layer = jnp.where(layer < half, layer, half + depth - 1 - layer)
        pick = jnp.where(row == (column % 2) * depth + layer, 1.0, 0.0).astype(jnp.bfloat16)
        for k in range(3):
            pick_ref[2 * depth * k : 2 * depth * (k + 1), :] = pick

    across = dot(rows_fold_ref[...], side_ref[1], NT) * (4.0 * TINY / row_ref[...])
    high = across.astype(jnp.bfloat16)
    rest = across - high.astype(jnp.float32)
    middle = rest.astype(jnp.bfloat16)
    low = (rest - middle.astype(jnp.float32)).astype(jnp.bfloat16)
    across = jnp.concatenate([high, middle, low], 1)
    for k in range(0, depth, 2):
        pair = bf16_dot(across, pick_ref[:, k * PANELS : (k + 2) * PANELS])
        across_ref[slot(k)] = pair[:, :PANELS]
        across_ref[slot(k + 1)] = pair[:, PANELS:]

    for part in range(grid // LANES):
        lanes = slice(part * LANES, (part + 1) * LANES)

        def rows(index, _, lanes=lanes):
            at = pl.ds(pl.multiple_of(index * TALL, 8), TALL)
            diag = row_eigen_ref[at, :] + col_eigen_ref[:, lanes] + 2.0
            zero = diag - diag

            def run(first, steps):
                def leap(turn, pair):
                    one, two = pair
                    for k in range(UNROLL):
                        here = first + turn * UNROLL + k
                        along = along_ref[here, :, lanes]
                        across = across_ref[here, at, :]
                        layer = jnp.concatenate([along] * (TALL // 8), 0) + jnp.concatenate(
                            [across] * (LANES // PANELS), 1
                        )
                        one, two = (layer - two) + diag * one, one
                    return one, two

                return lax.fori_loop(0, steps // UNROLL, leap, (zero, zero))[0]

            lower = run(0, lower_steps)
            upper = run(base, upper_steps)
            both = row_ref[at, :] * col_ref[:, lanes] * (1.0 / TINY)
            out_ref[at, lanes] = low_ref[at, lanes] * (
                both * lower + near_ref[at, lanes]
            ) + high_ref[at, lanes] * (both * upper + distant_ref[at, lanes])
            return 0

        lax.fori_loop(0, block // TALL, rows, 0)


def plane_layers(depth, place, low, high, eigen, edge_value, near, distant, side_v, fold, block):
    grid, cols = low.shape
    slots = whole_steps(depth // 2) + whole_steps(depth)
    f32 = jnp.float32
    wide = pl.BlockSpec((block, cols), lambda i, u: (i, 0))
    tall = pl.BlockSpec((block, 1), lambda i, u: (i, 0))
    flat = pl.BlockSpec((1, cols), lambda i, u: (0, 0))
    return pl.pallas_call(
        functools.partial(plane_body, depth),
        grid_spec=pltpu.PrefetchScalarGridSpec(
            num_scalar_prefetch=1,
            grid=(grid // block,),
            in_specs=[
                wide,
                wide,
                tall,
                flat,
                tall,
                flat,
                wide,
                wide,
                pl.BlockSpec(side_v.shape, lambda i, u: (0, 0, 0)),
                pl.BlockSpec((block, PANELS), lambda i, u: (i, 0)),
                pl.BlockSpec((cols, PANELS), lambda i, u: (0, 0)),
            ],
            out_specs=wide,
            scratch_shapes=[
                pltpu.VMEM((slots, 8, cols), f32),
                pltpu.VMEM((slots, block, PANELS), f32),
                pltpu.VMEM((6 * depth, depth * PANELS), jnp.bfloat16),
            ],
        ),
        out_shape=jax.ShapeDtypeStruct((grid, cols), f32),
        cost_estimate=pl.CostEstimate(
            flops=20 * depth * grid * cols, bytes_accessed=24 * grid * cols, transcendentals=0
        ),
    )(
        place, low, high, eigen[:, None], eigen[None, :], edge_value[:, None],
        edge_value[None, :], near, distant, side_v, fold, fold,
    )


def build(mesh, grid, depth):
    slow, fast = mesh.shape["px"], mesh.shape["py"]
    devices = slow * fast
    half = devices // 2
    rows = grid // half
    edge = grid // PANELS
    groups = [list(range(half)), list(range(half, devices))]
    local = depth <= 32 and rows % 8 == 0
    block = grid // 4
    split = grid // 2
    tables = {
        name: value.astype(np.float32) for name, value in small_tables(depth, grid, edge).items()
    }
    sine_np = sine_table(grid).astype(np.float32)
    sine_high = sine_np.astype(jnp.bfloat16)
    sine_low = (sine_np - sine_high.astype(np.float32)).astype(jnp.bfloat16)
    eigen_np = eigen_values(grid)
    fold_np = fold_panels(grid, edge).astype(np.float32)

    def exchange(x):
        return lax.all_to_all(
            x, AXES, split_axis=0, concat_axis=0, tiled=True, axis_index_groups=groups
        )

    def hop(x, bit):
        return lax.ppermute(x, "px", [(i, i ^ bit) for i in range(slow)])

    def on_device(charge):
        rank = lax.axis_index(AXES)
        upper = (rank // half).astype(jnp.int32).reshape(1)
        is_upper = rank // half == 1
        start = (rank % half) * rows
        sine_pair = (jnp.asarray(sine_high), jnp.asarray(sine_low))
        fold = jnp.asarray(fold_np)
        tb = {name: jnp.asarray(value) for name, value in tables.items()}
        eigen = jnp.asarray(eigen_np.astype(np.float32))
        edge_value = jnp.asarray(sine_np[:, 0])
        my_eigen = lax.dynamic_slice_in_dim(eigen, start, rows, 0)
        my_edge = lax.dynamic_slice_in_dim(edge_value, start, rows, 0)
        my_fold = lax.dynamic_slice_in_dim(fold, start, rows, 0)
        mu = my_eigen[:, None] + eigen[None, :]
        parity = jnp.arange(grid) % 2
        edge_pair = jnp.stack([edge_value * (parity == 0), edge_value * (parity == 1)])
        my_pair = jnp.stack([my_edge * (parity[:rows] == 0), my_edge * (parity[:rows] == 1)])

        plane = charge.reshape(grid, grid)
        spectrum = double_product([plane], *sine_pair)
        spectrum = exchange(spectrum.reshape(half, rows, grid))
        coef, join = factors(mu, half)
        mixed = mixed_table(edge, depth, tb["wave_x"])
        corner = corner_table(edge, depth, tb["lift"])
        if local:
            index = (rank % half).astype(jnp.int32)
            place = jnp.where(is_upper, half - index, index + 1).reshape(1)
            weight = weights(depth, place, eigen[:, None], eigen[None, :split], block)
            spectrum, mixed, corner, weight = lax.optimization_barrier(
                (spectrum, mixed, corner, weight)
            )
        else:
            spectrum, mixed, corner = lax.optimization_barrier((spectrum, mixed, corner))
        g, last = sweep(upper, spectrum, coef)
        far = lax.ppermute(last, AXES, [(i, i ^ half) for i in range(devices)])
        if local:
            u, sent, part = finish_boundary(
                upper, g, coef, join, far, my_edge[:, None], edge_value[None, :], fold, my_fold
            )
        else:
            u, outer = finish(upper, g, coef, join, far)

            face = dot(my_fold, dot(outer, fold), ((0,), (0,)))
            lines_y = jnp.einsum("tk,jkx->tjx", my_pair, u, precision=HIGHEST)
            lines_y = jnp.einsum("tjx,xb->tjb", lines_y, fold, precision=HIGHEST)
            lines_x = jnp.einsum("jkx,tx->tjk", u, edge_pair, precision=HIGHEST)
            lines_x = jnp.einsum("tjk,kb->tjb", lines_x, my_fold, precision=HIGHEST)
            lines = jnp.stack([lines_y, lines_x])
            lines = jnp.where(is_upper, lines[:, :, ::-1], lines)
            part = jnp.concatenate([face, lines.reshape(-1, PANELS)])
        part = lax.all_gather(part, "py", axis=0, tiled=False).sum(0)
        bit = 1
        while bit < slow // 2:
            part = part + hop(part, bit)
            bit *= 2
        other = hop(part, bit)
        if local:
            u, part, other = lax.optimization_barrier((u, part, other))
            u = exchange(u).reshape(grid, split)
        face_v, side_v = panel_potential(part, other, tb, mixed, corner)
        if local:
            back = fold[split:]
            near, distant = (
                4.0 * dot(dot(my_fold, face_v[i]), back, NT, precision=HIGH) for i in (0, 1)
            )
            along = 4.0 * dot(side_v[0], back, NT)
            across = 4.0 * dot(my_fold, side_v[1], NT)
            sent = add_ghost(
                upper, sent, coef, join, my_edge[:, None], edge_value[None, :], along, across,
                near, distant, split, 1,
            )
            sent = exchange(sent).reshape(grid, split)
            front = fold[:split]
            rows_v = dot(fold * 4.0, jnp.concatenate([face_v[0], face_v[1]], 1), precision=HIGH)
            near = dot(rows_v[:, :PANELS], front, NT, precision=HIGH)
            distant = dot(rows_v[:, PANELS:], front, NT, precision=HIGH)
            layers = plane_layers(
                depth, place, *weight, eigen, edge_value, near, distant, side_v, fold, block
            )
            return double_product([u, layers, sent], *sine_pair)[None]
        else:
            near, distant = (
                4.0 * dot(dot(my_fold, face_v[i]), fold, ((1,), (1,))) for i in (0, 1)
            )
            along = 4.0 * dot(side_v[0], fold, ((1,), (1,)))
            across = 4.0 * dot(my_fold, side_v[1], ((1,), (1,)))
            u = add_ghost(
                upper, u, coef, join, my_edge[:, None], edge_value[None, :], along, across, near, distant
            )
            u = exchange(u).reshape(grid, grid)
        return double_product([u], *sine_pair)[None]

    return on_device


def solution(mesh):
    spec = P(AXES, None, None)

    def run(charge):
        depth, grid, _ = charge.shape
        body = build(mesh, grid, depth)
        return jax.shard_map(body, mesh=mesh, in_specs=(spec,), out_specs=spec, check_vma=False)(
            charge
        )

    return run
```

```python
import functools
import math

import jax
import jax.numpy as jnp
import numpy as np
from jax import lax
from jax.experimental import pallas as pl
from jax.experimental.pallas import tpu as pltpu
from jax.sharding import PartitionSpec as P

PANELS = 128
HIGHEST = lax.Precision.HIGHEST
HIGH = lax.Precision.HIGH
FOUR_PI = 4.0 * math.pi
AXES = ("px", "py")


def dot(a, b, dims=((1,), (0,)), precision=HIGHEST):
    return lax.dot_general(
        a, b, (dims, ((), ())), precision=precision, preferred_element_type=jnp.float32
    )


def sine_table(n):
    order = np.arange(1, n + 1, dtype=np.int64)
    phase = (order[:, None] * order[None, :]) % (2 * (n + 1))
    return np.sqrt(2.0 / (n + 1)) * np.sin(np.pi * phase / (n + 1.0))


def eigen_values(n):
    return 2.0 - 2.0 * np.cos(np.pi * np.arange(1, n + 1) / (n + 1.0))


def fold_panels(grid, edge):
    sums = sine_table(grid).reshape(grid, PANELS, edge).sum(2)[:, : PANELS // 2]
    even = (np.arange(grid) % 2 == 0)[:, None]
    return np.concatenate([np.where(even, sums, 0.0), np.where(even, 0.0, sums)], axis=1)


def wave_basis(n):
    place = np.arange(n // 2) - (n - 1) / 2.0
    even = np.cos(np.pi * np.arange(n)[:, None] * place[None, :] / n)
    even *= np.sqrt(np.where(np.arange(n) == 0, 1.0, 2.0) / n)[:, None]
    odd = np.sin(np.pi * np.arange(1, n + 1)[:, None] * place[None, :] / n)
    odd *= np.sqrt(np.where(np.arange(1, n + 1) == n, 1.0, 2.0) / n)[:, None]
    return even, odd


def wave_values(n):
    distance = np.arange(n)[:, None]
    order = np.concatenate([np.arange(n), np.arange(1, n + 1)])[None, :]
    return np.where(distance == 0, 1.0, 2.0) * np.cos(np.pi * distance * order / n)


def halves(value):
    high = value.astype(jnp.bfloat16)
    return high, (value - high.astype(jnp.float32)).astype(jnp.bfloat16)


def bf16_dot(a, b):
    return lax.dot_general(a, b, (((1,), (0,)), ((), ())), preferred_element_type=jnp.float32)


STRIPE = 256


def product_body(count, high_ref, low_ref, *refs):
    in_refs, out_ref, mid_high_ref, mid_low_ref = refs[:count], *refs[count:]
    grid = out_ref.shape[0]

    def first(index, _):
        at = pl.ds(pl.multiple_of(index * STRIPE, STRIPE), STRIPE)
        value = in_refs[0][at, :]
        if count == 3:
            value = jnp.concatenate([value + in_refs[1][at, :], in_refs[2][at, :]], 1)
        high, low = halves(value)
        value = bf16_dot(high, high_ref[...])
        value = value + bf16_dot(high, low_ref[...])
        value = value + bf16_dot(low, high_ref[...])
        high, low = halves(value)
        mid_high_ref[at, :] = high
        mid_low_ref[at, :] = low
        return 0

    lax.fori_loop(0, grid // STRIPE, first, 0)

    def second(index, _):
        at = pl.ds(pl.multiple_of(index * STRIPE, STRIPE), STRIPE)
        value = bf16_dot(high_ref[at, :], mid_high_ref[...])
        value = value + bf16_dot(high_ref[at, :], mid_low_ref[...])
        value = value + bf16_dot(low_ref[at, :], mid_high_ref[...])
        out_ref[at, :] = value
        return 0

    lax.fori_loop(0, grid // STRIPE, second, 0)


def double_product(values, high, low):
    grid = high.shape[0]
    return pl.pallas_call(
        functools.partial(product_body, len(values)),
        out_shape=jax.ShapeDtypeStruct((grid, grid), jnp.float32),
        scratch_shapes=[
            pltpu.VMEM((grid, grid), jnp.bfloat16),
            pltpu.VMEM((grid, grid), jnp.bfloat16),
        ],
    )(high, low, *values)


def distance_power(*squares):
    return lax.rsqrt(functools.reduce(lambda a, b: a + b, squares))


def iota(shape, axis):
    return lax.broadcasted_iota(jnp.int32, shape, axis).astype(jnp.float32)


LEVELS = 4


def mixed_body(edge, depth, wave_ref, out_ref):
    hb = PANELS // 2
    soft = edge * edge / 4.0
    shape = (hb, PANELS)
    first = (edge - 1) / 2.0 + 1.0
    front = iota(shape, 0) * edge + first
    back = (PANELS - 1 - iota(shape, 0)) * edge + first
    along = iota(shape, 1) * edge
    along = along * along + soft
    front = front * front + along
    back = back * back + along
    rows = []
    for k in range(LEVELS):
        level = (pl.program_id(0) * LEVELS + k + 1).astype(jnp.float32)
        own = level * level
        far = (depth + 1.0 - level) * (depth + 1.0 - level)
        own_front, own_back = distance_power(front, own), distance_power(back, own)
        far_front, far_back = distance_power(front, far), distance_power(back, far)
        for sign in (1.0, -1.0):
            one, two = own_front + sign * far_front, own_back + sign * far_back
            rows += [one + two, one - two]
    value = dot(jnp.concatenate(rows, 0), wave_ref[...])
    for k in range(LEVELS):
        for s in (0, 1):
            at = (2 * k + s) * PANELS
            out_ref[s, k] = value[at : at + PANELS]


def mixed_table(edge, depth, wave):
    half = depth // 2
    return pl.pallas_call(
        functools.partial(mixed_body, edge, depth),
        grid=(half // LEVELS,),
        in_specs=[pl.BlockSpec((PANELS, 2 * PANELS), lambda i: (0, 0))],
        out_specs=pl.BlockSpec((2, LEVELS, PANELS, 2 * PANELS), lambda i: (0, i, 0, 0)),
        out_shape=jax.ShapeDtypeStruct((2, half, PANELS, 2 * PANELS), jnp.float32),
        cost_estimate=pl.CostEstimate(
            flops=2 * depth * PANELS**3, bytes_accessed=4 * depth * PANELS * PANELS,
            transcendentals=0,
        ),
    )(wave)


STRIP = 8


def corner_body(edge, depth, wave_ref, front_ref, back_ref):
    hb = PANELS // 2
    soft = edge * edge / 4.0
    shape = (hb, 2 * depth)
    first = (edge - 1) / 2.0 + 1.0
    lane = lax.broadcasted_iota(jnp.int32, shape, 1)
    odd = lane >= depth
    level = jnp.where(odd, lane - depth, lane).astype(jnp.float32)
    sign = jnp.where(odd, -1.0, 1.0)
    level = level * level + soft
    near = iota(shape, 0) * edge + first
    distant = (PANELS - 1 - iota(shape, 0)) * edge + first
    near = near * near + level
    distant = distant * distant + level
    sums, gaps = [], []
    for k in range(STRIP):
        b = (pl.program_id(0) * STRIP + k).astype(jnp.float32)
        front = b * edge + first
        back = (PANELS - 1 - b) * edge + first
        front, back = front * front, back * back
        one = distance_power(near, front) + sign * distance_power(distant, front)
        two = distance_power(near, back) + sign * distance_power(distant, back)
        sums.append(one + two)
        gaps.append(one - two)
    wave = wave_ref[...]
    front_ref[...] = dot(jnp.concatenate(sums, 0), wave).reshape(front_ref.shape)
    back_ref[...] = dot(jnp.concatenate(gaps, 0), wave).reshape(back_ref.shape)


def corner_table(edge, depth, wave):
    hb = PANELS // 2
    width = 4 * depth
    block = pl.BlockSpec((STRIP, hb, width), lambda i: (i, 0, 0))
    shape = jax.ShapeDtypeStruct((hb, hb, width), jnp.float32)
    return pl.pallas_call(
        functools.partial(corner_body, edge, depth),
        grid=(hb // STRIP,),
        in_specs=[pl.BlockSpec((2 * depth, width), lambda i: (0, 0))],
        out_specs=[block, block],
        out_shape=[shape, shape],
        cost_estimate=pl.CostEstimate(
            flops=2 * depth * PANELS**3, bytes_accessed=4 * depth * PANELS * PANELS,
            transcendentals=0,
        ),
    )(wave)


def small_tables(depth, grid, edge):
    half = depth // 2
    soft = edge * edge / 4.0

    def kernel(dz, dy, dx):
        return 1.0 / np.sqrt(dz * dz + dy * dy + dx * dx + soft) / FOUR_PI

    step = edge * np.arange(PANELS, dtype=np.float64)
    vx = wave_values(PANELS)
    vz = wave_values(depth)
    even, odd = wave_basis(PANELS)
    zero = np.zeros_like(even)
    basis_x = np.concatenate(
        [np.concatenate([even, zero], 1), np.concatenate([zero, odd], 1)], 0
    )
    bz = np.stack(wave_basis(depth))
    face, side = [], []
    z = np.arange(depth, dtype=np.float64)
    for s, sign in enumerate((1.0, -1.0)):
        k = kernel(0.0, step[:, None], step[None, :])
        k = k + sign * kernel(depth + 1.0, step[:, None], step[None, :])
        face.append(vx.T @ k @ vx)
        for other in (1.0, -1.0):
            k = kernel(z[:, None], 0.0, step[None, :])
            k = k + other * kernel(z[:, None], grid + 1.0, step[None, :])
            side.append(vz[:, s * depth : (s + 1) * depth].T @ k @ vx)
    level = np.zeros((2, 2, half, 2, 2, depth))
    cross = np.zeros((2, 2, half, 2, 2, depth))
    turn = np.zeros((2, 2, 2, half, 2, 2, 2, depth))
    for s in (0, 1):
        for t in (0, 1):
            level[s, t, :, s, t] = bz[s].T
            cross[s, t, :, t, s] = bz[s].T
            for x in (0, 1):
                turn[x, s, t, :, t, x, s] = bz[s].T
    lift = np.zeros((2, depth, 2, 2, depth))
    for x in (0, 1):
        for s in (0, 1):
            lift[x, :, x, s] = vz[:, s * depth : (s + 1) * depth]
    return dict(
        basis=basis_x,
        face=np.stack(face),
        side=np.concatenate(side),
        level=level.reshape(4 * half, 4 * depth),
        cross=cross.reshape(4 * half, 4 * depth),
        turn=turn.reshape(2, 4 * half, 8 * depth),
        wave_x=vx / FOUR_PI,
        lift=lift.reshape(2 * depth, 4 * depth) / FOUR_PI,
    )


NT = ((1,), (1,))
TN = ((0,), (0,))


def panels_body(
    own_ref, other_ref, basis_ref, face_ref, side_ref, level_ref, cross_ref, turn_ref,
    mixed_ref, front_ref, back_ref, face_out_ref, side_out_ref,
    fx_ref, hat_ref, acc_ref, toside_ref, xs_ref, tox_ref,
):
    half = mixed_ref.shape[1]
    hb = PANELS // 2
    total = (own_ref[...] + other_ref[...]) * 0.5
    gap = (own_ref[...] - other_ref[...]) * 0.5
    basis = basis_ref[...]
    level = level_ref[...]
    faces = [total[:PANELS], gap[:PANELS]]
    sides = []
    for axis in (0, 1):
        rows = slice(PANELS + axis * 2 * half, PANELS + (axis + 1) * 2 * half)
        sides.append(jnp.concatenate([total[rows], gap[rows]], 0))
        hat_ref[axis] = dot(sides[axis], basis, NT)
    for s in (0, 1):
        fx_ref[0, s] = dot(faces[s], basis, NT)
        fx_ref[1, s] = dot(faces[s], basis, ((0,), (1,)))

    for s in (0, 1):

        def face_rows(block, _, s=s):
            at = pl.multiple_of(block * 8, 8)
            odd = (block >= 8).astype(jnp.int32)
            base = (2 * s + odd) * half

            def add(chunk, acc):
                one, two = acc
                for k in range(8):
                    j = chunk * 8 + k
                    t = mixed_ref[s, j, pl.ds(at, 8), :]
                    one = one + t * hat_ref[0, pl.ds(base + j, 1), :]
                    two = two + t * hat_ref[1, pl.ds(base + j, 1), :]
                return one, two

            zero = jnp.zeros((8, 2 * PANELS), jnp.float32)
            one, two = lax.fori_loop(0, half // 8, add, (zero, zero))
            acc_ref[0, s, pl.ds(at, 8), :] = one
            acc_ref[1, s, pl.ds(at, 8), :] = two
            return 0

        lax.fori_loop(0, PANELS // 8, face_rows, 0)

        def side_rows(j, _, s=s):
            for t in (0, 1):
                sums = [None, None]
                for block in range(hb // 8):
                    rows = slice(t * hb + block * 8, t * hb + block * 8 + 8)
                    table = mixed_ref[s, j, rows, :]
                    for axis in (0, 1):
                        term = table * fx_ref[axis, s, rows, :]
                        sums[axis] = term if block == 0 else sums[axis] + term
                for axis in (0, 1):
                    toside_ref[axis, pl.ds((2 * s + t) * half + j, 1), :] = jnp.sum(
                        sums[axis], axis=0, keepdims=True
                    )
            return 0

        lax.fori_loop(0, half, side_rows, 0)

    xs_ref[...] = dot(sides[1], cross_ref[...], TN)
    ys = dot(sides[0][:, :hb], turn_ref[0], TN) + dot(sides[0][:, hb:], turn_ref[1], TN)
    width = xs_ref.shape[1]
    to_y = []
    for t, table_ref in ((0, front_ref), (1, back_ref)):
        mine = ys[:, t * width : (t + 1) * width]

        def corner_rows(b, acc, t=t, table_ref=table_ref, mine=mine):
            table = table_ref[b]
            row = pl.ds(t * hb + b, 1)
            tox_ref[row, :] = jnp.sum(table * mine, axis=0, keepdims=True)
            return acc + table * xs_ref[row, :]

        to_y.append(lax.fori_loop(0, hb, corner_rows, jnp.zeros((hb, width), jnp.float32)))
    to_y = jnp.concatenate(to_y, 1)
    corner = [
        jnp.concatenate([dot(turn_ref[x], to_y, NT) for x in (0, 1)], 1),
        dot(cross_ref[...], tox_ref[...], NT),
    ]
    for axis in (0, 1):
        waves = dot(level, hat_ref[axis], TN) * side_ref[...]
        waves = dot(level, waves) + toside_ref[axis]
        value = dot(waves, basis) + corner[axis]
        even, odd = value[: 2 * half], value[2 * half :]
        for part, v in ((0, even + odd), (1, even - odd)):
            for t in (0, 1):
                at = (2 * t + part) * half
                side_out_ref[axis, at : at + half, :] = v[t * half : (t + 1) * half]
    value = []
    for s in (0, 1):
        full = dot(basis, fx_ref[0, s]) * face_ref[s]
        rows = dot(basis, full, TN) + acc_ref[0, s]
        value.append(dot(rows, basis) + dot(basis, acc_ref[1, s], ((0,), (1,))))
    face_out_ref[0] = value[0] + value[1]
    face_out_ref[1] = value[0] - value[1]


def panel_potential(own, other, tb, mixed, corner):
    half = mixed.shape[1]
    width = corner[0].shape[2]
    f32 = jnp.float32
    return pl.pallas_call(
        panels_body,
        out_shape=[
            jax.ShapeDtypeStruct((2, PANELS, PANELS), f32),
            jax.ShapeDtypeStruct((2, 4 * half, PANELS), f32),
        ],
        scratch_shapes=[
            pltpu.VMEM((2, 2, PANELS, 2 * PANELS), f32),
            pltpu.VMEM((2, 4 * half, 2 * PANELS), f32),
            pltpu.VMEM((2, 2, PANELS, 2 * PANELS), f32),
            pltpu.VMEM((2, 4 * half, 2 * PANELS), f32),
            pltpu.VMEM((PANELS, width), f32),
            pltpu.VMEM((PANELS, width), f32),
        ],
    )(
        own, other, tb["basis"], tb["face"], tb["side"], tb["level"], tb["cross"], tb["turn"],
        mixed, *corner,
    )


WIDTH = 256


def block_specs(planes, rows, width=WIDTH, first=0):
    block = pl.BlockSpec((planes, rows, width), lambda i, *_: (0, 0, i + first))
    flat = pl.BlockSpec((rows, width), lambda i, *_: (0, i + first))
    return block, flat


def factor_body(mu_ref, coef_ref, join_ref):
    planes = coef_ref.shape[0]
    for col in range(0, WIDTH, 128):
        part = slice(col, col + 128)
        diag = mu_ref[:, part] + 2.0
        coef = 1.0 / diag
        coef_ref[0, :, part] = coef
        for j in range(1, planes):
            coef = 1.0 / (diag - coef)
            coef_ref[j, :, part] = coef
        join_ref[:, part] = 1.0 / (1.0 - coef * coef)


def factors(mu, planes):
    rows, cols = mu.shape
    block, flat = block_specs(planes, rows)
    return pl.pallas_call(
        factor_body,
        grid=(cols // WIDTH,),
        in_specs=[flat],
        out_specs=[block, flat],
        out_shape=[
            jax.ShapeDtypeStruct((planes, rows, cols), jnp.float32),
            jax.ShapeDtypeStruct((rows, cols), jnp.float32),
        ],
        cost_estimate=pl.CostEstimate(
            flops=20 * planes * rows * cols, bytes_accessed=4 * planes * rows * cols, transcendentals=0
        ),
    )(mu)


def sweep_body(half_ref, f_ref, coef_ref, g_ref, last_ref):
    planes = f_ref.shape[0]
    upper = half_ref[0]
    value = jnp.zeros_like(last_ref)
    for j in range(planes):
        place = jnp.where(upper == 1, planes - 1 - j, j)
        value = (f_ref[place] + value) * coef_ref[j]
        g_ref[j] = value
    last_ref[...] = value


def sweep(upper, spectrum, coef):
    planes, rows, cols = spectrum.shape
    block, flat = block_specs(planes, rows)
    return pl.pallas_call(
        sweep_body,
        grid_spec=pltpu.PrefetchScalarGridSpec(
            num_scalar_prefetch=1,
            grid=(cols // WIDTH,),
            in_specs=[block, block],
            out_specs=[block, flat],
        ),
        out_shape=[
            jax.ShapeDtypeStruct(spectrum.shape, jnp.float32),
            jax.ShapeDtypeStruct((rows, cols), jnp.float32),
        ],
    )(upper, spectrum, coef)


def reach_body(half_ref, f_ref, coef_ref, last_ref):
    planes = f_ref.shape[0]
    upper = half_ref[0]
    value = jnp.zeros_like(last_ref)
    for j in range(planes):
        place = jnp.where(upper == 1, planes - 1 - j, j)
        value = (f_ref[place] + value) * coef_ref[j]
    last_ref[...] = value


def reach(upper, spectrum, coef):
    planes, rows, cols = spectrum.shape
    block, flat = block_specs(planes, rows)
    return pl.pallas_call(
        reach_body,
        grid_spec=pltpu.PrefetchScalarGridSpec(
            num_scalar_prefetch=1,
            grid=(cols // WIDTH,),
            in_specs=[block, block],
            out_specs=flat,
        ),
        out_shape=jax.ShapeDtypeStruct((rows, cols), jnp.float32),
    )(upper, spectrum, coef)


def finish_body(half_ref, g_ref, coef_ref, join_ref, far_ref, u_ref, edge_ref):
    planes = g_ref.shape[0]
    upper = half_ref[0]
    value = (far_ref[...] + coef_ref[planes - 1] * g_ref[planes - 1]) * join_ref[...]
    for j in range(planes - 1, -1, -1):
        value = g_ref[j] + coef_ref[j] * value
        u_ref[jnp.where(upper == 1, planes - 1 - j, j)] = value
    edge_ref[...] = value


def finish(upper, g, coef, join, far):
    planes, rows, cols = g.shape
    block, flat = block_specs(planes, rows)
    return pl.pallas_call(
        finish_body,
        grid_spec=pltpu.PrefetchScalarGridSpec(
            num_scalar_prefetch=1,
            grid=(cols // WIDTH,),
            in_specs=[block, block, flat, flat],
            out_specs=[block, flat],
        ),
        out_shape=[
            jax.ShapeDtypeStruct(g.shape, jnp.float32),
            jax.ShapeDtypeStruct((rows, cols), jnp.float32),
        ],
    )(upper, g, coef, join, far)


def ghost_body(
    half_ref, u_ref, coef_ref, join_ref, row_ref, col_ref, along_ref, across_ref, near_ref,
    far_ref, out_ref, g_ref,
):
    planes, rows, width = u_ref.shape
    upper = half_ref[0]
    row_odd = lax.broadcasted_iota(jnp.int32, (rows, width), 0) % 2 == 1
    col_odd = lax.broadcasted_iota(jnp.int32, (rows, width), 1) % 2 == 1
    row_value, col_value = row_ref[...], col_ref[...]

    def layer(index):
        even = along_ref[index : index + 1, :]
        odd = along_ref[2 * planes + index : 2 * planes + index + 1, :]
        side_y = row_value * jnp.where(row_odd, odd, even)
        even = across_ref[:, index : index + 1]
        odd = across_ref[:, 2 * planes + index : 2 * planes + index + 1]
        return side_y + col_value * jnp.where(col_odd, odd, even)

    own, far = near_ref[...], far_ref[...]
    for j in range(planes):
        coef = coef_ref[j]
        own = (layer(j) + own) * coef
        far = (layer(planes + j) + far) * coef
        g_ref[j] = own
    value = (far + coef * own) * join_ref[...]
    for j in range(planes - 1, -1, -1):
        value = g_ref[j] + coef_ref[j] * value
        place = jnp.where(upper == 1, planes - 1 - j, j)
        out_ref[place] = u_ref[place] + value


def add_ghost(upper, u, coef, join, row_value, col_value, along, across, near, far):
    planes, rows, cols = u.shape
    width = WIDTH
    block, flat = block_specs(planes, rows)
    return pl.pallas_call(
        ghost_body,
        grid_spec=pltpu.PrefetchScalarGridSpec(
            num_scalar_prefetch=1,
            grid=(cols // width,),
            in_specs=[
                block,
                block,
                flat,
                pl.BlockSpec((rows, 1), lambda i, u: (0, 0)),
                pl.BlockSpec((1, width), lambda i, u: (0, i)),
                pl.BlockSpec((4 * planes, width), lambda i, u: (0, i)),
                pl.BlockSpec((rows, 4 * planes), lambda i, u: (0, 0)),
                flat,
                flat,
            ],
            out_specs=block,
            scratch_shapes=[pltpu.VMEM((planes, rows, width), jnp.float32)],
        ),
        out_shape=jax.ShapeDtypeStruct(u.shape, jnp.float32),
    )(upper, u, coef, join, row_value, col_value, along, across, near, far)


def late_body(
    half_ref, u_ref, coef_ref, join_ref, row_ref, col_ref, face_ref, side_ref, mine_ref, fold_ref,
    out_ref, g_ref, along_ref, across_ref, near_ref, far_ref,
):
    mine, fold = mine_ref[...], fold_ref[...]
    along_ref[...] = 4.0 * dot(side_ref[0], fold, NT)
    across_ref[...] = 4.0 * dot(mine, side_ref[1], NT)
    near_ref[...] = 4.0 * dot(dot(mine, face_ref[0]), fold, NT)
    far_ref[...] = 4.0 * dot(dot(mine, face_ref[1]), fold, NT)
    ghost_body(
        half_ref, u_ref, coef_ref, join_ref, row_ref, col_ref, along_ref, across_ref, near_ref,
        far_ref, out_ref, g_ref,
    )


def add_late(upper, u, coef, join, row_value, col_value, face_v, side_v, mine, fold, width):
    planes, rows, cols = u.shape
    first = (coef.shape[2] - cols) // width
    block, _ = block_specs(planes, rows, width)
    coef_block, join_block = block_specs(planes, rows, width, first)
    f32 = jnp.float32
    return pl.pallas_call(
        late_body,
        grid_spec=pltpu.PrefetchScalarGridSpec(
            num_scalar_prefetch=1,
            grid=(cols // width,),
            in_specs=[
                block,
                coef_block,
                join_block,
                pl.BlockSpec((rows, 1), lambda i, u: (0, 0)),
                pl.BlockSpec((1, width), lambda i, u: (0, i + first)),
                pl.BlockSpec(face_v.shape, lambda i, u: (0, 0, 0)),
                pl.BlockSpec(side_v.shape, lambda i, u: (0, 0, 0)),
                pl.BlockSpec(mine.shape, lambda i, u: (0, 0)),
                pl.BlockSpec((width, PANELS), lambda i, u: (i + first, 0)),
            ],
            out_specs=block,
            scratch_shapes=[
                pltpu.VMEM((planes, rows, width), f32),
                pltpu.VMEM((4 * planes, width), f32),
                pltpu.VMEM((rows, 4 * planes), f32),
                pltpu.VMEM((rows, width), f32),
                pltpu.VMEM((rows, width), f32),
            ],
        ),
        out_shape=jax.ShapeDtypeStruct(u.shape, f32),
    )(upper, u, coef, join, row_value, col_value, face_v, side_v, mine, fold)


def boundary_body(
    half_ref, f_ref, coef_ref, join_ref, far_ref, row_ref, col_ref, fold_ref, mine_ref,
    pick_row_ref, pick_col_ref, front_ref, back_ref, part_ref, face_ref, rows_ref, cols_ref,
    stage_ref, g_ref,
):
    planes, rows, width = f_ref.shape
    upper = half_ref[0]
    step = pl.program_id(0)

    @pl.when(step == 0)
    def _():
        face_ref[...] = jnp.zeros_like(face_ref)
        rows_ref[...] = jnp.zeros_like(rows_ref)
        cols_ref[...] = jnp.zeros_like(cols_ref)

    row_value, col_value = row_ref[...], col_ref[...]
    value = jnp.zeros_like(far_ref)
    for j in range(planes):
        value = (f_ref[jnp.where(upper == 1, planes - 1 - j, j)] + value) * coef_ref[j]
        g_ref[j] = value
    value = (far_ref[...] + coef_ref[planes - 1] * value) * join_ref[...]
    for j in range(planes - 1, -1, -1):
        value = g_ref[j] + coef_ref[j] * value
        place = jnp.where(upper == 1, planes - 1 - j, j)

        @pl.when(step == 0)
        def _(place=place, value=value):
            front_ref[place] = value

        @pl.when(step != 0)
        def _(place=place, value=value):
            back_ref[place] = value

        by_row = value * row_value
        total = by_row[:8]
        for k in range(8, rows, 8):
            total = total + by_row[k : k + 8]
        stage_ref[8 * j : 8 * j + 8, :] = total
        by_col = value * col_value
        total = by_col[:, :PANELS]
        for k in range(PANELS, width, PANELS):
            total = total + by_col[:, k : k + PANELS]
        cols_ref[:, j * PANELS : (j + 1) * PANELS] += total
    fold = fold_ref[...]
    face_ref[...] += dot(value, fold)
    rows_ref[...] += dot(stage_ref[...], fold)

    @pl.when(step == pl.num_programs(0) - 1)
    def _():
        mine = mine_ref[...]
        part_ref[:PANELS, :] = dot(mine, face_ref[...], TN)
        part_ref[PANELS : PANELS + 2 * planes, :] = dot(pick_row_ref[...], rows_ref[...])
        part_ref[PANELS + 2 * planes :, :] = dot(
            dot(cols_ref[...], pick_col_ref[...]), mine, TN
        )


def finish_boundary(upper, f, coef, join, far, row_value, col_value, fold, mine):
    planes, rows, cols = f.shape
    width = cols // 3
    block, flat = block_specs(planes, rows, width)
    front = pl.BlockSpec((planes, rows, width), lambda i, u: (0, 0, 0))
    back = pl.BlockSpec((planes, rows, width), lambda i, u: (0, 0, jnp.maximum(i - 1, 0)))
    pick_row = np.zeros((2, planes, planes, 8), np.float32)
    pick_col = np.zeros((planes, PANELS, 2, planes), np.float32)
    for j in range(planes):
        for t in (0, 1):
            pick_row[t, j, j, t::2] = 1.0
            pick_col[j, t::2, t, j] = 1.0
    whole = lambda shape: pl.BlockSpec(shape, lambda i, u: (0, 0))
    f32 = jnp.float32
    return pl.pallas_call(
        boundary_body,
        grid_spec=pltpu.PrefetchScalarGridSpec(
            num_scalar_prefetch=1,
            grid=(3,),
            in_specs=[
                block,
                block,
                flat,
                flat,
                whole((rows, 1)),
                pl.BlockSpec((1, width), lambda i, u: (0, i)),
                pl.BlockSpec((width, PANELS), lambda i, u: (i, 0)),
                whole((rows, PANELS)),
                whole((2 * planes, 8 * planes)),
                whole((planes * PANELS, 2 * planes)),
            ],
            out_specs=[front, back, whole((PANELS + 4 * planes, PANELS))],
            scratch_shapes=[
                pltpu.VMEM((rows, PANELS), f32),
                pltpu.VMEM((8 * planes, PANELS), f32),
                pltpu.VMEM((rows, planes * PANELS), f32),
                pltpu.VMEM((8 * planes, width), f32),
                pltpu.VMEM((planes, rows, width), f32),
            ],
        ),
        out_shape=[
            jax.ShapeDtypeStruct((planes, rows, width), f32),
            jax.ShapeDtypeStruct((planes, rows, 2 * width), f32),
            jax.ShapeDtypeStruct((PANELS + 4 * planes, PANELS), f32),
        ],
    )(
        upper, f, coef, join, far, row_value, col_value, fold, mine,
        pick_row.reshape(2 * planes, -1), pick_col.reshape(-1, 2 * planes),
    )


TINY = 2.0**-60
GROUP = 32
UNROLL = 4
TALL = 32
LANES = 256


def whole_steps(count):
    return (count + UNROLL - 1) // UNROLL * UNROLL


def weight_body(depth, place_ref, row_ref, col_ref, low_ref, high_ref):
    place = place_ref[0]
    first_steps = whole_steps(place - 1)
    behind = (first_steps - (place - 1)).astype(jnp.float32)
    pairs = depth // 2 - place

    def rows(index, _):
        at = pl.ds(pl.multiple_of(index * GROUP, GROUP), GROUP)
        diag = row_ref[at, :] + col_ref[...] + 2.0

        def advance(count, pair):
            for _ in range(count):
                pair = (pair[1], diag * pair[1] - pair[0])
            return pair

        zero = diag - diag
        back, here = zero, zero + 1.0
        for k in range(1, UNROLL):
            step = diag * back - here
            take = behind >= k
            back, here = jnp.where(take, step, back), jnp.where(take, back, here)
        pair = lax.fori_loop(
            0, first_steps // UNROLL, lambda _, pair: advance(UNROLL, pair), (back, here)
        )
        before, near = pair
        pair = advance(1, pair)
        pair = lax.fori_loop(0, pairs // 2, lambda _, pair: advance(4, pair), pair)
        pair = lax.fori_loop(0, pairs % 2, lambda _, pair: advance(2, pair), pair)
        distant = pair[1]
        after = diag * distant - pair[0]
        scale = 1.0 / (near * after - before * distant)
        low_ref[at, :] = distant * scale
        high_ref[at, :] = near * scale
        return 0

    lax.fori_loop(0, low_ref.shape[0] // GROUP, rows, 0)


def weights(depth, place, row_eigen, col_eigen, block):
    grid, cols = row_eigen.shape[0], col_eigen.shape[1]
    out = jax.ShapeDtypeStruct((grid, cols), jnp.float32)
    spec = pl.BlockSpec((block, cols), lambda i, u: (i, 0))
    return pl.pallas_call(
        functools.partial(weight_body, depth),
        grid_spec=pltpu.PrefetchScalarGridSpec(
            num_scalar_prefetch=1,
            grid=(grid // block,),
            in_specs=[
                pl.BlockSpec((block, 1), lambda i, u: (i, 0)),
                pl.BlockSpec((1, cols), lambda i, u: (0, 0)),
            ],
            out_specs=[spec, spec],
        ),
        out_shape=[out, out],
        cost_estimate=pl.CostEstimate(
            flops=4 * depth * grid * cols, bytes_accessed=8 * grid * cols, transcendentals=0
        ),
    )(place, row_eigen, col_eigen)


def plane_body(
    depth, place_ref, low_ref, high_ref, row_eigen_ref, col_eigen_ref, row_ref, col_ref,
    near_ref, distant_ref, side_ref, rows_fold_ref, fold_ref, out_ref, along_ref, across_ref,
    pick_ref,
):
    half = depth // 2
    block, grid = out_ref.shape
    place = place_ref[0]
    levels = [k if k < half else half + depth - 1 - k for k in range(depth)]
    base = whole_steps(half)
    lower_steps = whole_steps(place)
    upper_steps = whole_steps(depth - place)

    def slot(k):
        return jnp.where(
            k < place, lower_steps - 1 - k, base + upper_steps - depth + k
        )

    @pl.when(pl.program_id(0) == 0)
    def _():
        along = dot(side_ref[0], fold_ref[...], NT) * (4.0 * TINY / col_ref[...])
        odd = lax.broadcasted_iota(jnp.int32, (8, grid), 0) % 2 == 1
        for k in range(UNROLL - 1):
            along_ref[k] = jnp.zeros((8, grid), jnp.float32)
            along_ref[base + k] = jnp.zeros((8, grid), jnp.float32)
            across_ref[k] = jnp.zeros((block, PANELS), jnp.float32)
            across_ref[base + k] = jnp.zeros((block, PANELS), jnp.float32)
        for k, at in enumerate(levels):
            even_row = along[at : at + 1, :]
            odd_row = along[depth + at : depth + at + 1, :]
            along_ref[slot(k)] = jnp.where(odd, odd_row, even_row)
        shape = (2 * depth, depth * PANELS)
        column = lax.broadcasted_iota(jnp.int32, shape, 1)
        row = lax.broadcasted_iota(jnp.int32, shape, 0)
        layer = column // PANELS
        layer = jnp.where(layer < half, layer, half + depth - 1 - layer)
        pick = jnp.where(row == (column % 2) * depth + layer, 1.0, 0.0).astype(jnp.bfloat16)
        for k in range(3):
            pick_ref[2 * depth * k : 2 * depth * (k + 1), :] = pick

    across = dot(rows_fold_ref[...], side_ref[1], NT) * (4.0 * TINY / row_ref[...])
    high = across.astype(jnp.bfloat16)
    rest = across - high.astype(jnp.float32)
    middle = rest.astype(jnp.bfloat16)
    low = (rest - middle.astype(jnp.float32)).astype(jnp.bfloat16)
    across = jnp.concatenate([high, middle, low], 1)
    for k in range(0, depth, 2):
        pair = bf16_dot(across, pick_ref[:, k * PANELS : (k + 2) * PANELS])
        across_ref[slot(k)] = pair[:, :PANELS]
        across_ref[slot(k + 1)] = pair[:, PANELS:]

    for part in range(grid // LANES):
        lanes = slice(part * LANES, (part + 1) * LANES)

        def rows(index, _, lanes=lanes):
            at = pl.ds(pl.multiple_of(index * TALL, 8), TALL)
            diag = row_eigen_ref[at, :] + col_eigen_ref[:, lanes] + 2.0
            zero = diag - diag

            def run(first, steps):
                def leap(turn, pair):
                    one, two = pair
                    for k in range(UNROLL):
                        here = first + turn * UNROLL + k
                        along = along_ref[here, :, lanes]
                        across = across_ref[here, at, :]
                        layer = jnp.concatenate([along] * (TALL // 8), 0) + jnp.concatenate(
                            [across] * (LANES // PANELS), 1
                        )
                        one, two = (layer - two) + diag * one, one
                    return one, two

                return lax.fori_loop(0, steps // UNROLL, leap, (zero, zero))[0]

            lower = run(0, lower_steps)
            upper = run(base, upper_steps)
            both = row_ref[at, :] * col_ref[:, lanes] * (1.0 / TINY)
            out_ref[at, lanes] = low_ref[at, lanes] * (
                both * lower + near_ref[at, lanes]
            ) + high_ref[at, lanes] * (both * upper + distant_ref[at, lanes])
            return 0

        lax.fori_loop(0, block // TALL, rows, 0)


def plane_layers(depth, place, low, high, eigen, edge_value, near, distant, side_v, fold, block):
    grid, cols = low.shape
    slots = whole_steps(depth // 2) + whole_steps(depth)
    f32 = jnp.float32
    wide = pl.BlockSpec((block, cols), lambda i, u: (i, 0))
    tall = pl.BlockSpec((block, 1), lambda i, u: (i, 0))
    flat = pl.BlockSpec((1, cols), lambda i, u: (0, 0))
    return pl.pallas_call(
        functools.partial(plane_body, depth),
        grid_spec=pltpu.PrefetchScalarGridSpec(
            num_scalar_prefetch=1,
            grid=(grid // block,),
            in_specs=[
                wide,
                wide,
                tall,
                flat,
                tall,
                flat,
                wide,
                wide,
                pl.BlockSpec(side_v.shape, lambda i, u: (0, 0, 0)),
                pl.BlockSpec((block, PANELS), lambda i, u: (i, 0)),
                pl.BlockSpec((cols, PANELS), lambda i, u: (0, 0)),
            ],
            out_specs=wide,
            scratch_shapes=[
                pltpu.VMEM((slots, 8, cols), f32),
                pltpu.VMEM((slots, block, PANELS), f32),
                pltpu.VMEM((6 * depth, depth * PANELS), jnp.bfloat16),
            ],
        ),
        out_shape=jax.ShapeDtypeStruct((grid, cols), f32),
        cost_estimate=pl.CostEstimate(
            flops=20 * depth * grid * cols, bytes_accessed=24 * grid * cols, transcendentals=0
        ),
    )(
        place, low, high, eigen[:, None], eigen[None, :], edge_value[:, None],
        edge_value[None, :], near, distant, side_v, fold, fold,
    )


def build(mesh, grid, depth):
    slow, fast = mesh.shape["px"], mesh.shape["py"]
    devices = slow * fast
    half = devices // 2
    rows = grid // half
    edge = grid // PANELS
    groups = [list(range(half)), list(range(half, devices))]
    local = depth <= 32 and rows % 8 == 0
    block = grid // 4
    split = grid // 3
    tables = {
        name: value.astype(np.float32) for name, value in small_tables(depth, grid, edge).items()
    }
    sine_np = sine_table(grid).astype(np.float32)
    sine_high = sine_np.astype(jnp.bfloat16)
    sine_low = (sine_np - sine_high.astype(np.float32)).astype(jnp.bfloat16)
    eigen_np = eigen_values(grid)
    fold_np = fold_panels(grid, edge).astype(np.float32)

    def exchange(x):
        return lax.all_to_all(
            x, AXES, split_axis=0, concat_axis=0, tiled=True, axis_index_groups=groups
        )

    def hop(x, bit):
        return lax.ppermute(x, "px", [(i, i ^ bit) for i in range(slow)])

    def on_device(charge):
        rank = lax.axis_index(AXES)
        upper = (rank // half).astype(jnp.int32).reshape(1)
        is_upper = rank // half == 1
        start = (rank % half) * rows
        sine_pair = (jnp.asarray(sine_high), jnp.asarray(sine_low))
        fold = jnp.asarray(fold_np)
        tb = {name: jnp.asarray(value) for name, value in tables.items()}
        eigen = jnp.asarray(eigen_np.astype(np.float32))
        edge_value = jnp.asarray(sine_np[:, 0])
        my_eigen = lax.dynamic_slice_in_dim(eigen, start, rows, 0)
        my_edge = lax.dynamic_slice_in_dim(edge_value, start, rows, 0)
        my_fold = lax.dynamic_slice_in_dim(fold, start, rows, 0)
        mu = my_eigen[:, None] + eigen[None, :]
        parity = jnp.arange(grid) % 2
        edge_pair = jnp.stack([edge_value * (parity == 0), edge_value * (parity == 1)])
        my_pair = jnp.stack([my_edge * (parity[:rows] == 0), my_edge * (parity[:rows] == 1)])

        plane = charge.reshape(grid, grid)
        spectrum = double_product([plane], *sine_pair)
        spectrum = exchange(spectrum.reshape(half, rows, grid))
        coef, join = factors(mu, half)
        mixed = mixed_table(edge, depth, tb["wave_x"])
        corner = corner_table(edge, depth, tb["lift"])
        if local:
            index = (rank % half).astype(jnp.int32)
            place = jnp.where(is_upper, half - index, index + 1).reshape(1)
            weight = weights(depth, place, eigen[:, None], eigen[None, :split], block)
            spectrum, mixed, corner, weight = lax.optimization_barrier(
                (spectrum, mixed, corner, weight)
            )
        else:
            spectrum, mixed, corner = lax.optimization_barrier((spectrum, mixed, corner))
        if local:
            last = reach(upper, spectrum, coef)
        else:
            g, last = sweep(upper, spectrum, coef)
        far = lax.ppermute(last, AXES, [(i, i ^ half) for i in range(devices)])
        if local:
            u, sent, part = finish_boundary(
                upper, spectrum, coef, join, far, my_edge[:, None], edge_value[None, :], fold,
                my_fold,
            )
        else:
            u, outer = finish(upper, g, coef, join, far)

            face = dot(my_fold, dot(outer, fold), ((0,), (0,)))
            lines_y = jnp.einsum("tk,jkx->tjx", my_pair, u, precision=HIGHEST)
            lines_y = jnp.einsum("tjx,xb->tjb", lines_y, fold, precision=HIGHEST)
            lines_x = jnp.einsum("jkx,tx->tjk", u, edge_pair, precision=HIGHEST)
            lines_x = jnp.einsum("tjk,kb->tjb", lines_x, my_fold, precision=HIGHEST)
            lines = jnp.stack([lines_y, lines_x])
            lines = jnp.where(is_upper, lines[:, :, ::-1], lines)
            part = jnp.concatenate([face, lines.reshape(-1, PANELS)])
        part = lax.all_gather(part, "py", axis=0, tiled=False).sum(0)
        bit = 1
        while bit < slow // 2:
            part = part + hop(part, bit)
            bit *= 2
        other = hop(part, bit)
        if local:
            u, part, other = lax.optimization_barrier((u, part, other))
            u = exchange(u).reshape(grid, split)
        face_v, side_v = panel_potential(part, other, tb, mixed, corner)
        if local:
            sent = add_late(
                upper, sent, coef, join, my_edge[:, None], edge_value[None, :], face_v, side_v,
                my_fold, fold, split,
            )
            sent = exchange(sent).reshape(grid, grid - split)
            front = fold[:split]
            rows_v = dot(fold * 4.0, jnp.concatenate([face_v[0], face_v[1]], 1), precision=HIGH)
            near = dot(rows_v[:, :PANELS], front, NT, precision=HIGH)
            distant = dot(rows_v[:, PANELS:], front, NT, precision=HIGH)
            layers = plane_layers(
                depth, place, *weight, eigen, edge_value, near, distant, side_v, fold, block
            )
            return double_product([u, layers, sent], *sine_pair)[None]
        else:
            near, distant = (
                4.0 * dot(dot(my_fold, face_v[i]), fold, ((1,), (1,))) for i in (0, 1)
            )
            along = 4.0 * dot(side_v[0], fold, ((1,), (1,)))
            across = 4.0 * dot(my_fold, side_v[1], ((1,), (1,)))
            u = add_ghost(
                upper, u, coef, join, my_edge[:, None], edge_value[None, :], along, across, near, distant
            )
            u = exchange(u).reshape(grid, grid)
        return double_product([u], *sine_pair)[None]

    return on_device


def solution(mesh):
    spec = P(AXES, None, None)

    def run(charge):
        depth, grid, _ = charge.shape
        body = build(mesh, grid, depth)
        return jax.shard_map(body, mesh=mesh, in_specs=(spec,), out_specs=spec, check_vma=False)(
            charge
        )

    return run
```

```python
import functools
import math

import jax
import jax.numpy as jnp
import numpy as np
from jax import lax
from jax.experimental import pallas as pl
from jax.experimental.pallas import tpu as pltpu
from jax.sharding import PartitionSpec as P

PANELS = 128
HIGHEST = lax.Precision.HIGHEST
HIGH = lax.Precision.HIGH
FOUR_PI = 4.0 * math.pi
AXES = ("px", "py")


def dot(a, b, dims=((1,), (0,)), precision=HIGHEST):
    return lax.dot_general(
        a, b, (dims, ((), ())), precision=precision, preferred_element_type=jnp.float32
    )


def sine_table(n):
    order = np.arange(1, n + 1, dtype=np.int64)
    phase = (order[:, None] * order[None, :]) % (2 * (n + 1))
    return np.sqrt(2.0 / (n + 1)) * np.sin(np.pi * phase / (n + 1.0))


def eigen_values(n):
    return 2.0 - 2.0 * np.cos(np.pi * np.arange(1, n + 1) / (n + 1.0))


def fold_panels(grid, edge):
    sums = sine_table(grid).reshape(grid, PANELS, edge).sum(2)[:, : PANELS // 2]
    even = (np.arange(grid) % 2 == 0)[:, None]
    return np.concatenate([np.where(even, sums, 0.0), np.where(even, 0.0, sums)], axis=1)


def wave_basis(n):
    place = np.arange(n // 2) - (n - 1) / 2.0
    even = np.cos(np.pi * np.arange(n)[:, None] * place[None, :] / n)
    even *= np.sqrt(np.where(np.arange(n) == 0, 1.0, 2.0) / n)[:, None]
    odd = np.sin(np.pi * np.arange(1, n + 1)[:, None] * place[None, :] / n)
    odd *= np.sqrt(np.where(np.arange(1, n + 1) == n, 1.0, 2.0) / n)[:, None]
    return even, odd


def wave_values(n):
    distance = np.arange(n)[:, None]
    order = np.concatenate([np.arange(n), np.arange(1, n + 1)])[None, :]
    return np.where(distance == 0, 1.0, 2.0) * np.cos(np.pi * distance * order / n)


def halves(value):
    high = value.astype(jnp.bfloat16)
    return high, (value - high.astype(jnp.float32)).astype(jnp.bfloat16)


def bf16_dot(a, b, dims=((1,), (0,))):
    return lax.dot_general(a, b, (dims, ((), ())), preferred_element_type=jnp.float32)


def dot3(a, b, dims=((1,), (0,))):
    a_high, a_low = halves(a)
    b_high, b_low = halves(b)
    value = bf16_dot(a_high, b_high, dims)
    return value + (bf16_dot(a_high, b_low, dims) + bf16_dot(a_low, b_high, dims))


STRIPE = 256


def product_body(count, high_ref, low_ref, *refs):
    in_refs, out_ref, mid_high_ref, mid_low_ref = refs[:count], *refs[count:]
    step = pl.program_id(0)
    stripes = pl.num_programs(0) // 2

    @pl.when(step < stripes)
    def _():
        at = pl.ds(pl.multiple_of(step * STRIPE, STRIPE), STRIPE)
        value = in_refs[0][...]
        if count == 3:
            value = jnp.concatenate([value + in_refs[1][...].T, in_refs[2][...]], 1)
        high, low = halves(value)
        value = bf16_dot(high, high_ref[...])
        value = value + bf16_dot(high, low_ref[...])
        value = value + bf16_dot(low, high_ref[...])
        high, low = halves(value)
        mid_high_ref[at, :] = high
        mid_low_ref[at, :] = low

    @pl.when(step >= stripes)
    def _():
        at = pl.ds(pl.multiple_of((step - stripes) * STRIPE, STRIPE), STRIPE)
        value = bf16_dot(high_ref[at, :], mid_high_ref[...])
        value = value + bf16_dot(high_ref[at, :], mid_low_ref[...])
        value = value + bf16_dot(low_ref[at, :], mid_high_ref[...])
        out_ref[...] = value


def double_product(values, high, low):
    grid = high.shape[0]
    stripes = grid // STRIPE
    table = pl.BlockSpec((grid, grid), lambda i: (0, 0), pipeline_mode=pl.Buffered(1))
    return pl.pallas_call(
        functools.partial(product_body, len(values)),
        grid=(2 * stripes,),
        in_specs=[table, table]
        + [
            pl.BlockSpec((v.shape[0], STRIPE), lambda i: (0, jnp.minimum(i, stripes - 1)))
            if k == 1
            else pl.BlockSpec((STRIPE, v.shape[1]), lambda i: (jnp.minimum(i, stripes - 1), 0))
            for k, v in enumerate(values)
        ],
        out_specs=pl.BlockSpec((STRIPE, grid), lambda i: (jnp.maximum(i - stripes, 0), 0)),
        out_shape=jax.ShapeDtypeStruct((grid, grid), jnp.float32),
        scratch_shapes=[
            pltpu.VMEM((grid, grid), jnp.bfloat16),
            pltpu.VMEM((grid, grid), jnp.bfloat16),
        ],
    )(high, low, *values)


def distance_power(*squares):
    return lax.rsqrt(functools.reduce(lambda a, b: a + b, squares))


def iota(shape, axis):
    return lax.broadcasted_iota(jnp.int32, shape, axis).astype(jnp.float32)


LEVELS = 4


def mixed_body(edge, depth, wave_ref, out_ref):
    hb = PANELS // 2
    soft = edge * edge / 4.0
    shape = (hb, PANELS)
    first = (edge - 1) / 2.0 + 1.0
    front = iota(shape, 0) * edge + first
    back = (PANELS - 1 - iota(shape, 0)) * edge + first
    along = iota(shape, 1) * edge
    along = along * along + soft
    front = front * front + along
    back = back * back + along
    rows = []
    for k in range(LEVELS):
        level = (pl.program_id(0) * LEVELS + k + 1).astype(jnp.float32)
        own = level * level
        far = (depth + 1.0 - level) * (depth + 1.0 - level)
        own_front, own_back = distance_power(front, own), distance_power(back, own)
        far_front, far_back = distance_power(front, far), distance_power(back, far)
        for sign in (1.0, -1.0):
            one, two = own_front + sign * far_front, own_back + sign * far_back
            rows += [one + two, one - two]
    value = dot(jnp.concatenate(rows, 0), wave_ref[...])
    for k in range(LEVELS):
        for s in (0, 1):
            at = (2 * k + s) * PANELS
            out_ref[s, k] = value[at : at + PANELS]


def mixed_table(edge, depth, wave):
    half = depth // 2
    return pl.pallas_call(
        functools.partial(mixed_body, edge, depth),
        grid=(half // LEVELS,),
        in_specs=[pl.BlockSpec((PANELS, 2 * PANELS), lambda i: (0, 0))],
        out_specs=pl.BlockSpec((2, LEVELS, PANELS, 2 * PANELS), lambda i: (0, i, 0, 0)),
        out_shape=jax.ShapeDtypeStruct((2, half, PANELS, 2 * PANELS), jnp.float32),
        cost_estimate=pl.CostEstimate(
            flops=2 * depth * PANELS**3, bytes_accessed=4 * depth * PANELS * PANELS,
            transcendentals=0,
        ),
    )(wave)


STRIP = 8


def corner_body(edge, depth, wave_ref, front_ref, back_ref):
    hb = PANELS // 2
    soft = edge * edge / 4.0
    shape = (hb, 2 * depth)
    first = (edge - 1) / 2.0 + 1.0
    lane = lax.broadcasted_iota(jnp.int32, shape, 1)
    odd = lane >= depth
    level = jnp.where(odd, lane - depth, lane).astype(jnp.float32)
    sign = jnp.where(odd, -1.0, 1.0)
    level = level * level + soft
    near = iota(shape, 0) * edge + first
    distant = (PANELS - 1 - iota(shape, 0)) * edge + first
    near = near * near + level
    distant = distant * distant + level
    sums, gaps = [], []
    for k in range(STRIP):
        b = (pl.program_id(0) * STRIP + k).astype(jnp.float32)
        front = b * edge + first
        back = (PANELS - 1 - b) * edge + first
        front, back = front * front, back * back
        one = distance_power(near, front) + sign * distance_power(distant, front)
        two = distance_power(near, back) + sign * distance_power(distant, back)
        sums.append(one + two)
        gaps.append(one - two)
    wave = wave_ref[...]
    front_ref[...] = dot(jnp.concatenate(sums, 0), wave).reshape(front_ref.shape)
    back_ref[...] = dot(jnp.concatenate(gaps, 0), wave).reshape(back_ref.shape)


def corner_table(edge, depth, wave):
    hb = PANELS // 2
    width = 4 * depth
    block = pl.BlockSpec((STRIP, hb, width), lambda i: (i, 0, 0))
    shape = jax.ShapeDtypeStruct((hb, hb, width), jnp.float32)
    return pl.pallas_call(
        functools.partial(corner_body, edge, depth),
        grid=(hb // STRIP,),
        in_specs=[pl.BlockSpec((2 * depth, width), lambda i: (0, 0))],
        out_specs=[block, block],
        out_shape=[shape, shape],
        cost_estimate=pl.CostEstimate(
            flops=2 * depth * PANELS**3, bytes_accessed=4 * depth * PANELS * PANELS,
            transcendentals=0,
        ),
    )(wave)


def small_tables(depth, grid, edge):
    half = depth // 2
    soft = edge * edge / 4.0

    def kernel(dz, dy, dx):
        return 1.0 / np.sqrt(dz * dz + dy * dy + dx * dx + soft) / FOUR_PI

    step = edge * np.arange(PANELS, dtype=np.float64)
    vx = wave_values(PANELS)
    vz = wave_values(depth)
    even, odd = wave_basis(PANELS)
    zero = np.zeros_like(even)
    basis_x = np.concatenate(
        [np.concatenate([even, zero], 1), np.concatenate([zero, odd], 1)], 0
    )
    bz = np.stack(wave_basis(depth))
    face, side = [], []
    z = np.arange(depth, dtype=np.float64)
    for s, sign in enumerate((1.0, -1.0)):
        k = kernel(0.0, step[:, None], step[None, :])
        k = k + sign * kernel(depth + 1.0, step[:, None], step[None, :])
        face.append(vx.T @ k @ vx)
        for other in (1.0, -1.0):
            k = kernel(z[:, None], 0.0, step[None, :])
            k = k + other * kernel(z[:, None], grid + 1.0, step[None, :])
            side.append(vz[:, s * depth : (s + 1) * depth].T @ k @ vx)
    level = np.zeros((2, 2, half, 2, 2, depth))
    cross = np.zeros((2, 2, half, 2, 2, depth))
    turn = np.zeros((2, 2, 2, half, 2, 2, 2, depth))
    for s in (0, 1):
        for t in (0, 1):
            level[s, t, :, s, t] = bz[s].T
            cross[s, t, :, t, s] = bz[s].T
            for x in (0, 1):
                turn[x, s, t, :, t, x, s] = bz[s].T
    lift = np.zeros((2, depth, 2, 2, depth))
    for x in (0, 1):
        for s in (0, 1):
            lift[x, :, x, s] = vz[:, s * depth : (s + 1) * depth]
    return dict(
        basis=basis_x,
        face=np.stack(face),
        side=np.concatenate(side),
        level=level.reshape(4 * half, 4 * depth),
        cross=cross.reshape(4 * half, 4 * depth),
        turn=turn.reshape(2, 4 * half, 8 * depth),
        wave_x=vx / FOUR_PI,
        lift=lift.reshape(2 * depth, 4 * depth) / FOUR_PI,
    )


NT = ((1,), (1,))
TN = ((0,), (0,))


def panels_body(
    own_ref, other_ref, basis_ref, face_ref, side_ref, level_ref, cross_ref, turn_ref,
    mixed_ref, front_ref, back_ref, face_out_ref, side_out_ref,
    fx_ref, hat_ref, acc_ref, toside_ref, xs_ref, tox_ref,
):
    half = mixed_ref.shape[1]
    hb = PANELS // 2
    total = (own_ref[...] + other_ref[...]) * 0.5
    gap = (own_ref[...] - other_ref[...]) * 0.5
    basis = basis_ref[...]
    level = level_ref[...]
    faces = [total[:PANELS], gap[:PANELS]]
    sides = []
    for axis in (0, 1):
        rows = slice(PANELS + axis * 2 * half, PANELS + (axis + 1) * 2 * half)
        sides.append(jnp.concatenate([total[rows], gap[rows]], 0))
        hat_ref[axis] = dot3(sides[axis], basis, NT)
    for s in (0, 1):
        fx_ref[0, s] = dot3(faces[s], basis, NT)
        fx_ref[1, s] = dot3(faces[s], basis, ((0,), (1,)))

    for s in (0, 1):

        def face_rows(block, _, s=s):
            at = pl.multiple_of(block * 8, 8)
            odd = (block >= 8).astype(jnp.int32)
            base = (2 * s + odd) * half

            def add(chunk, acc):
                one, two = acc
                for k in range(8):
                    j = chunk * 8 + k
                    t = mixed_ref[s, j, pl.ds(at, 8), :]
                    one = one + t * hat_ref[0, pl.ds(base + j, 1), :]
                    two = two + t * hat_ref[1, pl.ds(base + j, 1), :]
                return one, two

            zero = jnp.zeros((8, 2 * PANELS), jnp.float32)
            one, two = lax.fori_loop(0, half // 8, add, (zero, zero))
            acc_ref[0, s, pl.ds(at, 8), :] = one
            acc_ref[1, s, pl.ds(at, 8), :] = two
            return 0

        lax.fori_loop(0, PANELS // 8, face_rows, 0)

        def side_rows(j, _, s=s):
            for t in (0, 1):
                sums = [None, None]
                for block in range(hb // 8):
                    rows = slice(t * hb + block * 8, t * hb + block * 8 + 8)
                    table = mixed_ref[s, j, rows, :]
                    for axis in (0, 1):
                        term = table * fx_ref[axis, s, rows, :]
                        sums[axis] = term if block == 0 else sums[axis] + term
                for axis in (0, 1):
                    toside_ref[axis, pl.ds((2 * s + t) * half + j, 1), :] = jnp.sum(
                        sums[axis], axis=0, keepdims=True
                    )
            return 0

        lax.fori_loop(0, half, side_rows, 0)

    xs_ref[...] = dot3(sides[1], cross_ref[...], TN)
    ys = dot3(sides[0][:, :hb], turn_ref[0], TN) + dot3(sides[0][:, hb:], turn_ref[1], TN)
    width = xs_ref.shape[1]
    to_y = []
    for t, table_ref in ((0, front_ref), (1, back_ref)):
        mine = ys[:, t * width : (t + 1) * width]

        def corner_rows(b, acc, t=t, table_ref=table_ref, mine=mine):
            table = table_ref[b]
            row = pl.ds(t * hb + b, 1)
            tox_ref[row, :] = jnp.sum(table * mine, axis=0, keepdims=True)
            return acc + table * xs_ref[row, :]

        to_y.append(lax.fori_loop(0, hb, corner_rows, jnp.zeros((hb, width), jnp.float32)))
    to_y = jnp.concatenate(to_y, 1)
    corner = [
        jnp.concatenate([dot3(turn_ref[x], to_y, NT) for x in (0, 1)], 1),
        dot3(cross_ref[...], tox_ref[...], NT),
    ]
    for axis in (0, 1):
        waves = dot3(level, hat_ref[axis], TN) * side_ref[...]
        waves = dot3(level, waves) + toside_ref[axis]
        value = dot3(waves, basis) + corner[axis]
        even, odd = value[: 2 * half], value[2 * half :]
        for part, v in ((0, even + odd), (1, even - odd)):
            for t in (0, 1):
                at = (2 * t + part) * half
                side_out_ref[axis, at : at + half, :] = v[t * half : (t + 1) * half]
    value = []
    for s in (0, 1):
        full = dot3(basis, fx_ref[0, s]) * face_ref[s]
        rows = dot3(basis, full, TN) + acc_ref[0, s]
        value.append(dot3(rows, basis) + dot3(basis, acc_ref[1, s], ((0,), (1,))))
    face_out_ref[0] = value[0] + value[1]
    face_out_ref[1] = value[0] - value[1]


def panel_potential(own, other, tb, mixed, corner):
    half = mixed.shape[1]
    width = corner[0].shape[2]
    f32 = jnp.float32
    return pl.pallas_call(
        panels_body,
        out_shape=[
            jax.ShapeDtypeStruct((2, PANELS, PANELS), f32),
            jax.ShapeDtypeStruct((2, 4 * half, PANELS), f32),
        ],
        scratch_shapes=[
            pltpu.VMEM((2, 2, PANELS, 2 * PANELS), f32),
            pltpu.VMEM((2, 4 * half, 2 * PANELS), f32),
            pltpu.VMEM((2, 2, PANELS, 2 * PANELS), f32),
            pltpu.VMEM((2, 4 * half, 2 * PANELS), f32),
            pltpu.VMEM((PANELS, width), f32),
            pltpu.VMEM((PANELS, width), f32),
        ],
        cost_estimate=pl.CostEstimate(
            flops=5_000_000_000, bytes_accessed=4 * (mixed.size + 2 * corner[0].size),
            transcendentals=0,
        ),
    )(
        own, other, tb["basis"], tb["face"], tb["side"], tb["level"], tb["cross"], tb["turn"],
        mixed, *corner,
    )


WIDTH = 256


def block_specs(planes, rows, width=WIDTH, first=0):
    block = pl.BlockSpec((planes, rows, width), lambda i, *_: (0, 0, i + first))
    flat = pl.BlockSpec((rows, width), lambda i, *_: (0, i + first))
    return block, flat


def factor_body(mu_ref, coef_ref, join_ref):
    planes = coef_ref.shape[0]
    for col in range(0, WIDTH, 128):
        part = slice(col, col + 128)
        diag = mu_ref[:, part] + 2.0
        coef = 1.0 / diag
        coef_ref[0, :, part] = coef
        for j in range(1, planes):
            coef = 1.0 / (diag - coef)
            coef_ref[j, :, part] = coef
        join_ref[:, part] = 1.0 / (1.0 - coef * coef)


def factors(mu, planes):
    rows, cols = mu.shape
    block, flat = block_specs(planes, rows)
    return pl.pallas_call(
        factor_body,
        grid=(cols // WIDTH,),
        in_specs=[flat],
        out_specs=[block, flat],
        out_shape=[
            jax.ShapeDtypeStruct((planes, rows, cols), jnp.float32),
            jax.ShapeDtypeStruct((rows, cols), jnp.float32),
        ],
        cost_estimate=pl.CostEstimate(
            flops=20 * planes * rows * cols, bytes_accessed=4 * planes * rows * cols, transcendentals=0
        ),
    )(mu)


def sweep_body(half_ref, f_ref, coef_ref, g_ref, last_ref):
    planes = f_ref.shape[0]
    upper = half_ref[0]
    value = jnp.zeros_like(last_ref)
    for j in range(planes):
        place = jnp.where(upper == 1, planes - 1 - j, j)
        value = (f_ref[place] + value) * coef_ref[j]
        g_ref[j] = value
    last_ref[...] = value


def sweep(upper, spectrum, coef):
    planes, rows, cols = spectrum.shape
    block, flat = block_specs(planes, rows)
    return pl.pallas_call(
        sweep_body,
        grid_spec=pltpu.PrefetchScalarGridSpec(
            num_scalar_prefetch=1,
            grid=(cols // WIDTH,),
            in_specs=[block, block],
            out_specs=[block, flat],
        ),
        out_shape=[
            jax.ShapeDtypeStruct(spectrum.shape, jnp.float32),
            jax.ShapeDtypeStruct((rows, cols), jnp.float32),
        ],
    )(upper, spectrum, coef)


def reach_body(half_ref, f_ref, coef_ref, last_ref):
    planes = f_ref.shape[0]
    upper = half_ref[0]
    value = jnp.zeros_like(last_ref)
    for j in range(planes):
        place = jnp.where(upper == 1, planes - 1 - j, j)
        value = (f_ref[place] + value) * coef_ref[j]
    last_ref[...] = value


def reach(upper, spectrum, coef):
    planes, rows, cols = spectrum.shape
    block, flat = block_specs(planes, rows)
    return pl.pallas_call(
        reach_body,
        grid_spec=pltpu.PrefetchScalarGridSpec(
            num_scalar_prefetch=1,
            grid=(cols // WIDTH,),
            in_specs=[block, block],
            out_specs=flat,
        ),
        out_shape=jax.ShapeDtypeStruct((rows, cols), jnp.float32),
    )(upper, spectrum, coef)


def finish_body(half_ref, g_ref, coef_ref, join_ref, far_ref, u_ref, edge_ref):
    planes = g_ref.shape[0]
    upper = half_ref[0]
    value = (far_ref[...] + coef_ref[planes - 1] * g_ref[planes - 1]) * join_ref[...]
    for j in range(planes - 1, -1, -1):
        value = g_ref[j] + coef_ref[j] * value
        u_ref[jnp.where(upper == 1, planes - 1 - j, j)] = value
    edge_ref[...] = value


def finish(upper, g, coef, join, far):
    planes, rows, cols = g.shape
    block, flat = block_specs(planes, rows)
    return pl.pallas_call(
        finish_body,
        grid_spec=pltpu.PrefetchScalarGridSpec(
            num_scalar_prefetch=1,
            grid=(cols // WIDTH,),
            in_specs=[block, block, flat, flat],
            out_specs=[block, flat],
        ),
        out_shape=[
            jax.ShapeDtypeStruct(g.shape, jnp.float32),
            jax.ShapeDtypeStruct((rows, cols), jnp.float32),
        ],
    )(upper, g, coef, join, far)


def ghost_body(
    half_ref, u_ref, coef_ref, join_ref, row_ref, col_ref, along_ref, across_ref, near_ref,
    far_ref, out_ref, g_ref,
):
    planes, rows, width = u_ref.shape
    upper = half_ref[0]
    row_odd = lax.broadcasted_iota(jnp.int32, (rows, width), 0) % 2 == 1
    col_odd = lax.broadcasted_iota(jnp.int32, (rows, width), 1) % 2 == 1
    row_value, col_value = row_ref[...], col_ref[...]

    def layer(index):
        even = along_ref[index : index + 1, :]
        odd = along_ref[2 * planes + index : 2 * planes + index + 1, :]
        side_y = row_value * jnp.where(row_odd, odd, even)
        even = across_ref[:, index : index + 1]
        odd = across_ref[:, 2 * planes + index : 2 * planes + index + 1]
        return side_y + col_value * jnp.where(col_odd, odd, even)

    own, far = near_ref[...], far_ref[...]
    for j in range(planes):
        coef = coef_ref[j]
        own = (layer(j) + own) * coef
        far = (layer(planes + j) + far) * coef
        g_ref[j] = own
    value = (far + coef * own) * join_ref[...]
    for j in range(planes - 1, -1, -1):
        value = g_ref[j] + coef_ref[j] * value
        place = jnp.where(upper == 1, planes - 1 - j, j)
        out_ref[place] = u_ref[place] + value


def add_ghost(upper, u, coef, join, row_value, col_value, along, across, near, far):
    planes, rows, cols = u.shape
    width = WIDTH
    block, flat = block_specs(planes, rows)
    return pl.pallas_call(
        ghost_body,
        grid_spec=pltpu.PrefetchScalarGridSpec(
            num_scalar_prefetch=1,
            grid=(cols // width,),
            in_specs=[
                block,
                block,
                flat,
                pl.BlockSpec((rows, 1), lambda i, u: (0, 0)),
                pl.BlockSpec((1, width), lambda i, u: (0, i)),
                pl.BlockSpec((4 * planes, width), lambda i, u: (0, i)),
                pl.BlockSpec((rows, 4 * planes), lambda i, u: (0, 0)),
                flat,
                flat,
            ],
            out_specs=block,
            scratch_shapes=[pltpu.VMEM((planes, rows, width), jnp.float32)],
        ),
        out_shape=jax.ShapeDtypeStruct(u.shape, jnp.float32),
    )(upper, u, coef, join, row_value, col_value, along, across, near, far)


def late_body(
    half_ref, u_ref, coef_ref, join_ref, row_ref, col_ref, face_ref, side_ref, mine_ref, fold_ref,
    out_ref, g_ref, along_ref, across_ref, near_ref, far_ref,
):
    mine, fold = mine_ref[...], fold_ref[...]
    along_ref[...] = 4.0 * dot3(side_ref[0], fold, NT)
    across_ref[...] = 4.0 * dot3(mine, side_ref[1], NT)
    near_ref[...] = 4.0 * dot3(dot3(mine, face_ref[0]), fold, NT)
    far_ref[...] = 4.0 * dot3(dot3(mine, face_ref[1]), fold, NT)
    ghost_body(
        half_ref, u_ref, coef_ref, join_ref, row_ref, col_ref, along_ref, across_ref, near_ref,
        far_ref, out_ref, g_ref,
    )


def add_late(upper, u, coef, join, row_value, col_value, face_v, side_v, mine, fold, width):
    planes, rows, cols = u.shape
    first = (coef.shape[2] - cols) // width
    block, _ = block_specs(planes, rows, width)
    coef_block, join_block = block_specs(planes, rows, width, first)
    f32 = jnp.float32
    return pl.pallas_call(
        late_body,
        grid_spec=pltpu.PrefetchScalarGridSpec(
            num_scalar_prefetch=1,
            grid=(cols // width,),
            in_specs=[
                block,
                coef_block,
                join_block,
                pl.BlockSpec((rows, 1), lambda i, u: (0, 0)),
                pl.BlockSpec((1, width), lambda i, u: (0, i + first)),
                pl.BlockSpec(face_v.shape, lambda i, u: (0, 0, 0)),
                pl.BlockSpec(side_v.shape, lambda i, u: (0, 0, 0)),
                pl.BlockSpec(mine.shape, lambda i, u: (0, 0)),
                pl.BlockSpec((width, PANELS), lambda i, u: (i + first, 0)),
            ],
            out_specs=block,
            scratch_shapes=[
                pltpu.VMEM((planes, rows, width), f32),
                pltpu.VMEM((4 * planes, width), f32),
                pltpu.VMEM((rows, 4 * planes), f32),
                pltpu.VMEM((rows, width), f32),
                pltpu.VMEM((rows, width), f32),
            ],
        ),
        out_shape=jax.ShapeDtypeStruct(u.shape, f32),
        cost_estimate=pl.CostEstimate(
            flops=40 * planes * rows * cols, bytes_accessed=12 * planes * rows * cols,
            transcendentals=0,
        ),
    )(upper, u, coef, join, row_value, col_value, face_v, side_v, mine, fold)


def boundary_body(
    half_ref, f_ref, coef_ref, join_ref, far_ref, row_ref, col_ref, fold_ref, mine_ref,
    pick_row_ref, pick_col_ref, front_ref, back_ref, part_ref, face_ref, rows_ref, cols_ref,
    stage_ref, g_ref,
):
    planes, rows, width = f_ref.shape
    upper = half_ref[0]
    step = pl.program_id(0)

    @pl.when(step == 0)
    def _():
        face_ref[...] = jnp.zeros_like(face_ref)
        rows_ref[...] = jnp.zeros_like(rows_ref)
        cols_ref[...] = jnp.zeros_like(cols_ref)

    row_value, col_value = row_ref[...], col_ref[...]
    value = jnp.zeros_like(far_ref)
    for j in range(planes):
        value = (f_ref[jnp.where(upper == 1, planes - 1 - j, j)] + value) * coef_ref[j]
        g_ref[j] = value
    value = (far_ref[...] + coef_ref[planes - 1] * value) * join_ref[...]
    for j in range(planes - 1, -1, -1):
        value = g_ref[j] + coef_ref[j] * value
        place = jnp.where(upper == 1, planes - 1 - j, j)

        @pl.when(step == 0)
        def _(place=place, value=value):
            front_ref[place] = value

        @pl.when(step != 0)
        def _(place=place, value=value):
            back_ref[place] = value

        by_row = value * row_value
        total = by_row[:8]
        for k in range(8, rows, 8):
            total = total + by_row[k : k + 8]
        stage_ref[8 * j : 8 * j + 8, :] = total
        by_col = value * col_value
        total = by_col[:, :PANELS]
        for k in range(PANELS, width, PANELS):
            total = total + by_col[:, k : k + PANELS]
        cols_ref[:, j * PANELS : (j + 1) * PANELS] += total
    fold = fold_ref[...]
    face_ref[...] += dot3(value, fold)
    rows_ref[...] += dot3(stage_ref[...], fold)

    @pl.when(step == pl.num_programs(0) - 1)
    def _():
        mine = mine_ref[...]
        part_ref[:PANELS, :] = dot3(mine, face_ref[...], TN)
        part_ref[PANELS : PANELS + 2 * planes, :] = dot3(pick_row_ref[...], rows_ref[...])
        part_ref[PANELS + 2 * planes :, :] = dot3(
            dot3(cols_ref[...], pick_col_ref[...]), mine, TN
        )


def finish_boundary(upper, f, coef, join, far, row_value, col_value, fold, mine):
    planes, rows, cols = f.shape
    width = cols // 2
    block, flat = block_specs(planes, rows, width)
    front = pl.BlockSpec((planes, rows, width), lambda i, u: (0, 0, 0))
    back = pl.BlockSpec((planes, rows, width), lambda i, u: (0, 0, jnp.maximum(i - 1, 0)))
    pick_row = np.zeros((2, planes, planes, 8), np.float32)
    pick_col = np.zeros((planes, PANELS, 2, planes), np.float32)
    for j in range(planes):
        for t in (0, 1):
            pick_row[t, j, j, t::2] = 1.0
            pick_col[j, t::2, t, j] = 1.0
    whole = lambda shape: pl.BlockSpec(shape, lambda i, u: (0, 0))
    f32 = jnp.float32
    return pl.pallas_call(
        boundary_body,
        grid_spec=pltpu.PrefetchScalarGridSpec(
            num_scalar_prefetch=1,
            grid=(2,),
            in_specs=[
                block,
                block,
                flat,
                flat,
                whole((rows, 1)),
                pl.BlockSpec((1, width), lambda i, u: (0, i)),
                pl.BlockSpec((width, PANELS), lambda i, u: (i, 0)),
                whole((rows, PANELS)),
                whole((2 * planes, 8 * planes)),
                whole((planes * PANELS, 2 * planes)),
            ],
            out_specs=[front, back, whole((PANELS + 4 * planes, PANELS))],
            scratch_shapes=[
                pltpu.VMEM((rows, PANELS), f32),
                pltpu.VMEM((8 * planes, PANELS), f32),
                pltpu.VMEM((rows, planes * PANELS), f32),
                pltpu.VMEM((8 * planes, width), f32),
                pltpu.VMEM((planes, rows, width), f32),
            ],
        ),
        out_shape=[
            jax.ShapeDtypeStruct((planes, rows, width), f32),
            jax.ShapeDtypeStruct((planes, rows, cols - width), f32),
            jax.ShapeDtypeStruct((PANELS + 4 * planes, PANELS), f32),
        ],
    )(
        upper, f, coef, join, far, row_value, col_value, fold, mine,
        pick_row.reshape(2 * planes, -1), pick_col.reshape(-1, 2 * planes),
    )


TINY = 2.0**-60
GROUP = 16
UNROLL = 4
TALL = 32
LANES = 256


def whole_steps(count):
    return (count + UNROLL - 1) // UNROLL * UNROLL


def weight_body(depth, place_ref, row_ref, col_ref, low_ref, high_ref):
    place = place_ref[0]
    first_steps = whole_steps(place - 1)
    behind = (first_steps - (place - 1)).astype(jnp.float32)
    pairs = depth // 2 - place

    def rows(index, _):
        at = pl.ds(pl.multiple_of(index * GROUP, GROUP), GROUP)
        diag = row_ref[at, :] + col_ref[...] + 2.0

        def advance(count, pair):
            for _ in range(count):
                pair = (pair[1], diag * pair[1] - pair[0])
            return pair

        zero = diag - diag
        back, here = zero, zero + 1.0
        for k in range(1, UNROLL):
            step = diag * back - here
            take = behind >= k
            back, here = jnp.where(take, step, back), jnp.where(take, back, here)
        pair = lax.fori_loop(
            0, first_steps // UNROLL, lambda _, pair: advance(UNROLL, pair), (back, here)
        )
        before, near = pair
        pair = advance(1, pair)
        pair = lax.fori_loop(0, pairs // 2, lambda _, pair: advance(4, pair), pair)
        pair = lax.fori_loop(0, pairs % 2, lambda _, pair: advance(2, pair), pair)
        distant = pair[1]
        after = diag * distant - pair[0]
        scale = 1.0 / (near * after - before * distant)
        low_ref[at, :] = distant * scale
        high_ref[at, :] = near * scale
        return 0

    lax.fori_loop(0, low_ref.shape[0] // GROUP, rows, 0)


def weights(depth, place, row_eigen, col_eigen, block):
    grid, cols = row_eigen.shape[0], col_eigen.shape[1]
    out = jax.ShapeDtypeStruct((grid, cols), jnp.float32)
    spec = pl.BlockSpec((block, cols), lambda i, u: (i, 0))
    return pl.pallas_call(
        functools.partial(weight_body, depth),
        grid_spec=pltpu.PrefetchScalarGridSpec(
            num_scalar_prefetch=1,
            grid=(grid // block,),
            in_specs=[
                pl.BlockSpec((block, 1), lambda i, u: (i, 0)),
                pl.BlockSpec((1, cols), lambda i, u: (0, 0)),
            ],
            out_specs=[spec, spec],
        ),
        out_shape=[out, out],
        cost_estimate=pl.CostEstimate(
            flops=4 * depth * grid * cols, bytes_accessed=8 * grid * cols, transcendentals=0
        ),
    )(place, row_eigen, col_eigen)


def plane_body(
    depth, place_ref, low_ref, high_ref, row_eigen_ref, col_eigen_ref, row_ref, col_ref,
    near_ref, distant_ref, side_ref, rows_fold_ref, fold_ref, out_ref, along_ref, across_ref,
    pick_ref,
):
    half = depth // 2
    block, grid = out_ref.shape
    place = place_ref[0]
    levels = [k if k < half else half + depth - 1 - k for k in range(depth)]
    base = whole_steps(half)
    lower_steps = whole_steps(place)
    upper_steps = whole_steps(depth - place)

    def slot(k):
        return jnp.where(
            k < place, lower_steps - 1 - k, base + upper_steps - depth + k
        )

    @pl.when(pl.program_id(0) == 0)
    def _():
        along = dot(side_ref[1], fold_ref[...], NT) * (4.0 * TINY / col_ref[...])
        odd = lax.broadcasted_iota(jnp.int32, (8, grid), 0) % 2 == 1
        for k in range(UNROLL - 1):
            along_ref[k] = jnp.zeros((8, grid), jnp.float32)
            along_ref[base + k] = jnp.zeros((8, grid), jnp.float32)
            across_ref[k] = jnp.zeros((block, PANELS), jnp.float32)
            across_ref[base + k] = jnp.zeros((block, PANELS), jnp.float32)
        for k, at in enumerate(levels):
            even_row = along[at : at + 1, :]
            odd_row = along[depth + at : depth + at + 1, :]
            along_ref[slot(k)] = jnp.where(odd, odd_row, even_row)
        shape = (2 * depth, depth * PANELS)
        column = lax.broadcasted_iota(jnp.int32, shape, 1)
        row = lax.broadcasted_iota(jnp.int32, shape, 0)
        layer = column // PANELS
        layer = jnp.where(layer < half, layer, half + depth - 1 - layer)
        pick = jnp.where(row == (column % 2) * depth + layer, 1.0, 0.0).astype(jnp.bfloat16)
        for k in range(3):
            pick_ref[2 * depth * k : 2 * depth * (k + 1), :] = pick

    across = dot(rows_fold_ref[...], side_ref[0], NT) * (4.0 * TINY / row_ref[...])
    high = across.astype(jnp.bfloat16)
    rest = across - high.astype(jnp.float32)
    middle = rest.astype(jnp.bfloat16)
    low = (rest - middle.astype(jnp.float32)).astype(jnp.bfloat16)
    across = jnp.concatenate([high, middle, low], 1)
    for k in range(0, depth, 2):
        pair = bf16_dot(across, pick_ref[:, k * PANELS : (k + 2) * PANELS])
        across_ref[slot(k)] = pair[:, :PANELS]
        across_ref[slot(k + 1)] = pair[:, PANELS:]

    for part in range(grid // LANES):
        lanes = slice(part * LANES, (part + 1) * LANES)

        def rows(index, _, lanes=lanes):
            at = pl.ds(pl.multiple_of(index * TALL, 8), TALL)
            diag = row_eigen_ref[at, :] + col_eigen_ref[:, lanes] + 2.0
            zero = diag - diag

            def run(first, steps):
                def leap(turn, pair):
                    one, two = pair
                    for k in range(UNROLL):
                        here = first + turn * UNROLL + k
                        along = along_ref[here, :, lanes]
                        across = across_ref[here, at, :]
                        layer = jnp.concatenate([along] * (TALL // 8), 0) + jnp.concatenate(
                            [across] * (LANES // PANELS), 1
                        )
                        one, two = (layer - two) + diag * one, one
                    return one, two

                return lax.fori_loop(0, steps // UNROLL, leap, (zero, zero))[0]

            lower = run(0, lower_steps)
            upper = run(base, upper_steps)
            both = row_ref[at, :] * col_ref[:, lanes] * (1.0 / TINY)
            out_ref[at, lanes] = low_ref[at, lanes] * (
                both * lower + near_ref[at, lanes]
            ) + high_ref[at, lanes] * (both * upper + distant_ref[at, lanes])
            return 0

        lax.fori_loop(0, block // TALL, rows, 0)


def plane_layers(depth, place, low, high, eigen, edge_value, near, distant, side_v, fold, block):
    grid, cols = low.shape
    slots = whole_steps(depth // 2) + whole_steps(depth)
    f32 = jnp.float32
    wide = pl.BlockSpec((block, cols), lambda i, u: (i, 0))
    tall = pl.BlockSpec((block, 1), lambda i, u: (i, 0))
    flat = pl.BlockSpec((1, cols), lambda i, u: (0, 0))
    return pl.pallas_call(
        functools.partial(plane_body, depth),
        grid_spec=pltpu.PrefetchScalarGridSpec(
            num_scalar_prefetch=1,
            grid=(grid // block,),
            in_specs=[
                wide,
                wide,
                tall,
                flat,
                tall,
                flat,
                wide,
                wide,
                pl.BlockSpec(side_v.shape, lambda i, u: (0, 0, 0)),
                pl.BlockSpec((block, PANELS), lambda i, u: (i, 0)),
                pl.BlockSpec((cols, PANELS), lambda i, u: (0, 0)),
            ],
            out_specs=wide,
            scratch_shapes=[
                pltpu.VMEM((slots, 8, cols), f32),
                pltpu.VMEM((slots, block, PANELS), f32),
                pltpu.VMEM((6 * depth, depth * PANELS), jnp.bfloat16),
            ],
        ),
        out_shape=jax.ShapeDtypeStruct((grid, cols), f32),
        cost_estimate=pl.CostEstimate(
            flops=20 * depth * grid * cols, bytes_accessed=24 * grid * cols, transcendentals=0
        ),
    )(
        place, low, high, eigen[:grid, None], eigen[None, :], edge_value[:grid, None],
        edge_value[None, :], near, distant, side_v, fold, fold,
    )


def build(mesh, grid, depth):
    slow, fast = mesh.shape["px"], mesh.shape["py"]
    devices = slow * fast
    half = devices // 2
    rows = grid // half
    edge = grid // PANELS
    groups = [list(range(half)), list(range(half, devices))]
    local = depth <= 32 and rows % 8 == 0
    split = grid // 2
    block = split // 2
    tables = {
        name: value.astype(np.float32) for name, value in small_tables(depth, grid, edge).items()
    }
    sine_np = sine_table(grid).astype(np.float32)
    sine_high = sine_np.astype(jnp.bfloat16)
    sine_low = (sine_np - sine_high.astype(np.float32)).astype(jnp.bfloat16)
    eigen_np = eigen_values(grid)
    fold_np = fold_panels(grid, edge).astype(np.float32)

    def exchange(x):
        return lax.all_to_all(
            x, AXES, split_axis=0, concat_axis=0, tiled=True, axis_index_groups=groups
        )

    def hop(x, bit):
        return lax.ppermute(x, "px", [(i, i ^ bit) for i in range(slow)])

    def on_device(charge):
        rank = lax.axis_index(AXES)
        upper = (rank // half).astype(jnp.int32).reshape(1)
        is_upper = rank // half == 1
        start = (rank % half) * rows
        sine_pair = (jnp.asarray(sine_high), jnp.asarray(sine_low))
        fold = jnp.asarray(fold_np)
        tb = {name: jnp.asarray(value) for name, value in tables.items()}
        eigen = jnp.asarray(eigen_np.astype(np.float32))
        edge_value = jnp.asarray(sine_np[:, 0])
        my_eigen = lax.dynamic_slice_in_dim(eigen, start, rows, 0)
        my_edge = lax.dynamic_slice_in_dim(edge_value, start, rows, 0)
        my_fold = lax.dynamic_slice_in_dim(fold, start, rows, 0)
        mu = my_eigen[:, None] + eigen[None, :]
        parity = jnp.arange(grid) % 2
        edge_pair = jnp.stack([edge_value * (parity == 0), edge_value * (parity == 1)])
        my_pair = jnp.stack([my_edge * (parity[:rows] == 0), my_edge * (parity[:rows] == 1)])

        plane = charge.reshape(grid, grid)
        spectrum = double_product([plane], *sine_pair)
        spectrum = exchange(spectrum.reshape(half, rows, grid))
        coef, join = factors(mu, half)
        mixed = mixed_table(edge, depth, tb["wave_x"])
        corner = corner_table(edge, depth, tb["lift"])
        if local:
            index = (rank % half).astype(jnp.int32)
            place = jnp.where(is_upper, half - index, index + 1).reshape(1)
            weight = weights(depth, place, eigen[:split, None], eigen[None, :], block)
            spectrum, mixed, corner, weight = lax.optimization_barrier(
                (spectrum, mixed, corner, weight)
            )
        else:
            spectrum, mixed, corner = lax.optimization_barrier((spectrum, mixed, corner))
        if local:
            last = reach(upper, spectrum, coef)
        else:
            g, last = sweep(upper, spectrum, coef)
        far = lax.ppermute(last, AXES, [(i, i ^ half) for i in range(devices)])
        if local:
            u, sent, part = finish_boundary(
                upper, spectrum, coef, join, far, my_edge[:, None], edge_value[None, :], fold,
                my_fold,
            )
        else:
            u, outer = finish(upper, g, coef, join, far)

            face = dot(my_fold, dot(outer, fold), ((0,), (0,)))
            lines_y = jnp.einsum("tk,jkx->tjx", my_pair, u, precision=HIGHEST)
            lines_y = jnp.einsum("tjx,xb->tjb", lines_y, fold, precision=HIGHEST)
            lines_x = jnp.einsum("jkx,tx->tjk", u, edge_pair, precision=HIGHEST)
            lines_x = jnp.einsum("tjk,kb->tjb", lines_x, my_fold, precision=HIGHEST)
            lines = jnp.stack([lines_y, lines_x])
            lines = jnp.where(is_upper, lines[:, :, ::-1], lines)
            part = jnp.concatenate([face, lines.reshape(-1, PANELS)])
        part = lax.all_gather(part, "py", axis=0, tiled=False).sum(0)
        bit = 1
        while bit < slow // 2:
            part = part + hop(part, bit)
            bit *= 2
        other = hop(part, bit)
        if local:
            early, part, other = lax.optimization_barrier((u, part, other))
            u = exchange(early).reshape(grid, split)
        face_v, side_v = panel_potential(part, other, tb, mixed, corner)
        if local:
            sent = add_late(
                upper, sent, coef, join, my_edge[:, None], edge_value[None, :], face_v, side_v,
                my_fold, fold, split,
            )
            u, sent = lax.optimization_barrier((u, sent))
            sent = exchange(sent).reshape(grid, grid - split)
            near, distant = (
                dot(dot(4.0 * fold[:split], face_v[i], NT, precision=HIGH), fold, NT, precision=HIGH)
                for i in (0, 1)
            )
            layers = plane_layers(
                depth, place, *weight, eigen, edge_value, near, distant, side_v, fold, block,
            )
            return double_product([u, layers, sent], *sine_pair)[None]
        else:
            near, distant = (
                4.0 * dot(dot(my_fold, face_v[i]), fold, ((1,), (1,))) for i in (0, 1)
            )
            along = 4.0 * dot(side_v[0], fold, ((1,), (1,)))
            across = 4.0 * dot(my_fold, side_v[1], ((1,), (1,)))
            u = add_ghost(
                upper, u, coef, join, my_edge[:, None], edge_value[None, :], along, across, near, distant
            )
            u = exchange(u).reshape(grid, grid)
        return double_product([u], *sine_pair)[None]

    return on_device


def solution(mesh):
    spec = P(AXES, None, None)

    def run(charge):
        depth, grid, _ = charge.shape
        body = build(mesh, grid, depth)
        return jax.shard_map(body, mesh=mesh, in_specs=(spec,), out_specs=spec, check_vma=False)(
            charge
        )

    return run
```

```python
import functools
import math

import jax
import jax.numpy as jnp
import numpy as np
from jax import lax
from jax.experimental import pallas as pl
from jax.experimental.pallas import tpu as pltpu
from jax.sharding import PartitionSpec as P

PANELS = 128
HIGHEST = lax.Precision.HIGHEST
HIGH = lax.Precision.HIGH
FOUR_PI = 4.0 * math.pi
AXES = ("px", "py")


def dot(a, b, dims=((1,), (0,)), precision=HIGHEST):
    return lax.dot_general(
        a, b, (dims, ((), ())), precision=precision, preferred_element_type=jnp.float32
    )


def sine_table(n):
    order = np.arange(1, n + 1, dtype=np.int64)
    phase = (order[:, None] * order[None, :]) % (2 * (n + 1))
    return np.sqrt(2.0 / (n + 1)) * np.sin(np.pi * phase / (n + 1.0))


def eigen_values(n):
    return 2.0 - 2.0 * np.cos(np.pi * np.arange(1, n + 1) / (n + 1.0))


def fold_panels(grid, edge):
    sums = sine_table(grid).reshape(grid, PANELS, edge).sum(2)[:, : PANELS // 2]
    even = (np.arange(grid) % 2 == 0)[:, None]
    return np.concatenate([np.where(even, sums, 0.0), np.where(even, 0.0, sums)], axis=1)


def wave_basis(n):
    place = np.arange(n // 2) - (n - 1) / 2.0
    even = np.cos(np.pi * np.arange(n)[:, None] * place[None, :] / n)
    even *= np.sqrt(np.where(np.arange(n) == 0, 1.0, 2.0) / n)[:, None]
    odd = np.sin(np.pi * np.arange(1, n + 1)[:, None] * place[None, :] / n)
    odd *= np.sqrt(np.where(np.arange(1, n + 1) == n, 1.0, 2.0) / n)[:, None]
    return even, odd


def wave_values(n):
    distance = np.arange(n)[:, None]
    order = np.concatenate([np.arange(n), np.arange(1, n + 1)])[None, :]
    return np.where(distance == 0, 1.0, 2.0) * np.cos(np.pi * distance * order / n)


def halves(value):
    high = value.astype(jnp.bfloat16)
    return high, (value - high.astype(jnp.float32)).astype(jnp.bfloat16)


def bf16_dot(a, b, dims=((1,), (0,))):
    return lax.dot_general(a, b, (dims, ((), ())), preferred_element_type=jnp.float32)


def dot3(a, b, dims=((1,), (0,))):
    a_high, a_low = halves(a)
    b_high, b_low = halves(b)
    value = bf16_dot(a_high, b_high, dims)
    return value + (bf16_dot(a_high, b_low, dims) + bf16_dot(a_low, b_high, dims))


STRIPE = 256


def product_body(count, high_ref, low_ref, *refs):
    in_refs, out_ref, mid_high_ref, mid_low_ref = refs[:count], *refs[count:]
    step = pl.program_id(0)
    stripes = pl.num_programs(0) // 2

    @pl.when(step < stripes)
    def _():
        at = pl.ds(pl.multiple_of(step * STRIPE, STRIPE), STRIPE)
        value = in_refs[0][...]
        if count == 3:
            value = jnp.concatenate([value + in_refs[1][...].T, in_refs[2][...]], 1)
        high, low = halves(value)
        value = bf16_dot(high, high_ref[...])
        value = value + bf16_dot(high, low_ref[...])
        value = value + bf16_dot(low, high_ref[...])
        high, low = halves(value)
        mid_high_ref[at, :] = high
        mid_low_ref[at, :] = low

    @pl.when(step >= stripes)
    def _():
        at = pl.ds(pl.multiple_of((step - stripes) * STRIPE, STRIPE), STRIPE)
        value = bf16_dot(high_ref[at, :], mid_high_ref[...])
        value = value + bf16_dot(high_ref[at, :], mid_low_ref[...])
        value = value + bf16_dot(low_ref[at, :], mid_high_ref[...])
        out_ref[...] = value


def double_product(values, high, low):
    grid = high.shape[0]
    stripes = grid // STRIPE
    table = pl.BlockSpec((grid, grid), lambda i: (0, 0), pipeline_mode=pl.Buffered(1))
    return pl.pallas_call(
        functools.partial(product_body, len(values)),
        grid=(2 * stripes,),
        in_specs=[table, table]
        + [
            pl.BlockSpec((v.shape[0], STRIPE), lambda i: (0, jnp.minimum(i, stripes - 1)))
            if k == 1
            else pl.BlockSpec((STRIPE, v.shape[1]), lambda i: (jnp.minimum(i, stripes - 1), 0))
            for k, v in enumerate(values)
        ],
        out_specs=pl.BlockSpec((STRIPE, grid), lambda i: (jnp.maximum(i - stripes, 0), 0)),
        out_shape=jax.ShapeDtypeStruct((grid, grid), jnp.float32),
        scratch_shapes=[
            pltpu.VMEM((grid, grid), jnp.bfloat16),
            pltpu.VMEM((grid, grid), jnp.bfloat16),
        ],
    )(high, low, *values)


def distance_power(*squares):
    return lax.rsqrt(functools.reduce(lambda a, b: a + b, squares))


def iota(shape, axis):
    return lax.broadcasted_iota(jnp.int32, shape, axis).astype(jnp.float32)


LEVELS = 4


def mixed_body(edge, depth, wave_ref, out_ref):
    hb = PANELS // 2
    soft = edge * edge / 4.0
    shape = (hb, PANELS)
    first = (edge - 1) / 2.0 + 1.0
    front = iota(shape, 0) * edge + first
    back = (PANELS - 1 - iota(shape, 0)) * edge + first
    along = iota(shape, 1) * edge
    along = along * along + soft
    front = front * front + along
    back = back * back + along
    rows = []
    for k in range(LEVELS):
        level = (pl.program_id(0) * LEVELS + k + 1).astype(jnp.float32)
        own = level * level
        far = (depth + 1.0 - level) * (depth + 1.0 - level)
        own_front, own_back = distance_power(front, own), distance_power(back, own)
        far_front, far_back = distance_power(front, far), distance_power(back, far)
        for sign in (1.0, -1.0):
            one, two = own_front + sign * far_front, own_back + sign * far_back
            rows += [one + two, one - two]
    value = dot(jnp.concatenate(rows, 0), wave_ref[...])
    for k in range(LEVELS):
        for s in (0, 1):
            at = (2 * k + s) * PANELS
            out_ref[s, k] = value[at : at + PANELS]


def mixed_table(edge, depth, wave):
    half = depth // 2
    return pl.pallas_call(
        functools.partial(mixed_body, edge, depth),
        grid=(half // LEVELS,),
        in_specs=[pl.BlockSpec((PANELS, 2 * PANELS), lambda i: (0, 0))],
        out_specs=pl.BlockSpec((2, LEVELS, PANELS, 2 * PANELS), lambda i: (0, i, 0, 0)),
        out_shape=jax.ShapeDtypeStruct((2, half, PANELS, 2 * PANELS), jnp.float32),
        cost_estimate=pl.CostEstimate(
            flops=2 * depth * PANELS**3, bytes_accessed=4 * depth * PANELS * PANELS,
            transcendentals=0,
        ),
    )(wave)


STRIP = 8


def corner_body(edge, depth, wave_ref, front_ref, back_ref):
    hb = PANELS // 2
    soft = edge * edge / 4.0
    shape = (hb, 2 * depth)
    first = (edge - 1) / 2.0 + 1.0
    lane = lax.broadcasted_iota(jnp.int32, shape, 1)
    odd = lane >= depth
    level = jnp.where(odd, lane - depth, lane).astype(jnp.float32)
    sign = jnp.where(odd, -1.0, 1.0)
    level = level * level + soft
    near = iota(shape, 0) * edge + first
    distant = (PANELS - 1 - iota(shape, 0)) * edge + first
    near = near * near + level
    distant = distant * distant + level
    sums, gaps = [], []
    for k in range(STRIP):
        b = (pl.program_id(0) * STRIP + k).astype(jnp.float32)
        front = b * edge + first
        back = (PANELS - 1 - b) * edge + first
        front, back = front * front, back * back
        one = distance_power(near, front) + sign * distance_power(distant, front)
        two = distance_power(near, back) + sign * distance_power(distant, back)
        sums.append(one + two)
        gaps.append(one - two)
    wave = wave_ref[...]
    front_ref[...] = dot(jnp.concatenate(sums, 0), wave).reshape(front_ref.shape)
    back_ref[...] = dot(jnp.concatenate(gaps, 0), wave).reshape(back_ref.shape)


def corner_table(edge, depth, wave):
    hb = PANELS // 2
    width = 4 * depth
    block = pl.BlockSpec((STRIP, hb, width), lambda i: (i, 0, 0))
    shape = jax.ShapeDtypeStruct((hb, hb, width), jnp.float32)
    return pl.pallas_call(
        functools.partial(corner_body, edge, depth),
        grid=(hb // STRIP,),
        in_specs=[pl.BlockSpec((2 * depth, width), lambda i: (0, 0))],
        out_specs=[block, block],
        out_shape=[shape, shape],
        cost_estimate=pl.CostEstimate(
            flops=2 * depth * PANELS**3, bytes_accessed=4 * depth * PANELS * PANELS,
            transcendentals=0,
        ),
    )(wave)


def small_tables(depth, grid, edge):
    half = depth // 2
    soft = edge * edge / 4.0

    def kernel(dz, dy, dx):
        return 1.0 / np.sqrt(dz * dz + dy * dy + dx * dx + soft) / FOUR_PI

    step = edge * np.arange(PANELS, dtype=np.float64)
    vx = wave_values(PANELS)
    vz = wave_values(depth)
    even, odd = wave_basis(PANELS)
    zero = np.zeros_like(even)
    basis_x = np.concatenate(
        [np.concatenate([even, zero], 1), np.concatenate([zero, odd], 1)], 0
    )
    bz = np.stack(wave_basis(depth))
    face, side = [], []
    z = np.arange(depth, dtype=np.float64)
    for s, sign in enumerate((1.0, -1.0)):
        k = kernel(0.0, step[:, None], step[None, :])
        k = k + sign * kernel(depth + 1.0, step[:, None], step[None, :])
        face.append(vx.T @ k @ vx)
        for other in (1.0, -1.0):
            k = kernel(z[:, None], 0.0, step[None, :])
            k = k + other * kernel(z[:, None], grid + 1.0, step[None, :])
            side.append(vz[:, s * depth : (s + 1) * depth].T @ k @ vx)
    level = np.zeros((2, 2, half, 2, 2, depth))
    cross = np.zeros((2, 2, half, 2, 2, depth))
    turn = np.zeros((2, 2, 2, half, 2, 2, 2, depth))
    for s in (0, 1):
        for t in (0, 1):
            level[s, t, :, s, t] = bz[s].T
            cross[s, t, :, t, s] = bz[s].T
            for x in (0, 1):
                turn[x, s, t, :, t, x, s] = bz[s].T
    lift = np.zeros((2, depth, 2, 2, depth))
    for x in (0, 1):
        for s in (0, 1):
            lift[x, :, x, s] = vz[:, s * depth : (s + 1) * depth]
    return dict(
        basis=basis_x,
        face=np.stack(face),
        side=np.concatenate(side),
        level=level.reshape(4 * half, 4 * depth),
        cross=cross.reshape(4 * half, 4 * depth),
        turn=turn.reshape(2, 4 * half, 8 * depth),
        wave_x=vx / FOUR_PI,
        lift=lift.reshape(2 * depth, 4 * depth) / FOUR_PI,
    )


NT = ((1,), (1,))
TN = ((0,), (0,))


def panels_body(
    own_ref, other_ref, basis_ref, face_ref, side_ref, level_ref, cross_ref, turn_ref,
    mixed_hbm, front_hbm, back_hbm, face_out_ref, side_out_ref,
    fx_ref, hat_ref, acc_ref, toside_ref, xs_ref, tox_ref, mixed_ref, front_ref, back_ref, sems,
):
    half = mixed_ref.shape[1]
    loads = [
        pltpu.make_async_copy(source, target, sems.at[k])
        for k, (source, target) in enumerate(
            ((mixed_hbm, mixed_ref), (front_hbm, front_ref), (back_hbm, back_ref))
        )
    ]
    for load in loads:
        load.start()
    hb = PANELS // 2
    total = (own_ref[...] + other_ref[...]) * 0.5
    gap = (own_ref[...] - other_ref[...]) * 0.5
    basis = basis_ref[...]
    level = level_ref[...]
    faces = [total[:PANELS], gap[:PANELS]]
    sides = []
    for axis in (0, 1):
        rows = slice(PANELS + axis * 2 * half, PANELS + (axis + 1) * 2 * half)
        sides.append(jnp.concatenate([total[rows], gap[rows]], 0))
        hat_ref[axis] = dot3(sides[axis], basis, NT)
    for s in (0, 1):
        fx_ref[0, s] = dot3(faces[s], basis, NT)
        fx_ref[1, s] = dot3(faces[s], basis, ((0,), (1,)))

    loads[0].wait()
    for s in (0, 1):

        def face_rows(block, _, s=s):
            at = pl.multiple_of(block * 8, 8)
            odd = (block >= 8).astype(jnp.int32)
            base = (2 * s + odd) * half

            def add(chunk, acc):
                one, two = acc
                for k in range(8):
                    j = chunk * 8 + k
                    t = mixed_ref[s, j, pl.ds(at, 8), :]
                    one = one + t * hat_ref[0, pl.ds(base + j, 1), :]
                    two = two + t * hat_ref[1, pl.ds(base + j, 1), :]
                return one, two

            zero = jnp.zeros((8, 2 * PANELS), jnp.float32)
            one, two = lax.fori_loop(0, half // 8, add, (zero, zero))
            acc_ref[0, s, pl.ds(at, 8), :] = one
            acc_ref[1, s, pl.ds(at, 8), :] = two
            return 0

        lax.fori_loop(0, PANELS // 8, face_rows, 0)

        def side_rows(j, _, s=s):
            for t in (0, 1):
                sums = [None, None]
                for block in range(hb // 8):
                    rows = slice(t * hb + block * 8, t * hb + block * 8 + 8)
                    table = mixed_ref[s, j, rows, :]
                    for axis in (0, 1):
                        term = table * fx_ref[axis, s, rows, :]
                        sums[axis] = term if block == 0 else sums[axis] + term
                for axis in (0, 1):
                    toside_ref[axis, pl.ds((2 * s + t) * half + j, 1), :] = jnp.sum(
                        sums[axis], axis=0, keepdims=True
                    )
            return 0

        lax.fori_loop(0, half, side_rows, 0)

    xs_ref[...] = dot3(sides[1], cross_ref[...], TN)
    ys = dot3(sides[0][:, :hb], turn_ref[0], TN) + dot3(sides[0][:, hb:], turn_ref[1], TN)
    width = xs_ref.shape[1]
    to_y = []
    loads[1].wait()
    loads[2].wait()
    for t, table_ref in ((0, front_ref), (1, back_ref)):
        mine = ys[:, t * width : (t + 1) * width]

        def corner_rows(b, acc, t=t, table_ref=table_ref, mine=mine):
            table = table_ref[b]
            row = pl.ds(t * hb + b, 1)
            tox_ref[row, :] = jnp.sum(table * mine, axis=0, keepdims=True)
            return acc + table * xs_ref[row, :]

        to_y.append(lax.fori_loop(0, hb, corner_rows, jnp.zeros((hb, width), jnp.float32)))
    to_y = jnp.concatenate(to_y, 1)
    corner = [
        jnp.concatenate([dot3(turn_ref[x], to_y, NT) for x in (0, 1)], 1),
        dot3(cross_ref[...], tox_ref[...], NT),
    ]
    for axis in (0, 1):
        waves = dot3(level, hat_ref[axis], TN) * side_ref[...]
        waves = dot3(level, waves) + toside_ref[axis]
        value = dot3(waves, basis) + corner[axis]
        even, odd = value[: 2 * half], value[2 * half :]
        for part, v in ((0, even + odd), (1, even - odd)):
            for t in (0, 1):
                at = (2 * t + part) * half
                side_out_ref[axis, at : at + half, :] = v[t * half : (t + 1) * half]
    value = []
    for s in (0, 1):
        full = dot3(basis, fx_ref[0, s]) * face_ref[s]
        rows = dot3(basis, full, TN) + acc_ref[0, s]
        value.append(dot3(rows, basis) + dot3(basis, acc_ref[1, s], ((0,), (1,))))
    face_out_ref[0] = value[0] + value[1]
    face_out_ref[1] = value[0] - value[1]


def panel_potential(own, other, tb, mixed, corner):
    half = mixed.shape[1]
    width = corner[0].shape[2]
    f32 = jnp.float32
    vmem = pl.BlockSpec(memory_space=pltpu.VMEM)
    return pl.pallas_call(
        panels_body,
        in_specs=[vmem] * 8 + [pl.BlockSpec(memory_space=pl.ANY)] * 3,
        out_shape=[
            jax.ShapeDtypeStruct((2, PANELS, PANELS), f32),
            jax.ShapeDtypeStruct((2, 4 * half, PANELS), f32),
        ],
        scratch_shapes=[
            pltpu.VMEM((2, 2, PANELS, 2 * PANELS), f32),
            pltpu.VMEM((2, 4 * half, 2 * PANELS), f32),
            pltpu.VMEM((2, 2, PANELS, 2 * PANELS), f32),
            pltpu.VMEM((2, 4 * half, 2 * PANELS), f32),
            pltpu.VMEM((PANELS, width), f32),
            pltpu.VMEM((PANELS, width), f32),
            pltpu.VMEM(mixed.shape, f32),
            pltpu.VMEM(corner[0].shape, f32),
            pltpu.VMEM(corner[1].shape, f32),
            pltpu.SemaphoreType.DMA((3,)),
        ],
        cost_estimate=pl.CostEstimate(
            flops=5_000_000_000, bytes_accessed=4 * (mixed.size + 2 * corner[0].size),
            transcendentals=0,
        ),
    )(
        own, other, tb["basis"], tb["face"], tb["side"], tb["level"], tb["cross"], tb["turn"],
        mixed, *corner,
    )


WIDTH = 256


def block_specs(planes, rows, width=WIDTH, first=0):
    block = pl.BlockSpec((planes, rows, width), lambda i, *_: (0, 0, i + first))
    flat = pl.BlockSpec((rows, width), lambda i, *_: (0, i + first))
    return block, flat


def factor_body(mu_ref, coef_ref, join_ref):
    planes = coef_ref.shape[0]
    for col in range(0, WIDTH, 128):
        part = slice(col, col + 128)
        diag = mu_ref[:, part] + 2.0
        coef = 1.0 / diag
        coef_ref[0, :, part] = coef
        for j in range(1, planes):
            coef = 1.0 / (diag - coef)
            coef_ref[j, :, part] = coef
        join_ref[:, part] = 1.0 / (1.0 - coef * coef)


def factors(mu, planes):
    rows, cols = mu.shape
    block, flat = block_specs(planes, rows)
    return pl.pallas_call(
        factor_body,
        grid=(cols // WIDTH,),
        in_specs=[flat],
        out_specs=[block, flat],
        out_shape=[
            jax.ShapeDtypeStruct((planes, rows, cols), jnp.float32),
            jax.ShapeDtypeStruct((rows, cols), jnp.float32),
        ],
        cost_estimate=pl.CostEstimate(
            flops=20 * planes * rows * cols, bytes_accessed=4 * planes * rows * cols, transcendentals=0
        ),
    )(mu)


def sweep_body(half_ref, f_ref, coef_ref, g_ref, last_ref):
    planes = f_ref.shape[0]
    upper = half_ref[0]
    value = jnp.zeros_like(last_ref)
    for j in range(planes):
        place = jnp.where(upper == 1, planes - 1 - j, j)
        value = (f_ref[place] + value) * coef_ref[j]
        g_ref[j] = value
    last_ref[...] = value


def sweep(upper, spectrum, coef):
    planes, rows, cols = spectrum.shape
    block, flat = block_specs(planes, rows)
    return pl.pallas_call(
        sweep_body,
        grid_spec=pltpu.PrefetchScalarGridSpec(
            num_scalar_prefetch=1,
            grid=(cols // WIDTH,),
            in_specs=[block, block],
            out_specs=[block, flat],
        ),
        out_shape=[
            jax.ShapeDtypeStruct(spectrum.shape, jnp.float32),
            jax.ShapeDtypeStruct((rows, cols), jnp.float32),
        ],
    )(upper, spectrum, coef)


def reach_body(half_ref, f_ref, coef_ref, last_ref):
    planes = f_ref.shape[0]
    upper = half_ref[0]
    value = jnp.zeros_like(last_ref)
    for j in range(planes):
        place = jnp.where(upper == 1, planes - 1 - j, j)
        value = (f_ref[place] + value) * coef_ref[j]
    last_ref[...] = value


def reach(upper, spectrum, coef):
    planes, rows, cols = spectrum.shape
    block, flat = block_specs(planes, rows)
    return pl.pallas_call(
        reach_body,
        grid_spec=pltpu.PrefetchScalarGridSpec(
            num_scalar_prefetch=1,
            grid=(cols // WIDTH,),
            in_specs=[block, block],
            out_specs=flat,
        ),
        out_shape=jax.ShapeDtypeStruct((rows, cols), jnp.float32),
    )(upper, spectrum, coef)


def finish_body(half_ref, g_ref, coef_ref, join_ref, far_ref, u_ref, edge_ref):
    planes = g_ref.shape[0]
    upper = half_ref[0]
    value = (far_ref[...] + coef_ref[planes - 1] * g_ref[planes - 1]) * join_ref[...]
    for j in range(planes - 1, -1, -1):
        value = g_ref[j] + coef_ref[j] * value
        u_ref[jnp.where(upper == 1, planes - 1 - j, j)] = value
    edge_ref[...] = value


def finish(upper, g, coef, join, far):
    planes, rows, cols = g.shape
    block, flat = block_specs(planes, rows)
    return pl.pallas_call(
        finish_body,
        grid_spec=pltpu.PrefetchScalarGridSpec(
            num_scalar_prefetch=1,
            grid=(cols // WIDTH,),
            in_specs=[block, block, flat, flat],
            out_specs=[block, flat],
        ),
        out_shape=[
            jax.ShapeDtypeStruct(g.shape, jnp.float32),
            jax.ShapeDtypeStruct((rows, cols), jnp.float32),
        ],
    )(upper, g, coef, join, far)


def ghost_body(
    half_ref, u_ref, coef_ref, join_ref, row_ref, col_ref, along_ref, across_ref, near_ref,
    far_ref, out_ref, g_ref,
):
    planes, rows, width = u_ref.shape
    upper = half_ref[0]
    row_odd = lax.broadcasted_iota(jnp.int32, (rows, width), 0) % 2 == 1
    col_odd = lax.broadcasted_iota(jnp.int32, (rows, width), 1) % 2 == 1
    row_value, col_value = row_ref[...], col_ref[...]

    def layer(index):
        even = along_ref[index : index + 1, :]
        odd = along_ref[2 * planes + index : 2 * planes + index + 1, :]
        side_y = row_value * jnp.where(row_odd, odd, even)
        even = across_ref[:, index : index + 1]
        odd = across_ref[:, 2 * planes + index : 2 * planes + index + 1]
        return side_y + col_value * jnp.where(col_odd, odd, even)

    own, far = near_ref[...], far_ref[...]
    for j in range(planes):
        coef = coef_ref[j]
        own = (layer(j) + own) * coef
        far = (layer(planes + j) + far) * coef
        g_ref[j] = own
    value = (far + coef * own) * join_ref[...]
    for j in range(planes - 1, -1, -1):
        value = g_ref[j] + coef_ref[j] * value
        place = jnp.where(upper == 1, planes - 1 - j, j)
        out_ref[place] = u_ref[place] + value


def add_ghost(upper, u, coef, join, row_value, col_value, along, across, near, far):
    planes, rows, cols = u.shape
    width = WIDTH
    block, flat = block_specs(planes, rows)
    return pl.pallas_call(
        ghost_body,
        grid_spec=pltpu.PrefetchScalarGridSpec(
            num_scalar_prefetch=1,
            grid=(cols // width,),
            in_specs=[
                block,
                block,
                flat,
                pl.BlockSpec((rows, 1), lambda i, u: (0, 0)),
                pl.BlockSpec((1, width), lambda i, u: (0, i)),
                pl.BlockSpec((4 * planes, width), lambda i, u: (0, i)),
                pl.BlockSpec((rows, 4 * planes), lambda i, u: (0, 0)),
                flat,
                flat,
            ],
            out_specs=block,
            scratch_shapes=[pltpu.VMEM((planes, rows, width), jnp.float32)],
        ),
        out_shape=jax.ShapeDtypeStruct(u.shape, jnp.float32),
    )(upper, u, coef, join, row_value, col_value, along, across, near, far)


def late_body(
    half_ref, u_ref, coef_ref, join_ref, row_ref, col_ref, face_ref, side_ref, mine_ref, fold_ref,
    out_ref, g_ref, along_ref, across_ref, near_ref, far_ref,
):
    mine, fold = mine_ref[...], fold_ref[...]
    along_ref[...] = 4.0 * dot3(side_ref[0], fold, NT)
    across_ref[...] = 4.0 * dot3(mine, side_ref[1], NT)
    near_ref[...] = 4.0 * dot3(dot3(mine, face_ref[0]), fold, NT)
    far_ref[...] = 4.0 * dot3(dot3(mine, face_ref[1]), fold, NT)
    ghost_body(
        half_ref, u_ref, coef_ref, join_ref, row_ref, col_ref, along_ref, across_ref, near_ref,
        far_ref, out_ref, g_ref,
    )


def add_late(upper, u, coef, join, row_value, col_value, face_v, side_v, mine, fold, width):
    planes, rows, cols = u.shape
    first = (coef.shape[2] - cols) // width
    block, _ = block_specs(planes, rows, width)
    coef_block, join_block = block_specs(planes, rows, width, first)
    f32 = jnp.float32
    return pl.pallas_call(
        late_body,
        grid_spec=pltpu.PrefetchScalarGridSpec(
            num_scalar_prefetch=1,
            grid=(cols // width,),
            in_specs=[
                block,
                coef_block,
                join_block,
                pl.BlockSpec((rows, 1), lambda i, u: (0, 0)),
                pl.BlockSpec((1, width), lambda i, u: (0, i + first)),
                pl.BlockSpec(face_v.shape, lambda i, u: (0, 0, 0)),
                pl.BlockSpec(side_v.shape, lambda i, u: (0, 0, 0)),
                pl.BlockSpec(mine.shape, lambda i, u: (0, 0)),
                pl.BlockSpec((width, PANELS), lambda i, u: (i + first, 0)),
            ],
            out_specs=block,
            scratch_shapes=[
                pltpu.VMEM((planes, rows, width), f32),
                pltpu.VMEM((4 * planes, width), f32),
                pltpu.VMEM((rows, 4 * planes), f32),
                pltpu.VMEM((rows, width), f32),
                pltpu.VMEM((rows, width), f32),
            ],
        ),
        out_shape=jax.ShapeDtypeStruct(u.shape, f32),
        cost_estimate=pl.CostEstimate(
            flops=40 * planes * rows * cols, bytes_accessed=12 * planes * rows * cols,
            transcendentals=0,
        ),
    )(upper, u, coef, join, row_value, col_value, face_v, side_v, mine, fold)


def boundary_body(
    half_ref, f_ref, coef_ref, join_ref, far_ref, row_ref, col_ref, fold_ref, mine_ref,
    pick_row_ref, pick_col_ref, front_ref, back_ref, part_ref, face_ref, rows_ref, cols_ref,
    stage_ref, g_ref,
):
    planes, rows, width = f_ref.shape
    upper = half_ref[0]
    step = pl.program_id(0)

    @pl.when(step == 0)
    def _():
        face_ref[...] = jnp.zeros_like(face_ref)
        rows_ref[...] = jnp.zeros_like(rows_ref)
        cols_ref[...] = jnp.zeros_like(cols_ref)

    row_value, col_value = row_ref[...], col_ref[...]
    value = jnp.zeros_like(far_ref)
    for j in range(planes):
        value = (f_ref[jnp.where(upper == 1, planes - 1 - j, j)] + value) * coef_ref[j]
        g_ref[j] = value
    value = (far_ref[...] + coef_ref[planes - 1] * value) * join_ref[...]
    for j in range(planes - 1, -1, -1):
        value = g_ref[j] + coef_ref[j] * value
        place = jnp.where(upper == 1, planes - 1 - j, j)

        @pl.when(step == 0)
        def _(place=place, value=value):
            front_ref[place] = value

        @pl.when(step != 0)
        def _(place=place, value=value):
            back_ref[place] = value

        by_row = value * row_value
        total = by_row[:8]
        for k in range(8, rows, 8):
            total = total + by_row[k : k + 8]
        stage_ref[8 * j : 8 * j + 8, :] = total
        by_col = value * col_value
        total = by_col[:, :PANELS]
        for k in range(PANELS, width, PANELS):
            total = total + by_col[:, k : k + PANELS]
        cols_ref[:, j * PANELS : (j + 1) * PANELS] += total
    fold = fold_ref[...]
    face_ref[...] += dot3(value, fold)
    rows_ref[...] += dot3(stage_ref[...], fold)

    @pl.when(step == pl.num_programs(0) - 1)
    def _():
        mine = mine_ref[...]
        part_ref[:PANELS, :] = dot3(mine, face_ref[...], TN)
        part_ref[PANELS : PANELS + 2 * planes, :] = dot3(pick_row_ref[...], rows_ref[...])
        part_ref[PANELS + 2 * planes :, :] = dot3(
            dot3(cols_ref[...], pick_col_ref[...]), mine, TN
        )


def finish_boundary(upper, f, coef, join, far, row_value, col_value, fold, mine):
    planes, rows, cols = f.shape
    width = cols // 2
    block, flat = block_specs(planes, rows, width)
    front = pl.BlockSpec((planes, rows, width), lambda i, u: (0, 0, 0))
    back = pl.BlockSpec((planes, rows, width), lambda i, u: (0, 0, jnp.maximum(i - 1, 0)))
    pick_row = np.zeros((2, planes, planes, 8), np.float32)
    pick_col = np.zeros((planes, PANELS, 2, planes), np.float32)
    for j in range(planes):
        for t in (0, 1):
            pick_row[t, j, j, t::2] = 1.0
            pick_col[j, t::2, t, j] = 1.0
    whole = lambda shape: pl.BlockSpec(shape, lambda i, u: (0, 0))
    f32 = jnp.float32
    return pl.pallas_call(
        boundary_body,
        grid_spec=pltpu.PrefetchScalarGridSpec(
            num_scalar_prefetch=1,
            grid=(2,),
            in_specs=[
                block,
                block,
                flat,
                flat,
                whole((rows, 1)),
                pl.BlockSpec((1, width), lambda i, u: (0, i)),
                pl.BlockSpec((width, PANELS), lambda i, u: (i, 0)),
                whole((rows, PANELS)),
                whole((2 * planes, 8 * planes)),
                whole((planes * PANELS, 2 * planes)),
            ],
            out_specs=[front, back, whole((PANELS + 4 * planes, PANELS))],
            scratch_shapes=[
                pltpu.VMEM((rows, PANELS), f32),
                pltpu.VMEM((8 * planes, PANELS), f32),
                pltpu.VMEM((rows, planes * PANELS), f32),
                pltpu.VMEM((8 * planes, width), f32),
                pltpu.VMEM((planes, rows, width), f32),
            ],
        ),
        out_shape=[
            jax.ShapeDtypeStruct((planes, rows, width), f32),
            jax.ShapeDtypeStruct((planes, rows, cols - width), f32),
            jax.ShapeDtypeStruct((PANELS + 4 * planes, PANELS), f32),
        ],
    )(
        upper, f, coef, join, far, row_value, col_value, fold, mine,
        pick_row.reshape(2 * planes, -1), pick_col.reshape(-1, 2 * planes),
    )


TINY = 2.0**-60
GROUP = 16
UNROLL = 4
TALL = 32
LANES = 256


def whole_steps(count):
    return (count + UNROLL - 1) // UNROLL * UNROLL


def weight_body(depth, place_ref, row_ref, col_ref, low_ref, high_ref):
    place = place_ref[0]
    first_steps = whole_steps(place - 1)
    behind = (first_steps - (place - 1)).astype(jnp.float32)
    pairs = depth // 2 - place

    def rows(index, _):
        at = pl.ds(pl.multiple_of(index * GROUP, GROUP), GROUP)
        diag = row_ref[at, :] + col_ref[...] + 2.0

        def advance(count, pair):
            for _ in range(count):
                pair = (pair[1], diag * pair[1] - pair[0])
            return pair

        zero = diag - diag
        back, here = zero, zero + 1.0
        for k in range(1, UNROLL):
            step = diag * back - here
            take = behind >= k
            back, here = jnp.where(take, step, back), jnp.where(take, back, here)
        pair = lax.fori_loop(
            0, first_steps // UNROLL, lambda _, pair: advance(UNROLL, pair), (back, here)
        )
        before, near = pair
        pair = advance(1, pair)
        pair = lax.fori_loop(0, pairs // 2, lambda _, pair: advance(4, pair), pair)
        pair = lax.fori_loop(0, pairs % 2, lambda _, pair: advance(2, pair), pair)
        distant = pair[1]
        after = diag * distant - pair[0]
        scale = 1.0 / (near * after - before * distant)
        low_ref[at, :] = distant * scale
        high_ref[at, :] = near * scale
        return 0

    lax.fori_loop(0, low_ref.shape[0] // GROUP, rows, 0)


def weights(depth, place, row_eigen, col_eigen, block):
    grid, cols = row_eigen.shape[0], col_eigen.shape[1]
    out = jax.ShapeDtypeStruct((grid, cols), jnp.float32)
    spec = pl.BlockSpec((block, cols), lambda i, u: (i, 0))
    return pl.pallas_call(
        functools.partial(weight_body, depth),
        grid_spec=pltpu.PrefetchScalarGridSpec(
            num_scalar_prefetch=1,
            grid=(grid // block,),
            in_specs=[
                pl.BlockSpec((block, 1), lambda i, u: (i, 0)),
                pl.BlockSpec((1, cols), lambda i, u: (0, 0)),
            ],
            out_specs=[spec, spec],
        ),
        out_shape=[out, out],
        cost_estimate=pl.CostEstimate(
            flops=4 * depth * grid * cols, bytes_accessed=8 * grid * cols, transcendentals=0
        ),
    )(place, row_eigen, col_eigen)


def plane_body(
    depth, place_ref, low_ref, high_ref, row_eigen_ref, col_eigen_ref, row_ref, col_ref,
    face_ref, side_ref, rows_fold_ref, fold_ref, out_ref, along_ref, across_ref, pick_ref,
    near_ref, distant_ref,
):
    half = depth // 2
    block, grid = out_ref.shape
    place = place_ref[0]
    levels = [k if k < half else half + depth - 1 - k for k in range(depth)]
    base = whole_steps(half)
    lower_steps = whole_steps(place)
    upper_steps = whole_steps(depth - place)

    def slot(k):
        return jnp.where(
            k < place, lower_steps - 1 - k, base + upper_steps - depth + k
        )

    @pl.when(pl.program_id(0) == 0)
    def _():
        along = dot(side_ref[1], fold_ref[...], NT) * (4.0 * TINY / col_ref[...])
        odd = lax.broadcasted_iota(jnp.int32, (8, grid), 0) % 2 == 1
        for k in range(UNROLL - 1):
            along_ref[k] = jnp.zeros((8, grid), jnp.float32)
            along_ref[base + k] = jnp.zeros((8, grid), jnp.float32)
            across_ref[k] = jnp.zeros((block, PANELS), jnp.float32)
            across_ref[base + k] = jnp.zeros((block, PANELS), jnp.float32)
        for k, at in enumerate(levels):
            even_row = along[at : at + 1, :]
            odd_row = along[depth + at : depth + at + 1, :]
            along_ref[slot(k)] = jnp.where(odd, odd_row, even_row)
        shape = (2 * depth, depth * PANELS)
        column = lax.broadcasted_iota(jnp.int32, shape, 1)
        row = lax.broadcasted_iota(jnp.int32, shape, 0)
        layer = column // PANELS
        layer = jnp.where(layer < half, layer, half + depth - 1 - layer)
        pick = jnp.where(row == (column % 2) * depth + layer, 1.0, 0.0).astype(jnp.bfloat16)
        for k in range(3):
            pick_ref[2 * depth * k : 2 * depth * (k + 1), :] = pick

    across = dot(rows_fold_ref[...], side_ref[0], NT) * (4.0 * TINY / row_ref[...])
    high = across.astype(jnp.bfloat16)
    rest = across - high.astype(jnp.float32)
    middle = rest.astype(jnp.bfloat16)
    low = (rest - middle.astype(jnp.float32)).astype(jnp.bfloat16)
    across = jnp.concatenate([high, middle, low], 1)
    for k in range(0, depth, 2):
        pair = bf16_dot(across, pick_ref[:, k * PANELS : (k + 2) * PANELS])
        across_ref[slot(k)] = pair[:, :PANELS]
        across_ref[slot(k + 1)] = pair[:, PANELS:]

    for k, target in ((0, near_ref), (1, distant_ref)):
        face = dot3(4.0 * rows_fold_ref[...], face_ref[k], NT)
        for at in range(0, grid, LANES):
            lanes = slice(at, at + LANES)
            target[:, lanes] = dot3(face, fold_ref[lanes, :], NT)

    for part in range(grid // LANES):
        lanes = slice(part * LANES, (part + 1) * LANES)

        def rows(index, _, lanes=lanes):
            at = pl.ds(pl.multiple_of(index * TALL, 8), TALL)
            diag = row_eigen_ref[at, :] + col_eigen_ref[:, lanes] + 2.0
            zero = diag - diag

            def run(first, steps):
                def leap(turn, pair):
                    one, two = pair
                    for k in range(UNROLL):
                        here = first + turn * UNROLL + k
                        along = along_ref[here, :, lanes]
                        across = across_ref[here, at, :]
                        layer = jnp.concatenate([along] * (TALL // 8), 0) + jnp.concatenate(
                            [across] * (LANES // PANELS), 1
                        )
                        one, two = (layer - two) + diag * one, one
                    return one, two

                return lax.fori_loop(0, steps // UNROLL, leap, (zero, zero))[0]

            lower = run(0, lower_steps)
            upper = run(base, upper_steps)
            both = row_ref[at, :] * col_ref[:, lanes] * (1.0 / TINY)
            out_ref[at, lanes] = low_ref[at, lanes] * (
                both * lower + near_ref[at, lanes]
            ) + high_ref[at, lanes] * (both * upper + distant_ref[at, lanes])
            return 0

        lax.fori_loop(0, block // TALL, rows, 0)


def plane_layers(depth, place, low, high, eigen, edge_value, face_v, side_v, fold, block):
    grid, cols = low.shape
    slots = whole_steps(depth // 2) + whole_steps(depth)
    f32 = jnp.float32
    wide = pl.BlockSpec((block, cols), lambda i, u: (i, 0))
    tall = pl.BlockSpec((block, 1), lambda i, u: (i, 0))
    flat = pl.BlockSpec((1, cols), lambda i, u: (0, 0))
    return pl.pallas_call(
        functools.partial(plane_body, depth),
        grid_spec=pltpu.PrefetchScalarGridSpec(
            num_scalar_prefetch=1,
            grid=(grid // block,),
            in_specs=[
                wide,
                wide,
                tall,
                flat,
                tall,
                flat,
                pl.BlockSpec(face_v.shape, lambda i, u: (0, 0, 0)),
                pl.BlockSpec(side_v.shape, lambda i, u: (0, 0, 0)),
                pl.BlockSpec((block, PANELS), lambda i, u: (i, 0)),
                pl.BlockSpec((cols, PANELS), lambda i, u: (0, 0)),
            ],
            out_specs=wide,
            scratch_shapes=[
                pltpu.VMEM((slots, 8, cols), f32),
                pltpu.VMEM((slots, block, PANELS), f32),
                pltpu.VMEM((6 * depth, depth * PANELS), jnp.bfloat16),
                pltpu.VMEM((block, cols), f32),
                pltpu.VMEM((block, cols), f32),
            ],
        ),
        out_shape=jax.ShapeDtypeStruct((grid, cols), f32),
        cost_estimate=pl.CostEstimate(
            flops=20 * depth * grid * cols, bytes_accessed=24 * grid * cols, transcendentals=0
        ),
    )(
        place, low, high, eigen[:grid, None], eigen[None, :], edge_value[:grid, None],
        edge_value[None, :], face_v, side_v, fold, fold,
    )


def build(mesh, grid, depth):
    slow, fast = mesh.shape["px"], mesh.shape["py"]
    devices = slow * fast
    half = devices // 2
    rows = grid // half
    edge = grid // PANELS
    groups = [list(range(half)), list(range(half, devices))]
    local = depth <= 32 and rows % 8 == 0
    split = grid // 2
    block = split // 2
    tables = {
        name: value.astype(np.float32) for name, value in small_tables(depth, grid, edge).items()
    }
    sine_np = sine_table(grid).astype(np.float32)
    sine_high = sine_np.astype(jnp.bfloat16)
    sine_low = (sine_np - sine_high.astype(np.float32)).astype(jnp.bfloat16)
    eigen_np = eigen_values(grid)
    fold_np = fold_panels(grid, edge).astype(np.float32)

    def exchange(x):
        return lax.all_to_all(
            x, AXES, split_axis=0, concat_axis=0, tiled=True, axis_index_groups=groups
        )

    def hop(x, bit):
        return lax.ppermute(x, "px", [(i, i ^ bit) for i in range(slow)])

    def swap(x):
        return lax.ppermute(x, "py", [(i, i ^ 1) for i in range(fast)])

    alternate = [list(range(0, fast, 2)), list(range(1, fast, 2))]

    def on_device(charge):
        rank = lax.axis_index(AXES)
        upper = (rank // half).astype(jnp.int32).reshape(1)
        is_upper = rank // half == 1
        start = (rank % half) * rows
        sine_pair = (jnp.asarray(sine_high), jnp.asarray(sine_low))
        fold = jnp.asarray(fold_np)
        tb = {name: jnp.asarray(value) for name, value in tables.items()}
        eigen = jnp.asarray(eigen_np.astype(np.float32))
        edge_value = jnp.asarray(sine_np[:, 0])
        my_eigen = lax.dynamic_slice_in_dim(eigen, start, rows, 0)
        my_edge = lax.dynamic_slice_in_dim(edge_value, start, rows, 0)
        my_fold = lax.dynamic_slice_in_dim(fold, start, rows, 0)
        mu = my_eigen[:, None] + eigen[None, :]
        parity = jnp.arange(grid) % 2
        edge_pair = jnp.stack([edge_value * (parity == 0), edge_value * (parity == 1)])
        my_pair = jnp.stack([my_edge * (parity[:rows] == 0), my_edge * (parity[:rows] == 1)])

        plane = charge.reshape(grid, grid)
        spectrum = double_product([plane], *sine_pair)
        spectrum = exchange(spectrum.reshape(half, rows, grid))
        coef, join = factors(mu, half)
        mixed = mixed_table(edge, depth, tb["wave_x"])
        corner = corner_table(edge, depth, tb["lift"])
        if local:
            index = (rank % half).astype(jnp.int32)
            place = jnp.where(is_upper, half - index, index + 1).reshape(1)
            weight = weights(depth, place, eigen[:split, None], eigen[None, :], block)
            spectrum, mixed, corner, weight = lax.optimization_barrier(
                (spectrum, mixed, corner, weight)
            )
        else:
            spectrum, mixed, corner = lax.optimization_barrier((spectrum, mixed, corner))
        if local:
            last = reach(upper, spectrum, coef)
        else:
            g, last = sweep(upper, spectrum, coef)
        far = lax.ppermute(last, AXES, [(i, i ^ half) for i in range(devices)])
        if local:
            u, sent, part = finish_boundary(
                upper, spectrum, coef, join, far, my_edge[:, None], edge_value[None, :], fold,
                my_fold,
            )
        else:
            u, outer = finish(upper, g, coef, join, far)

            face = dot(my_fold, dot(outer, fold), ((0,), (0,)))
            lines_y = jnp.einsum("tk,jkx->tjx", my_pair, u, precision=HIGHEST)
            lines_y = jnp.einsum("tjx,xb->tjb", lines_y, fold, precision=HIGHEST)
            lines_x = jnp.einsum("jkx,tx->tjk", u, edge_pair, precision=HIGHEST)
            lines_x = jnp.einsum("tjk,kb->tjb", lines_x, my_fold, precision=HIGHEST)
            lines = jnp.stack([lines_y, lines_x])
            lines = jnp.where(is_upper, lines[:, :, ::-1], lines)
            part = jnp.concatenate([face, lines.reshape(-1, PANELS)])
        middle = part.shape[0] // 2
        first = lax.axis_index("py") % 2 == 0
        part = part + swap(part)
        part = jnp.where(first, part[:middle], part[middle:])
        part = lax.all_gather(part, "py", axis=0, tiled=False, axis_index_groups=alternate).sum(0)
        bit = 1
        while bit < slow // 2:
            part = part + hop(part, bit)
            bit *= 2
        both = jnp.concatenate([part, hop(part, bit)])
        back = swap(both)
        low, high = jnp.where(first, both, back), jnp.where(first, back, both)
        part = jnp.concatenate([low[:middle], high[:middle]])
        other = jnp.concatenate([low[middle:], high[middle:]])
        if local:
            early, part, other = lax.optimization_barrier((u, part, other))
            u = exchange(early).reshape(grid, split)
        face_v, side_v = panel_potential(part, other, tb, mixed, corner)
        if local:
            sent = add_late(
                upper, sent, coef, join, my_edge[:, None], edge_value[None, :], face_v, side_v,
                my_fold, fold, split,
            )
            u, sent = lax.optimization_barrier((u, sent))
            sent = exchange(sent).reshape(grid, grid - split)
            layers = plane_layers(
                depth, place, *weight, eigen, edge_value, face_v, side_v, fold, block,
            )
            return double_product([u, layers, sent], *sine_pair)[None]
        else:
            near, distant = (
                4.0 * dot(dot(my_fold, face_v[i]), fold, ((1,), (1,))) for i in (0, 1)
            )
            along = 4.0 * dot(side_v[0], fold, ((1,), (1,)))
            across = 4.0 * dot(my_fold, side_v[1], ((1,), (1,)))
            u = add_ghost(
                upper, u, coef, join, my_edge[:, None], edge_value[None, :], along, across, near, distant
            )
            u = exchange(u).reshape(grid, grid)
        return double_product([u], *sine_pair)[None]

    return on_device


def solution(mesh):
    spec = P(AXES, None, None)

    def run(charge):
        depth, grid, _ = charge.shape
        body = build(mesh, grid, depth)
        return jax.shard_map(body, mesh=mesh, in_specs=(spec,), out_specs=spec, check_vma=False)(
            charge
        )

    return run
```

```python
import functools
import math

import jax
import jax.numpy as jnp
import numpy as np
from jax import lax
from jax.experimental import pallas as pl
from jax.experimental.pallas import tpu as pltpu
from jax.sharding import PartitionSpec as P

PANELS = 128
HIGHEST = lax.Precision.HIGHEST
HIGH = lax.Precision.HIGH
FOUR_PI = 4.0 * math.pi
AXES = ("px", "py")


def dot(a, b, dims=((1,), (0,)), precision=HIGHEST):
    return lax.dot_general(
        a, b, (dims, ((), ())), precision=precision, preferred_element_type=jnp.float32
    )


def sine_table(n):
    order = np.arange(1, n + 1, dtype=np.int64)
    phase = (order[:, None] * order[None, :]) % (2 * (n + 1))
    return np.sqrt(2.0 / (n + 1)) * np.sin(np.pi * phase / (n + 1.0))


def eigen_values(n):
    return 2.0 - 2.0 * np.cos(np.pi * np.arange(1, n + 1) / (n + 1.0))


def fold_panels(grid, edge):
    sums = sine_table(grid).reshape(grid, PANELS, edge).sum(2)[:, : PANELS // 2]
    even = (np.arange(grid) % 2 == 0)[:, None]
    return np.concatenate([np.where(even, sums, 0.0), np.where(even, 0.0, sums)], axis=1)


def wave_basis(n):
    place = np.arange(n // 2) - (n - 1) / 2.0
    even = np.cos(np.pi * np.arange(n)[:, None] * place[None, :] / n)
    even *= np.sqrt(np.where(np.arange(n) == 0, 1.0, 2.0) / n)[:, None]
    odd = np.sin(np.pi * np.arange(1, n + 1)[:, None] * place[None, :] / n)
    odd *= np.sqrt(np.where(np.arange(1, n + 1) == n, 1.0, 2.0) / n)[:, None]
    return even, odd


def wave_values(n):
    distance = np.arange(n)[:, None]
    order = np.concatenate([np.arange(n), np.arange(1, n + 1)])[None, :]
    return np.where(distance == 0, 1.0, 2.0) * np.cos(np.pi * distance * order / n)


def halves(value):
    high = value.astype(jnp.bfloat16)
    return high, (value - high.astype(jnp.float32)).astype(jnp.bfloat16)


def bf16_dot(a, b, dims=((1,), (0,))):
    return lax.dot_general(a, b, (dims, ((), ())), preferred_element_type=jnp.float32)


def dot3(a, b, dims=((1,), (0,))):
    a_high, a_low = halves(a)
    b_high, b_low = halves(b)
    value = bf16_dot(a_high, b_high, dims)
    return value + (bf16_dot(a_high, b_low, dims) + bf16_dot(a_low, b_high, dims))


STRIPE = 256


def product_body(count, high_ref, low_ref, *refs):
    in_refs, out_ref, mid_high_ref, mid_low_ref = refs[:count], *refs[count:]
    step = pl.program_id(0)
    stripes = pl.num_programs(0) // 2

    @pl.when(step < stripes)
    def _():
        at = pl.ds(pl.multiple_of(step * STRIPE, STRIPE), STRIPE)
        value = in_refs[0][...]
        if count == 3:
            value = jnp.concatenate([value + in_refs[1][...].T, in_refs[2][...]], 1)
        high, low = halves(value)
        value = bf16_dot(high, high_ref[...])
        value = value + bf16_dot(high, low_ref[...])
        value = value + bf16_dot(low, high_ref[...])
        high, low = halves(value)
        mid_high_ref[at, :] = high
        mid_low_ref[at, :] = low

    @pl.when(step >= stripes)
    def _():
        at = pl.ds(pl.multiple_of((step - stripes) * STRIPE, STRIPE), STRIPE)
        value = bf16_dot(high_ref[at, :], mid_high_ref[...])
        value = value + bf16_dot(high_ref[at, :], mid_low_ref[...])
        value = value + bf16_dot(low_ref[at, :], mid_high_ref[...])
        out_ref[...] = value


def double_product(values, high, low):
    grid = high.shape[0]
    stripes = grid // STRIPE
    table = pl.BlockSpec((grid, grid), lambda i: (0, 0), pipeline_mode=pl.Buffered(1))
    return pl.pallas_call(
        functools.partial(product_body, len(values)),
        grid=(2 * stripes,),
        in_specs=[table, table]
        + [
            pl.BlockSpec((v.shape[0], STRIPE), lambda i: (0, jnp.minimum(i, stripes - 1)))
            if k == 1
            else pl.BlockSpec((STRIPE, v.shape[1]), lambda i: (jnp.minimum(i, stripes - 1), 0))
            for k, v in enumerate(values)
        ],
        out_specs=pl.BlockSpec((STRIPE, grid), lambda i: (jnp.maximum(i - stripes, 0), 0)),
        out_shape=jax.ShapeDtypeStruct((grid, grid), jnp.float32),
        scratch_shapes=[
            pltpu.VMEM((grid, grid), jnp.bfloat16),
            pltpu.VMEM((grid, grid), jnp.bfloat16),
        ],
    )(high, low, *values)


def distance_power(*squares):
    return lax.rsqrt(functools.reduce(lambda a, b: a + b, squares))


def iota(shape, axis):
    return lax.broadcasted_iota(jnp.int32, shape, axis).astype(jnp.float32)


LEVELS = 4


def mixed_body(edge, depth, wave_ref, out_ref):
    hb = PANELS // 2
    soft = edge * edge / 4.0
    shape = (hb, PANELS)
    first = (edge - 1) / 2.0 + 1.0
    front = iota(shape, 0) * edge + first
    back = (PANELS - 1 - iota(shape, 0)) * edge + first
    along = iota(shape, 1) * edge
    along = along * along + soft
    front = front * front + along
    back = back * back + along
    rows = []
    for k in range(LEVELS):
        level = (pl.program_id(0) * LEVELS + k + 1).astype(jnp.float32)
        own = level * level
        far = (depth + 1.0 - level) * (depth + 1.0 - level)
        own_front, own_back = distance_power(front, own), distance_power(back, own)
        far_front, far_back = distance_power(front, far), distance_power(back, far)
        for sign in (1.0, -1.0):
            one, two = own_front + sign * far_front, own_back + sign * far_back
            rows += [one + two, one - two]
    value = dot(jnp.concatenate(rows, 0), wave_ref[...])
    for k in range(LEVELS):
        for s in (0, 1):
            at = (2 * k + s) * PANELS
            out_ref[s, k] = value[at : at + PANELS]


def mixed_table(edge, depth, wave):
    half = depth // 2
    return pl.pallas_call(
        functools.partial(mixed_body, edge, depth),
        grid=(half // LEVELS,),
        in_specs=[pl.BlockSpec((PANELS, 2 * PANELS), lambda i: (0, 0))],
        out_specs=pl.BlockSpec((2, LEVELS, PANELS, 2 * PANELS), lambda i: (0, i, 0, 0)),
        out_shape=jax.ShapeDtypeStruct((2, half, PANELS, 2 * PANELS), jnp.float32),
        cost_estimate=pl.CostEstimate(
            flops=2 * depth * PANELS**3, bytes_accessed=4 * depth * PANELS * PANELS,
            transcendentals=0,
        ),
    )(wave)


STRIP = 8


def corner_body(edge, depth, wave_ref, front_ref, back_ref):
    hb = PANELS // 2
    soft = edge * edge / 4.0
    shape = (hb, 2 * depth)
    first = (edge - 1) / 2.0 + 1.0
    lane = lax.broadcasted_iota(jnp.int32, shape, 1)
    odd = lane >= depth
    level = jnp.where(odd, lane - depth, lane).astype(jnp.float32)
    sign = jnp.where(odd, -1.0, 1.0)
    level = level * level + soft
    near = iota(shape, 0) * edge + first
    distant = (PANELS - 1 - iota(shape, 0)) * edge + first
    near = near * near + level
    distant = distant * distant + level
    sums, gaps = [], []
    for k in range(STRIP):
        b = (pl.program_id(0) * STRIP + k).astype(jnp.float32)
        front = b * edge + first
        back = (PANELS - 1 - b) * edge + first
        front, back = front * front, back * back
        one = distance_power(near, front) + sign * distance_power(distant, front)
        two = distance_power(near, back) + sign * distance_power(distant, back)
        sums.append(one + two)
        gaps.append(one - two)
    wave = wave_ref[...]
    front_ref[...] = dot(jnp.concatenate(sums, 0), wave).reshape(front_ref.shape)
    back_ref[...] = dot(jnp.concatenate(gaps, 0), wave).reshape(back_ref.shape)


def corner_table(edge, depth, wave):
    hb = PANELS // 2
    width = 4 * depth
    block = pl.BlockSpec((STRIP, hb, width), lambda i: (i, 0, 0))
    shape = jax.ShapeDtypeStruct((hb, hb, width), jnp.float32)
    return pl.pallas_call(
        functools.partial(corner_body, edge, depth),
        grid=(hb // STRIP,),
        in_specs=[pl.BlockSpec((2 * depth, width), lambda i: (0, 0))],
        out_specs=[block, block],
        out_shape=[shape, shape],
        cost_estimate=pl.CostEstimate(
            flops=2 * depth * PANELS**3, bytes_accessed=4 * depth * PANELS * PANELS,
            transcendentals=0,
        ),
    )(wave)


def small_tables(depth, grid, edge):
    half = depth // 2
    soft = edge * edge / 4.0

    def kernel(dz, dy, dx):
        return 1.0 / np.sqrt(dz * dz + dy * dy + dx * dx + soft) / FOUR_PI

    step = edge * np.arange(PANELS, dtype=np.float64)
    vx = wave_values(PANELS)
    vz = wave_values(depth)
    even, odd = wave_basis(PANELS)
    zero = np.zeros_like(even)
    basis_x = np.concatenate(
        [np.concatenate([even, zero], 1), np.concatenate([zero, odd], 1)], 0
    )
    bz = np.stack(wave_basis(depth))
    face, side = [], []
    z = np.arange(depth, dtype=np.float64)
    for s, sign in enumerate((1.0, -1.0)):
        k = kernel(0.0, step[:, None], step[None, :])
        k = k + sign * kernel(depth + 1.0, step[:, None], step[None, :])
        face.append(vx.T @ k @ vx)
        for other in (1.0, -1.0):
            k = kernel(z[:, None], 0.0, step[None, :])
            k = k + other * kernel(z[:, None], grid + 1.0, step[None, :])
            side.append(vz[:, s * depth : (s + 1) * depth].T @ k @ vx)
    level = np.zeros((2, 2, half, 2, 2, depth))
    cross = np.zeros((2, 2, half, 2, 2, depth))
    turn = np.zeros((2, 2, 2, half, 2, 2, 2, depth))
    for s in (0, 1):
        for t in (0, 1):
            level[s, t, :, s, t] = bz[s].T
            cross[s, t, :, t, s] = bz[s].T
            for x in (0, 1):
                turn[x, s, t, :, t, x, s] = bz[s].T
    lift = np.zeros((2, depth, 2, 2, depth))
    for x in (0, 1):
        for s in (0, 1):
            lift[x, :, x, s] = vz[:, s * depth : (s + 1) * depth]
    return dict(
        basis=basis_x,
        face=np.stack(face),
        side=np.concatenate(side),
        level=level.reshape(4 * half, 4 * depth),
        cross=cross.reshape(4 * half, 4 * depth),
        turn=turn.reshape(2, 4 * half, 8 * depth),
        wave_x=vx / FOUR_PI,
        lift=lift.reshape(2 * depth, 4 * depth) / FOUR_PI,
    )


NT = ((1,), (1,))
TN = ((0,), (0,))


def panels_body(
    first_ref, mine_ref, mate_ref, basis_ref, face_ref, side_ref, level_ref, cross_ref, turn_ref,
    mixed_hbm, front_hbm, back_hbm, face_out_ref, side_out_ref,
    fx_ref, hat_ref, acc_ref, toside_ref, xs_ref, tox_ref, mixed_ref, front_ref, back_ref, sems,
):
    half = mixed_ref.shape[1]
    loads = [
        pltpu.make_async_copy(source, target, sems.at[k])
        for k, (source, target) in enumerate(
            ((mixed_hbm, mixed_ref), (front_hbm, front_ref), (back_hbm, back_ref))
        )
    ]
    for load in loads:
        load.start()
    hb = PANELS // 2
    first = first_ref[0] == 1
    low = jnp.where(first, mine_ref[...], mate_ref[...])
    high = jnp.where(first, mate_ref[...], mine_ref[...])
    middle = low.shape[0] // 2
    own = jnp.concatenate([low[:middle], high[:middle]], 0)
    other = jnp.concatenate([low[middle:], high[middle:]], 0)
    total = (own + other) * 0.5
    gap = (own - other) * 0.5
    basis = basis_ref[...]
    level = level_ref[...]
    faces = [total[:PANELS], gap[:PANELS]]
    sides = []
    for axis in (0, 1):
        rows = slice(PANELS + axis * 2 * half, PANELS + (axis + 1) * 2 * half)
        sides.append(jnp.concatenate([total[rows], gap[rows]], 0))
        hat_ref[axis] = dot3(sides[axis], basis, NT)
    for s in (0, 1):
        fx_ref[0, s] = dot3(faces[s], basis, NT)
        fx_ref[1, s] = dot3(faces[s], basis, ((0,), (1,)))

    loads[0].wait()
    for s in (0, 1):

        def face_rows(block, _, s=s):
            at = pl.multiple_of(block * 8, 8)
            odd = (block >= 8).astype(jnp.int32)
            base = (2 * s + odd) * half

            def add(chunk, acc):
                one, two = acc
                for k in range(8):
                    j = chunk * 8 + k
                    t = mixed_ref[s, j, pl.ds(at, 8), :]
                    one = one + t * hat_ref[0, pl.ds(base + j, 1), :]
                    two = two + t * hat_ref[1, pl.ds(base + j, 1), :]
                return one, two

            zero = jnp.zeros((8, 2 * PANELS), jnp.float32)
            one, two = lax.fori_loop(0, half // 8, add, (zero, zero))
            acc_ref[0, s, pl.ds(at, 8), :] = one
            acc_ref[1, s, pl.ds(at, 8), :] = two
            return 0

        lax.fori_loop(0, PANELS // 8, face_rows, 0)

        def side_rows(j, _, s=s):
            for t in (0, 1):
                sums = [None, None]
                for block in range(hb // 8):
                    rows = slice(t * hb + block * 8, t * hb + block * 8 + 8)
                    table = mixed_ref[s, j, rows, :]
                    for axis in (0, 1):
                        term = table * fx_ref[axis, s, rows, :]
                        sums[axis] = term if block == 0 else sums[axis] + term
                for axis in (0, 1):
                    toside_ref[axis, pl.ds((2 * s + t) * half + j, 1), :] = jnp.sum(
                        sums[axis], axis=0, keepdims=True
                    )
            return 0

        lax.fori_loop(0, half, side_rows, 0)

    xs_ref[...] = dot3(sides[1], cross_ref[...], TN)
    ys = dot3(sides[0][:, :hb], turn_ref[0], TN) + dot3(sides[0][:, hb:], turn_ref[1], TN)
    width = xs_ref.shape[1]
    to_y = []
    loads[1].wait()
    loads[2].wait()
    for t, table_ref in ((0, front_ref), (1, back_ref)):
        mine = ys[:, t * width : (t + 1) * width]

        def corner_rows(b, acc, t=t, table_ref=table_ref, mine=mine):
            table = table_ref[b]
            row = pl.ds(t * hb + b, 1)
            tox_ref[row, :] = jnp.sum(table * mine, axis=0, keepdims=True)
            return acc + table * xs_ref[row, :]

        to_y.append(lax.fori_loop(0, hb, corner_rows, jnp.zeros((hb, width), jnp.float32)))
    to_y = jnp.concatenate(to_y, 1)
    corner = [
        jnp.concatenate([dot3(turn_ref[x], to_y, NT) for x in (0, 1)], 1),
        dot3(cross_ref[...], tox_ref[...], NT),
    ]
    for axis in (0, 1):
        waves = dot3(level, hat_ref[axis], TN) * side_ref[...]
        waves = dot3(level, waves) + toside_ref[axis]
        value = dot3(waves, basis) + corner[axis]
        even, odd = value[: 2 * half], value[2 * half :]
        for part, v in ((0, even + odd), (1, even - odd)):
            for t in (0, 1):
                at = (2 * t + part) * half
                side_out_ref[axis, at : at + half, :] = v[t * half : (t + 1) * half]
    value = []
    for s in (0, 1):
        full = dot3(basis, fx_ref[0, s]) * face_ref[s]
        rows = dot3(basis, full, TN) + acc_ref[0, s]
        value.append(dot3(rows, basis) + dot3(basis, acc_ref[1, s], ((0,), (1,))))
    face_out_ref[0] = value[0] + value[1]
    face_out_ref[1] = value[0] - value[1]


def panel_potential(first, mine, mate, tb, mixed, corner):
    half = mixed.shape[1]
    width = corner[0].shape[2]
    f32 = jnp.float32
    vmem = pl.BlockSpec(memory_space=pltpu.VMEM)
    return pl.pallas_call(
        panels_body,
        in_specs=[pl.BlockSpec(memory_space=pltpu.SMEM)]
        + [vmem] * 8
        + [pl.BlockSpec(memory_space=pl.ANY)] * 3,
        out_shape=[
            jax.ShapeDtypeStruct((2, PANELS, PANELS), f32),
            jax.ShapeDtypeStruct((2, 4 * half, PANELS), f32),
        ],
        scratch_shapes=[
            pltpu.VMEM((2, 2, PANELS, 2 * PANELS), f32),
            pltpu.VMEM((2, 4 * half, 2 * PANELS), f32),
            pltpu.VMEM((2, 2, PANELS, 2 * PANELS), f32),
            pltpu.VMEM((2, 4 * half, 2 * PANELS), f32),
            pltpu.VMEM((PANELS, width), f32),
            pltpu.VMEM((PANELS, width), f32),
            pltpu.VMEM(mixed.shape, f32),
            pltpu.VMEM(corner[0].shape, f32),
            pltpu.VMEM(corner[1].shape, f32),
            pltpu.SemaphoreType.DMA((3,)),
        ],
        cost_estimate=pl.CostEstimate(
            flops=5_000_000_000, bytes_accessed=4 * (mixed.size + 2 * corner[0].size),
            transcendentals=0,
        ),
    )(
        first, mine, mate, tb["basis"], tb["face"], tb["side"], tb["level"], tb["cross"], tb["turn"],
        mixed, *corner,
    )


WIDTH = 256


def block_specs(planes, rows, width=WIDTH, first=0):
    block = pl.BlockSpec((planes, rows, width), lambda i, *_: (0, 0, i + first))
    flat = pl.BlockSpec((rows, width), lambda i, *_: (0, i + first))
    return block, flat


def factor_body(mu_ref, coef_ref, join_ref):
    planes = coef_ref.shape[0]
    for col in range(0, WIDTH, 128):
        part = slice(col, col + 128)
        diag = mu_ref[:, part] + 2.0
        coef = 1.0 / diag
        coef_ref[0, :, part] = coef
        for j in range(1, planes):
            coef = 1.0 / (diag - coef)
            coef_ref[j, :, part] = coef
        join_ref[:, part] = 1.0 / (1.0 - coef * coef)


def factors(mu, planes):
    rows, cols = mu.shape
    block, flat = block_specs(planes, rows)
    return pl.pallas_call(
        factor_body,
        grid=(cols // WIDTH,),
        in_specs=[flat],
        out_specs=[block, flat],
        out_shape=[
            jax.ShapeDtypeStruct((planes, rows, cols), jnp.float32),
            jax.ShapeDtypeStruct((rows, cols), jnp.float32),
        ],
        cost_estimate=pl.CostEstimate(
            flops=20 * planes * rows * cols, bytes_accessed=4 * planes * rows * cols, transcendentals=0
        ),
    )(mu)


def sweep_body(half_ref, f_ref, coef_ref, g_ref, last_ref):
    planes = f_ref.shape[0]
    upper = half_ref[0]
    value = jnp.zeros_like(last_ref)
    for j in range(planes):
        place = jnp.where(upper == 1, planes - 1 - j, j)
        value = (f_ref[place] + value) * coef_ref[j]
        g_ref[j] = value
    last_ref[...] = value


def sweep(upper, spectrum, coef):
    planes, rows, cols = spectrum.shape
    block, flat = block_specs(planes, rows)
    return pl.pallas_call(
        sweep_body,
        grid_spec=pltpu.PrefetchScalarGridSpec(
            num_scalar_prefetch=1,
            grid=(cols // WIDTH,),
            in_specs=[block, block],
            out_specs=[block, flat],
        ),
        out_shape=[
            jax.ShapeDtypeStruct(spectrum.shape, jnp.float32),
            jax.ShapeDtypeStruct((rows, cols), jnp.float32),
        ],
    )(upper, spectrum, coef)


def reach_body(half_ref, f_ref, coef_ref, last_ref):
    planes = f_ref.shape[0]
    upper = half_ref[0]
    value = jnp.zeros_like(last_ref)
    for j in range(planes):
        place = jnp.where(upper == 1, planes - 1 - j, j)
        value = (f_ref[place] + value) * coef_ref[j]
    last_ref[...] = value


def reach(upper, spectrum, coef):
    planes, rows, cols = spectrum.shape
    block, flat = block_specs(planes, rows)
    return pl.pallas_call(
        reach_body,
        grid_spec=pltpu.PrefetchScalarGridSpec(
            num_scalar_prefetch=1,
            grid=(cols // WIDTH,),
            in_specs=[block, block],
            out_specs=flat,
        ),
        out_shape=jax.ShapeDtypeStruct((rows, cols), jnp.float32),
    )(upper, spectrum, coef)


def finish_body(half_ref, g_ref, coef_ref, join_ref, far_ref, u_ref, edge_ref):
    planes = g_ref.shape[0]
    upper = half_ref[0]
    value = (far_ref[...] + coef_ref[planes - 1] * g_ref[planes - 1]) * join_ref[...]
    for j in range(planes - 1, -1, -1):
        value = g_ref[j] + coef_ref[j] * value
        u_ref[jnp.where(upper == 1, planes - 1 - j, j)] = value
    edge_ref[...] = value


def finish(upper, g, coef, join, far):
    planes, rows, cols = g.shape
    block, flat = block_specs(planes, rows)
    return pl.pallas_call(
        finish_body,
        grid_spec=pltpu.PrefetchScalarGridSpec(
            num_scalar_prefetch=1,
            grid=(cols // WIDTH,),
            in_specs=[block, block, flat, flat],
            out_specs=[block, flat],
        ),
        out_shape=[
            jax.ShapeDtypeStruct(g.shape, jnp.float32),
            jax.ShapeDtypeStruct((rows, cols), jnp.float32),
        ],
    )(upper, g, coef, join, far)


def ghost_body(
    half_ref, u_ref, coef_ref, join_ref, row_ref, col_ref, along_ref, across_ref, near_ref,
    far_ref, out_ref, g_ref,
):
    planes, rows, width = u_ref.shape
    upper = half_ref[0]
    row_odd = lax.broadcasted_iota(jnp.int32, (rows, width), 0) % 2 == 1
    col_odd = lax.broadcasted_iota(jnp.int32, (rows, width), 1) % 2 == 1
    row_value, col_value = row_ref[...], col_ref[...]

    def layer(index):
        even = along_ref[index : index + 1, :]
        odd = along_ref[2 * planes + index : 2 * planes + index + 1, :]
        side_y = row_value * jnp.where(row_odd, odd, even)
        even = across_ref[:, index : index + 1]
        odd = across_ref[:, 2 * planes + index : 2 * planes + index + 1]
        return side_y + col_value * jnp.where(col_odd, odd, even)

    own, far = near_ref[...], far_ref[...]
    for j in range(planes):
        coef = coef_ref[j]
        own = (layer(j) + own) * coef
        far = (layer(planes + j) + far) * coef
        g_ref[j] = own
    value = (far + coef * own) * join_ref[...]
    for j in range(planes - 1, -1, -1):
        value = g_ref[j] + coef_ref[j] * value
        place = jnp.where(upper == 1, planes - 1 - j, j)
        out_ref[place] = u_ref[place] + value


def add_ghost(upper, u, coef, join, row_value, col_value, along, across, near, far):
    planes, rows, cols = u.shape
    width = WIDTH
    block, flat = block_specs(planes, rows)
    return pl.pallas_call(
        ghost_body,
        grid_spec=pltpu.PrefetchScalarGridSpec(
            num_scalar_prefetch=1,
            grid=(cols // width,),
            in_specs=[
                block,
                block,
                flat,
                pl.BlockSpec((rows, 1), lambda i, u: (0, 0)),
                pl.BlockSpec((1, width), lambda i, u: (0, i)),
                pl.BlockSpec((4 * planes, width), lambda i, u: (0, i)),
                pl.BlockSpec((rows, 4 * planes), lambda i, u: (0, 0)),
                flat,
                flat,
            ],
            out_specs=block,
            scratch_shapes=[pltpu.VMEM((planes, rows, width), jnp.float32)],
        ),
        out_shape=jax.ShapeDtypeStruct(u.shape, jnp.float32),
    )(upper, u, coef, join, row_value, col_value, along, across, near, far)


def late_body(
    half_ref, u_ref, coef_ref, join_ref, row_ref, col_ref, face_ref, side_ref, mine_ref, fold_ref,
    out_ref, g_ref, along_ref, across_ref, near_ref, far_ref,
):
    mine, fold = mine_ref[...], fold_ref[...]
    along_ref[...] = 4.0 * dot3(side_ref[0], fold, NT)
    across_ref[...] = 4.0 * dot3(mine, side_ref[1], NT)
    near_ref[...] = 4.0 * dot3(dot3(mine, face_ref[0]), fold, NT)
    far_ref[...] = 4.0 * dot3(dot3(mine, face_ref[1]), fold, NT)
    ghost_body(
        half_ref, u_ref, coef_ref, join_ref, row_ref, col_ref, along_ref, across_ref, near_ref,
        far_ref, out_ref, g_ref,
    )


def add_late(upper, u, coef, join, row_value, col_value, face_v, side_v, mine, fold, width):
    planes, rows, cols = u.shape
    first = (coef.shape[2] - cols) // width
    block, _ = block_specs(planes, rows, width)
    coef_block, join_block = block_specs(planes, rows, width, first)
    f32 = jnp.float32
    return pl.pallas_call(
        late_body,
        grid_spec=pltpu.PrefetchScalarGridSpec(
            num_scalar_prefetch=1,
            grid=(cols // width,),
            in_specs=[
                block,
                coef_block,
                join_block,
                pl.BlockSpec((rows, 1), lambda i, u: (0, 0)),
                pl.BlockSpec((1, width), lambda i, u: (0, i + first)),
                pl.BlockSpec(face_v.shape, lambda i, u: (0, 0, 0)),
                pl.BlockSpec(side_v.shape, lambda i, u: (0, 0, 0)),
                pl.BlockSpec(mine.shape, lambda i, u: (0, 0)),
                pl.BlockSpec((width, PANELS), lambda i, u: (i + first, 0)),
            ],
            out_specs=block,
            scratch_shapes=[
                pltpu.VMEM((planes, rows, width), f32),
                pltpu.VMEM((4 * planes, width), f32),
                pltpu.VMEM((rows, 4 * planes), f32),
                pltpu.VMEM((rows, width), f32),
                pltpu.VMEM((rows, width), f32),
            ],
        ),
        out_shape=jax.ShapeDtypeStruct(u.shape, f32),
        cost_estimate=pl.CostEstimate(
            flops=40 * planes * rows * cols, bytes_accessed=12 * planes * rows * cols,
            transcendentals=0,
        ),
    )(upper, u, coef, join, row_value, col_value, face_v, side_v, mine, fold)


def boundary_body(
    half_ref, f_ref, coef_ref, join_ref, far_ref, row_ref, col_ref, fold_ref, mine_ref,
    pick_row_ref, pick_col_ref, front_ref, back_ref, part_ref, face_ref, rows_ref, cols_ref,
    stage_ref, g_ref,
):
    planes, rows, width = f_ref.shape
    upper = half_ref[0]
    step = pl.program_id(0)

    @pl.when(step == 0)
    def _():
        face_ref[...] = jnp.zeros_like(face_ref)
        rows_ref[...] = jnp.zeros_like(rows_ref)
        cols_ref[...] = jnp.zeros_like(cols_ref)

    row_value, col_value = row_ref[...], col_ref[...]
    value = jnp.zeros_like(far_ref)
    for j in range(planes):
        value = (f_ref[jnp.where(upper == 1, planes - 1 - j, j)] + value) * coef_ref[j]
        g_ref[j] = value
    value = (far_ref[...] + coef_ref[planes - 1] * value) * join_ref[...]
    for j in range(planes - 1, -1, -1):
        value = g_ref[j] + coef_ref[j] * value
        place = jnp.where(upper == 1, planes - 1 - j, j)

        @pl.when(step == 0)
        def _(place=place, value=value):
            front_ref[place] = value

        @pl.when(step != 0)
        def _(place=place, value=value):
            back_ref[place] = value

        by_row = value * row_value
        total = by_row[:8]
        for k in range(8, rows, 8):
            total = total + by_row[k : k + 8]
        stage_ref[8 * j : 8 * j + 8, :] = total
        by_col = value * col_value
        total = by_col[:, :PANELS]
        for k in range(PANELS, width, PANELS):
            total = total + by_col[:, k : k + PANELS]
        cols_ref[:, j * PANELS : (j + 1) * PANELS] += total
    fold = fold_ref[...]
    face_ref[...] += dot3(value, fold)
    rows_ref[...] += dot3(stage_ref[...], fold)

    @pl.when(step == pl.num_programs(0) - 1)
    def _():
        mine = mine_ref[...]
        part_ref[:PANELS, :] = dot3(mine, face_ref[...], TN)
        part_ref[PANELS : PANELS + 2 * planes, :] = dot3(pick_row_ref[...], rows_ref[...])
        part_ref[PANELS + 2 * planes :, :] = dot3(
            dot3(cols_ref[...], pick_col_ref[...]), mine, TN
        )


def finish_boundary(upper, f, coef, join, far, row_value, col_value, fold, mine):
    planes, rows, cols = f.shape
    width = cols // 2
    block, flat = block_specs(planes, rows, width)
    front = pl.BlockSpec((planes, rows, width), lambda i, u: (0, 0, 0))
    back = pl.BlockSpec((planes, rows, width), lambda i, u: (0, 0, jnp.maximum(i - 1, 0)))
    pick_row = np.zeros((2, planes, planes, 8), np.float32)
    pick_col = np.zeros((planes, PANELS, 2, planes), np.float32)
    for j in range(planes):
        for t in (0, 1):
            pick_row[t, j, j, t::2] = 1.0
            pick_col[j, t::2, t, j] = 1.0
    whole = lambda shape: pl.BlockSpec(shape, lambda i, u: (0, 0))
    f32 = jnp.float32
    return pl.pallas_call(
        boundary_body,
        grid_spec=pltpu.PrefetchScalarGridSpec(
            num_scalar_prefetch=1,
            grid=(2,),
            in_specs=[
                block,
                block,
                flat,
                flat,
                whole((rows, 1)),
                pl.BlockSpec((1, width), lambda i, u: (0, i)),
                pl.BlockSpec((width, PANELS), lambda i, u: (i, 0)),
                whole((rows, PANELS)),
                whole((2 * planes, 8 * planes)),
                whole((planes * PANELS, 2 * planes)),
            ],
            out_specs=[front, back, whole((PANELS + 4 * planes, PANELS))],
            scratch_shapes=[
                pltpu.VMEM((rows, PANELS), f32),
                pltpu.VMEM((8 * planes, PANELS), f32),
                pltpu.VMEM((rows, planes * PANELS), f32),
                pltpu.VMEM((8 * planes, width), f32),
                pltpu.VMEM((planes, rows, width), f32),
            ],
        ),
        out_shape=[
            jax.ShapeDtypeStruct((planes, rows, width), f32),
            jax.ShapeDtypeStruct((planes, rows, cols - width), f32),
            jax.ShapeDtypeStruct((PANELS + 4 * planes, PANELS), f32),
        ],
    )(
        upper, f, coef, join, far, row_value, col_value, fold, mine,
        pick_row.reshape(2 * planes, -1), pick_col.reshape(-1, 2 * planes),
    )


TINY = 2.0**-60
GROUP = 16
UNROLL = 4
TALL = 32
LANES = 256


def whole_steps(count):
    return (count + UNROLL - 1) // UNROLL * UNROLL


def weight_body(depth, place_ref, row_ref, col_ref, low_ref, high_ref):
    place = place_ref[0]
    first_steps = whole_steps(place - 1)
    behind = (first_steps - (place - 1)).astype(jnp.float32)
    pairs = depth // 2 - place

    def rows(index, _):
        at = pl.ds(pl.multiple_of(index * GROUP, GROUP), GROUP)
        diag = row_ref[at, :] + col_ref[...] + 2.0

        def advance(count, pair):
            for _ in range(count):
                pair = (pair[1], diag * pair[1] - pair[0])
            return pair

        zero = diag - diag
        back, here = zero, zero + 1.0
        for k in range(1, UNROLL):
            step = diag * back - here
            take = behind >= k
            back, here = jnp.where(take, step, back), jnp.where(take, back, here)
        pair = lax.fori_loop(
            0, first_steps // UNROLL, lambda _, pair: advance(UNROLL, pair), (back, here)
        )
        before, near = pair
        pair = advance(1, pair)
        pair = lax.fori_loop(0, pairs // 2, lambda _, pair: advance(4, pair), pair)
        pair = lax.fori_loop(0, pairs % 2, lambda _, pair: advance(2, pair), pair)
        distant = pair[1]
        after = diag * distant - pair[0]
        scale = 1.0 / (near * after - before * distant)
        low_ref[at, :] = distant * scale
        high_ref[at, :] = near * scale
        return 0

    lax.fori_loop(0, low_ref.shape[0] // GROUP, rows, 0)


def weights(depth, place, row_eigen, col_eigen, block):
    grid, cols = row_eigen.shape[0], col_eigen.shape[1]
    out = jax.ShapeDtypeStruct((grid, cols), jnp.float32)
    spec = pl.BlockSpec((block, cols), lambda i, u: (i, 0))
    return pl.pallas_call(
        functools.partial(weight_body, depth),
        grid_spec=pltpu.PrefetchScalarGridSpec(
            num_scalar_prefetch=1,
            grid=(grid // block,),
            in_specs=[
                pl.BlockSpec((block, 1), lambda i, u: (i, 0)),
                pl.BlockSpec((1, cols), lambda i, u: (0, 0)),
            ],
            out_specs=[spec, spec],
        ),
        out_shape=[out, out],
        cost_estimate=pl.CostEstimate(
            flops=4 * depth * grid * cols, bytes_accessed=8 * grid * cols, transcendentals=0
        ),
    )(place, row_eigen, col_eigen)


def plane_body(
    depth, place_ref, low_ref, high_ref, row_eigen_ref, col_eigen_ref, row_ref, col_ref,
    face_ref, side_ref, rows_fold_ref, fold_ref, out_ref, along_ref, across_ref, pick_ref,
    near_ref, distant_ref,
):
    half = depth // 2
    block, grid = out_ref.shape
    place = place_ref[0]
    levels = [k if k < half else half + depth - 1 - k for k in range(depth)]
    base = whole_steps(half)
    lower_steps = whole_steps(place)
    upper_steps = whole_steps(depth - place)

    def slot(k):
        return jnp.where(
            k < place, lower_steps - 1 - k, base + upper_steps - depth + k
        )

    @pl.when(pl.program_id(0) == 0)
    def _():
        along = dot(side_ref[1], fold_ref[...], NT) * (4.0 * TINY / col_ref[...])
        odd = lax.broadcasted_iota(jnp.int32, (8, grid), 0) % 2 == 1
        for k in range(UNROLL - 1):
            along_ref[k] = jnp.zeros((8, grid), jnp.float32)
            along_ref[base + k] = jnp.zeros((8, grid), jnp.float32)
            across_ref[k] = jnp.zeros((block, PANELS), jnp.float32)
            across_ref[base + k] = jnp.zeros((block, PANELS), jnp.float32)
        for k, at in enumerate(levels):
            even_row = along[at : at + 1, :]
            odd_row = along[depth + at : depth + at + 1, :]
            along_ref[slot(k)] = jnp.where(odd, odd_row, even_row)
        shape = (2 * depth, depth * PANELS)
        column = lax.broadcasted_iota(jnp.int32, shape, 1)
        row = lax.broadcasted_iota(jnp.int32, shape, 0)
        layer = column // PANELS
        layer = jnp.where(layer < half, layer, half + depth - 1 - layer)
        pick = jnp.where(row == (column % 2) * depth + layer, 1.0, 0.0).astype(jnp.bfloat16)
        for k in range(3):
            pick_ref[2 * depth * k : 2 * depth * (k + 1), :] = pick

    across = dot(rows_fold_ref[...], side_ref[0], NT) * (4.0 * TINY / row_ref[...])
    high = across.astype(jnp.bfloat16)
    rest = across - high.astype(jnp.float32)
    middle = rest.astype(jnp.bfloat16)
    low = (rest - middle.astype(jnp.float32)).astype(jnp.bfloat16)
    across = jnp.concatenate([high, middle, low], 1)
    for k in range(0, depth, 2):
        pair = bf16_dot(across, pick_ref[:, k * PANELS : (k + 2) * PANELS])
        across_ref[slot(k)] = pair[:, :PANELS]
        across_ref[slot(k + 1)] = pair[:, PANELS:]

    for k, target in ((0, near_ref), (1, distant_ref)):
        face = dot3(4.0 * rows_fold_ref[...], face_ref[k], NT)
        for at in range(0, grid, LANES):
            lanes = slice(at, at + LANES)
            target[:, lanes] = dot3(face, fold_ref[lanes, :], NT)

    for part in range(grid // LANES):
        lanes = slice(part * LANES, (part + 1) * LANES)

        def rows(index, _, lanes=lanes):
            at = pl.ds(pl.multiple_of(index * TALL, 8), TALL)
            diag = row_eigen_ref[at, :] + col_eigen_ref[:, lanes] + 2.0
            zero = diag - diag

            def run(first, steps):
                def leap(turn, pair):
                    one, two = pair
                    for k in range(UNROLL):
                        here = first + turn * UNROLL + k
                        along = along_ref[here, :, lanes]
                        across = across_ref[here, at, :]
                        layer = jnp.concatenate([along] * (TALL // 8), 0) + jnp.concatenate(
                            [across] * (LANES // PANELS), 1
                        )
                        one, two = (layer - two) + diag * one, one
                    return one, two

                return lax.fori_loop(0, steps // UNROLL, leap, (zero, zero))[0]

            lower = run(0, lower_steps)
            upper = run(base, upper_steps)
            both = row_ref[at, :] * col_ref[:, lanes] * (1.0 / TINY)
            out_ref[at, lanes] = low_ref[at, lanes] * (
                both * lower + near_ref[at, lanes]
            ) + high_ref[at, lanes] * (both * upper + distant_ref[at, lanes])
            return 0

        lax.fori_loop(0, block // TALL, rows, 0)


def plane_layers(depth, place, low, high, eigen, edge_value, face_v, side_v, fold, block):
    grid, cols = low.shape
    slots = whole_steps(depth // 2) + whole_steps(depth)
    f32 = jnp.float32
    wide = pl.BlockSpec((block, cols), lambda i, u: (i, 0))
    tall = pl.BlockSpec((block, 1), lambda i, u: (i, 0))
    flat = pl.BlockSpec((1, cols), lambda i, u: (0, 0))
    return pl.pallas_call(
        functools.partial(plane_body, depth),
        grid_spec=pltpu.PrefetchScalarGridSpec(
            num_scalar_prefetch=1,
            grid=(grid // block,),
            in_specs=[
                wide,
                wide,
                tall,
                flat,
                tall,
                flat,
                pl.BlockSpec(face_v.shape, lambda i, u: (0, 0, 0)),
                pl.BlockSpec(side_v.shape, lambda i, u: (0, 0, 0)),
                pl.BlockSpec((block, PANELS), lambda i, u: (i, 0)),
                pl.BlockSpec((cols, PANELS), lambda i, u: (0, 0)),
            ],
            out_specs=wide,
            scratch_shapes=[
                pltpu.VMEM((slots, 8, cols), f32),
                pltpu.VMEM((slots, block, PANELS), f32),
                pltpu.VMEM((6 * depth, depth * PANELS), jnp.bfloat16),
                pltpu.VMEM((block, cols), f32),
                pltpu.VMEM((block, cols), f32),
            ],
        ),
        out_shape=jax.ShapeDtypeStruct((grid, cols), f32),
        cost_estimate=pl.CostEstimate(
            flops=20 * depth * grid * cols, bytes_accessed=24 * grid * cols, transcendentals=0
        ),
    )(
        place, low, high, eigen[:grid, None], eigen[None, :], edge_value[:grid, None],
        edge_value[None, :], face_v, side_v, fold, fold,
    )


def build(mesh, grid, depth):
    slow, fast = mesh.shape["px"], mesh.shape["py"]
    devices = slow * fast
    half = devices // 2
    rows = grid // half
    edge = grid // PANELS
    groups = [list(range(half)), list(range(half, devices))]
    local = depth <= 32 and rows % 8 == 0
    split = grid // 2
    block = split // 2
    tables = {
        name: value.astype(np.float32) for name, value in small_tables(depth, grid, edge).items()
    }
    sine_np = sine_table(grid).astype(np.float32)
    sine_high = sine_np.astype(jnp.bfloat16)
    sine_low = (sine_np - sine_high.astype(np.float32)).astype(jnp.bfloat16)
    eigen_np = eigen_values(grid)
    fold_np = fold_panels(grid, edge).astype(np.float32)

    def exchange(x):
        return lax.all_to_all(
            x, AXES, split_axis=0, concat_axis=0, tiled=True, axis_index_groups=groups
        )

    def hop(x, bit):
        return lax.ppermute(x, "px", [(i, i ^ bit) for i in range(slow)])

    def swap(x):
        return lax.ppermute(x, "py", [(i, i ^ 1) for i in range(fast)])

    alternate = [list(range(0, fast, 2)), list(range(1, fast, 2))]

    def on_device(charge):
        rank = lax.axis_index(AXES)
        upper = (rank // half).astype(jnp.int32).reshape(1)
        is_upper = rank // half == 1
        start = (rank % half) * rows
        sine_pair = (jnp.asarray(sine_high), jnp.asarray(sine_low))
        fold = jnp.asarray(fold_np)
        tb = {name: jnp.asarray(value) for name, value in tables.items()}
        eigen = jnp.asarray(eigen_np.astype(np.float32))
        edge_value = jnp.asarray(sine_np[:, 0])
        my_eigen = lax.dynamic_slice_in_dim(eigen, start, rows, 0)
        my_edge = lax.dynamic_slice_in_dim(edge_value, start, rows, 0)
        my_fold = lax.dynamic_slice_in_dim(fold, start, rows, 0)
        mu = my_eigen[:, None] + eigen[None, :]
        parity = jnp.arange(grid) % 2
        edge_pair = jnp.stack([edge_value * (parity == 0), edge_value * (parity == 1)])
        my_pair = jnp.stack([my_edge * (parity[:rows] == 0), my_edge * (parity[:rows] == 1)])

        plane = charge.reshape(grid, grid)
        spectrum = double_product([plane], *sine_pair)
        spectrum = exchange(spectrum.reshape(half, rows, grid))
        coef, join = factors(mu, half)
        mixed = mixed_table(edge, depth, tb["wave_x"])
        corner = corner_table(edge, depth, tb["lift"])
        if local:
            index = (rank % half).astype(jnp.int32)
            place = jnp.where(is_upper, half - index, index + 1).reshape(1)
            weight = weights(depth, place, eigen[:split, None], eigen[None, :], block)
            spectrum, mixed, corner, weight = lax.optimization_barrier(
                (spectrum, mixed, corner, weight)
            )
        else:
            spectrum, mixed, corner = lax.optimization_barrier((spectrum, mixed, corner))
        if local:
            last = reach(upper, spectrum, coef)
        else:
            g, last = sweep(upper, spectrum, coef)
        far = lax.ppermute(last, AXES, [(i, i ^ half) for i in range(devices)])
        if local:
            u, sent, part = finish_boundary(
                upper, spectrum, coef, join, far, my_edge[:, None], edge_value[None, :], fold,
                my_fold,
            )
        else:
            u, outer = finish(upper, g, coef, join, far)

            face = dot(my_fold, dot(outer, fold), ((0,), (0,)))
            lines_y = jnp.einsum("tk,jkx->tjx", my_pair, u, precision=HIGHEST)
            lines_y = jnp.einsum("tjx,xb->tjb", lines_y, fold, precision=HIGHEST)
            lines_x = jnp.einsum("jkx,tx->tjk", u, edge_pair, precision=HIGHEST)
            lines_x = jnp.einsum("tjk,kb->tjb", lines_x, my_fold, precision=HIGHEST)
            lines = jnp.stack([lines_y, lines_x])
            lines = jnp.where(is_upper, lines[:, :, ::-1], lines)
            part = jnp.concatenate([face, lines.reshape(-1, PANELS)])
        middle = part.shape[0] // 2
        first = lax.axis_index("py") % 2 == 0
        part = part + swap(part)
        part = jnp.where(first, part[:middle], part[middle:])
        part = lax.all_gather(part, "py", axis=0, tiled=False, axis_index_groups=alternate).sum(0)
        bit = 1
        while bit < slow // 2:
            part = part + hop(part, bit)
            bit *= 2
        mine = jnp.concatenate([part, hop(part, bit)])
        if local:
            early, mine = lax.optimization_barrier((u, mine))
        mate = swap(mine)
        if local:
            u = exchange(early).reshape(grid, split)
        face_v, side_v = panel_potential(
            first.astype(jnp.int32).reshape(1), mine, mate, tb, mixed, corner
        )
        if local:
            sent = add_late(
                upper, sent, coef, join, my_edge[:, None], edge_value[None, :], face_v, side_v,
                my_fold, fold, split,
            )
            u, sent = lax.optimization_barrier((u, sent))
            sent = exchange(sent).reshape(grid, grid - split)
            layers = plane_layers(
                depth, place, *weight, eigen, edge_value, face_v, side_v, fold, block,
            )
            return double_product([u, layers, sent], *sine_pair)[None]
        else:
            near, distant = (
                4.0 * dot(dot(my_fold, face_v[i]), fold, ((1,), (1,))) for i in (0, 1)
            )
            along = 4.0 * dot(side_v[0], fold, ((1,), (1,)))
            across = 4.0 * dot(my_fold, side_v[1], ((1,), (1,)))
            u = add_ghost(
                upper, u, coef, join, my_edge[:, None], edge_value[None, :], along, across, near, distant
            )
            u = exchange(u).reshape(grid, grid)
        return double_product([u], *sine_pair)[None]

    return on_device


def solution(mesh):
    spec = P(AXES, None, None)

    def run(charge):
        depth, grid, _ = charge.shape
        body = build(mesh, grid, depth)
        return jax.shard_map(body, mesh=mesh, in_specs=(spec,), out_specs=spec, check_vma=False)(
            charge
        )

    return run
```

```python
import functools
import math

import jax
import jax.numpy as jnp
import numpy as np
from jax import lax
from jax.experimental import pallas as pl
from jax.experimental.pallas import tpu as pltpu
from jax.sharding import PartitionSpec as P

PANELS = 128
HIGHEST = lax.Precision.HIGHEST
HIGH = lax.Precision.HIGH
FOUR_PI = 4.0 * math.pi
AXES = ("px", "py")


def dot(a, b, dims=((1,), (0,)), precision=HIGHEST):
    return lax.dot_general(
        a, b, (dims, ((), ())), precision=precision, preferred_element_type=jnp.float32
    )


def sine_table(n):
    order = np.arange(1, n + 1, dtype=np.int64)
    phase = (order[:, None] * order[None, :]) % (2 * (n + 1))
    return np.sqrt(2.0 / (n + 1)) * np.sin(np.pi * phase / (n + 1.0))


def eigen_values(n):
    return 2.0 - 2.0 * np.cos(np.pi * np.arange(1, n + 1) / (n + 1.0))


def fold_panels(grid, edge):
    sums = sine_table(grid).reshape(grid, PANELS, edge).sum(2)[:, : PANELS // 2]
    even = (np.arange(grid) % 2 == 0)[:, None]
    return np.concatenate([np.where(even, sums, 0.0), np.where(even, 0.0, sums)], axis=1)


def wave_basis(n):
    place = np.arange(n // 2) - (n - 1) / 2.0
    even = np.cos(np.pi * np.arange(n)[:, None] * place[None, :] / n)
    even *= np.sqrt(np.where(np.arange(n) == 0, 1.0, 2.0) / n)[:, None]
    odd = np.sin(np.pi * np.arange(1, n + 1)[:, None] * place[None, :] / n)
    odd *= np.sqrt(np.where(np.arange(1, n + 1) == n, 1.0, 2.0) / n)[:, None]
    return even, odd


def wave_values(n):
    distance = np.arange(n)[:, None]
    order = np.concatenate([np.arange(n), np.arange(1, n + 1)])[None, :]
    return np.where(distance == 0, 1.0, 2.0) * np.cos(np.pi * distance * order / n)


def halves(value):
    high = value.astype(jnp.bfloat16)
    return high, (value - high.astype(jnp.float32)).astype(jnp.bfloat16)


def bf16_dot(a, b, dims=((1,), (0,))):
    return lax.dot_general(a, b, (dims, ((), ())), preferred_element_type=jnp.float32)


def dot3(a, b, dims=((1,), (0,))):
    a_high, a_low = halves(a)
    b_high, b_low = halves(b)
    value = bf16_dot(a_high, b_high, dims)
    return value + (bf16_dot(a_high, b_low, dims) + bf16_dot(a_low, b_high, dims))


STRIPE = 256


def product_body(count, high_ref, low_ref, *refs):
    in_refs, out_ref, mid_high_ref, mid_low_ref = refs[:count], *refs[count:]
    step = pl.program_id(0)
    stripes = pl.num_programs(0) // 2

    @pl.when(step < stripes)
    def _():
        at = pl.ds(pl.multiple_of(step * STRIPE, STRIPE), STRIPE)
        value = in_refs[0][...]
        if count == 3:
            value = jnp.concatenate([value + in_refs[1][...].T, in_refs[2][...]], 1)
        high, low = halves(value)
        value = bf16_dot(high, high_ref[...])
        value = value + bf16_dot(high, low_ref[...])
        value = value + bf16_dot(low, high_ref[...])
        high, low = halves(value)
        mid_high_ref[at, :] = high
        mid_low_ref[at, :] = low

    @pl.when(step >= stripes)
    def _():
        at = pl.ds(pl.multiple_of((step - stripes) * STRIPE, STRIPE), STRIPE)
        value = bf16_dot(high_ref[at, :], mid_high_ref[...])
        value = value + bf16_dot(high_ref[at, :], mid_low_ref[...])
        value = value + bf16_dot(low_ref[at, :], mid_high_ref[...])
        out_ref[...] = value


def double_product(values, high, low):
    grid = high.shape[0]
    stripes = grid // STRIPE
    table = pl.BlockSpec((grid, grid), lambda i: (0, 0), pipeline_mode=pl.Buffered(1))
    return pl.pallas_call(
        functools.partial(product_body, len(values)),
        grid=(2 * stripes,),
        in_specs=[table, table]
        + [
            pl.BlockSpec((v.shape[0], STRIPE), lambda i: (0, jnp.minimum(i, stripes - 1)))
            if k == 1
            else pl.BlockSpec((STRIPE, v.shape[1]), lambda i: (jnp.minimum(i, stripes - 1), 0))
            for k, v in enumerate(values)
        ],
        out_specs=pl.BlockSpec((STRIPE, grid), lambda i: (jnp.maximum(i - stripes, 0), 0)),
        out_shape=jax.ShapeDtypeStruct((grid, grid), jnp.float32),
        scratch_shapes=[
            pltpu.VMEM((grid, grid), jnp.bfloat16),
            pltpu.VMEM((grid, grid), jnp.bfloat16),
        ],
    )(high, low, *values)


def distance_power(*squares):
    return lax.rsqrt(functools.reduce(lambda a, b: a + b, squares))


def iota(shape, axis):
    return lax.broadcasted_iota(jnp.int32, shape, axis).astype(jnp.float32)


LEVELS = 4


def mixed_body(edge, depth, wave_ref, out_ref):
    hb = PANELS // 2
    soft = edge * edge / 4.0
    shape = (hb, PANELS)
    first = (edge - 1) / 2.0 + 1.0
    front = iota(shape, 0) * edge + first
    back = (PANELS - 1 - iota(shape, 0)) * edge + first
    along = iota(shape, 1) * edge
    along = along * along + soft
    front = front * front + along
    back = back * back + along
    rows = []
    for k in range(LEVELS):
        level = (pl.program_id(0) * LEVELS + k + 1).astype(jnp.float32)
        own = level * level
        far = (depth + 1.0 - level) * (depth + 1.0 - level)
        own_front, own_back = distance_power(front, own), distance_power(back, own)
        far_front, far_back = distance_power(front, far), distance_power(back, far)
        for sign in (1.0, -1.0):
            one, two = own_front + sign * far_front, own_back + sign * far_back
            rows += [one + two, one - two]
    value = dot(jnp.concatenate(rows, 0), wave_ref[...])
    for k in range(LEVELS):
        for s in (0, 1):
            at = (2 * k + s) * PANELS
            out_ref[s, k] = value[at : at + PANELS]


def mixed_table(edge, depth, wave):
    half = depth // 2
    return pl.pallas_call(
        functools.partial(mixed_body, edge, depth),
        grid=(half // LEVELS,),
        in_specs=[pl.BlockSpec((PANELS, 2 * PANELS), lambda i: (0, 0))],
        out_specs=pl.BlockSpec((2, LEVELS, PANELS, 2 * PANELS), lambda i: (0, i, 0, 0)),
        out_shape=jax.ShapeDtypeStruct((2, half, PANELS, 2 * PANELS), jnp.float32),
        cost_estimate=pl.CostEstimate(
            flops=2 * depth * PANELS**3, bytes_accessed=4 * depth * PANELS * PANELS,
            transcendentals=0,
        ),
    )(wave)


STRIP = 8


def corner_body(edge, depth, wave_ref, front_ref, back_ref):
    hb = PANELS // 2
    soft = edge * edge / 4.0
    shape = (hb, 2 * depth)
    first = (edge - 1) / 2.0 + 1.0
    lane = lax.broadcasted_iota(jnp.int32, shape, 1)
    odd = lane >= depth
    level = jnp.where(odd, lane - depth, lane).astype(jnp.float32)
    sign = jnp.where(odd, -1.0, 1.0)
    level = level * level + soft
    near = iota(shape, 0) * edge + first
    distant = (PANELS - 1 - iota(shape, 0)) * edge + first
    near = near * near + level
    distant = distant * distant + level
    sums, gaps = [], []
    for k in range(STRIP):
        b = (pl.program_id(0) * STRIP + k).astype(jnp.float32)
        front = b * edge + first
        back = (PANELS - 1 - b) * edge + first
        front, back = front * front, back * back
        one = distance_power(near, front) + sign * distance_power(distant, front)
        two = distance_power(near, back) + sign * distance_power(distant, back)
        sums.append(one + two)
        gaps.append(one - two)
    wave = wave_ref[...]
    front_ref[...] = dot(jnp.concatenate(sums, 0), wave).reshape(front_ref.shape)
    back_ref[...] = dot(jnp.concatenate(gaps, 0), wave).reshape(back_ref.shape)


def corner_table(edge, depth, wave):
    hb = PANELS // 2
    width = 4 * depth
    block = pl.BlockSpec((STRIP, hb, width), lambda i: (i, 0, 0))
    shape = jax.ShapeDtypeStruct((hb, hb, width), jnp.float32)
    return pl.pallas_call(
        functools.partial(corner_body, edge, depth),
        grid=(hb // STRIP,),
        in_specs=[pl.BlockSpec((2 * depth, width), lambda i: (0, 0))],
        out_specs=[block, block],
        out_shape=[shape, shape],
        cost_estimate=pl.CostEstimate(
            flops=2 * depth * PANELS**3, bytes_accessed=4 * depth * PANELS * PANELS,
            transcendentals=0,
        ),
    )(wave)


def small_tables(depth, grid, edge):
    half = depth // 2
    soft = edge * edge / 4.0

    def kernel(dz, dy, dx):
        return 1.0 / np.sqrt(dz * dz + dy * dy + dx * dx + soft) / FOUR_PI

    step = edge * np.arange(PANELS, dtype=np.float64)
    vx = wave_values(PANELS)
    vz = wave_values(depth)
    even, odd = wave_basis(PANELS)
    zero = np.zeros_like(even)
    basis_x = np.concatenate(
        [np.concatenate([even, zero], 1), np.concatenate([zero, odd], 1)], 0
    )
    bz = np.stack(wave_basis(depth))
    face, side = [], []
    z = np.arange(depth, dtype=np.float64)
    for s, sign in enumerate((1.0, -1.0)):
        k = kernel(0.0, step[:, None], step[None, :])
        k = k + sign * kernel(depth + 1.0, step[:, None], step[None, :])
        face.append(vx.T @ k @ vx)
        for other in (1.0, -1.0):
            k = kernel(z[:, None], 0.0, step[None, :])
            k = k + other * kernel(z[:, None], grid + 1.0, step[None, :])
            side.append(vz[:, s * depth : (s + 1) * depth].T @ k @ vx)
    level = np.zeros((2, 2, half, 2, 2, depth))
    cross = np.zeros((2, 2, half, 2, 2, depth))
    turn = np.zeros((2, 2, 2, half, 2, 2, 2, depth))
    for s in (0, 1):
        for t in (0, 1):
            level[s, t, :, s, t] = bz[s].T
            cross[s, t, :, t, s] = bz[s].T
            for x in (0, 1):
                turn[x, s, t, :, t, x, s] = bz[s].T
    lift = np.zeros((2, depth, 2, 2, depth))
    for x in (0, 1):
        for s in (0, 1):
            lift[x, :, x, s] = vz[:, s * depth : (s + 1) * depth]
    return dict(
        basis=basis_x,
        face=np.stack(face),
        side=np.concatenate(side),
        level=level.reshape(4 * half, 4 * depth),
        cross=cross.reshape(4 * half, 4 * depth),
        turn=turn.reshape(2, 4 * half, 8 * depth),
        wave_x=vx / FOUR_PI,
        lift=lift.reshape(2 * depth, 4 * depth) / FOUR_PI,
    )


NT = ((1,), (1,))
TN = ((0,), (0,))


def panels_body(
    first_ref, mine_ref, mate_ref, basis_ref, face_ref, side_ref, level_ref, cross_ref, turn_ref,
    mixed_hbm, front_hbm, back_hbm, face_out_ref, side_out_ref,
    fx_ref, hat_ref, acc_ref, toside_ref, xs_ref, tox_ref, mixed_ref, front_ref, back_ref, sems,
):
    half = mixed_ref.shape[1]
    loads = [
        pltpu.make_async_copy(source, target, sems.at[k])
        for k, (source, target) in enumerate(
            ((mixed_hbm, mixed_ref), (front_hbm, front_ref), (back_hbm, back_ref))
        )
    ]
    for load in loads:
        load.start()
    hb = PANELS // 2
    first = first_ref[0] == 1
    low = jnp.where(first, mine_ref[...], mate_ref[...])
    high = jnp.where(first, mate_ref[...], mine_ref[...])
    middle = low.shape[0] // 2
    own = jnp.concatenate([low[:middle], high[:middle]], 0)
    other = jnp.concatenate([low[middle:], high[middle:]], 0)
    total = (own + other) * 0.5
    gap = (own - other) * 0.5
    basis = basis_ref[...]
    level = level_ref[...]
    faces = [total[:PANELS], gap[:PANELS]]
    sides = []
    for axis in (0, 1):
        rows = slice(PANELS + axis * 2 * half, PANELS + (axis + 1) * 2 * half)
        sides.append(jnp.concatenate([total[rows], gap[rows]], 0))
        hat_ref[axis] = dot3(sides[axis], basis, NT)
    for s in (0, 1):
        fx_ref[0, s] = dot3(faces[s], basis, NT)
        fx_ref[1, s] = dot3(faces[s], basis, ((0,), (1,)))

    loads[0].wait()
    for s in (0, 1):

        def face_rows(block, _, s=s):
            at = pl.multiple_of(block * 8, 8)
            odd = (block >= 8).astype(jnp.int32)
            base = (2 * s + odd) * half

            def add(chunk, acc):
                one, two = acc
                for k in range(8):
                    j = chunk * 8 + k
                    t = mixed_ref[s, j, pl.ds(at, 8), :]
                    one = one + t * hat_ref[0, pl.ds(base + j, 1), :]
                    two = two + t * hat_ref[1, pl.ds(base + j, 1), :]
                return one, two

            zero = jnp.zeros((8, 2 * PANELS), jnp.float32)
            one, two = lax.fori_loop(0, half // 8, add, (zero, zero))
            acc_ref[0, s, pl.ds(at, 8), :] = one
            acc_ref[1, s, pl.ds(at, 8), :] = two
            return 0

        lax.fori_loop(0, PANELS // 8, face_rows, 0)

        def side_rows(j, _, s=s):
            for t in (0, 1):
                sums = [None, None]
                for block in range(hb // 8):
                    rows = slice(t * hb + block * 8, t * hb + block * 8 + 8)
                    table = mixed_ref[s, j, rows, :]
                    for axis in (0, 1):
                        term = table * fx_ref[axis, s, rows, :]
                        sums[axis] = term if block == 0 else sums[axis] + term
                for axis in (0, 1):
                    toside_ref[axis, pl.ds((2 * s + t) * half + j, 1), :] = jnp.sum(
                        sums[axis], axis=0, keepdims=True
                    )
            return 0

        lax.fori_loop(0, half, side_rows, 0)

    xs_ref[...] = dot3(sides[1], cross_ref[...], TN)
    ys = dot3(sides[0][:, :hb], turn_ref[0], TN) + dot3(sides[0][:, hb:], turn_ref[1], TN)
    width = xs_ref.shape[1]
    to_y = []
    loads[1].wait()
    loads[2].wait()
    for t, table_ref in ((0, front_ref), (1, back_ref)):
        mine = ys[:, t * width : (t + 1) * width]

        def corner_rows(b, acc, t=t, table_ref=table_ref, mine=mine):
            table = table_ref[b]
            row = pl.ds(t * hb + b, 1)
            tox_ref[row, :] = jnp.sum(table * mine, axis=0, keepdims=True)
            return acc + table * xs_ref[row, :]

        to_y.append(lax.fori_loop(0, hb, corner_rows, jnp.zeros((hb, width), jnp.float32)))
    to_y = jnp.concatenate(to_y, 1)
    corner = [
        jnp.concatenate([dot3(turn_ref[x], to_y, NT) for x in (0, 1)], 1),
        dot3(cross_ref[...], tox_ref[...], NT),
    ]
    for axis in (0, 1):
        waves = dot3(level, hat_ref[axis], TN) * side_ref[...]
        waves = dot3(level, waves) + toside_ref[axis]
        value = dot3(waves, basis) + corner[axis]
        even, odd = value[: 2 * half], value[2 * half :]
        for part, v in ((0, even + odd), (1, even - odd)):
            for t in (0, 1):
                at = (2 * t + part) * half
                side_out_ref[axis, at : at + half, :] = v[t * half : (t + 1) * half]
    value = []
    for s in (0, 1):
        full = dot3(basis, fx_ref[0, s]) * face_ref[s]
        rows = dot3(basis, full, TN) + acc_ref[0, s]
        value.append(dot3(rows, basis) + dot3(basis, acc_ref[1, s], ((0,), (1,))))
    face_out_ref[0] = value[0] + value[1]
    face_out_ref[1] = value[0] - value[1]


def panel_potential(first, mine, mate, tb, mixed, corner):
    half = mixed.shape[1]
    width = corner[0].shape[2]
    f32 = jnp.float32
    vmem = pl.BlockSpec(memory_space=pltpu.VMEM)
    return pl.pallas_call(
        panels_body,
        in_specs=[pl.BlockSpec(memory_space=pltpu.SMEM)]
        + [vmem] * 8
        + [pl.BlockSpec(memory_space=pl.ANY)] * 3,
        out_shape=[
            jax.ShapeDtypeStruct((2, PANELS, PANELS), f32),
            jax.ShapeDtypeStruct((2, 4 * half, PANELS), f32),
        ],
        scratch_shapes=[
            pltpu.VMEM((2, 2, PANELS, 2 * PANELS), f32),
            pltpu.VMEM((2, 4 * half, 2 * PANELS), f32),
            pltpu.VMEM((2, 2, PANELS, 2 * PANELS), f32),
            pltpu.VMEM((2, 4 * half, 2 * PANELS), f32),
            pltpu.VMEM((PANELS, width), f32),
            pltpu.VMEM((PANELS, width), f32),
            pltpu.VMEM(mixed.shape, f32),
            pltpu.VMEM(corner[0].shape, f32),
            pltpu.VMEM(corner[1].shape, f32),
            pltpu.SemaphoreType.DMA((3,)),
        ],
        cost_estimate=pl.CostEstimate(
            flops=5_000_000_000, bytes_accessed=4 * (mixed.size + 2 * corner[0].size),
            transcendentals=0,
        ),
    )(
        first, mine, mate, tb["basis"], tb["face"], tb["side"], tb["level"], tb["cross"], tb["turn"],
        mixed, *corner,
    )


WIDTH = 256


def block_specs(planes, rows, width=WIDTH, first=0):
    block = pl.BlockSpec((planes, rows, width), lambda i, *_: (0, 0, i + first))
    flat = pl.BlockSpec((rows, width), lambda i, *_: (0, i + first))
    return block, flat


def factor_body(mu_ref, coef_ref, join_ref):
    planes = coef_ref.shape[0]
    for col in range(0, WIDTH, 128):
        part = slice(col, col + 128)
        diag = mu_ref[:, part] + 2.0
        coef = 1.0 / diag
        coef_ref[0, :, part] = coef
        for j in range(1, planes):
            coef = 1.0 / (diag - coef)
            coef_ref[j, :, part] = coef
        join_ref[:, part] = 1.0 / (1.0 - coef * coef)


def factors(mu, planes):
    rows, cols = mu.shape
    block, flat = block_specs(planes, rows)
    return pl.pallas_call(
        factor_body,
        grid=(cols // WIDTH,),
        in_specs=[flat],
        out_specs=[block, flat],
        out_shape=[
            jax.ShapeDtypeStruct((planes, rows, cols), jnp.float32),
            jax.ShapeDtypeStruct((rows, cols), jnp.float32),
        ],
        cost_estimate=pl.CostEstimate(
            flops=20 * planes * rows * cols, bytes_accessed=4 * planes * rows * cols, transcendentals=0
        ),
    )(mu)


def sweep_body(half_ref, f_ref, coef_ref, g_ref, last_ref):
    planes = f_ref.shape[0]
    upper = half_ref[0]
    value = jnp.zeros_like(last_ref)
    for j in range(planes):
        place = jnp.where(upper == 1, planes - 1 - j, j)
        value = (f_ref[place] + value) * coef_ref[j]
        g_ref[j] = value
    last_ref[...] = value


def sweep(upper, spectrum, coef):
    planes, rows, cols = spectrum.shape
    block, flat = block_specs(planes, rows)
    return pl.pallas_call(
        sweep_body,
        grid_spec=pltpu.PrefetchScalarGridSpec(
            num_scalar_prefetch=1,
            grid=(cols // WIDTH,),
            in_specs=[block, block],
            out_specs=[block, flat],
        ),
        out_shape=[
            jax.ShapeDtypeStruct(spectrum.shape, jnp.float32),
            jax.ShapeDtypeStruct((rows, cols), jnp.float32),
        ],
    )(upper, spectrum, coef)


def reach_body(half_ref, f_ref, mu_ref, last_ref):
    planes, _, cols = f_ref.shape
    upper = half_ref[0]
    for at in range(0, cols, WIDTH):
        part = slice(at, at + WIDTH)
        diag = mu_ref[:, part] + 2.0
        coef = 1.0 / diag
        value = f_ref[jnp.where(upper == 1, planes - 1, 0), :, part] * coef
        for j in range(1, planes):
            coef = 1.0 / (diag - coef)
            value = (f_ref[jnp.where(upper == 1, planes - 1 - j, j), :, part] + value) * coef
        last_ref[:, part] = value


def reach(upper, spectrum, mu):
    vmem = pl.BlockSpec(memory_space=pltpu.VMEM)
    return pl.pallas_call(
        reach_body,
        in_specs=[pl.BlockSpec(memory_space=pltpu.SMEM), vmem, vmem],
        out_specs=vmem,
        out_shape=jax.ShapeDtypeStruct(mu.shape, jnp.float32),
    )(upper, spectrum, mu)


def finish_body(half_ref, g_ref, coef_ref, join_ref, far_ref, u_ref, edge_ref):
    planes = g_ref.shape[0]
    upper = half_ref[0]
    value = (far_ref[...] + coef_ref[planes - 1] * g_ref[planes - 1]) * join_ref[...]
    for j in range(planes - 1, -1, -1):
        value = g_ref[j] + coef_ref[j] * value
        u_ref[jnp.where(upper == 1, planes - 1 - j, j)] = value
    edge_ref[...] = value


def finish(upper, g, coef, join, far):
    planes, rows, cols = g.shape
    block, flat = block_specs(planes, rows)
    return pl.pallas_call(
        finish_body,
        grid_spec=pltpu.PrefetchScalarGridSpec(
            num_scalar_prefetch=1,
            grid=(cols // WIDTH,),
            in_specs=[block, block, flat, flat],
            out_specs=[block, flat],
        ),
        out_shape=[
            jax.ShapeDtypeStruct(g.shape, jnp.float32),
            jax.ShapeDtypeStruct((rows, cols), jnp.float32),
        ],
    )(upper, g, coef, join, far)


def ghost_body(
    half_ref, u_ref, coef_ref, join_ref, row_ref, col_ref, along_ref, across_ref, near_ref,
    far_ref, out_ref, g_ref,
):
    planes, rows, width = u_ref.shape
    upper = half_ref[0]
    row_odd = lax.broadcasted_iota(jnp.int32, (rows, width), 0) % 2 == 1
    col_odd = lax.broadcasted_iota(jnp.int32, (rows, width), 1) % 2 == 1
    row_value, col_value = row_ref[...], col_ref[...]

    def layer(index):
        even = along_ref[index : index + 1, :]
        odd = along_ref[2 * planes + index : 2 * planes + index + 1, :]
        side_y = row_value * jnp.where(row_odd, odd, even)
        even = across_ref[:, index : index + 1]
        odd = across_ref[:, 2 * planes + index : 2 * planes + index + 1]
        return side_y + col_value * jnp.where(col_odd, odd, even)

    own, far = near_ref[...], far_ref[...]
    for j in range(planes):
        coef = coef_ref[j]
        own = (layer(j) + own) * coef
        far = (layer(planes + j) + far) * coef
        g_ref[j] = own
    value = (far + coef * own) * join_ref[...]
    for j in range(planes - 1, -1, -1):
        value = g_ref[j] + coef_ref[j] * value
        place = jnp.where(upper == 1, planes - 1 - j, j)
        out_ref[place] = u_ref[place] + value


def add_ghost(upper, u, coef, join, row_value, col_value, along, across, near, far):
    planes, rows, cols = u.shape
    width = WIDTH
    block, flat = block_specs(planes, rows)
    return pl.pallas_call(
        ghost_body,
        grid_spec=pltpu.PrefetchScalarGridSpec(
            num_scalar_prefetch=1,
            grid=(cols // width,),
            in_specs=[
                block,
                block,
                flat,
                pl.BlockSpec((rows, 1), lambda i, u: (0, 0)),
                pl.BlockSpec((1, width), lambda i, u: (0, i)),
                pl.BlockSpec((4 * planes, width), lambda i, u: (0, i)),
                pl.BlockSpec((rows, 4 * planes), lambda i, u: (0, 0)),
                flat,
                flat,
            ],
            out_specs=block,
            scratch_shapes=[pltpu.VMEM((planes, rows, width), jnp.float32)],
        ),
        out_shape=jax.ShapeDtypeStruct(u.shape, jnp.float32),
    )(upper, u, coef, join, row_value, col_value, along, across, near, far)


def late_body(
    half_ref, u_ref, coef_ref, join_ref, row_ref, col_ref, face_ref, side_ref, mine_ref, fold_ref,
    out_ref, g_ref, along_ref, across_ref, near_ref, far_ref,
):
    mine, fold = mine_ref[...], fold_ref[...]
    along_ref[...] = 4.0 * dot3(side_ref[0], fold, NT)
    across_ref[...] = 4.0 * dot3(mine, side_ref[1], NT)
    near_ref[...] = 4.0 * dot3(dot3(mine, face_ref[0]), fold, NT)
    far_ref[...] = 4.0 * dot3(dot3(mine, face_ref[1]), fold, NT)
    ghost_body(
        half_ref, u_ref, coef_ref, join_ref, row_ref, col_ref, along_ref, across_ref, near_ref,
        far_ref, out_ref, g_ref,
    )


def add_late(upper, u, coef, join, row_value, col_value, face_v, side_v, mine, fold, width):
    planes, rows, cols = u.shape
    first = (coef.shape[2] - cols) // width
    block, _ = block_specs(planes, rows, width)
    coef_block, join_block = block_specs(planes, rows, width, first)
    f32 = jnp.float32
    return pl.pallas_call(
        late_body,
        grid_spec=pltpu.PrefetchScalarGridSpec(
            num_scalar_prefetch=1,
            grid=(cols // width,),
            in_specs=[
                block,
                coef_block,
                join_block,
                pl.BlockSpec((rows, 1), lambda i, u: (0, 0)),
                pl.BlockSpec((1, width), lambda i, u: (0, i + first)),
                pl.BlockSpec(face_v.shape, lambda i, u: (0, 0, 0)),
                pl.BlockSpec(side_v.shape, lambda i, u: (0, 0, 0)),
                pl.BlockSpec(mine.shape, lambda i, u: (0, 0)),
                pl.BlockSpec((width, PANELS), lambda i, u: (i + first, 0)),
            ],
            out_specs=block,
            scratch_shapes=[
                pltpu.VMEM((planes, rows, width), f32),
                pltpu.VMEM((4 * planes, width), f32),
                pltpu.VMEM((rows, 4 * planes), f32),
                pltpu.VMEM((rows, width), f32),
                pltpu.VMEM((rows, width), f32),
            ],
        ),
        out_shape=jax.ShapeDtypeStruct(u.shape, f32),
        cost_estimate=pl.CostEstimate(
            flops=40 * planes * rows * cols, bytes_accessed=12 * planes * rows * cols,
            transcendentals=0,
        ),
    )(upper, u, coef, join, row_value, col_value, face_v, side_v, mine, fold)


def boundary_body(
    half_ref, f_ref, coef_ref, join_ref, far_ref, row_ref, col_ref, fold_ref, mine_ref,
    pick_row_ref, pick_col_ref, front_ref, back_ref, part_ref, face_ref, rows_ref, cols_ref,
    stage_ref, g_ref,
):
    planes, rows, width = f_ref.shape
    upper = half_ref[0]
    step = pl.program_id(0)

    @pl.when(step == 0)
    def _():
        face_ref[...] = jnp.zeros_like(face_ref)
        rows_ref[...] = jnp.zeros_like(rows_ref)
        cols_ref[...] = jnp.zeros_like(cols_ref)

    row_value, col_value = row_ref[...], col_ref[...]
    value = jnp.zeros_like(far_ref)
    for j in range(planes):
        value = (f_ref[jnp.where(upper == 1, planes - 1 - j, j)] + value) * coef_ref[j]
        g_ref[j] = value
    value = (far_ref[...] + coef_ref[planes - 1] * value) * join_ref[...]
    for j in range(planes - 1, -1, -1):
        value = g_ref[j] + coef_ref[j] * value
        place = jnp.where(upper == 1, planes - 1 - j, j)

        @pl.when(step == 0)
        def _(place=place, value=value):
            front_ref[place] = value

        @pl.when(step != 0)
        def _(place=place, value=value):
            back_ref[place] = value

        by_row = value * row_value
        total = by_row[:8]
        for k in range(8, rows, 8):
            total = total + by_row[k : k + 8]
        stage_ref[8 * j : 8 * j + 8, :] = total
        by_col = value * col_value
        total = by_col[:, :PANELS]
        for k in range(PANELS, width, PANELS):
            total = total + by_col[:, k : k + PANELS]
        cols_ref[:, j * PANELS : (j + 1) * PANELS] += total
    fold = fold_ref[...]
    face_ref[...] += dot3(value, fold)
    rows_ref[...] += dot3(stage_ref[...], fold)

    @pl.when(step == pl.num_programs(0) - 1)
    def _():
        mine = mine_ref[...]
        part_ref[:PANELS, :] = dot3(mine, face_ref[...], TN)
        part_ref[PANELS : PANELS + 2 * planes, :] = dot3(pick_row_ref[...], rows_ref[...])
        part_ref[PANELS + 2 * planes :, :] = dot3(
            dot3(cols_ref[...], pick_col_ref[...]), mine, TN
        )


def finish_boundary(upper, f, coef, join, far, row_value, col_value, fold, mine):
    planes, rows, cols = f.shape
    width = cols // 2
    block, flat = block_specs(planes, rows, width)
    front = pl.BlockSpec((planes, rows, width), lambda i, u: (0, 0, 0))
    back = pl.BlockSpec((planes, rows, width), lambda i, u: (0, 0, jnp.maximum(i - 1, 0)))
    pick_row = np.zeros((2, planes, planes, 8), np.float32)
    pick_col = np.zeros((planes, PANELS, 2, planes), np.float32)
    for j in range(planes):
        for t in (0, 1):
            pick_row[t, j, j, t::2] = 1.0
            pick_col[j, t::2, t, j] = 1.0
    whole = lambda shape: pl.BlockSpec(shape, lambda i, u: (0, 0))
    f32 = jnp.float32
    return pl.pallas_call(
        boundary_body,
        grid_spec=pltpu.PrefetchScalarGridSpec(
            num_scalar_prefetch=1,
            grid=(2,),
            in_specs=[
                block,
                block,
                flat,
                flat,
                whole((rows, 1)),
                pl.BlockSpec((1, width), lambda i, u: (0, i)),
                pl.BlockSpec((width, PANELS), lambda i, u: (i, 0)),
                whole((rows, PANELS)),
                whole((2 * planes, 8 * planes)),
                whole((planes * PANELS, 2 * planes)),
            ],
            out_specs=[front, back, whole((PANELS + 4 * planes, PANELS))],
            scratch_shapes=[
                pltpu.VMEM((rows, PANELS), f32),
                pltpu.VMEM((8 * planes, PANELS), f32),
                pltpu.VMEM((rows, planes * PANELS), f32),
                pltpu.VMEM((8 * planes, width), f32),
                pltpu.VMEM((planes, rows, width), f32),
            ],
        ),
        out_shape=[
            jax.ShapeDtypeStruct((planes, rows, width), f32),
            jax.ShapeDtypeStruct((planes, rows, cols - width), f32),
            jax.ShapeDtypeStruct((PANELS + 4 * planes, PANELS), f32),
        ],
    )(
        upper, f, coef, join, far, row_value, col_value, fold, mine,
        pick_row.reshape(2 * planes, -1), pick_col.reshape(-1, 2 * planes),
    )


TINY = 2.0**-60
GROUP = 16
UNROLL = 4
TALL = 32
LANES = 256


def whole_steps(count):
    return (count + UNROLL - 1) // UNROLL * UNROLL


def weight_body(depth, place_ref, row_ref, col_ref, low_ref, high_ref):
    place = place_ref[0]
    first_steps = whole_steps(place - 1)
    behind = (first_steps - (place - 1)).astype(jnp.float32)
    pairs = depth // 2 - place

    def rows(index, _):
        at = pl.ds(pl.multiple_of(index * GROUP, GROUP), GROUP)
        diag = row_ref[at, :] + col_ref[...] + 2.0

        def advance(count, pair):
            for _ in range(count):
                pair = (pair[1], diag * pair[1] - pair[0])
            return pair

        zero = diag - diag
        back, here = zero, zero + 1.0
        for k in range(1, UNROLL):
            step = diag * back - here
            take = behind >= k
            back, here = jnp.where(take, step, back), jnp.where(take, back, here)
        pair = lax.fori_loop(
            0, first_steps // UNROLL, lambda _, pair: advance(UNROLL, pair), (back, here)
        )
        before, near = pair
        pair = advance(1, pair)
        pair = lax.fori_loop(0, pairs // 2, lambda _, pair: advance(4, pair), pair)
        pair = lax.fori_loop(0, pairs % 2, lambda _, pair: advance(2, pair), pair)
        distant = pair[1]
        after = diag * distant - pair[0]
        scale = 1.0 / (near * after - before * distant)
        low_ref[at, :] = distant * scale
        high_ref[at, :] = near * scale
        return 0

    lax.fori_loop(0, low_ref.shape[0] // GROUP, rows, 0)


def weights(depth, place, row_eigen, col_eigen, block):
    grid, cols = row_eigen.shape[0], col_eigen.shape[1]
    out = jax.ShapeDtypeStruct((grid, cols), jnp.float32)
    spec = pl.BlockSpec((block, cols), lambda i, u: (i, 0))
    return pl.pallas_call(
        functools.partial(weight_body, depth),
        grid_spec=pltpu.PrefetchScalarGridSpec(
            num_scalar_prefetch=1,
            grid=(grid // block,),
            in_specs=[
                pl.BlockSpec((block, 1), lambda i, u: (i, 0)),
                pl.BlockSpec((1, cols), lambda i, u: (0, 0)),
            ],
            out_specs=[spec, spec],
        ),
        out_shape=[out, out],
        cost_estimate=pl.CostEstimate(
            flops=4 * depth * grid * cols, bytes_accessed=8 * grid * cols, transcendentals=0
        ),
    )(place, row_eigen, col_eigen)


def plane_body(
    depth, place_ref, low_ref, high_ref, row_eigen_ref, col_eigen_ref, row_ref, col_ref,
    face_ref, side_ref, rows_fold_ref, fold_ref, out_ref, along_ref, across_ref, pick_ref,
    near_ref, distant_ref,
):
    half = depth // 2
    block, grid = out_ref.shape
    place = place_ref[0]
    levels = [k if k < half else half + depth - 1 - k for k in range(depth)]
    base = whole_steps(half)
    lower_steps = whole_steps(place)
    upper_steps = whole_steps(depth - place)

    def slot(k):
        return jnp.where(
            k < place, lower_steps - 1 - k, base + upper_steps - depth + k
        )

    @pl.when(pl.program_id(0) == 0)
    def _():
        along = dot(side_ref[1], fold_ref[...], NT) * (4.0 * TINY / col_ref[...])
        odd = lax.broadcasted_iota(jnp.int32, (8, grid), 0) % 2 == 1
        for k in range(UNROLL - 1):
            along_ref[k] = jnp.zeros((8, grid), jnp.float32)
            along_ref[base + k] = jnp.zeros((8, grid), jnp.float32)
            across_ref[k] = jnp.zeros((block, PANELS), jnp.float32)
            across_ref[base + k] = jnp.zeros((block, PANELS), jnp.float32)
        for k, at in enumerate(levels):
            even_row = along[at : at + 1, :]
            odd_row = along[depth + at : depth + at + 1, :]
            along_ref[slot(k)] = jnp.where(odd, odd_row, even_row)
        shape = (2 * depth, depth * PANELS)
        column = lax.broadcasted_iota(jnp.int32, shape, 1)
        row = lax.broadcasted_iota(jnp.int32, shape, 0)
        layer = column // PANELS
        layer = jnp.where(layer < half, layer, half + depth - 1 - layer)
        pick = jnp.where(row == (column % 2) * depth + layer, 1.0, 0.0).astype(jnp.bfloat16)
        for k in range(3):
            pick_ref[2 * depth * k : 2 * depth * (k + 1), :] = pick

    across = dot(rows_fold_ref[...], side_ref[0], NT) * (4.0 * TINY / row_ref[...])
    high = across.astype(jnp.bfloat16)
    rest = across - high.astype(jnp.float32)
    middle = rest.astype(jnp.bfloat16)
    low = (rest - middle.astype(jnp.float32)).astype(jnp.bfloat16)
    across = jnp.concatenate([high, middle, low], 1)
    for k in range(0, depth, 2):
        pair = bf16_dot(across, pick_ref[:, k * PANELS : (k + 2) * PANELS])
        across_ref[slot(k)] = pair[:, :PANELS]
        across_ref[slot(k + 1)] = pair[:, PANELS:]

    for k, target in ((0, near_ref), (1, distant_ref)):
        face = dot3(4.0 * rows_fold_ref[...], face_ref[k], NT)
        for at in range(0, grid, LANES):
            lanes = slice(at, at + LANES)
            target[:, lanes] = dot3(face, fold_ref[lanes, :], NT)

    for part in range(grid // LANES):
        lanes = slice(part * LANES, (part + 1) * LANES)

        def rows(index, _, lanes=lanes):
            at = pl.ds(pl.multiple_of(index * TALL, 8), TALL)
            diag = row_eigen_ref[at, :] + col_eigen_ref[:, lanes] + 2.0
            zero = diag - diag

            def run(first, steps):
                def leap(turn, pair):
                    one, two = pair
                    for k in range(UNROLL):
                        here = first + turn * UNROLL + k
                        along = along_ref[here, :, lanes]
                        across = across_ref[here, at, :]
                        layer = jnp.concatenate([along] * (TALL // 8), 0) + jnp.concatenate(
                            [across] * (LANES // PANELS), 1
                        )
                        one, two = (layer - two) + diag * one, one
                    return one, two

                return lax.fori_loop(0, steps // UNROLL, leap, (zero, zero))[0]

            lower = run(0, lower_steps)
            upper = run(base, upper_steps)
            both = row_ref[at, :] * col_ref[:, lanes] * (1.0 / TINY)
            out_ref[at, lanes] = low_ref[at, lanes] * (
                both * lower + near_ref[at, lanes]
            ) + high_ref[at, lanes] * (both * upper + distant_ref[at, lanes])
            return 0

        lax.fori_loop(0, block // TALL, rows, 0)


def plane_layers(depth, place, low, high, eigen, edge_value, face_v, side_v, fold, block):
    grid, cols = low.shape
    slots = whole_steps(depth // 2) + whole_steps(depth)
    f32 = jnp.float32
    wide = pl.BlockSpec((block, cols), lambda i, u: (i, 0))
    tall = pl.BlockSpec((block, 1), lambda i, u: (i, 0))
    flat = pl.BlockSpec((1, cols), lambda i, u: (0, 0))
    return pl.pallas_call(
        functools.partial(plane_body, depth),
        grid_spec=pltpu.PrefetchScalarGridSpec(
            num_scalar_prefetch=1,
            grid=(grid // block,),
            in_specs=[
                wide,
                wide,
                tall,
                flat,
                tall,
                flat,
                pl.BlockSpec(face_v.shape, lambda i, u: (0, 0, 0)),
                pl.BlockSpec(side_v.shape, lambda i, u: (0, 0, 0)),
                pl.BlockSpec((block, PANELS), lambda i, u: (i, 0)),
                pl.BlockSpec((cols, PANELS), lambda i, u: (0, 0)),
            ],
            out_specs=wide,
            scratch_shapes=[
                pltpu.VMEM((slots, 8, cols), f32),
                pltpu.VMEM((slots, block, PANELS), f32),
                pltpu.VMEM((6 * depth, depth * PANELS), jnp.bfloat16),
                pltpu.VMEM((block, cols), f32),
                pltpu.VMEM((block, cols), f32),
            ],
        ),
        out_shape=jax.ShapeDtypeStruct((grid, cols), f32),
        cost_estimate=pl.CostEstimate(
            flops=20 * depth * grid * cols, bytes_accessed=24 * grid * cols, transcendentals=0
        ),
    )(
        place, low, high, eigen[:grid, None], eigen[None, :], edge_value[:grid, None],
        edge_value[None, :], face_v, side_v, fold, fold,
    )


def build(mesh, grid, depth):
    slow, fast = mesh.shape["px"], mesh.shape["py"]
    devices = slow * fast
    half = devices // 2
    rows = grid // half
    edge = grid // PANELS
    groups = [list(range(half)), list(range(half, devices))]
    local = depth <= 32 and rows % 8 == 0
    split = grid // 2
    block = split // 2
    tables = {
        name: value.astype(np.float32) for name, value in small_tables(depth, grid, edge).items()
    }
    sine_np = sine_table(grid).astype(np.float32)
    sine_high = sine_np.astype(jnp.bfloat16)
    sine_low = (sine_np - sine_high.astype(np.float32)).astype(jnp.bfloat16)
    eigen_np = eigen_values(grid)
    fold_np = fold_panels(grid, edge).astype(np.float32)

    def exchange(x):
        return lax.all_to_all(
            x, AXES, split_axis=0, concat_axis=0, tiled=True, axis_index_groups=groups
        )

    def hop(x, bit):
        return lax.ppermute(x, "px", [(i, i ^ bit) for i in range(slow)])

    def swap(x):
        return lax.ppermute(x, "py", [(i, i ^ 1) for i in range(fast)])

    alternate = [list(range(0, fast, 2)), list(range(1, fast, 2))]

    def on_device(charge):
        rank = lax.axis_index(AXES)
        upper = (rank // half).astype(jnp.int32).reshape(1)
        is_upper = rank // half == 1
        start = (rank % half) * rows
        sine_pair = (jnp.asarray(sine_high), jnp.asarray(sine_low))
        fold = jnp.asarray(fold_np)
        tb = {name: jnp.asarray(value) for name, value in tables.items()}
        eigen = jnp.asarray(eigen_np.astype(np.float32))
        edge_value = jnp.asarray(sine_np[:, 0])
        my_eigen = lax.dynamic_slice_in_dim(eigen, start, rows, 0)
        my_edge = lax.dynamic_slice_in_dim(edge_value, start, rows, 0)
        my_fold = lax.dynamic_slice_in_dim(fold, start, rows, 0)
        mu = my_eigen[:, None] + eigen[None, :]
        parity = jnp.arange(grid) % 2
        edge_pair = jnp.stack([edge_value * (parity == 0), edge_value * (parity == 1)])
        my_pair = jnp.stack([my_edge * (parity[:rows] == 0), my_edge * (parity[:rows] == 1)])

        plane = charge.reshape(grid, grid)
        spectrum = double_product([plane], *sine_pair)
        spectrum = exchange(spectrum.reshape(half, rows, grid))
        coef, join = factors(mu, half)
        mixed = mixed_table(edge, depth, tb["wave_x"])
        corner = corner_table(edge, depth, tb["lift"])
        if local:
            index = (rank % half).astype(jnp.int32)
            place = jnp.where(is_upper, half - index, index + 1).reshape(1)
            weight = weights(depth, place, eigen[:split, None], eigen[None, :], block)
            spectrum, mixed, corner, weight = lax.optimization_barrier(
                (spectrum, mixed, corner, weight)
            )
        else:
            spectrum, mixed, corner = lax.optimization_barrier((spectrum, mixed, corner))
        if local:
            last = reach(upper, spectrum, mu)
        else:
            g, last = sweep(upper, spectrum, coef)
        far = lax.ppermute(last, AXES, [(i, i ^ half) for i in range(devices)])
        if local:
            u, sent, part = finish_boundary(
                upper, spectrum, coef, join, far, my_edge[:, None], edge_value[None, :], fold,
                my_fold,
            )
        else:
            u, outer = finish(upper, g, coef, join, far)

            face = dot(my_fold, dot(outer, fold), ((0,), (0,)))
            lines_y = jnp.einsum("tk,jkx->tjx", my_pair, u, precision=HIGHEST)
            lines_y = jnp.einsum("tjx,xb->tjb", lines_y, fold, precision=HIGHEST)
            lines_x = jnp.einsum("jkx,tx->tjk", u, edge_pair, precision=HIGHEST)
            lines_x = jnp.einsum("tjk,kb->tjb", lines_x, my_fold, precision=HIGHEST)
            lines = jnp.stack([lines_y, lines_x])
            lines = jnp.where(is_upper, lines[:, :, ::-1], lines)
            part = jnp.concatenate([face, lines.reshape(-1, PANELS)])
        middle = part.shape[0] // 2
        first = lax.axis_index("py") % 2 == 0
        part = part + swap(part)
        part = jnp.where(first, part[:middle], part[middle:])
        part = lax.all_gather(part, "py", axis=0, tiled=False, axis_index_groups=alternate).sum(0)
        bit = 1
        while bit < slow // 2:
            part = part + hop(part, bit)
            bit *= 2
        mine = jnp.concatenate([part, hop(part, bit)])
        if local:
            early, mine = lax.optimization_barrier((u, mine))
        mate = swap(mine)
        if local:
            u = exchange(early).reshape(grid, split)
        face_v, side_v = panel_potential(
            first.astype(jnp.int32).reshape(1), mine, mate, tb, mixed, corner
        )
        if local:
            sent = add_late(
                upper, sent, coef, join, my_edge[:, None], edge_value[None, :], face_v, side_v,
                my_fold, fold, split,
            )
            u, sent = lax.optimization_barrier((u, sent))
            sent = exchange(sent).reshape(grid, grid - split)
            layers = plane_layers(
                depth, place, *weight, eigen, edge_value, face_v, side_v, fold, block,
            )
            return double_product([u, layers, sent], *sine_pair)[None]
        else:
            near, distant = (
                4.0 * dot(dot(my_fold, face_v[i]), fold, ((1,), (1,))) for i in (0, 1)
            )
            along = 4.0 * dot(side_v[0], fold, ((1,), (1,)))
            across = 4.0 * dot(my_fold, side_v[1], ((1,), (1,)))
            u = add_ghost(
                upper, u, coef, join, my_edge[:, None], edge_value[None, :], along, across, near, distant
            )
            u = exchange(u).reshape(grid, grid)
        return double_product([u], *sine_pair)[None]

    return on_device


def solution(mesh):
    spec = P(AXES, None, None)

    def run(charge):
        depth, grid, _ = charge.shape
        body = build(mesh, grid, depth)
        return jax.shard_map(body, mesh=mesh, in_specs=(spec,), out_specs=spec, check_vma=False)(
            charge
        )

    return run
```

```python
import functools
import math

import jax
import jax.numpy as jnp
import numpy as np
from jax import lax
from jax.experimental import pallas as pl
from jax.experimental.pallas import tpu as pltpu
from jax.sharding import PartitionSpec as P

PANELS = 128
HIGHEST = lax.Precision.HIGHEST
HIGH = lax.Precision.HIGH
FOUR_PI = 4.0 * math.pi
AXES = ("px", "py")


def dot(a, b, dims=((1,), (0,)), precision=HIGHEST):
    return lax.dot_general(
        a, b, (dims, ((), ())), precision=precision, preferred_element_type=jnp.float32
    )


def sine_table(n):
    order = np.arange(1, n + 1, dtype=np.int64)
    phase = (order[:, None] * order[None, :]) % (2 * (n + 1))
    return np.sqrt(2.0 / (n + 1)) * np.sin(np.pi * phase / (n + 1.0))


def eigen_values(n):
    return 2.0 - 2.0 * np.cos(np.pi * np.arange(1, n + 1) / (n + 1.0))


def fold_panels(grid, edge):
    sums = sine_table(grid).reshape(grid, PANELS, edge).sum(2)[:, : PANELS // 2]
    even = (np.arange(grid) % 2 == 0)[:, None]
    return np.concatenate([np.where(even, sums, 0.0), np.where(even, 0.0, sums)], axis=1)


def wave_basis(n):
    place = np.arange(n // 2) - (n - 1) / 2.0
    even = np.cos(np.pi * np.arange(n)[:, None] * place[None, :] / n)
    even *= np.sqrt(np.where(np.arange(n) == 0, 1.0, 2.0) / n)[:, None]
    odd = np.sin(np.pi * np.arange(1, n + 1)[:, None] * place[None, :] / n)
    odd *= np.sqrt(np.where(np.arange(1, n + 1) == n, 1.0, 2.0) / n)[:, None]
    return even, odd


def wave_values(n):
    distance = np.arange(n)[:, None]
    order = np.concatenate([np.arange(n), np.arange(1, n + 1)])[None, :]
    return np.where(distance == 0, 1.0, 2.0) * np.cos(np.pi * distance * order / n)


def halves(value):
    high = value.astype(jnp.bfloat16)
    return high, (value - high.astype(jnp.float32)).astype(jnp.bfloat16)


def bf16_dot(a, b, dims=((1,), (0,))):
    return lax.dot_general(a, b, (dims, ((), ())), preferred_element_type=jnp.float32)


def dot3(a, b, dims=((1,), (0,))):
    a_high, a_low = halves(a)
    b_high, b_low = halves(b)
    value = bf16_dot(a_high, b_high, dims)
    return value + (bf16_dot(a_high, b_low, dims) + bf16_dot(a_low, b_high, dims))


STRIPE = 384


def product_body(count, high_ref, low_ref, *refs):
    in_refs, out_ref, mid_high_ref, mid_low_ref = refs[:count], *refs[count:]
    step = pl.program_id(0)
    stripes = pl.num_programs(0) // 2

    @pl.when(step < stripes)
    def _():
        at = pl.ds(pl.multiple_of(step * STRIPE, STRIPE), STRIPE)
        value = in_refs[0][...]
        if count == 3:
            value = jnp.concatenate([value + in_refs[1][...].T, in_refs[2][...]], 1)
        high, low = halves(value)
        value = bf16_dot(high, high_ref[...])
        value = value + bf16_dot(high, low_ref[...])
        value = value + bf16_dot(low, high_ref[...])
        high, low = halves(value)
        mid_high_ref[at, :] = high
        mid_low_ref[at, :] = low

    @pl.when(step >= stripes)
    def _():
        at = pl.ds(pl.multiple_of((step - stripes) * STRIPE, STRIPE), STRIPE)
        value = bf16_dot(high_ref[at, :], mid_high_ref[...])
        value = value + bf16_dot(high_ref[at, :], mid_low_ref[...])
        value = value + bf16_dot(low_ref[at, :], mid_high_ref[...])
        out_ref[...] = value


def double_product(values, high, low):
    grid = high.shape[0]
    stripes = grid // STRIPE
    table = pl.BlockSpec((grid, grid), lambda i: (0, 0), pipeline_mode=pl.Buffered(1))
    return pl.pallas_call(
        functools.partial(product_body, len(values)),
        grid=(2 * stripes,),
        in_specs=[table, table]
        + [
            pl.BlockSpec((v.shape[0], STRIPE), lambda i: (0, jnp.minimum(i, stripes - 1)))
            if k == 1
            else pl.BlockSpec((STRIPE, v.shape[1]), lambda i: (jnp.minimum(i, stripes - 1), 0))
            for k, v in enumerate(values)
        ],
        out_specs=pl.BlockSpec((STRIPE, grid), lambda i: (jnp.maximum(i - stripes, 0), 0)),
        out_shape=jax.ShapeDtypeStruct((grid, grid), jnp.float32),
        scratch_shapes=[
            pltpu.VMEM((grid, grid), jnp.bfloat16),
            pltpu.VMEM((grid, grid), jnp.bfloat16),
        ],
    )(high, low, *values)


def distance_power(*squares):
    return lax.rsqrt(functools.reduce(lambda a, b: a + b, squares))


def iota(shape, axis):
    return lax.broadcasted_iota(jnp.int32, shape, axis).astype(jnp.float32)


LEVELS = 4


def mixed_body(edge, depth, wave_ref, out_ref):
    hb = PANELS // 2
    soft = edge * edge / 4.0
    shape = (hb, PANELS)
    first = (edge - 1) / 2.0 + 1.0
    front = iota(shape, 0) * edge + first
    back = (PANELS - 1 - iota(shape, 0)) * edge + first
    along = iota(shape, 1) * edge
    along = along * along + soft
    front = front * front + along
    back = back * back + along
    rows = []
    for k in range(LEVELS):
        level = (pl.program_id(0) * LEVELS + k + 1).astype(jnp.float32)
        own = level * level
        far = (depth + 1.0 - level) * (depth + 1.0 - level)
        own_front, own_back = distance_power(front, own), distance_power(back, own)
        far_front, far_back = distance_power(front, far), distance_power(back, far)
        for sign in (1.0, -1.0):
            one, two = own_front + sign * far_front, own_back + sign * far_back
            rows += [one + two, one - two]
    value = dot(jnp.concatenate(rows, 0), wave_ref[...])
    for k in range(LEVELS):
        for s in (0, 1):
            at = (2 * k + s) * PANELS
            out_ref[s, k] = value[at : at + PANELS]


def mixed_table(edge, depth, wave):
    half = depth // 2
    return pl.pallas_call(
        functools.partial(mixed_body, edge, depth),
        grid=(half // LEVELS,),
        in_specs=[pl.BlockSpec((PANELS, 2 * PANELS), lambda i: (0, 0))],
        out_specs=pl.BlockSpec((2, LEVELS, PANELS, 2 * PANELS), lambda i: (0, i, 0, 0)),
        out_shape=jax.ShapeDtypeStruct((2, half, PANELS, 2 * PANELS), jnp.float32),
        cost_estimate=pl.CostEstimate(
            flops=2 * depth * PANELS**3, bytes_accessed=4 * depth * PANELS * PANELS,
            transcendentals=0,
        ),
    )(wave)


STRIP = 8


def corner_body(edge, depth, wave_ref, front_ref, back_ref):
    hb = PANELS // 2
    soft = edge * edge / 4.0
    shape = (hb, 2 * depth)
    first = (edge - 1) / 2.0 + 1.0
    lane = lax.broadcasted_iota(jnp.int32, shape, 1)
    odd = lane >= depth
    level = jnp.where(odd, lane - depth, lane).astype(jnp.float32)
    sign = jnp.where(odd, -1.0, 1.0)
    level = level * level + soft
    near = iota(shape, 0) * edge + first
    distant = (PANELS - 1 - iota(shape, 0)) * edge + first
    near = near * near + level
    distant = distant * distant + level
    sums, gaps = [], []
    for k in range(STRIP):
        b = (pl.program_id(0) * STRIP + k).astype(jnp.float32)
        front = b * edge + first
        back = (PANELS - 1 - b) * edge + first
        front, back = front * front, back * back
        one = distance_power(near, front) + sign * distance_power(distant, front)
        two = distance_power(near, back) + sign * distance_power(distant, back)
        sums.append(one + two)
        gaps.append(one - two)
    wave = wave_ref[...]
    front_ref[...] = dot(jnp.concatenate(sums, 0), wave).reshape(front_ref.shape)
    back_ref[...] = dot(jnp.concatenate(gaps, 0), wave).reshape(back_ref.shape)


def corner_table(edge, depth, wave):
    hb = PANELS // 2
    width = 4 * depth
    block = pl.BlockSpec((STRIP, hb, width), lambda i: (i, 0, 0))
    shape = jax.ShapeDtypeStruct((hb, hb, width), jnp.float32)
    return pl.pallas_call(
        functools.partial(corner_body, edge, depth),
        grid=(hb // STRIP,),
        in_specs=[pl.BlockSpec((2 * depth, width), lambda i: (0, 0))],
        out_specs=[block, block],
        out_shape=[shape, shape],
        cost_estimate=pl.CostEstimate(
            flops=2 * depth * PANELS**3, bytes_accessed=4 * depth * PANELS * PANELS,
            transcendentals=0,
        ),
    )(wave)


def small_tables(depth, grid, edge):
    half = depth // 2
    soft = edge * edge / 4.0

    def kernel(dz, dy, dx):
        return 1.0 / np.sqrt(dz * dz + dy * dy + dx * dx + soft) / FOUR_PI

    step = edge * np.arange(PANELS, dtype=np.float64)
    vx = wave_values(PANELS)
    vz = wave_values(depth)
    even, odd = wave_basis(PANELS)
    zero = np.zeros_like(even)
    basis_x = np.concatenate(
        [np.concatenate([even, zero], 1), np.concatenate([zero, odd], 1)], 0
    )
    bz = np.stack(wave_basis(depth))
    face, side = [], []
    z = np.arange(depth, dtype=np.float64)
    for s, sign in enumerate((1.0, -1.0)):
        k = kernel(0.0, step[:, None], step[None, :])
        k = k + sign * kernel(depth + 1.0, step[:, None], step[None, :])
        face.append(vx.T @ k @ vx)
        for other in (1.0, -1.0):
            k = kernel(z[:, None], 0.0, step[None, :])
            k = k + other * kernel(z[:, None], grid + 1.0, step[None, :])
            side.append(vz[:, s * depth : (s + 1) * depth].T @ k @ vx)
    level = np.zeros((2, 2, half, 2, 2, depth))
    cross = np.zeros((2, 2, half, 2, 2, depth))
    turn = np.zeros((2, 2, 2, half, 2, 2, 2, depth))
    for s in (0, 1):
        for t in (0, 1):
            level[s, t, :, s, t] = bz[s].T
            cross[s, t, :, t, s] = bz[s].T
            for x in (0, 1):
                turn[x, s, t, :, t, x, s] = bz[s].T
    lift = np.zeros((2, depth, 2, 2, depth))
    for x in (0, 1):
        for s in (0, 1):
            lift[x, :, x, s] = vz[:, s * depth : (s + 1) * depth]
    return dict(
        basis=basis_x,
        face=np.stack(face),
        side=np.concatenate(side),
        level=level.reshape(4 * half, 4 * depth),
        cross=cross.reshape(4 * half, 4 * depth),
        turn=turn.reshape(2, 4 * half, 8 * depth),
        wave_x=vx / FOUR_PI,
        lift=lift.reshape(2 * depth, 4 * depth) / FOUR_PI,
    )


NT = ((1,), (1,))
TN = ((0,), (0,))


def panels_body(
    first_ref, mine_ref, mate_ref, basis_ref, face_ref, side_ref, level_ref, cross_ref, turn_ref,
    mixed_hbm, front_hbm, back_hbm, face_out_ref, side_out_ref,
    fx_ref, hat_ref, acc_ref, toside_ref, xs_ref, tox_ref, mixed_ref, front_ref, back_ref, sems,
):
    half = mixed_ref.shape[1]
    loads = [
        pltpu.make_async_copy(source, target, sems.at[k])
        for k, (source, target) in enumerate(
            ((mixed_hbm, mixed_ref), (front_hbm, front_ref), (back_hbm, back_ref))
        )
    ]
    for load in loads:
        load.start()
    hb = PANELS // 2
    first = first_ref[0] == 1
    low = jnp.where(first, mine_ref[...], mate_ref[...])
    high = jnp.where(first, mate_ref[...], mine_ref[...])
    middle = low.shape[0] // 2
    own = jnp.concatenate([low[:middle], high[:middle]], 0)
    other = jnp.concatenate([low[middle:], high[middle:]], 0)
    total = (own + other) * 0.5
    gap = (own - other) * 0.5
    basis = basis_ref[...]
    level = level_ref[...]
    faces = [total[:PANELS], gap[:PANELS]]
    sides = []
    for axis in (0, 1):
        rows = slice(PANELS + axis * 2 * half, PANELS + (axis + 1) * 2 * half)
        sides.append(jnp.concatenate([total[rows], gap[rows]], 0))
        hat_ref[axis] = dot3(sides[axis], basis, NT)
    for s in (0, 1):
        fx_ref[0, s] = dot3(faces[s], basis, NT)
        fx_ref[1, s] = dot3(faces[s], basis, ((0,), (1,)))

    loads[0].wait()
    for s in (0, 1):

        def face_rows(block, _, s=s):
            at = pl.multiple_of(block * 8, 8)
            odd = (block >= 8).astype(jnp.int32)
            base = (2 * s + odd) * half

            def add(chunk, acc):
                one, two = acc
                for k in range(8):
                    j = chunk * 8 + k
                    t = mixed_ref[s, j, pl.ds(at, 8), :]
                    one = one + t * hat_ref[0, pl.ds(base + j, 1), :]
                    two = two + t * hat_ref[1, pl.ds(base + j, 1), :]
                return one, two

            zero = jnp.zeros((8, 2 * PANELS), jnp.float32)
            one, two = lax.fori_loop(0, half // 8, add, (zero, zero))
            acc_ref[0, s, pl.ds(at, 8), :] = one
            acc_ref[1, s, pl.ds(at, 8), :] = two
            return 0

        lax.fori_loop(0, PANELS // 8, face_rows, 0)

        def side_rows(j, _, s=s):
            for t in (0, 1):
                sums = [None, None]
                for block in range(hb // 8):
                    rows = slice(t * hb + block * 8, t * hb + block * 8 + 8)
                    table = mixed_ref[s, j, rows, :]
                    for axis in (0, 1):
                        term = table * fx_ref[axis, s, rows, :]
                        sums[axis] = term if block == 0 else sums[axis] + term
                for axis in (0, 1):
                    toside_ref[axis, pl.ds((2 * s + t) * half + j, 1), :] = jnp.sum(
                        sums[axis], axis=0, keepdims=True
                    )
            return 0

        lax.fori_loop(0, half, side_rows, 0)

    xs_ref[...] = dot3(sides[1], cross_ref[...], TN)
    ys = dot3(sides[0][:, :hb], turn_ref[0], TN) + dot3(sides[0][:, hb:], turn_ref[1], TN)
    width = xs_ref.shape[1]
    to_y = []
    loads[1].wait()
    loads[2].wait()
    for t, table_ref in ((0, front_ref), (1, back_ref)):
        mine = ys[:, t * width : (t + 1) * width]

        def corner_rows(b, acc, t=t, table_ref=table_ref, mine=mine):
            table = table_ref[b]
            row = pl.ds(t * hb + b, 1)
            tox_ref[row, :] = jnp.sum(table * mine, axis=0, keepdims=True)
            return acc + table * xs_ref[row, :]

        to_y.append(lax.fori_loop(0, hb, corner_rows, jnp.zeros((hb, width), jnp.float32)))
    to_y = jnp.concatenate(to_y, 1)
    corner = [
        jnp.concatenate([dot3(turn_ref[x], to_y, NT) for x in (0, 1)], 1),
        dot3(cross_ref[...], tox_ref[...], NT),
    ]
    for axis in (0, 1):
        waves = dot3(level, hat_ref[axis], TN) * side_ref[...]
        waves = dot3(level, waves) + toside_ref[axis]
        value = dot3(waves, basis) + corner[axis]
        even, odd = value[: 2 * half], value[2 * half :]
        for part, v in ((0, even + odd), (1, even - odd)):
            for t in (0, 1):
                at = (2 * t + part) * half
                side_out_ref[axis, at : at + half, :] = v[t * half : (t + 1) * half]
    value = []
    for s in (0, 1):
        full = dot3(basis, fx_ref[0, s]) * face_ref[s]
        rows = dot3(basis, full, TN) + acc_ref[0, s]
        value.append(dot3(rows, basis) + dot3(basis, acc_ref[1, s], ((0,), (1,))))
    face_out_ref[0] = value[0] + value[1]
    face_out_ref[1] = value[0] - value[1]


def panel_potential(first, mine, mate, tb, mixed, corner):
    half = mixed.shape[1]
    width = corner[0].shape[2]
    f32 = jnp.float32
    vmem = pl.BlockSpec(memory_space=pltpu.VMEM)
    return pl.pallas_call(
        panels_body,
        in_specs=[pl.BlockSpec(memory_space=pltpu.SMEM)]
        + [vmem] * 8
        + [pl.BlockSpec(memory_space=pl.ANY)] * 3,
        out_shape=[
            jax.ShapeDtypeStruct((2, PANELS, PANELS), f32),
            jax.ShapeDtypeStruct((2, 4 * half, PANELS), f32),
        ],
        scratch_shapes=[
            pltpu.VMEM((2, 2, PANELS, 2 * PANELS), f32),
            pltpu.VMEM((2, 4 * half, 2 * PANELS), f32),
            pltpu.VMEM((2, 2, PANELS, 2 * PANELS), f32),
            pltpu.VMEM((2, 4 * half, 2 * PANELS), f32),
            pltpu.VMEM((PANELS, width), f32),
            pltpu.VMEM((PANELS, width), f32),
            pltpu.VMEM(mixed.shape, f32),
            pltpu.VMEM(corner[0].shape, f32),
            pltpu.VMEM(corner[1].shape, f32),
            pltpu.SemaphoreType.DMA((3,)),
        ],
        cost_estimate=pl.CostEstimate(
            flops=5_000_000_000, bytes_accessed=4 * (mixed.size + 2 * corner[0].size),
            transcendentals=0,
        ),
    )(
        first, mine, mate, tb["basis"], tb["face"], tb["side"], tb["level"], tb["cross"], tb["turn"],
        mixed, *corner,
    )


WIDTH = 256


def block_specs(planes, rows, width=WIDTH, first=0):
    block = pl.BlockSpec((planes, rows, width), lambda i, *_: (0, 0, i + first))
    flat = pl.BlockSpec((rows, width), lambda i, *_: (0, i + first))
    return block, flat


def factor_body(mu_ref, coef_ref, join_ref):
    planes = coef_ref.shape[0]
    for col in range(0, WIDTH, 128):
        part = slice(col, col + 128)
        diag = mu_ref[:, part] + 2.0
        coef = 1.0 / diag
        coef_ref[0, :, part] = coef
        for j in range(1, planes):
            coef = 1.0 / (diag - coef)
            coef_ref[j, :, part] = coef
        join_ref[:, part] = 1.0 / (1.0 - coef * coef)


def factors(mu, planes):
    rows, cols = mu.shape
    block, flat = block_specs(planes, rows)
    return pl.pallas_call(
        factor_body,
        grid=(cols // WIDTH,),
        in_specs=[flat],
        out_specs=[block, flat],
        out_shape=[
            jax.ShapeDtypeStruct((planes, rows, cols), jnp.float32),
            jax.ShapeDtypeStruct((rows, cols), jnp.float32),
        ],
        cost_estimate=pl.CostEstimate(
            flops=20 * planes * rows * cols, bytes_accessed=4 * planes * rows * cols, transcendentals=0
        ),
    )(mu)


def sweep_body(half_ref, f_ref, coef_ref, g_ref, last_ref):
    planes = f_ref.shape[0]
    upper = half_ref[0]
    value = jnp.zeros_like(last_ref)
    for j in range(planes):
        place = jnp.where(upper == 1, planes - 1 - j, j)
        value = (f_ref[place] + value) * coef_ref[j]
        g_ref[j] = value
    last_ref[...] = value


def sweep(upper, spectrum, coef):
    planes, rows, cols = spectrum.shape
    block, flat = block_specs(planes, rows)
    return pl.pallas_call(
        sweep_body,
        grid_spec=pltpu.PrefetchScalarGridSpec(
            num_scalar_prefetch=1,
            grid=(cols // WIDTH,),
            in_specs=[block, block],
            out_specs=[block, flat],
        ),
        out_shape=[
            jax.ShapeDtypeStruct(spectrum.shape, jnp.float32),
            jax.ShapeDtypeStruct((rows, cols), jnp.float32),
        ],
    )(upper, spectrum, coef)


def reach_body(half_ref, f_ref, mu_ref, last_ref):
    planes, _, cols = f_ref.shape
    upper = half_ref[0]
    for at in range(0, cols, WIDTH):
        part = slice(at, at + WIDTH)
        diag = mu_ref[:, part] + 2.0
        coef = 1.0 / diag
        value = f_ref[jnp.where(upper == 1, planes - 1, 0), :, part] * coef
        for j in range(1, planes):
            coef = 1.0 / (diag - coef)
            value = (f_ref[jnp.where(upper == 1, planes - 1 - j, j), :, part] + value) * coef
        last_ref[:, part] = value


def reach(upper, spectrum, mu):
    vmem = pl.BlockSpec(memory_space=pltpu.VMEM)
    return pl.pallas_call(
        reach_body,
        in_specs=[pl.BlockSpec(memory_space=pltpu.SMEM), vmem, vmem],
        out_specs=vmem,
        out_shape=jax.ShapeDtypeStruct(mu.shape, jnp.float32),
    )(upper, spectrum, mu)


def finish_body(half_ref, g_ref, coef_ref, join_ref, far_ref, u_ref, edge_ref):
    planes = g_ref.shape[0]
    upper = half_ref[0]
    value = (far_ref[...] + coef_ref[planes - 1] * g_ref[planes - 1]) * join_ref[...]
    for j in range(planes - 1, -1, -1):
        value = g_ref[j] + coef_ref[j] * value
        u_ref[jnp.where(upper == 1, planes - 1 - j, j)] = value
    edge_ref[...] = value


def finish(upper, g, coef, join, far):
    planes, rows, cols = g.shape
    block, flat = block_specs(planes, rows)
    return pl.pallas_call(
        finish_body,
        grid_spec=pltpu.PrefetchScalarGridSpec(
            num_scalar_prefetch=1,
            grid=(cols // WIDTH,),
            in_specs=[block, block, flat, flat],
            out_specs=[block, flat],
        ),
        out_shape=[
            jax.ShapeDtypeStruct(g.shape, jnp.float32),
            jax.ShapeDtypeStruct((rows, cols), jnp.float32),
        ],
    )(upper, g, coef, join, far)


def ghost_body(
    half_ref, u_ref, coef_ref, join_ref, row_ref, col_ref, along_ref, across_ref, near_ref,
    far_ref, out_ref, g_ref,
):
    planes, rows, width = u_ref.shape
    upper = half_ref[0]
    row_odd = lax.broadcasted_iota(jnp.int32, (rows, width), 0) % 2 == 1
    col_odd = lax.broadcasted_iota(jnp.int32, (rows, width), 1) % 2 == 1
    row_value, col_value = row_ref[...], col_ref[...]

    def layer(index):
        even = along_ref[index : index + 1, :]
        odd = along_ref[2 * planes + index : 2 * planes + index + 1, :]
        side_y = row_value * jnp.where(row_odd, odd, even)
        even = across_ref[:, index : index + 1]
        odd = across_ref[:, 2 * planes + index : 2 * planes + index + 1]
        return side_y + col_value * jnp.where(col_odd, odd, even)

    own, far = near_ref[...], far_ref[...]
    for j in range(planes):
        coef = coef_ref[j]
        own = (layer(j) + own) * coef
        far = (layer(planes + j) + far) * coef
        g_ref[j] = own
    value = (far + coef * own) * join_ref[...]
    for j in range(planes - 1, -1, -1):
        value = g_ref[j] + coef_ref[j] * value
        place = jnp.where(upper == 1, planes - 1 - j, j)
        out_ref[place] = u_ref[place] + value


def add_ghost(upper, u, coef, join, row_value, col_value, along, across, near, far):
    planes, rows, cols = u.shape
    width = WIDTH
    block, flat = block_specs(planes, rows)
    return pl.pallas_call(
        ghost_body,
        grid_spec=pltpu.PrefetchScalarGridSpec(
            num_scalar_prefetch=1,
            grid=(cols // width,),
            in_specs=[
                block,
                block,
                flat,
                pl.BlockSpec((rows, 1), lambda i, u: (0, 0)),
                pl.BlockSpec((1, width), lambda i, u: (0, i)),
                pl.BlockSpec((4 * planes, width), lambda i, u: (0, i)),
                pl.BlockSpec((rows, 4 * planes), lambda i, u: (0, 0)),
                flat,
                flat,
            ],
            out_specs=block,
            scratch_shapes=[pltpu.VMEM((planes, rows, width), jnp.float32)],
        ),
        out_shape=jax.ShapeDtypeStruct(u.shape, jnp.float32),
    )(upper, u, coef, join, row_value, col_value, along, across, near, far)


def late_body(
    half_ref, u_ref, coef_ref, join_ref, row_ref, col_ref, face_ref, side_ref, mine_ref, fold_ref,
    out_ref, g_ref, along_ref, across_ref, near_ref, far_ref,
):
    mine, fold = mine_ref[...], fold_ref[...]
    along_ref[...] = 4.0 * dot3(side_ref[0], fold, NT)
    across_ref[...] = 4.0 * dot3(mine, side_ref[1], NT)
    near_ref[...] = 4.0 * dot3(dot3(mine, face_ref[0]), fold, NT)
    far_ref[...] = 4.0 * dot3(dot3(mine, face_ref[1]), fold, NT)
    ghost_body(
        half_ref, u_ref, coef_ref, join_ref, row_ref, col_ref, along_ref, across_ref, near_ref,
        far_ref, out_ref, g_ref,
    )


def add_late(upper, u, coef, join, row_value, col_value, face_v, side_v, mine, fold, width):
    planes, rows, cols = u.shape
    first = (coef.shape[2] - cols) // width
    block, _ = block_specs(planes, rows, width)
    coef_block, join_block = block_specs(planes, rows, width, first)
    f32 = jnp.float32
    return pl.pallas_call(
        late_body,
        grid_spec=pltpu.PrefetchScalarGridSpec(
            num_scalar_prefetch=1,
            grid=(cols // width,),
            in_specs=[
                block,
                coef_block,
                join_block,
                pl.BlockSpec((rows, 1), lambda i, u: (0, 0)),
                pl.BlockSpec((1, width), lambda i, u: (0, i + first)),
                pl.BlockSpec(face_v.shape, lambda i, u: (0, 0, 0)),
                pl.BlockSpec(side_v.shape, lambda i, u: (0, 0, 0)),
                pl.BlockSpec(mine.shape, lambda i, u: (0, 0)),
                pl.BlockSpec((width, PANELS), lambda i, u: (i + first, 0)),
            ],
            out_specs=block,
            scratch_shapes=[
                pltpu.VMEM((planes, rows, width), f32),
                pltpu.VMEM((4 * planes, width), f32),
                pltpu.VMEM((rows, 4 * planes), f32),
                pltpu.VMEM((rows, width), f32),
                pltpu.VMEM((rows, width), f32),
            ],
        ),
        out_shape=jax.ShapeDtypeStruct(u.shape, f32),
        cost_estimate=pl.CostEstimate(
            flops=40 * planes * rows * cols, bytes_accessed=12 * planes * rows * cols,
            transcendentals=0,
        ),
    )(upper, u, coef, join, row_value, col_value, face_v, side_v, mine, fold)


def boundary_body(
    half_ref, f_ref, coef_ref, join_ref, far_ref, row_ref, col_ref, fold_ref, mine_ref,
    pick_row_ref, pick_col_ref, front_ref, back_ref, part_ref, face_ref, rows_ref, cols_ref,
    stage_ref, g_ref,
):
    planes, rows, width = f_ref.shape
    upper = half_ref[0]
    step = pl.program_id(0)

    @pl.when(step == 0)
    def _():
        face_ref[...] = jnp.zeros_like(face_ref)
        rows_ref[...] = jnp.zeros_like(rows_ref)
        cols_ref[...] = jnp.zeros_like(cols_ref)

    row_value, col_value = row_ref[...], col_ref[...]
    value = jnp.zeros_like(far_ref)
    for j in range(planes):
        value = (f_ref[jnp.where(upper == 1, planes - 1 - j, j)] + value) * coef_ref[j]
        g_ref[j] = value
    value = (far_ref[...] + coef_ref[planes - 1] * value) * join_ref[...]
    for j in range(planes - 1, -1, -1):
        value = g_ref[j] + coef_ref[j] * value
        place = jnp.where(upper == 1, planes - 1 - j, j)

        @pl.when(step == 0)
        def _(place=place, value=value):
            front_ref[place] = value

        @pl.when(step != 0)
        def _(place=place, value=value):
            back_ref[place] = value

        by_row = value * row_value
        total = by_row[:8]
        for k in range(8, rows, 8):
            total = total + by_row[k : k + 8]
        stage_ref[8 * j : 8 * j + 8, :] = total
        by_col = value * col_value
        total = by_col[:, :PANELS]
        for k in range(PANELS, width, PANELS):
            total = total + by_col[:, k : k + PANELS]
        cols_ref[:, j * PANELS : (j + 1) * PANELS] += total
    fold = fold_ref[...]
    face_ref[...] += dot3(value, fold)
    rows_ref[...] += dot3(stage_ref[...], fold)

    @pl.when(step == pl.num_programs(0) - 1)
    def _():
        mine = mine_ref[...]
        part_ref[:PANELS, :] = dot3(mine, face_ref[...], TN)
        part_ref[PANELS : PANELS + 2 * planes, :] = dot3(pick_row_ref[...], rows_ref[...])
        part_ref[PANELS + 2 * planes :, :] = dot3(
            dot3(cols_ref[...], pick_col_ref[...]), mine, TN
        )


def finish_boundary(upper, f, coef, join, far, row_value, col_value, fold, mine):
    planes, rows, cols = f.shape
    width = cols // 2
    block, flat = block_specs(planes, rows, width)
    front = pl.BlockSpec((planes, rows, width), lambda i, u: (0, 0, 0))
    back = pl.BlockSpec((planes, rows, width), lambda i, u: (0, 0, jnp.maximum(i - 1, 0)))
    pick_row = np.zeros((2, planes, planes, 8), np.float32)
    pick_col = np.zeros((planes, PANELS, 2, planes), np.float32)
    for j in range(planes):
        for t in (0, 1):
            pick_row[t, j, j, t::2] = 1.0
            pick_col[j, t::2, t, j] = 1.0
    whole = lambda shape: pl.BlockSpec(shape, lambda i, u: (0, 0))
    f32 = jnp.float32
    return pl.pallas_call(
        boundary_body,
        grid_spec=pltpu.PrefetchScalarGridSpec(
            num_scalar_prefetch=1,
            grid=(2,),
            in_specs=[
                block,
                block,
                flat,
                flat,
                whole((rows, 1)),
                pl.BlockSpec((1, width), lambda i, u: (0, i)),
                pl.BlockSpec((width, PANELS), lambda i, u: (i, 0)),
                whole((rows, PANELS)),
                whole((2 * planes, 8 * planes)),
                whole((planes * PANELS, 2 * planes)),
            ],
            out_specs=[front, back, whole((PANELS + 4 * planes, PANELS))],
            scratch_shapes=[
                pltpu.VMEM((rows, PANELS), f32),
                pltpu.VMEM((8 * planes, PANELS), f32),
                pltpu.VMEM((rows, planes * PANELS), f32),
                pltpu.VMEM((8 * planes, width), f32),
                pltpu.VMEM((planes, rows, width), f32),
            ],
        ),
        out_shape=[
            jax.ShapeDtypeStruct((planes, rows, width), f32),
            jax.ShapeDtypeStruct((planes, rows, cols - width), f32),
            jax.ShapeDtypeStruct((PANELS + 4 * planes, PANELS), f32),
        ],
    )(
        upper, f, coef, join, far, row_value, col_value, fold, mine,
        pick_row.reshape(2 * planes, -1), pick_col.reshape(-1, 2 * planes),
    )


TINY = 2.0**-60
GROUP = 16
UNROLL = 4
TALL = 32
LANES = 256


def whole_steps(count):
    return (count + UNROLL - 1) // UNROLL * UNROLL


def weight_body(depth, place_ref, row_ref, col_ref, low_ref, high_ref):
    place = place_ref[0]
    first_steps = whole_steps(place - 1)
    behind = (first_steps - (place - 1)).astype(jnp.float32)
    pairs = depth // 2 - place

    def rows(index, _):
        at = pl.ds(pl.multiple_of(index * GROUP, GROUP), GROUP)
        diag = row_ref[at, :] + col_ref[...] + 2.0

        def advance(count, pair):
            for _ in range(count):
                pair = (pair[1], diag * pair[1] - pair[0])
            return pair

        zero = diag - diag
        back, here = zero, zero + 1.0
        for k in range(1, UNROLL):
            step = diag * back - here
            take = behind >= k
            back, here = jnp.where(take, step, back), jnp.where(take, back, here)
        pair = lax.fori_loop(
            0, first_steps // UNROLL, lambda _, pair: advance(UNROLL, pair), (back, here)
        )
        before, near = pair
        pair = advance(1, pair)
        pair = lax.fori_loop(0, pairs // 2, lambda _, pair: advance(4, pair), pair)
        pair = lax.fori_loop(0, pairs % 2, lambda _, pair: advance(2, pair), pair)
        distant = pair[1]
        after = diag * distant - pair[0]
        scale = 1.0 / (near * after - before * distant)
        low_ref[at, :] = distant * scale
        high_ref[at, :] = near * scale
        return 0

    lax.fori_loop(0, low_ref.shape[0] // GROUP, rows, 0)


def weights(depth, place, row_eigen, col_eigen, block):
    grid, cols = row_eigen.shape[0], col_eigen.shape[1]
    out = jax.ShapeDtypeStruct((grid, cols), jnp.float32)
    spec = pl.BlockSpec((block, cols), lambda i, u: (i, 0))
    return pl.pallas_call(
        functools.partial(weight_body, depth),
        grid_spec=pltpu.PrefetchScalarGridSpec(
            num_scalar_prefetch=1,
            grid=(grid // block,),
            in_specs=[
                pl.BlockSpec((block, 1), lambda i, u: (i, 0)),
                pl.BlockSpec((1, cols), lambda i, u: (0, 0)),
            ],
            out_specs=[spec, spec],
        ),
        out_shape=[out, out],
        cost_estimate=pl.CostEstimate(
            flops=4 * depth * grid * cols, bytes_accessed=8 * grid * cols, transcendentals=0
        ),
    )(place, row_eigen, col_eigen)


def plane_body(
    depth, place_ref, low_ref, high_ref, row_eigen_ref, col_eigen_ref, row_ref, col_ref,
    face_ref, side_ref, rows_fold_ref, fold_ref, out_ref, along_ref, across_ref, pick_ref,
    near_ref, distant_ref,
):
    half = depth // 2
    block, grid = out_ref.shape
    place = place_ref[0]
    levels = [k if k < half else half + depth - 1 - k for k in range(depth)]
    base = whole_steps(half)
    lower_steps = whole_steps(place)
    upper_steps = whole_steps(depth - place)

    def slot(k):
        return jnp.where(
            k < place, lower_steps - 1 - k, base + upper_steps - depth + k
        )

    @pl.when(pl.program_id(0) == 0)
    def _():
        along = dot(side_ref[1], fold_ref[...], NT) * (4.0 * TINY / col_ref[...])
        odd = lax.broadcasted_iota(jnp.int32, (8, grid), 0) % 2 == 1
        for k in range(UNROLL - 1):
            along_ref[k] = jnp.zeros((8, grid), jnp.float32)
            along_ref[base + k] = jnp.zeros((8, grid), jnp.float32)
            across_ref[k] = jnp.zeros((block, PANELS), jnp.float32)
            across_ref[base + k] = jnp.zeros((block, PANELS), jnp.float32)
        for k, at in enumerate(levels):
            even_row = along[at : at + 1, :]
            odd_row = along[depth + at : depth + at + 1, :]
            along_ref[slot(k)] = jnp.where(odd, odd_row, even_row)
        shape = (2 * depth, depth * PANELS)
        column = lax.broadcasted_iota(jnp.int32, shape, 1)
        row = lax.broadcasted_iota(jnp.int32, shape, 0)
        layer = column // PANELS
        layer = jnp.where(layer < half, layer, half + depth - 1 - layer)
        pick = jnp.where(row == (column % 2) * depth + layer, 1.0, 0.0).astype(jnp.bfloat16)
        for k in range(3):
            pick_ref[2 * depth * k : 2 * depth * (k + 1), :] = pick

    across = dot(rows_fold_ref[...], side_ref[0], NT) * (4.0 * TINY / row_ref[...])
    high = across.astype(jnp.bfloat16)
    rest = across - high.astype(jnp.float32)
    middle = rest.astype(jnp.bfloat16)
    low = (rest - middle.astype(jnp.float32)).astype(jnp.bfloat16)
    across = jnp.concatenate([high, middle, low], 1)
    for k in range(0, depth, 2):
        pair = bf16_dot(across, pick_ref[:, k * PANELS : (k + 2) * PANELS])
        across_ref[slot(k)] = pair[:, :PANELS]
        across_ref[slot(k + 1)] = pair[:, PANELS:]

    for k, target in ((0, near_ref), (1, distant_ref)):
        face = dot3(4.0 * rows_fold_ref[...], face_ref[k], NT)
        for at in range(0, grid, LANES):
            lanes = slice(at, at + LANES)
            target[:, lanes] = dot3(face, fold_ref[lanes, :], NT)

    for part in range(grid // LANES):
        lanes = slice(part * LANES, (part + 1) * LANES)

        def rows(index, _, lanes=lanes):
            at = pl.ds(pl.multiple_of(index * TALL, 8), TALL)
            diag = row_eigen_ref[at, :] + col_eigen_ref[:, lanes] + 2.0
            zero = diag - diag

            def run(first, steps):
                def leap(turn, pair):
                    one, two = pair
                    for k in range(UNROLL):
                        here = first + turn * UNROLL + k
                        along = along_ref[here, :, lanes]
                        across = across_ref[here, at, :]
                        layer = jnp.concatenate([along] * (TALL // 8), 0) + jnp.concatenate(
                            [across] * (LANES // PANELS), 1
                        )
                        one, two = (layer - two) + diag * one, one
                    return one, two

                return lax.fori_loop(0, steps // UNROLL, leap, (zero, zero))[0]

            lower = run(0, lower_steps)
            upper = run(base, upper_steps)
            both = row_ref[at, :] * col_ref[:, lanes] * (1.0 / TINY)
            out_ref[at, lanes] = low_ref[at, lanes] * (
                both * lower + near_ref[at, lanes]
            ) + high_ref[at, lanes] * (both * upper + distant_ref[at, lanes])
            return 0

        lax.fori_loop(0, block // TALL, rows, 0)


def plane_layers(depth, place, low, high, eigen, edge_value, face_v, side_v, fold, block):
    grid, cols = low.shape
    slots = whole_steps(depth // 2) + whole_steps(depth)
    f32 = jnp.float32
    wide = pl.BlockSpec((block, cols), lambda i, u: (i, 0))
    tall = pl.BlockSpec((block, 1), lambda i, u: (i, 0))
    flat = pl.BlockSpec((1, cols), lambda i, u: (0, 0))
    return pl.pallas_call(
        functools.partial(plane_body, depth),
        grid_spec=pltpu.PrefetchScalarGridSpec(
            num_scalar_prefetch=1,
            grid=(grid // block,),
            in_specs=[
                wide,
                wide,
                tall,
                flat,
                tall,
                flat,
                pl.BlockSpec(face_v.shape, lambda i, u: (0, 0, 0)),
                pl.BlockSpec(side_v.shape, lambda i, u: (0, 0, 0)),
                pl.BlockSpec((block, PANELS), lambda i, u: (i, 0)),
                pl.BlockSpec((cols, PANELS), lambda i, u: (0, 0)),
            ],
            out_specs=wide,
            scratch_shapes=[
                pltpu.VMEM((slots, 8, cols), f32),
                pltpu.VMEM((slots, block, PANELS), f32),
                pltpu.VMEM((6 * depth, depth * PANELS), jnp.bfloat16),
                pltpu.VMEM((block, cols), f32),
                pltpu.VMEM((block, cols), f32),
            ],
        ),
        out_shape=jax.ShapeDtypeStruct((grid, cols), f32),
        cost_estimate=pl.CostEstimate(
            flops=20 * depth * grid * cols, bytes_accessed=24 * grid * cols, transcendentals=0
        ),
    )(
        place, low, high, eigen[:grid, None], eigen[None, :], edge_value[:grid, None],
        edge_value[None, :], face_v, side_v, fold, fold,
    )


def build(mesh, grid, depth):
    slow, fast = mesh.shape["px"], mesh.shape["py"]
    devices = slow * fast
    half = devices // 2
    rows = grid // half
    edge = grid // PANELS
    groups = [list(range(half)), list(range(half, devices))]
    local = depth <= 32 and rows % 8 == 0
    split = grid // 2
    block = split // 2
    tables = {
        name: value.astype(np.float32) for name, value in small_tables(depth, grid, edge).items()
    }
    sine_np = sine_table(grid).astype(np.float32)
    sine_high = sine_np.astype(jnp.bfloat16)
    sine_low = (sine_np - sine_high.astype(np.float32)).astype(jnp.bfloat16)
    eigen_np = eigen_values(grid)
    fold_np = fold_panels(grid, edge).astype(np.float32)

    def exchange(x):
        return lax.all_to_all(
            x, AXES, split_axis=0, concat_axis=0, tiled=True, axis_index_groups=groups
        )

    def hop(x, bit):
        return lax.ppermute(x, "px", [(i, i ^ bit) for i in range(slow)])

    def swap(x):
        return lax.ppermute(x, "py", [(i, i ^ 1) for i in range(fast)])

    alternate = [list(range(0, fast, 2)), list(range(1, fast, 2))]

    def on_device(charge):
        rank = lax.axis_index(AXES)
        upper = (rank // half).astype(jnp.int32).reshape(1)
        is_upper = rank // half == 1
        start = (rank % half) * rows
        sine_pair = (jnp.asarray(sine_high), jnp.asarray(sine_low))
        fold = jnp.asarray(fold_np)
        tb = {name: jnp.asarray(value) for name, value in tables.items()}
        eigen = jnp.asarray(eigen_np.astype(np.float32))
        edge_value = jnp.asarray(sine_np[:, 0])
        my_eigen = lax.dynamic_slice_in_dim(eigen, start, rows, 0)
        my_edge = lax.dynamic_slice_in_dim(edge_value, start, rows, 0)
        my_fold = lax.dynamic_slice_in_dim(fold, start, rows, 0)
        mu = my_eigen[:, None] + eigen[None, :]
        parity = jnp.arange(grid) % 2
        edge_pair = jnp.stack([edge_value * (parity == 0), edge_value * (parity == 1)])
        my_pair = jnp.stack([my_edge * (parity[:rows] == 0), my_edge * (parity[:rows] == 1)])

        plane = charge.reshape(grid, grid)
        spectrum = double_product([plane], *sine_pair)
        spectrum = exchange(spectrum.reshape(half, rows, grid))
        coef, join = factors(mu, half)
        mixed = mixed_table(edge, depth, tb["wave_x"])
        corner = corner_table(edge, depth, tb["lift"])
        if local:
            index = (rank % half).astype(jnp.int32)
            place = jnp.where(is_upper, half - index, index + 1).reshape(1)
            weight = weights(depth, place, eigen[:split, None], eigen[None, :], block)
            spectrum, mixed, corner, weight = lax.optimization_barrier(
                (spectrum, mixed, corner, weight)
            )
        else:
            spectrum, mixed, corner = lax.optimization_barrier((spectrum, mixed, corner))
        if local:
            last = reach(upper, spectrum, mu)
        else:
            g, last = sweep(upper, spectrum, coef)
        far = lax.ppermute(last, AXES, [(i, i ^ half) for i in range(devices)])
        if local:
            u, sent, part = finish_boundary(
                upper, spectrum, coef, join, far, my_edge[:, None], edge_value[None, :], fold,
                my_fold,
            )
        else:
            u, outer = finish(upper, g, coef, join, far)

            face = dot(my_fold, dot(outer, fold), ((0,), (0,)))
            lines_y = jnp.einsum("tk,jkx->tjx", my_pair, u, precision=HIGHEST)
            lines_y = jnp.einsum("tjx,xb->tjb", lines_y, fold, precision=HIGHEST)
            lines_x = jnp.einsum("jkx,tx->tjk", u, edge_pair, precision=HIGHEST)
            lines_x = jnp.einsum("tjk,kb->tjb", lines_x, my_fold, precision=HIGHEST)
            lines = jnp.stack([lines_y, lines_x])
            lines = jnp.where(is_upper, lines[:, :, ::-1], lines)
            part = jnp.concatenate([face, lines.reshape(-1, PANELS)])
        middle = part.shape[0] // 2
        first = lax.axis_index("py") % 2 == 0
        part = part + swap(part)
        part = jnp.where(first, part[:middle], part[middle:])
        part = lax.all_gather(part, "py", axis=0, tiled=False, axis_index_groups=alternate).sum(0)
        bit = 1
        while bit < slow // 2:
            part = part + hop(part, bit)
            bit *= 2
        mine = jnp.concatenate([part, hop(part, bit)])
        if local:
            early, mine = lax.optimization_barrier((u, mine))
        mate = swap(mine)
        if local:
            u = exchange(early).reshape(grid, split)
        face_v, side_v = panel_potential(
            first.astype(jnp.int32).reshape(1), mine, mate, tb, mixed, corner
        )
        if local:
            sent = add_late(
                upper, sent, coef, join, my_edge[:, None], edge_value[None, :], face_v, side_v,
                my_fold, fold, split,
            )
            u, sent = lax.optimization_barrier((u, sent))
            sent = exchange(sent).reshape(grid, grid - split)
            layers = plane_layers(
                depth, place, *weight, eigen, edge_value, face_v, side_v, fold, block,
            )
            return double_product([u, layers, sent], *sine_pair)[None]
        else:
            near, distant = (
                4.0 * dot(dot(my_fold, face_v[i]), fold, ((1,), (1,))) for i in (0, 1)
            )
            along = 4.0 * dot(side_v[0], fold, ((1,), (1,)))
            across = 4.0 * dot(my_fold, side_v[1], ((1,), (1,)))
            u = add_ghost(
                upper, u, coef, join, my_edge[:, None], edge_value[None, :], along, across, near, distant
            )
            u = exchange(u).reshape(grid, grid)
        return double_product([u], *sine_pair)[None]

    return on_device


def solution(mesh):
    spec = P(AXES, None, None)

    def run(charge):
        depth, grid, _ = charge.shape
        body = build(mesh, grid, depth)
        return jax.shard_map(body, mesh=mesh, in_specs=(spec,), out_specs=spec, check_vma=False)(
            charge
        )

    return run
```
